32 devices in a mesh: pairs: 16 (over z, y, core), mod: 2 (over x).
Axes of the slice: x: 2, y: 2, z: 4, core: 2. Of those that a mesh axis runs over, the one named last changes fastest.
Arguments:
- inputs: bfloat16 [2, 64, 240, 768], P('mod', 'pairs'), may hold values from -6 to 6
- cotangent: bfloat16 [2, 64, 240, 768], P('mod', 'pairs'), may hold values from -6 to 6
- text_len: int32 [64], P('pairs'), may hold values from 8 to 40, as said below
- patch_count: int32 [64], P('pairs'), may hold values from 100 to 240, as said below
- norm1_gain: float32 [768], replicated, may hold values from 0.5 to 1.5
- norm1_bias: float32 [768], replicated, may hold values from -3 to 3
- qkv_weight: bfloat16 [768, 2304], replicated, may hold values from -0.21875 to 0.21875
- query_bias: float32 [768], replicated, may hold values from -3 to 3
- value_bias: float32 [768], replicated, may hold values from -3 to 3
- out_weight: bfloat16 [768, 768], replicated, may hold values from -0.875 to 0.875
- out_bias: float32 [768], replicated, may hold values from -3 to 3
- norm2_gain: float32 [768], replicated, may hold values from 0.5 to 1.5
- norm2_bias: float32 [768], replicated, may hold values from -3 to 3
- hidden_weight: bfloat16 [768, 3072], replicated, may hold values from -0.21875 to 0.21875
- hidden_bias: float32 [3072], replicated, may hold values from -3 to 3
- down_weight: bfloat16 [3072, 768], replicated, may hold values from -0.109375 to 0.109375
- down_bias: float32 [768], replicated, may hold values from -3 to 3
Outputs:
- block_out: bfloat16 [2, 64, 240, 768], P('mod', 'pairs')
- input_grad: bfloat16 [2, 64, 240, 768], P('mod', 'pairs')
- norm1_gain_grad: float32 [768], P(('pairs', 'mod'))
- norm1_bias_grad: float32 [768], P(('pairs', 'mod'))
- qkv_weight_grad: float32 [768, 2304], P(('pairs', 'mod'))
- query_bias_grad: float32 [768], P(('pairs', 'mod'))
- value_bias_grad: float32 [768], P(('pairs', 'mod'))
- out_weight_grad: float32 [768, 768], P(('pairs', 'mod'))
- out_bias_grad: float32 [768], P(('pairs', 'mod'))
- norm2_gain_grad: float32 [768], P(('pairs', 'mod'))
- norm2_bias_grad: float32 [768], P(('pairs', 'mod'))
- hidden_weight_grad: float32 [768, 3072], P(('pairs', 'mod'))
- hidden_bias_grad: float32 [3072], P(('pairs', 'mod'))
- down_weight_grad: float32 [3072, 768], P(('pairs', 'mod'))
- down_bias_grad: float32 [768], P(('pairs', 'mod'))
The draws below stay inside these ranges and needn't reach their ends.
Inputs may be any that keep to these rules, and one draw needn't show every extreme that they name: Rows 0 to text_len[p] - 1 of pair p's text slots are words, the rest padding; some pair has all 40. Rows 0 to patch_count[p] - 1 of pair p's patch slots are patches, the rest padding; some pair has all 240.
All inputs are finite; a program needn't handle non-finite values.
Results may differ from the reference program's by a relative error of at most 0.012.
Values may be sent and summed in bfloat16 or wider, within the bound.
A program may use at most 192 MiB of HBM per device.

```python
import jax
import jax.numpy as jnp
from jax import lax

D = 768
HEADS = 12
HEAD_DIM = 64
FF = 3072
TEXT = 40
SLOT = 240
PAIRS = 64


def draw_text_len(key, part):
    first_key, second_key = jax.random.split(jax.random.fold_in(key, 11))
    lowest = max(1, TEXT // 5)
    counts = jax.random.randint(first_key, (PAIRS,), lowest, TEXT + 1)
    chosen = jax.random.randint(second_key, (), 0, PAIRS)
    return jnp.where(jnp.arange(PAIRS) == chosen, TEXT, counts).astype(jnp.int32)


def draw_patch_count(key, part):
    first_key, second_key = jax.random.split(jax.random.fold_in(key, 23))
    lowest = max(1, SLOT * 5 // 12)
    counts = jax.random.randint(first_key, (PAIRS,), lowest, SLOT + 1)
    chosen = jax.random.randint(second_key, (), 0, PAIRS)
    return jnp.where(jnp.arange(PAIRS) == chosen, SLOT, counts).astype(jnp.int32)


def with_spikes(drawn, stream_key, source, target, shards_of, factor):
    def block_of(dim):
        return (jnp.arange(drawn.shape[dim]) // (drawn.shape[dim] // shards_of)).reshape((-1,) + (1,) * (drawn.ndim - 1 - dim))

    one_side = jax.random.permutation(stream_key, shards_of)[block_of(target)]
    far = (block_of(target) + shards_of // 2) % shards_of
    return jnp.where((block_of(source) == one_side) | (block_of(source) == far), factor * drawn, drawn)


def shard_levels(rng, shape, cuts, low, high):
    gain = 1.0
    for dim, shards_of in cuts:
        draws = jax.random.uniform(jax.random.fold_in(jax.random.fold_in(rng, 6), dim), (shards_of,), jnp.float32, low / len(cuts), high / len(cuts))
        gain = gain * jnp.repeat(jnp.exp(draws), shape[dim] // shards_of).reshape((-1,) + (1,) * (len(shape) - 1 - dim))
    return gain


def noise(key, shape, deviation, bound, pieces=(), held_as=jnp.bfloat16):
    array = deviation * jax.random.normal(key, shape, jnp.float32)
    if pieces:
        array = array * shard_levels(key, shape, pieces, -0.22, 0.18)
    return jnp.clip(array, -bound, bound).astype(held_as)


def heavy_noise(own_key, extent, width, reach, shards, heavy, kind=jnp.bfloat16):
    entries = width * jax.random.normal(own_key, extent, jnp.float32)
    if shards:
        entries = entries * shard_levels(own_key, extent, shards, -0.22, 0.18)
    return jnp.clip(with_spikes(entries, jax.random.fold_in(own_key, 3), *heavy), -reach, reach).astype(kind)


def setup_inputs(seed: int = 0) -> dict:
    splits = jax.random.split(jax.random.key(seed), 18)
    inputs = noise(splits[0], (2, PAIRS, SLOT, D), 1.0, 6.0, ((0, 2), (1, 16)))
    cotangent = heavy_noise(splits[1], (2, PAIRS, SLOT, D), 1.0, 6.0, ((0, 2), (1, 16)), (1, 3, 16, 2.0))
    text_len = draw_text_len(jax.random.fold_in(splits[17], 71), 0)
    patch_count = draw_patch_count(jax.random.fold_in(splits[17], 71), 0)
    norm1_gain = jnp.clip(1.0 + 0.1 * jax.random.normal(splits[4], (D,), jnp.float32), 0.5, 1.5)
    norm1_bias = noise(splits[5], (D,), 0.5, 3.0, (), jnp.float32)
    qkv_weight = noise(splits[6], (D, 3 * D), D ** -0.5, 0.21875)
    query_bias = noise(splits[7], (D,), 0.5, 3.0, (), jnp.float32)
    value_bias = noise(splits[8], (D,), 0.5, 3.0, (), jnp.float32)
    out_weight = noise(splits[9], (D, D), (D // 16) ** -0.5, 0.875)
    out_bias = noise(splits[10], (D,), 0.5, 3.0, (), jnp.float32)
    norm2_gain = jnp.clip(1.0 + 0.1 * jax.random.normal(splits[11], (D,), jnp.float32), 0.5, 1.5)
    norm2_bias = noise(splits[12], (D,), 0.5, 3.0, (), jnp.float32)
    hidden_weight = noise(splits[13], (D, FF), D ** -0.5, 0.21875)
    hidden_bias = noise(splits[14], (FF,), 0.5, 3.0, (), jnp.float32)
    down_weight = noise(splits[15], (FF, D), FF ** -0.5, 0.109375)
    down_bias = noise(splits[16], (D,), 0.5, 3.0, (), jnp.float32)
    return {"inputs": inputs, "cotangent": cotangent, "text_len": text_len, "patch_count": patch_count, "norm1_gain": norm1_gain, "norm1_bias": norm1_bias, "qkv_weight": qkv_weight, "query_bias": query_bias, "value_bias": value_bias, "out_weight": out_weight, "out_bias": out_bias, "norm2_gain": norm2_gain, "norm2_bias": norm2_bias, "hidden_weight": hidden_weight, "hidden_bias": hidden_bias, "down_weight": down_weight, "down_bias": down_bias}


@jax.custom_vjp
def low(v):
    return lax.optimization_barrier(v.astype(jnp.bfloat16)).astype(jnp.float32)

@jax.custom_vjp
def low_back(v):
    return v

def low_keep(v):
    return (low(v), None)

def low_pass(kept, grad):
    return (grad,)

def back_keep(v):
    return (v, None)

def back_low(kept, grad):
    return (low(grad),)
low.defvjp(low_keep, low_pass)
low_back.defvjp(back_keep, back_low)
EPSILON = 1e-06
MASKED = -1e+30
PRECISE = lax.Precision.HIGHEST

def layer_norm(values, norm_gain, norm_shift):
    centre = lax.optimization_barrier(jnp.mean(values, axis=-1, keepdims=True))
    centred = values - centre
    spread = lax.optimization_barrier(jnp.mean(centred * centred, axis=-1, keepdims=True))
    return centred * lax.rsqrt(spread + EPSILON) * norm_gain + norm_shift

def pair_block(sequence, key_mask, params):
    norm1_gain, norm1_bias, qkv_weight, query_bias, value_bias, out_weight, out_bias, norm2_gain, norm2_bias, hidden_weight, hidden_bias, down_weight, down_bias = params
    model_width = sequence.shape[-1]
    normal1 = low(layer_norm(sequence, norm1_gain, norm1_bias))
    projected = jnp.einsum('gtd,de->gte', normal1, qkv_weight, precision=PRECISE)
    queries = low(low_back((projected[..., :model_width] + query_bias) * 0.125))
    key_rows = low(low_back(projected[..., model_width:2 * model_width]))
    values = low(low_back(projected[..., 2 * model_width:] + value_bias))
    head_shape = sequence.shape[:2] + (HEADS, HEAD_DIM)
    scores = low_back(jnp.einsum('gqhe,gkhe->ghqk', queries.reshape(head_shape), key_rows.reshape(head_shape), precision=PRECISE))
    scores = jnp.where(key_mask[:, None, None, :] > 0, scores, MASKED)
    weights = low(jax.nn.softmax(scores, axis=-1))
    mixed_heads = jnp.einsum('ghqk,gkhe->gqhe', weights, values.reshape(head_shape), precision=PRECISE)
    mixed_heads = low(low_back(mixed_heads.reshape(sequence.shape)))
    attended = jnp.einsum('gtd,de->gte', mixed_heads, out_weight, precision=PRECISE) + out_bias
    hidden = sequence + low_back(attended)
    normal2 = low(layer_norm(hidden, norm2_gain, norm2_bias))
    before = low_back(jnp.einsum('gtd,df->gtf', normal2, hidden_weight, precision=PRECISE) + hidden_bias)
    activated = low(jax.nn.gelu(before, approximate=False))
    branch = jnp.einsum('gtf,fd->gtd', activated, down_weight, precision=PRECISE) + down_bias
    return hidden + low_back(branch)

def forward(tokens, params, text_len, patch_count):
    pair_total = tokens.shape[1]
    model_width = tokens.shape[3]
    key_count = TEXT + SLOT
    sequence = jnp.concatenate([tokens[0, :, :TEXT], tokens[1]], axis=1)
    slot_index = jnp.arange(SLOT, dtype=jnp.int32)
    text_live = slot_index[None, :TEXT] < text_len[:, None].astype(jnp.int32)
    patch_live = slot_index[None, :] < patch_count[:, None].astype(jnp.int32)
    live_rows = jnp.concatenate([text_live, patch_live], axis=1).astype(jnp.float32)
    limit = max(1, 4096 // key_count)
    group_size = max((divisor for divisor in range(1, limit + 1) if pair_total % divisor == 0))
    group_count = pair_total // group_size
    blocks = sequence.reshape(group_count, group_size, key_count, model_width)
    mask_blocks = live_rows.reshape(group_count, group_size, key_count)
    stepper = jax.checkpoint(lambda bundle: pair_block(bundle[0], bundle[1], params))
    outcome = lax.map(stepper, (blocks, mask_blocks))
    outcome = outcome.reshape(pair_total, key_count, model_width) * live_rows[..., None]
    text_part = jnp.pad(outcome[:, :TEXT], ((0, 0), (0, SLOT - TEXT), (0, 0)))
    return jnp.stack([text_part, outcome[:, TEXT:]])

def reference(inputs, cotangent, text_len, patch_count, norm1_gain, norm1_bias, qkv_weight, query_bias, value_bias, out_weight, out_bias, norm2_gain, norm2_bias, hidden_weight, hidden_bias, down_weight, down_bias):
    params = tuple((member.astype(jnp.float32) for member in (norm1_gain, norm1_bias, qkv_weight, query_bias, value_bias, out_weight, out_bias, norm2_gain, norm2_bias, hidden_weight, hidden_bias, down_weight, down_bias)))

    def whole(tokens, *weights_in):
        return forward(tokens, weights_in, text_len, patch_count)
    result, pull_back = jax.vjp(whole, inputs.astype(jnp.float32), *params)
    gradients = pull_back(cotangent.astype(jnp.float32))
    return (result.astype(jnp.bfloat16), gradients[0].astype(jnp.bfloat16), gradients[1], gradients[2], gradients[3], gradients[4], gradients[5], gradients[6], gradients[7], gradients[8], gradients[9], gradients[10], gradients[11], gradients[12], gradients[13])
```

```python
import functools

import jax
import jax.numpy as jnp
from jax import lax
from jax.experimental import pallas as pl
from jax.experimental.pallas import tpu as pltpu
from jax.sharding import PartitionSpec as P

HEADS = 12
HEAD_DIM = 64
TEXT = 40
EPSILON = 1e-06
MASKED = -1e30
F32 = jnp.float32
BF16 = jnp.bfloat16
VMEM_LIMIT = 60 * 1024 * 1024


def padded(count):
    return -(-count // 32) * 32


def dot(a, b, ca=1, cb=0):
    return lax.dot_general(a, b, (((ca,), (cb,)), ((), ())), preferred_element_type=F32)


def norm_parts(values):
    centre = jnp.mean(values, axis=-1, keepdims=True)
    centred = values - centre
    spread = jnp.mean(centred * centred, axis=-1, keepdims=True)
    factor = lax.rsqrt(spread + EPSILON)
    return centred * factor, factor


def norm_back(grad_out, normed, factor, norm_gain):
    grad_norm = grad_out * norm_gain
    mean_grad = jnp.mean(grad_norm, axis=-1, keepdims=True)
    second = jnp.mean(grad_norm * normed, axis=-1, keepdims=True)
    return (grad_norm - mean_grad - normed * second) * factor


def live_slots(index, text_count, patch_count, slots):
    return (index < patch_count) | ((index >= slots) & (index - slots < text_count))


def live_rows(lens, pairs, rows, slots):
    parts = []
    for pair in range(pairs):
        index = lax.broadcasted_iota(jnp.int32, (rows, 1), 0)
        parts.append(live_slots(index, lens[pair], lens[pairs + pair], slots).astype(F32))
    return jnp.concatenate(parts, axis=0)


def forward_kernel(
    slots, lens, seq, gain, shift, wqkv, qkv_bias, wout, out_bias, q_out, k_out, v_out, mixed, hidden
):
    pairs, rows, width = seq.shape
    tokens = seq[...].reshape(pairs * rows, width).astype(F32)
    normed, _ = norm_parts(tokens)
    normal = (normed * gain[...] + shift[...]).astype(BF16)
    for part, ref in enumerate((q_out, k_out, v_out)):
        cols = slice(part * width, (part + 1) * width)
        made = dot(normal, wqkv[:, cols]) + qkv_bias[:, cols]
        if part == 0:
            made = made * 0.125
        ref[...] = made.astype(BF16).reshape(pairs, rows, width)
    first = lax.broadcasted_iota(jnp.int32, (rows, 128), 1) < HEAD_DIM
    column = lax.broadcasted_iota(jnp.int32, (1, rows), 1)
    groups = width // 128

    def step(it, carry):
        pair = it // groups
        off = pl.multiple_of((it % groups) * 128, 128)
        live = live_slots(column, lens[pair], lens[pairs + pair], slots)
        q2 = q_out[pair, :, pl.ds(off, 128)]
        k2 = k_out[pair, :, pl.ds(off, 128)]
        v2 = v_out[pair, :, pl.ds(off, 128)]
        halves = []
        for half in range(2):
            keep = first if half == 0 else ~first
            qm = jnp.where(keep, q2, jnp.zeros_like(q2))
            scores = jnp.where(live, dot(qm, k2, 1, 1), MASKED)
            highest = jnp.max(scores, axis=-1, keepdims=True)
            shifted = jnp.exp(scores - highest)
            total = jnp.sum(shifted, axis=-1, keepdims=True)
            halves.append(dot(shifted.astype(BF16), v2) / total)
        mixed[pair, :, pl.ds(off, 128)] = jnp.where(first, halves[0], halves[1]).astype(BF16)
        return carry

    lax.fori_loop(0, pairs * groups, step, 0)
    rows_mixed = mixed[...].reshape(pairs * rows, width)
    hidden[...] = tokens + dot(rows_mixed, wout[...]) + out_bias[...]


def gelu_parts(values):
    cumulative = 0.5 * (1.0 + lax.erf(values * 0.7071067811865476))
    density = jnp.exp(-0.5 * values * values) * 0.3989422804014327
    return values * cumulative, cumulative + values * density


def feed_kernel(
    pairs,
    slots,
    lens,
    hidden,
    cot,
    gain,
    shift,
    wh,
    hbias,
    wd,
    dbias,
    result,
    grad_hidden,
    wh_grad,
    wd_grad,
    hb_grad,
    vectors,
    normal,
    gdown,
    total,
    gnormal,
):
    chunk = pl.program_id(0)
    count = pl.num_programs(0)
    rows = hidden.shape[0] // pairs
    live = live_rows(lens, pairs, rows, slots)

    @pl.when(chunk == 0)
    def _():
        normed, _ = norm_parts(hidden[...])
        normal[...] = (normed * gain[...] + shift[...]).astype(BF16)
        gdown[...] = (cot[...].astype(F32) * live).astype(BF16)
        total[...] = hidden[...] + dbias[...]
        gnormal[...] = jnp.zeros_like(gnormal)

    before = dot(normal[...], wh[...]) + hbias[...]
    active, slope = gelu_parts(before)
    active = active.astype(BF16)
    total[...] += dot(active, wd[...])
    wd_grad[...] = dot(active, gdown[...], 0, 0).astype(BF16)
    gbefore = (dot(gdown[...], wd[...], 1, 1) * slope).astype(BF16)
    gnormal[...] += dot(gbefore, wh[...], 1, 1)
    wh_grad[...] = dot(normal[...], gbefore, 0, 0).astype(BF16)
    hb_grad[...] = jnp.sum(gbefore.astype(F32), axis=0, keepdims=True)

    @pl.when(chunk == count - 1)
    def _():
        result[...] = (total[...] * live).astype(BF16)
        normed, factor = norm_parts(hidden[...])
        gnorm = gnormal[...]
        vectors[0:1, :] = jnp.sum(gnorm * normed, axis=0, keepdims=True)
        vectors[1:2, :] = jnp.sum(gnorm, axis=0, keepdims=True)
        down = gdown[...].astype(F32)
        vectors[2:3, :] = jnp.sum(down, axis=0, keepdims=True)
        made = down + norm_back(gnorm, normed, factor, gain[...])
        vectors[3:4, :] = jnp.sum(made.astype(BF16).astype(F32), axis=0, keepdims=True)
        grad_hidden[...] = made


def backward_kernel(
    slots,
    lens,
    seq,
    gain,
    shift,
    q_in,
    k_in,
    v_in,
    mixed,
    ghidden,
    wqkv,
    wout,
    input_grad,
    weight_grad,
    vectors,
    gmixed,
    gproj,
):
    pairs, rows, width = seq.shape
    every = pairs * rows
    gattended = ghidden[...].astype(BF16)
    gmixed[...] = dot(gattended, wout[...], 1, 1).astype(BF16).reshape(pairs, rows, width)
    weight_grad[:, 3 * width : 4 * width] = dot(
        mixed[...].reshape(every, width), gattended, 0, 0
    ).astype(BF16)
    first = lax.broadcasted_iota(jnp.int32, (rows, 128), 1) < HEAD_DIM
    index = lax.broadcasted_iota(jnp.int32, (rows, 1), 0)
    groups = width // 128

    def step(it, carry):
        pair = it // groups
        base = (it % groups) * 128
        off = pl.multiple_of(base, 128)
        live = live_slots(index, lens[pair], lens[pairs + pair], slots)
        q2 = q_in[pair, :, pl.ds(off, 128)]
        k2 = k_in[pair, :, pl.ds(off, 128)]
        v2 = v_in[pair, :, pl.ds(off, 128)]
        g2 = gmixed[pair, :, pl.ds(off, 128)]
        gq = gk = gv = None
        for half in range(2):
            keep = first if half == 0 else ~first
            zero = jnp.zeros_like(q2)
            qm = jnp.where(keep, q2, zero)
            km = jnp.where(keep, k2, zero)
            gm = jnp.where(keep, g2, zero)
            scores = jnp.where(live, dot(k2, qm, 1, 1), MASKED)
            highest = jnp.max(scores, axis=0, keepdims=True)
            shifted = jnp.exp(scores - highest)
            probs = shifted * (1.0 / jnp.sum(shifted, axis=0, keepdims=True))
            gprobs = dot(v2, gm, 1, 1)
            row_dot = jnp.sum(probs * gprobs, axis=0, keepdims=True)
            gscores = (probs * (gprobs - row_dot)).astype(BF16)
            new_v = dot(probs.astype(BF16), gm)
            new_k = dot(gscores, qm)
            new_q = dot(gscores, km, 0, 0)
            gq = new_q if gq is None else gq + new_q
            gk = new_k if gk is None else gk + new_k
            gv = new_v if gv is None else gv + new_v
        gproj[pair, :, pl.ds(off, 128)] = (gq * 0.125).astype(BF16)
        gproj[pair, :, pl.ds(pl.multiple_of(base + width, 128), 128)] = gk.astype(BF16)
        gproj[pair, :, pl.ds(pl.multiple_of(base + 2 * width, 128), 128)] = gv.astype(BF16)
        return carry

    lax.fori_loop(0, pairs * groups, step, 0)
    tokens = seq[...].reshape(every, width).astype(F32)
    normed, factor = norm_parts(tokens)
    normal = (normed * gain[...] + shift[...]).astype(BF16)
    gnormal = jnp.zeros((every, width), F32)
    for part in range(3):
        cols = slice(part * width, (part + 1) * width)
        piece = gproj[:, :, cols].reshape(every, width)
        gnormal += dot(piece, wqkv[:, cols], 1, 1)
        weight_grad[:, cols] = dot(normal, piece, 0, 0).astype(BF16)
        if part == 0:
            vectors[2:3, :] = jnp.sum(piece.astype(F32), axis=0, keepdims=True)
        if part == 2:
            vectors[3:4, :] = jnp.sum(piece.astype(F32), axis=0, keepdims=True)
    vectors[0:1, :] = jnp.sum(gnormal * normed, axis=0, keepdims=True)
    vectors[1:2, :] = jnp.sum(gnormal, axis=0, keepdims=True)
    live = live_rows(lens, pairs, rows, slots)
    made = ghidden[...] + norm_back(gnormal, normed, factor, gain[...])
    input_grad[...] = (made * live).astype(BF16).reshape(pairs, rows, width)


def whole_spec():
    return pl.BlockSpec(memory_space=pltpu.VMEM)


def smem_spec():
    return pl.BlockSpec(memory_space=pltpu.SMEM)


def shape(dims, kind):
    return jax.ShapeDtypeStruct(dims, kind)


def run_forward(lens, seq, gain, shift, wqkv, qkv_bias, wout, out_bias, slots):
    pairs, rows, width = seq.shape
    seq_shape = shape((pairs, rows, width), BF16)
    every = pairs * rows
    return pl.pallas_call(
        functools.partial(forward_kernel, slots),
        out_shape=[seq_shape] * 4 + [shape((every, width), F32)],
        in_specs=[smem_spec()] + [whole_spec()] * 7,
        out_specs=[whole_spec()] * 5,
        compiler_params=pltpu.CompilerParams(vmem_limit_bytes=VMEM_LIMIT),
        cost_estimate=pl.CostEstimate(
            flops=2 * every * width * width * 4 + 8 * every * rows * width,
            bytes_accessed=12 * 2**20,
            transcendentals=every * rows * HEADS,
        ),
        name="attention_forward",
    )(lens, seq, gain, shift, wqkv, qkv_bias, wout, out_bias)


def run_feed(lens, hidden, cot, gain, shift, wh, hbias, wd, dbias, pairs, slots, chunks):
    every, width = hidden.shape
    ff = wh.shape[1]
    size = ff // chunks
    fixed = lambda dims: pl.BlockSpec(dims, lambda c: (0, 0))
    columns = lambda r: pl.BlockSpec((r, size), lambda c: (0, c))
    rows = pl.BlockSpec((size, width), lambda c: (c, 0))
    return pl.pallas_call(
        functools.partial(feed_kernel, pairs, slots),
        grid=(chunks,),
        out_shape=[
            shape((every, width), BF16),
            shape((every, width), F32),
            shape((width, ff), BF16),
            shape((ff, width), BF16),
            shape((1, ff), F32),
            shape((8, width), F32),
        ],
        in_specs=[
            smem_spec(),
            fixed((every, width)),
            fixed((every, width)),
            fixed((1, width)),
            fixed((1, width)),
            columns(width),
            columns(1),
            rows,
            fixed((1, width)),
        ],
        out_specs=[
            fixed((every, width)),
            fixed((every, width)),
            columns(width),
            rows,
            columns(1),
            fixed((8, width)),
        ],
        scratch_shapes=[
            pltpu.VMEM((every, width), BF16),
            pltpu.VMEM((every, width), BF16),
            pltpu.VMEM((every, width), F32),
            pltpu.VMEM((every, width), F32),
        ],
        compiler_params=pltpu.CompilerParams(vmem_limit_bytes=VMEM_LIMIT),
        cost_estimate=pl.CostEstimate(
            flops=12 * every * width * ff,
            bytes_accessed=24 * 2**20,
            transcendentals=2 * every * ff,
        ),
        name="feed_forward",
    )(lens, hidden, cot, gain, shift, wh, hbias, wd, dbias)


def run_backward(lens, seq, gain, shift, q, k, v, mixed, ghidden, wqkv, wout, slots):
    pairs, rows, width = seq.shape
    every = pairs * rows
    return pl.pallas_call(
        functools.partial(backward_kernel, slots),
        out_shape=[
            shape((pairs, rows, width), BF16),
            shape((width, 4 * width), BF16),
            shape((8, width), F32),
        ],
        in_specs=[smem_spec()] + [whole_spec()] * 10,
        out_specs=[whole_spec()] * 3,
        scratch_shapes=[
            pltpu.VMEM((pairs, rows, width), BF16),
            pltpu.VMEM((pairs, rows, 3 * width), BF16),
        ],
        compiler_params=pltpu.CompilerParams(vmem_limit_bytes=VMEM_LIMIT),
        cost_estimate=pl.CostEstimate(
            flops=4 * every * width * width * 4 + 20 * every * rows * width,
            bytes_accessed=20 * 2**20,
            transcendentals=every * rows * HEADS,
        ),
        name="attention_backward",
    )(lens, seq, gain, shift, q, k, v, mixed, ghidden, wqkv, wout)


def pair_bits():
    return lax.axis_size("pairs").bit_length() - 1


def swapped(array, axis, bit):
    size = lax.axis_size(axis)
    return lax.ppermute(array, axis, [(i, i ^ (1 << bit)) for i in range(size)])


def split_dims(array):
    bits = pair_bits() + 1
    return array.reshape((2,) * bits + (array.shape[0] >> bits,) + array.shape[1:])


def stage_orders():
    bits = pair_bits()
    ring = ["mod", 1, 2]
    orders = []
    for turn in range(3):
        orders.append([0] + ring[turn:] + ring[:turn] + list(range(3, bits)))
    return orders


def half_sum(array, names, name, last):
    axis, bit = ("mod", 0) if name == "mod" else ("pairs", name)
    mine = (lax.axis_index(axis) >> bit) & 1
    dim = names.index(name)
    sent = lax.dynamic_index_in_dim(array, 1 - mine, dim, keepdims=False)
    kept = lax.dynamic_index_in_dim(array, mine, dim, keepdims=False)
    came = swapped(sent, axis, bit)
    total = kept.astype(F32) + came.astype(F32)
    return (total if last else total.astype(BF16)), names[:dim] + names[dim + 1 :]


def scattered(array):
    width = array.shape[1]
    names0 = list(range(pair_bits() - 1, -1, -1)) + ["mod"]
    first, names1 = half_sum(split_dims(array), names0, 0, False)
    third = -(-width // 3 // 128) * 128
    pieces = []
    for turn, order in enumerate(stage_orders()):
        piece = first[..., turn * third : min(width, (turn + 1) * third)]
        names = list(names1)
        for place, name in enumerate(order[1:]):
            piece, names = half_sum(piece, names, name, place == len(order) - 2)
        pieces.append(piece)
    return jnp.concatenate(pieces, axis=1)


def on_device(
    inputs,
    cotangent,
    text_len,
    patch_count,
    norm1_gain,
    norm1_bias,
    qkv_weight,
    query_bias,
    value_bias,
    out_weight,
    out_bias,
    norm2_gain,
    norm2_bias,
    hidden_weight,
    hidden_bias,
    down_weight,
    down_bias,
):
    _, group, slots, width = inputs.shape
    half = group // 2
    rows = padded(TEXT + slots)
    mod = lax.axis_index("mod")
    is_text = mod == 0
    lens = lax.dynamic_slice_in_dim(jnp.stack([text_len, patch_count]), mod * half, half, 1)
    lens = lens.reshape(-1)

    def gathered(array):
        local = array[0]
        patches = lax.ppermute(local[:half], "mod", [(1, 0)])
        texts = lax.ppermute(local[half:, :TEXT], "mod", [(0, 1)])
        patches = jnp.where(is_text, patches, local[half:])
        texts = jnp.where(is_text, local[:half, :TEXT], texts)
        blank = jnp.zeros((half, rows - slots - TEXT, width), array.dtype)
        return jnp.concatenate([patches, texts, blank], axis=1)

    def returned(array):
        patches, texts = array[:, :slots], array[:, slots : slots + TEXT]
        far_patches = lax.ppermute(patches, "mod", [(0, 1)])
        far_texts = lax.ppermute(texts, "mod", [(1, 0)])
        texts = jnp.concatenate([texts, far_texts], axis=0)
        texts = jnp.pad(texts, ((0, 0), (0, slots - TEXT), (0, 0)))
        patches = jnp.concatenate([far_patches, patches], axis=0)
        return jnp.where(is_text, texts, patches)[None]

    row = lambda vector: vector.reshape(1, -1)
    seq = gathered(inputs)
    cot = gathered(cotangent)
    qkv_bias = row(jnp.concatenate([query_bias, jnp.zeros_like(query_bias), value_bias]))
    q, k, v, mixed, hidden = run_forward(
        lens, seq, row(norm1_gain), row(norm1_bias), qkv_weight, qkv_bias, out_weight, row(out_bias), slots
    )
    result, ghidden, wh_grad, wd_grad, hb_grad, vec2 = run_feed(
        lens,
        hidden,
        cot.reshape(half * rows, width),
        row(norm2_gain),
        row(norm2_bias),
        hidden_weight,
        row(hidden_bias),
        down_weight,
        row(down_bias),
        half,
        slots,
        8,
    )
    block_out = returned(result.reshape(half, rows, width))
    wd_out = scattered(wd_grad)
    wh_out = scattered(wh_grad)
    input_rows, qkvo_grad, vec1 = run_backward(
        lens, seq, row(norm1_gain), row(norm1_bias), q, k, v, mixed, ghidden, qkv_weight, out_weight, slots
    )
    input_grad = returned(input_rows)
    strip = jnp.concatenate([vec1[:4], vec2[:4]], axis=0).T
    strip = jnp.concatenate([strip, hb_grad.reshape(width, -1)], axis=1).astype(BF16)
    strip = jnp.pad(strip, ((0, 0), (0, 128 - strip.shape[1])))
    qkvo_out = scattered(jnp.concatenate([qkvo_grad, strip], axis=1))
    vec_out = qkvo_out[:, 4 * width :]
    return (
        block_out,
        input_grad,
        vec_out[:, 0],
        vec_out[:, 1],
        qkvo_out[:, : 3 * width],
        vec_out[:, 2],
        vec_out[:, 3],
        qkvo_out[:, 3 * width : 4 * width],
        vec_out[:, 7],
        vec_out[:, 4],
        vec_out[:, 5],
        wh_out,
        vec_out[:, 8 : 8 + hidden_bias.shape[0] // width].reshape(-1),
        wd_out,
        vec_out[:, 6],
    )


def solution(mesh):
    whole = P()
    split = P("mod", "pairs", None, None)
    vector = P(("pairs", "mod"))
    matrix = P(("pairs", "mod"), None)
    return jax.shard_map(
        on_device,
        mesh=mesh,
        in_specs=(split, split, P("pairs"), P("pairs")) + (whole,) * 13,
        out_specs=(
            split,
            split,
            vector,
            vector,
            matrix,
            vector,
            vector,
            matrix,
            vector,
            vector,
            vector,
            matrix,
            vector,
            matrix,
            vector,
        ),
        check_vma=False,
    )
```

```python
import functools

import jax
import jax.numpy as jnp
from jax import lax
from jax.experimental import pallas as pl
from jax.experimental.pallas import tpu as pltpu
from jax.sharding import PartitionSpec as P

HEADS = 12
HEAD_DIM = 64
TEXT = 40
EPSILON = 1e-06
MASKED = -1e30
F32 = jnp.float32
BF16 = jnp.bfloat16
VMEM_LIMIT = 60 * 1024 * 1024


def padded(count):
    return -(-count // 32) * 32


def dot(a, b, ca=1, cb=0):
    return lax.dot_general(a, b, (((ca,), (cb,)), ((), ())), preferred_element_type=F32)


def norm_parts(values):
    centre = jnp.mean(values, axis=-1, keepdims=True)
    centred = values - centre
    spread = jnp.mean(centred * centred, axis=-1, keepdims=True)
    factor = lax.rsqrt(spread + EPSILON)
    return centred * factor, factor


def norm_back(grad_out, normed, factor, norm_gain):
    grad_norm = grad_out * norm_gain
    mean_grad = jnp.mean(grad_norm, axis=-1, keepdims=True)
    second = jnp.mean(grad_norm * normed, axis=-1, keepdims=True)
    return (grad_norm - mean_grad - normed * second) * factor


def live_slots(index, text_count, patch_count, slots):
    return (index < patch_count) | ((index >= slots) & (index - slots < text_count))


def live_rows(lens, pairs, rows, slots):
    parts = []
    for pair in range(pairs):
        index = lax.broadcasted_iota(jnp.int32, (rows, 1), 0)
        parts.append(live_slots(index, lens[pair], lens[pairs + pair], slots).astype(F32))
    return jnp.concatenate(parts, axis=0)


def forward_kernel(
    slots, lens, seq, gain, shift, wqkv, qkv_bias, wout, out_bias, q_out, k_out, v_out, mixed, hidden
):
    pairs, rows, width = seq.shape
    tokens = seq[...].reshape(pairs * rows, width).astype(F32)
    normed, _ = norm_parts(tokens)
    normal = (normed * gain[...] + shift[...]).astype(BF16)
    for part, ref in enumerate((q_out, k_out, v_out)):
        cols = slice(part * width, (part + 1) * width)
        made = dot(normal, wqkv[:, cols]) + qkv_bias[:, cols]
        if part == 0:
            made = made * 0.125
        ref[...] = made.astype(BF16).reshape(pairs, rows, width)
    first = lax.broadcasted_iota(jnp.int32, (rows, 128), 1) < HEAD_DIM
    column = lax.broadcasted_iota(jnp.int32, (1, rows), 1)
    groups = width // 128

    def step(it, carry):
        pair = it // groups
        off = pl.multiple_of((it % groups) * 128, 128)
        live = live_slots(column, lens[pair], lens[pairs + pair], slots)
        q2 = q_out[pair, :, pl.ds(off, 128)]
        k2 = k_out[pair, :, pl.ds(off, 128)]
        v2 = v_out[pair, :, pl.ds(off, 128)]
        halves = []
        for half in range(2):
            keep = first if half == 0 else ~first
            qm = jnp.where(keep, q2, jnp.zeros_like(q2))
            scores = jnp.where(live, dot(qm, k2, 1, 1), MASKED)
            highest = jnp.max(scores, axis=-1, keepdims=True)
            shifted = jnp.exp(scores - highest)
            total = jnp.sum(shifted, axis=-1, keepdims=True)
            halves.append(dot(shifted.astype(BF16), v2) / total)
        mixed[pair, :, pl.ds(off, 128)] = jnp.where(first, halves[0], halves[1]).astype(BF16)
        return carry

    lax.fori_loop(0, pairs * groups, step, 0)
    rows_mixed = mixed[...].reshape(pairs * rows, width)
    hidden[...] = tokens + dot(rows_mixed, wout[...]) + out_bias[...]


def gelu_parts(values):
    cumulative = 0.5 * (1.0 + lax.erf(values * 0.7071067811865476))
    density = jnp.exp(-0.5 * values * values) * 0.3989422804014327
    return values * cumulative, cumulative + values * density


def feed_kernel(
    pairs,
    slots,
    lens,
    hidden,
    cot,
    gain,
    shift,
    wh,
    hbias,
    wd,
    dbias,
    order,
    result,
    grad_hidden,
    wh_grad,
    wd_grad,
    hb_grad,
    vectors,
    normal,
    ordered,
    gdown,
    total,
    gnormal,
):
    chunk = pl.program_id(0)
    count = pl.num_programs(0)
    rows = hidden.shape[0] // pairs
    live = live_rows(lens, pairs, rows, slots)

    @pl.when(chunk == 0)
    def _():
        normed, _ = norm_parts(hidden[...])
        made = (normed * gain[...] + shift[...]).astype(BF16)
        normal[...] = made
        ordered[...] = dot(made, order[...]).astype(BF16)
        gdown[...] = (cot[...].astype(F32) * live).astype(BF16)
        total[...] = hidden[...] + dbias[...]
        gnormal[...] = jnp.zeros_like(gnormal)

    before = dot(normal[...], wh[...]) + hbias[...]
    active, slope = gelu_parts(before)
    active = active.astype(BF16)
    total[...] += dot(active, wd[...])
    fresh = dot(active, gdown[...], 0, 0)
    if wd_grad.ndim == 2:
        wd_grad[...] = fresh.astype(BF16)
    else:
        size = fresh.shape[0] // 4
        base = 2 * pairs
        for core in range(2):
            for mod in range(2):
                start = (2 * core + mod) * size
                piece = fresh[start : start + size].reshape(size // 8, 8, fresh.shape[1])
                wd_grad[lens[base + core], 0, 0, lens[base + 2 + mod], 0] = piece.astype(BF16)
    gbefore = (dot(gdown[...], wd[...], 1, 1) * slope).astype(BF16)
    gnormal[...] += dot(gbefore, wh[...], 1, 1)
    wh_grad[...] = dot(ordered[...], gbefore, 0, 0).reshape(wh_grad.shape).astype(BF16)
    hb_grad[...] = jnp.sum(gbefore.astype(F32), axis=0, keepdims=True)

    @pl.when(chunk == count - 1)
    def _():
        result[...] = (total[...] * live).astype(BF16)
        normed, factor = norm_parts(hidden[...])
        gnorm = gnormal[...]
        vectors[0:1, :] = jnp.sum(gnorm * normed, axis=0, keepdims=True)
        vectors[1:2, :] = jnp.sum(gnorm, axis=0, keepdims=True)
        down = gdown[...].astype(F32)
        vectors[2:3, :] = jnp.sum(down, axis=0, keepdims=True)
        made = down + norm_back(gnorm, normed, factor, gain[...])
        vectors[3:4, :] = jnp.sum(made.astype(BF16).astype(F32), axis=0, keepdims=True)
        grad_hidden[...] = made


def backward_kernel(
    slots,
    lens,
    seq,
    gain,
    shift,
    q_in,
    k_in,
    v_in,
    mixed,
    ghidden,
    wqkv,
    wout,
    order,
    input_grad,
    weight_grad,
    vectors,
    gmixed,
    gproj,
):
    pairs, rows, width = seq.shape
    every = pairs * rows
    gattended = ghidden[...].astype(BF16)
    gmixed[...] = dot(gattended, wout[...], 1, 1).astype(BF16).reshape(pairs, rows, width)
    ordered = dot(mixed[...].reshape(every, width), order[...]).astype(BF16)

    def put(first, last, value):
        target = (slice(None),) * (len(weight_grad.shape) - 1) + (slice(first, last),)
        value = value.reshape(weight_grad.shape[:-1] + (last - first,))
        weight_grad[target] = value.astype(BF16)

    put(3 * width, 4 * width, dot(ordered, gattended, 0, 0))
    first = lax.broadcasted_iota(jnp.int32, (rows, 128), 1) < HEAD_DIM
    index = lax.broadcasted_iota(jnp.int32, (rows, 1), 0)
    groups = width // 128

    def step(it, carry):
        pair = it // groups
        base = (it % groups) * 128
        off = pl.multiple_of(base, 128)
        live = live_slots(index, lens[pair], lens[pairs + pair], slots)
        q2 = q_in[pair, :, pl.ds(off, 128)]
        k2 = k_in[pair, :, pl.ds(off, 128)]
        v2 = v_in[pair, :, pl.ds(off, 128)]
        g2 = gmixed[pair, :, pl.ds(off, 128)]
        gq = gk = gv = None
        for half in range(2):
            keep = first if half == 0 else ~first
            zero = jnp.zeros_like(q2)
            qm = jnp.where(keep, q2, zero)
            km = jnp.where(keep, k2, zero)
            gm = jnp.where(keep, g2, zero)
            scores = jnp.where(live, dot(k2, qm, 1, 1), MASKED)
            highest = jnp.max(scores, axis=0, keepdims=True)
            shifted = jnp.exp(scores - highest)
            probs = shifted * (1.0 / jnp.sum(shifted, axis=0, keepdims=True))
            gprobs = dot(v2, gm, 1, 1)
            row_dot = jnp.sum(probs * gprobs, axis=0, keepdims=True)
            gscores = (probs * (gprobs - row_dot)).astype(BF16)
            new_v = dot(probs.astype(BF16), gm)
            new_k = dot(gscores, qm)
            new_q = dot(gscores, km, 0, 0)
            gq = new_q if gq is None else gq + new_q
            gk = new_k if gk is None else gk + new_k
            gv = new_v if gv is None else gv + new_v
        gproj[pair, :, pl.ds(off, 128)] = (gq * 0.125).astype(BF16)
        gproj[pair, :, pl.ds(pl.multiple_of(base + width, 128), 128)] = gk.astype(BF16)
        gproj[pair, :, pl.ds(pl.multiple_of(base + 2 * width, 128), 128)] = gv.astype(BF16)
        return carry

    lax.fori_loop(0, pairs * groups, step, 0)
    tokens = seq[...].reshape(every, width).astype(F32)
    normed, factor = norm_parts(tokens)
    normal = (normed * gain[...] + shift[...]).astype(BF16)
    ordered = dot(normal, order[...]).astype(BF16)
    gnormal = jnp.zeros((every, width), F32)
    for part in range(3):
        cols = slice(part * width, (part + 1) * width)
        piece = gproj[:, :, cols].reshape(every, width)
        gnormal += dot(piece, wqkv[:, cols], 1, 1)
        put(part * width, (part + 1) * width, dot(ordered, piece, 0, 0))
        if part == 0:
            vectors[2:3, :] = jnp.sum(piece.astype(F32), axis=0, keepdims=True)
        if part == 2:
            vectors[3:4, :] = jnp.sum(piece.astype(F32), axis=0, keepdims=True)
    vectors[0:1, :] = jnp.sum(gnormal * normed, axis=0, keepdims=True)
    vectors[1:2, :] = jnp.sum(gnormal, axis=0, keepdims=True)
    live = live_rows(lens, pairs, rows, slots)
    made = ghidden[...] + norm_back(gnormal, normed, factor, gain[...])
    input_grad[...] = (made * live).astype(BF16).reshape(pairs, rows, width)


def whole_spec():
    return pl.BlockSpec(memory_space=pltpu.VMEM)


def smem_spec():
    return pl.BlockSpec(memory_space=pltpu.SMEM)


def shape(dims, kind):
    return jax.ShapeDtypeStruct(dims, kind)


def run_forward(lens, seq, gain, shift, wqkv, qkv_bias, wout, out_bias, slots):
    pairs, rows, width = seq.shape
    seq_shape = shape((pairs, rows, width), BF16)
    every = pairs * rows
    return pl.pallas_call(
        functools.partial(forward_kernel, slots),
        out_shape=[seq_shape] * 4 + [shape((every, width), F32)],
        in_specs=[smem_spec()] + [whole_spec()] * 7,
        out_specs=[whole_spec()] * 5,
        compiler_params=pltpu.CompilerParams(vmem_limit_bytes=VMEM_LIMIT),
        cost_estimate=pl.CostEstimate(
            flops=2 * every * width * width * 4 + 8 * every * rows * width,
            bytes_accessed=12 * 2**20,
            transcendentals=every * rows * HEADS,
        ),
        name="attention_forward",
    )(lens, seq, gain, shift, wqkv, qkv_bias, wout, out_bias)


def run_feed(lens, hidden, cot, gain, shift, wh, hbias, wd, dbias, order, pairs, slots, chunks, relative):
    every, width = hidden.shape
    ff = wh.shape[1]
    size = ff // chunks
    base = 2 * pairs + 4
    fixed = lambda dims: pl.BlockSpec(dims, lambda c, s: (0, 0))
    columns = lambda r: pl.BlockSpec((r, size), lambda c, s: (0, s[base + c]))
    rows = pl.BlockSpec((size, width), lambda c, s: (s[base + c], 0))
    if relative:
        part = size // 4 // 8
        wd_shape = shape((2, 2, 2, 2, 2, part, 8, width), BF16)
        wd_spec = pl.BlockSpec(
            (2, 1, 1, 2, 1, part, 8, width),
            lambda c, s: (0, c % 2, c // 2 % 2, 0, c // 4, 0, 0, 0),
        )
        wh_shape = shape((width // 8, 8, ff), BF16)
        wh_spec = pl.BlockSpec((width // 8, 8, size), lambda c, s: (0, 0, s[base + c]))
    else:
        wd_shape, wd_spec = shape((ff, width), BF16), rows
        wh_shape, wh_spec = shape((width, ff), BF16), columns(width)
    return pl.pallas_call(
        functools.partial(feed_kernel, pairs, slots),
        out_shape=[
            shape((every, width), BF16),
            shape((every, width), F32),
            wh_shape,
            wd_shape,
            shape((1, ff), F32),
            shape((8, width), F32),
        ],
        grid_spec=pltpu.PrefetchScalarGridSpec(
        num_scalar_prefetch=1,
        grid=(chunks,),
        in_specs=[
            fixed((every, width)),
            fixed((every, width)),
            fixed((1, width)),
            fixed((1, width)),
            columns(width),
            columns(1),
            rows,
            fixed((1, width)),
            fixed((width, width)),
        ],
        out_specs=[
            fixed((every, width)),
            fixed((every, width)),
            wh_spec,
            wd_spec,
            columns(1),
            fixed((8, width)),
        ],
        scratch_shapes=[
            pltpu.VMEM((every, width), BF16),
            pltpu.VMEM((every, width), BF16),
            pltpu.VMEM((every, width), BF16),
            pltpu.VMEM((every, width), F32),
            pltpu.VMEM((every, width), F32),
        ],
        ),
        compiler_params=pltpu.CompilerParams(vmem_limit_bytes=VMEM_LIMIT),
        cost_estimate=pl.CostEstimate(
            flops=12 * every * width * ff,
            bytes_accessed=24 * 2**20,
            transcendentals=2 * every * ff,
        ),
        name="feed_forward",
    )(lens, hidden, cot, gain, shift, wh, hbias, wd, dbias, order)


def run_backward(lens, seq, gain, shift, q, k, v, mixed, ghidden, wqkv, wout, order, slots, relative):
    pairs, rows, width = seq.shape
    every = pairs * rows
    return pl.pallas_call(
        functools.partial(backward_kernel, slots),
        out_shape=[
            shape((pairs, rows, width), BF16),
            shape((width // 8, 8, 4 * width) if relative else (width, 4 * width), BF16),
            shape((8, width), F32),
        ],
        in_specs=[smem_spec()] + [whole_spec()] * 11,
        out_specs=[whole_spec()] * 3,
        scratch_shapes=[
            pltpu.VMEM((pairs, rows, width), BF16),
            pltpu.VMEM((pairs, rows, 3 * width), BF16),
        ],
        compiler_params=pltpu.CompilerParams(vmem_limit_bytes=VMEM_LIMIT),
        cost_estimate=pl.CostEstimate(
            flops=4 * every * width * width * 4 + 20 * every * rows * width,
            bytes_accessed=20 * 2**20,
            transcendentals=every * rows * HEADS,
        ),
        name="attention_backward",
    )(lens, seq, gain, shift, q, k, v, mixed, ghidden, wqkv, wout, order)


BITS = ("core", "y", "z0", "x", "z1")
ORDERS = (("core", "y", "z0", "x", "z1"), ("core", "z0", "y", "x", "z1"))


def partner(bit):
    if bit == "x":
        return {"mod": 1 - lax.axis_index("mod")}
    size = {"core": 1, "y": 2, "z0": 4, "z1": 8}[bit]
    me = lax.axis_index("pairs")
    return {"pairs": me + size - 2 * size * (me // size % 2)}


def narrowed(ref, names, bit, value):
    dim = names.index(bit)
    index = (slice(None),) * dim + (value,)
    return ref.at[index], names[:dim] + names[dim + 1 :]


def piece_shapes(rows8, cols):
    return [(2,) * (4 - step) + (rows8, 8, cols) for step in range(5)]


def add_into(target, source):
    lead = target.shape[:-3]
    count = 1
    for size in lead:
        count *= size

    def body(it, carry):
        index = []
        left = it
        for size in reversed(lead):
            index.insert(0, left % size)
            left = left // size
        index = tuple(index)
        target[index] = (target[index].astype(F32) + source[index].astype(F32)).astype(BF16)
        return carry

    if count == 1:
        body(0, 0)
    else:
        lax.fori_loop(0, count, body, 0)


def scatter_kernel(plan, counts, *refs):
    sources = refs[: counts[0]]
    outs = refs[counts[0] : 2 * counts[0]]
    rest = refs[2 * counts[0] :]
    bufs, (send_sem, recv_sem, load_sem) = rest[:-3], rest[-3:]
    barrier = pltpu.get_barrier_semaphore()
    for bit in BITS:
        pl.semaphore_signal(barrier, inc=1, device_id=partner(bit), device_id_type=pl.DeviceIdType.MESH)
    pl.semaphore_wait(barrier, len(BITS))
    copies = {}
    loads = {}

    def send(unit, step, ref):
        bit = ORDERS[plan[unit][1]][step]
        copy = pltpu.make_async_remote_copy(
            src_ref=ref,
            dst_ref=bufs[6 * unit + 1 + step],
            send_sem=send_sem.at[5 * unit + step],
            recv_sem=recv_sem.at[5 * unit + step],
            device_id=partner(bit),
            device_id_type=pl.DeviceIdType.MESH,
        )
        copy.start()
        copies[unit, step] = copy

    def begin(unit):
        bucket, _, first, last = plan[unit]
        every = (slice(None),) * 6
        send(unit, 0, sources[bucket].at[(1,) + every + (slice(first, last),)])
        loads[unit] = pltpu.make_async_copy(
            sources[bucket].at[(0,) + every + (slice(first, last),)], bufs[6 * unit], load_sem.at[unit]
        )
        loads[unit].start()

    held = {}

    def advance(unit, step):
        bucket, turn, first, last = plan[unit]
        order = ORDERS[turn]
        if step == 0:
            loads[unit].wait()
            held[unit] = (bufs[6 * unit], tuple(b for b in BITS if b != "core"))
        copies[unit, step].wait_recv()
        ref, names = held[unit]
        arrived = bufs[6 * unit + 1 + step]
        if step == 4:
            total = ref[...].astype(F32) + arrived[...].astype(F32)
            outs[bucket][:, :, first:last] = total
            return
        add_into(ref, arrived)
        bit = order[step + 1]
        sent, _ = narrowed(ref, names, bit, 1)
        send(unit, step + 1, sent)
        held[unit] = narrowed(ref, names, bit, 0)

    units = len(plan)
    for unit in range(units):
        begin(unit)
    for step in range(5):
        for unit in range(units):
            advance(unit, step)
    for copy in copies.values():
        copy.wait_send()


def run_scatter(arrays, cuts):
    plan, shapes = [], []
    for index, array in enumerate(arrays):
        cols, rows8 = array.shape[-1], array.shape[-3]
        edges = [cols * place // cuts[index] // 128 * 128 for place in range(cuts[index])] + [cols]
        for place in range(cuts[index]):
            first, last = edges[place], edges[place + 1]
            plan.append((index, place % 2, first, last))
            arrivals = piece_shapes(rows8, last - first)
            shapes += [arrivals[0]] + arrivals
    units = len(plan)
    return pl.pallas_call(
        functools.partial(scatter_kernel, plan, (len(arrays),)),
        out_shape=[shape(a.shape[-3:], F32) for a in arrays],
        in_specs=[pl.BlockSpec(memory_space=pl.ANY)] * len(arrays),
        out_specs=[whole_spec()] * len(arrays),
        scratch_shapes=[pltpu.VMEM(dims, BF16) for dims in shapes]
        + [
            pltpu.SemaphoreType.DMA((5 * units,)),
            pltpu.SemaphoreType.DMA((5 * units,)),
            pltpu.SemaphoreType.DMA((units,)),
        ],
        compiler_params=pltpu.CompilerParams(
            collective_id=1, has_side_effects=True, vmem_limit_bytes=VMEM_LIMIT
        ),
        name="scatter",
    )(*arrays)


def pair_bits():
    return lax.axis_size("pairs").bit_length() - 1


def swapped(array, axis, bit):
    size = lax.axis_size(axis)
    return lax.ppermute(array, axis, [(i, i ^ (1 << bit)) for i in range(size)])


def split_dims(array):
    bits = pair_bits() + 1
    return array.reshape((2,) * bits + (array.shape[0] >> bits,) + array.shape[1:])


def stage_orders():
    bits = pair_bits()
    ring = ["mod", 1, 2]
    orders = []
    for turn in range(3):
        orders.append([0] + ring[turn:] + ring[:turn] + list(range(3, bits)))
    return orders


def half_sum(array, names, name, last):
    axis, bit = ("mod", 0) if name == "mod" else ("pairs", name)
    mine = (lax.axis_index(axis) >> bit) & 1
    dim = names.index(name)
    sent = lax.dynamic_index_in_dim(array, 1 - mine, dim, keepdims=False)
    kept = lax.dynamic_index_in_dim(array, mine, dim, keepdims=False)
    came = swapped(sent, axis, bit)
    total = kept.astype(F32) + came.astype(F32)
    return (total if last else total.astype(BF16)), names[:dim] + names[dim + 1 :]


def scattered(array):
    width = array.shape[1]
    names0 = list(range(pair_bits() - 1, -1, -1)) + ["mod"]
    first, names1 = half_sum(split_dims(array), names0, 0, False)
    third = -(-width // 3 // 128) * 128
    pieces = []
    for turn, order in enumerate(stage_orders()):
        piece = first[..., turn * third : min(width, (turn + 1) * third)]
        names = list(names1)
        for place, name in enumerate(order[1:]):
            piece, names = half_sum(piece, names, name, place == len(order) - 2)
        pieces.append(piece)
    return jnp.concatenate(pieces, axis=1)


def on_device(
    inputs,
    cotangent,
    text_len,
    patch_count,
    norm1_gain,
    norm1_bias,
    qkv_weight,
    query_bias,
    value_bias,
    out_weight,
    out_bias,
    norm2_gain,
    norm2_bias,
    hidden_weight,
    hidden_bias,
    down_weight,
    down_bias,
):
    _, group, slots, width = inputs.shape
    half = group // 2
    rows = padded(TEXT + slots)
    mod = lax.axis_index("mod")
    is_text = mod == 0
    lens = lax.dynamic_slice_in_dim(jnp.stack([text_len, patch_count]), mod * half, half, 1)
    lens = lens.reshape(-1)

    def gathered(array):
        local = array[0]
        patches = lax.ppermute(local[:half], "mod", [(1, 0)])
        texts = lax.ppermute(local[half:, :TEXT], "mod", [(0, 1)])
        patches = jnp.where(is_text, patches, local[half:])
        texts = jnp.where(is_text, local[:half, :TEXT], texts)
        blank = jnp.zeros((half, rows - slots - TEXT, width), array.dtype)
        return jnp.concatenate([patches, texts, blank], axis=1)

    def returned(array):
        patches, texts = array[:, :slots], array[:, slots : slots + TEXT]
        far_patches = lax.ppermute(patches, "mod", [(0, 1)])
        far_texts = lax.ppermute(texts, "mod", [(1, 0)])
        texts = jnp.concatenate([texts, far_texts], axis=0)
        texts = jnp.pad(texts, ((0, 0), (0, slots - TEXT), (0, 0)))
        patches = jnp.concatenate([far_patches, patches], axis=0)
        return jnp.where(is_text, texts, patches)[None]

    row = lambda vector: vector.reshape(1, -1)
    chunks = 8
    relative = lax.axis_size("pairs") == 16
    chip = lax.axis_index("pairs") // 2
    core = lax.axis_index("pairs") % 2
    steps = jnp.arange(chunks, dtype=jnp.int32)
    if relative:
        extra = jnp.concatenate([jnp.stack([core, 1 - core, mod, 1 - mod]), steps ^ chip])
        place = jnp.arange(width, dtype=jnp.int32)
        block = place // (width // 32)
        bit = lambda shift: (block >> shift) & 1
        owner = (bit(0) << 4) + (bit(2) << 3) + (bit(3) << 2) + (bit(4) << 1) + bit(1)
        owner = owner ^ (lax.axis_index("pairs") * 2 + mod)
        source = owner * (width // 32) + place % (width // 32)
    else:
        extra = jnp.concatenate([jnp.zeros(4, jnp.int32), steps])
        source = jnp.arange(width, dtype=jnp.int32)
    order = (jnp.arange(width, dtype=jnp.int32)[:, None] == source[None, :]).astype(BF16)
    lens = jnp.concatenate([lens, extra.astype(jnp.int32)])
    seq = gathered(inputs)
    cot = gathered(cotangent)
    qkv_bias = row(jnp.concatenate([query_bias, jnp.zeros_like(query_bias), value_bias]))
    q, k, v, mixed, hidden = run_forward(
        lens, seq, row(norm1_gain), row(norm1_bias), qkv_weight, qkv_bias, out_weight, row(out_bias), slots
    )
    result, ghidden, wh_grad, wd_grad, hb_grad, vec2 = run_feed(
        lens,
        hidden,
        cot.reshape(half * rows, width),
        row(norm2_gain),
        row(norm2_bias),
        hidden_weight,
        row(hidden_bias),
        down_weight,
        row(down_bias),
        order,
        half,
        slots,
        chunks,
        relative,
    )
    block_out = returned(result.reshape(half, rows, width))
    input_rows, qkvo_grad, vec1 = run_backward(
        lens,
        seq,
        row(norm1_gain),
        row(norm1_bias),
        q,
        k,
        v,
        mixed,
        ghidden,
        qkv_weight,
        out_weight,
        order,
        slots,
        relative,
    )
    input_grad = returned(input_rows)
    strip = jnp.concatenate([vec1[:4], vec2[:4]], axis=0).T
    strip = jnp.concatenate([strip, hb_grad.reshape(width, -1)], axis=1).astype(BF16)
    strip = jnp.pad(strip, ((0, 0), (0, 128 - strip.shape[1])))
    if relative:
        strip = dot(order, strip, 0, 0).astype(BF16).reshape(width // 8, 8, 128)
        qkvo_grad = jnp.concatenate([qkvo_grad, strip], axis=2)
        split = lambda array: array.reshape((2,) * 5 + (array.shape[0] // 32,) + array.shape[1:])
        wd_out, wh_out, qkvo_out = run_scatter([wd_grad, split(wh_grad), split(qkvo_grad)], (2, 4, 4))
        flat = lambda array: array.reshape(-1, array.shape[-1])
        wd_out, wh_out, qkvo_out = flat(wd_out), flat(wh_out), flat(qkvo_out)
    else:
        wd_out, wh_out = scattered(wd_grad), scattered(wh_grad)
        qkvo_out = scattered(jnp.concatenate([qkvo_grad, strip], axis=1))
    vec_out = qkvo_out[:, 4 * width :]
    return (
        block_out,
        input_grad,
        vec_out[:, 0],
        vec_out[:, 1],
        qkvo_out[:, : 3 * width],
        vec_out[:, 2],
        vec_out[:, 3],
        qkvo_out[:, 3 * width : 4 * width],
        vec_out[:, 7],
        vec_out[:, 4],
        vec_out[:, 5],
        wh_out,
        vec_out[:, 8 : 8 + hidden_bias.shape[0] // width].reshape(-1),
        wd_out,
        vec_out[:, 6],
    )


def solution(mesh):
    whole = P()
    split = P("mod", "pairs", None, None)
    vector = P(("pairs", "mod"))
    matrix = P(("pairs", "mod"), None)
    return jax.shard_map(
        on_device,
        mesh=mesh,
        in_specs=(split, split, P("pairs"), P("pairs")) + (whole,) * 13,
        out_specs=(
            split,
            split,
            vector,
            vector,
            matrix,
            vector,
            vector,
            matrix,
            vector,
            vector,
            vector,
            matrix,
            vector,
            matrix,
            vector,
        ),
        check_vma=False,
    )
```

```python
import functools
import types

import jax
import jax.numpy as jnp
from jax import lax
from jax.experimental import pallas as pl
from jax.experimental.pallas import tpu as pltpu
from jax.sharding import PartitionSpec as P

HEADS = 12
HEAD_DIM = 64
TEXT = 40
EPSILON = 1e-06
MASKED = -1e30
F32 = jnp.float32
BF16 = jnp.bfloat16
VMEM_LIMIT = 60 * 1024 * 1024


def padded(count):
    return -(-count // 32) * 32


def dot(a, b, ca=1, cb=0):
    return lax.dot_general(a, b, (((ca,), (cb,)), ((), ())), preferred_element_type=F32)


def norm_parts(values):
    centre = jnp.mean(values, axis=-1, keepdims=True)
    centred = values - centre
    spread = jnp.mean(centred * centred, axis=-1, keepdims=True)
    factor = lax.rsqrt(spread + EPSILON)
    return centred * factor, factor


def norm_back(grad_out, normed, factor, norm_gain):
    grad_norm = grad_out * norm_gain
    mean_grad = jnp.mean(grad_norm, axis=-1, keepdims=True)
    second = jnp.mean(grad_norm * normed, axis=-1, keepdims=True)
    return (grad_norm - mean_grad - normed * second) * factor


def live_slots(index, text_count, patch_count, slots):
    return (index < patch_count) | ((index >= slots) & (index - slots < text_count))


def live_rows(lens, pairs, rows, slots):
    parts = []
    for pair in range(pairs):
        index = lax.broadcasted_iota(jnp.int32, (rows, 1), 0)
        parts.append(live_slots(index, lens[pair], lens[pairs + pair], slots).astype(F32))
    return jnp.concatenate(parts, axis=0)


def mix_heads(pair, group, text_count, patch_count, slots, q_in, k_in, v_in, mixed):
    rows = q_in.shape[1]
    first = lax.broadcasted_iota(jnp.int32, (rows, 128), 1) < HEAD_DIM
    column = lax.broadcasted_iota(jnp.int32, (1, rows), 1)
    off = pl.multiple_of(group * 128, 128)
    live = live_slots(column, text_count, patch_count, slots)
    q2 = q_in[pair, :, pl.ds(off, 128)]
    k2 = k_in[pair, :, pl.ds(off, 128)]
    v2 = v_in[pair, :, pl.ds(off, 128)]
    halves = []
    for half in range(2):
        keep = first if half == 0 else ~first
        qm = jnp.where(keep, q2, jnp.zeros_like(q2))
        scores = jnp.where(live, dot(qm, k2, 1, 1), MASKED)
        highest = jnp.max(scores, axis=-1, keepdims=True)
        shifted = jnp.exp(scores - highest)
        total = jnp.sum(shifted, axis=-1, keepdims=True)
        halves.append(dot(shifted.astype(BF16), v2) / total)
    mixed[pair, :, pl.ds(off, 128)] = jnp.where(first, halves[0], halves[1]).astype(BF16)


def forward_kernel(
    slots,
    lens,
    seq,
    gain,
    shift,
    wqkv,
    qkv_bias,
    wout,
    out_bias,
    q_out,
    k_out,
    v_out,
    hidden,
    mixed_out,
    mixed,
):
    pairs, rows, width = seq.shape
    tokens = seq[...].reshape(pairs * rows, width).astype(F32)
    normed, _ = norm_parts(tokens)
    normal = (normed * gain[...] + shift[...]).astype(BF16)
    for part, ref in enumerate((q_out, k_out, v_out)):
        cols = slice(part * width, (part + 1) * width)
        made = dot(normal, wqkv[:, cols]) + qkv_bias[:, cols]
        if part == 0:
            made = made * 0.125
        ref[...] = made.astype(BF16).reshape(pairs, rows, width)
    groups = width // 128

    def step(it, carry):
        pair = it // groups
        mix_heads(pair, it % groups, lens[pair], lens[pairs + pair], slots, q_out, k_out, v_out, mixed)
        return carry

    lax.fori_loop(0, pairs * groups, step, 0)
    rows_mixed = mixed[...].reshape(pairs * rows, width)
    mixed_out[...] = mixed[...]
    hidden[...] = tokens + dot(rows_mixed, wout[...]) + out_bias[...]


def gelu_parts(values):
    cumulative = 0.5 * (1.0 + lax.erf(values * 0.7071067811865476))
    density = jnp.exp(-0.5 * values * values) * 0.3989422804014327
    return values * cumulative, cumulative + values * density


def feed_kernel(
    pairs,
    slots,
    lens,
    hidden,
    cot,
    gain,
    shift,
    wh,
    hbias,
    wd,
    dbias,
    order,
    result,
    grad_hidden,
    wh_grad,
    wd_grad,
    hb_grad,
    vectors,
    normal,
    ordered,
    gdown,
    total,
    gnormal,
):
    chunk = pl.program_id(0)
    count = pl.num_programs(0)
    rows = hidden.shape[0] // pairs
    live = live_rows(lens, pairs, rows, slots)

    @pl.when(chunk == 0)
    def _():
        normed, _ = norm_parts(hidden[...])
        made = (normed * gain[...] + shift[...]).astype(BF16)
        normal[...] = made
        ordered[...] = dot(made, order[...]).astype(BF16)
        gdown[...] = (cot[...].astype(F32) * live).astype(BF16)
        total[...] = hidden[...] + dbias[...]
        gnormal[...] = jnp.zeros_like(gnormal)

    before = dot(normal[...], wh[...]) + hbias[...]
    active, slope = gelu_parts(before)
    active = active.astype(BF16)
    total[...] += dot(active, wd[...])
    fresh = dot(active, gdown[...], 0, 0)
    if wd_grad.ndim == 2:
        wd_grad[...] = fresh.astype(BF16)
    else:
        size = fresh.shape[0] // 4
        base = 2 * pairs
        for core in range(2):
            for mod in range(2):
                start = (2 * core + mod) * size
                piece = fresh[start : start + size].reshape(size // 8, 8, fresh.shape[1])
                wd_grad[lens[base + core], 0, 0, lens[base + 2 + mod], 0] = piece.astype(BF16)
    gbefore = (dot(gdown[...], wd[...], 1, 1) * slope).astype(BF16)
    gnormal[...] += dot(gbefore, wh[...], 1, 1)
    wh_grad[...] = dot(ordered[...], gbefore, 0, 0).reshape(wh_grad.shape).astype(BF16)
    hb_grad[...] = jnp.sum(gbefore.astype(F32), axis=0, keepdims=True)

    @pl.when(chunk == count - 1)
    def _():
        result[...] = (total[...] * live).astype(BF16)
        normed, factor = norm_parts(hidden[...])
        gnorm = gnormal[...]
        vectors[0:1, :] = jnp.sum(gnorm * normed, axis=0, keepdims=True)
        vectors[1:2, :] = jnp.sum(gnorm, axis=0, keepdims=True)
        down = gdown[...].astype(F32)
        vectors[2:3, :] = jnp.sum(down, axis=0, keepdims=True)
        made = down + norm_back(gnorm, normed, factor, gain[...])
        vectors[3:4, :] = jnp.sum(made.astype(BF16).astype(F32), axis=0, keepdims=True)
        grad_hidden[...] = made


def backward_kernel(
    slots,
    lens,
    seq,
    gain,
    shift,
    q_in,
    k_in,
    v_in,
    mixed,
    ghidden,
    wqkv,
    wout,
    order,
    input_grad,
    weight_grad,
    vectors,
    gmixed,
    gproj,
):
    pairs, rows, width = seq.shape
    every = pairs * rows
    gattended = ghidden[...].astype(BF16)
    gmixed[...] = dot(gattended, wout[...], 1, 1).astype(BF16).reshape(pairs, rows, width)
    ordered = dot(mixed[...].reshape(every, width), order[...]).astype(BF16)

    def put(first, last, value):
        target = (slice(None),) * (len(weight_grad.shape) - 1) + (slice(first, last),)
        value = value.reshape(weight_grad.shape[:-1] + (last - first,))
        weight_grad[target] = value.astype(BF16)

    put(3 * width, 4 * width, dot(ordered, gattended, 0, 0))
    first = lax.broadcasted_iota(jnp.int32, (rows, 128), 1) < HEAD_DIM
    index = lax.broadcasted_iota(jnp.int32, (rows, 1), 0)
    groups = width // 128

    def step(it, carry):
        pair = it // groups
        base = (it % groups) * 128
        off = pl.multiple_of(base, 128)
        live = live_slots(index, lens[pair], lens[pairs + pair], slots)
        q2 = q_in[pair, :, pl.ds(off, 128)]
        k2 = k_in[pair, :, pl.ds(off, 128)]
        v2 = v_in[pair, :, pl.ds(off, 128)]
        g2 = gmixed[pair, :, pl.ds(off, 128)]
        gq = gk = gv = None
        for half in range(2):
            keep = first if half == 0 else ~first
            zero = jnp.zeros_like(q2)
            qm = jnp.where(keep, q2, zero)
            km = jnp.where(keep, k2, zero)
            gm = jnp.where(keep, g2, zero)
            scores = jnp.where(live, dot(k2, qm, 1, 1), MASKED)
            highest = jnp.max(scores, axis=0, keepdims=True)
            shifted = jnp.exp(scores - highest)
            probs = shifted * (1.0 / jnp.sum(shifted, axis=0, keepdims=True))
            gprobs = dot(v2, gm, 1, 1)
            row_dot = jnp.sum(probs * gprobs, axis=0, keepdims=True)
            gscores = (probs * (gprobs - row_dot)).astype(BF16)
            new_v = dot(probs.astype(BF16), gm)
            new_k = dot(gscores, qm)
            new_q = dot(gscores, km, 0, 0)
            gq = new_q if gq is None else gq + new_q
            gk = new_k if gk is None else gk + new_k
            gv = new_v if gv is None else gv + new_v
        gproj[pair, :, pl.ds(off, 128)] = (gq * 0.125).astype(BF16)
        gproj[pair, :, pl.ds(pl.multiple_of(base + width, 128), 128)] = gk.astype(BF16)
        gproj[pair, :, pl.ds(pl.multiple_of(base + 2 * width, 128), 128)] = gv.astype(BF16)
        return carry

    lax.fori_loop(0, pairs * groups, step, 0)
    tokens = seq[...].reshape(every, width).astype(F32)
    normed, factor = norm_parts(tokens)
    normal = (normed * gain[...] + shift[...]).astype(BF16)
    ordered = dot(normal, order[...]).astype(BF16)
    gnormal = jnp.zeros((every, width), F32)
    for part in range(3):
        cols = slice(part * width, (part + 1) * width)
        piece = gproj[:, :, cols].reshape(every, width)
        gnormal += dot(piece, wqkv[:, cols], 1, 1)
        put(part * width, (part + 1) * width, dot(ordered, piece, 0, 0))
        if part == 0:
            vectors[2:3, :] = jnp.sum(piece.astype(F32), axis=0, keepdims=True)
        if part == 2:
            vectors[3:4, :] = jnp.sum(piece.astype(F32), axis=0, keepdims=True)
    vectors[0:1, :] = jnp.sum(gnormal * normed, axis=0, keepdims=True)
    vectors[1:2, :] = jnp.sum(gnormal, axis=0, keepdims=True)
    live = live_rows(lens, pairs, rows, slots)
    made = ghidden[...] + norm_back(gnormal, normed, factor, gain[...])
    input_grad[...] = (made * live).astype(BF16).reshape(pairs, rows, width)


def whole_spec():
    return pl.BlockSpec(memory_space=pltpu.VMEM)


def smem_spec():
    return pl.BlockSpec(memory_space=pltpu.SMEM)


def shape(dims, kind):
    return jax.ShapeDtypeStruct(dims, kind)


def run_forward(lens, seq, gain, shift, wqkv, qkv_bias, wout, out_bias, slots):
    pairs, rows, width = seq.shape
    every = pairs * rows
    cube = shape((pairs, rows, width), BF16)
    return pl.pallas_call(
        functools.partial(forward_kernel, slots),
        out_shape=[cube, cube, cube, shape((every, width), F32), cube],
        in_specs=[smem_spec()] + [whole_spec()] * 7,
        out_specs=[whole_spec()] * 5,
        scratch_shapes=[pltpu.VMEM((pairs, rows, width), BF16)],
        compiler_params=pltpu.CompilerParams(vmem_limit_bytes=VMEM_LIMIT),
        name="attention_forward",
    )(lens, seq, gain, shift, wqkv, qkv_bias, wout, out_bias)


def run_feed(lens, hidden, cot, gain, shift, wh, hbias, wd, dbias, order, pairs, slots, chunks, relative):
    every, width = hidden.shape
    ff = wh.shape[1]
    size = ff // chunks
    base = 2 * pairs + 4
    fixed = lambda dims: pl.BlockSpec(dims, lambda c, s: (0, 0))
    columns = lambda r: pl.BlockSpec((r, size), lambda c, s: (0, s[base + c]))
    rows = pl.BlockSpec((size, width), lambda c, s: (s[base + c], 0))
    if relative:
        part = size // 4 // 8
        wd_shape = shape((2, 2, 2, 2, 2, part, 8, width), BF16)
        wd_spec = pl.BlockSpec(
            (2, 1, 1, 2, 1, part, 8, width),
            lambda c, s: (0, c % 2, c // 2 % 2, 0, c // 4, 0, 0, 0),
        )
        wh_shape = shape((width // 8, 8, ff), BF16)
        wh_spec = pl.BlockSpec((width // 8, 8, size), lambda c, s: (0, 0, s[base + c]))
    else:
        wd_shape, wd_spec = shape((ff, width), BF16), rows
        wh_shape, wh_spec = shape((width, ff), BF16), columns(width)
    return pl.pallas_call(
        functools.partial(feed_kernel, pairs, slots),
        out_shape=[
            shape((every, width), BF16),
            shape((every, width), F32),
            wh_shape,
            wd_shape,
            shape((1, ff), F32),
            shape((8, width), F32),
        ],
        grid_spec=pltpu.PrefetchScalarGridSpec(
        num_scalar_prefetch=1,
        grid=(chunks,),
        in_specs=[
            fixed((every, width)),
            fixed((every, width)),
            fixed((1, width)),
            fixed((1, width)),
            columns(width),
            columns(1),
            rows,
            fixed((1, width)),
            fixed((width, width)),
        ],
        out_specs=[
            fixed((every, width)),
            fixed((every, width)),
            wh_spec,
            wd_spec,
            columns(1),
            fixed((8, width)),
        ],
        scratch_shapes=[
            pltpu.VMEM((every, width), BF16),
            pltpu.VMEM((every, width), BF16),
            pltpu.VMEM((every, width), BF16),
            pltpu.VMEM((every, width), F32),
            pltpu.VMEM((every, width), F32),
        ],
        ),
        compiler_params=pltpu.CompilerParams(vmem_limit_bytes=VMEM_LIMIT),
        cost_estimate=pl.CostEstimate(
            flops=12 * every * width * ff,
            bytes_accessed=24 * 2**20,
            transcendentals=2 * every * ff,
        ),
        name="feed_forward",
    )(lens, hidden, cot, gain, shift, wh, hbias, wd, dbias, order)


def run_backward(lens, seq, gain, shift, q, k, v, mixed, ghidden, wqkv, wout, order, slots, relative):
    pairs, rows, width = seq.shape
    every = pairs * rows
    return pl.pallas_call(
        functools.partial(backward_kernel, slots),
        out_shape=[
            shape((pairs, rows, width), BF16),
            shape((width // 8, 8, 4 * width) if relative else (width, 4 * width), BF16),
            shape((8, width), F32),
        ],
        in_specs=[smem_spec()] + [whole_spec()] * 11,
        out_specs=[whole_spec()] * 3,
        scratch_shapes=[
            pltpu.VMEM((pairs, rows, width), BF16),
            pltpu.VMEM((pairs, rows, 3 * width), BF16),
        ],
        compiler_params=pltpu.CompilerParams(vmem_limit_bytes=VMEM_LIMIT),
        cost_estimate=pl.CostEstimate(
            flops=4 * every * width * width * 4 + 20 * every * rows * width,
            bytes_accessed=20 * 2**20,
            transcendentals=every * rows * HEADS,
        ),
        name="attention_backward",
    )(lens, seq, gain, shift, q, k, v, mixed, ghidden, wqkv, wout, order)


BITS = ("core", "y", "z0", "x", "z1")
ORDERS = (("core", "y", "z0", "x", "z1"), ("core", "z0", "y", "x", "z1"))


def partner(bit):
    if bit == "x":
        return {"mod": 1 - lax.axis_index("mod")}
    size = {"core": 1, "y": 2, "z0": 4, "z1": 8}[bit]
    me = lax.axis_index("pairs")
    return {"pairs": me + size - 2 * size * (me // size % 2)}


def narrowed(ref, names, bit, value):
    dim = names.index(bit)
    index = (slice(None),) * dim + (value,)
    return ref.at[index], names[:dim] + names[dim + 1 :]


def flip(value, bit):
    return value + bit - 2 * value * bit


def place():
    pairs = lax.axis_index("pairs")
    return {
        "core": pairs % 2,
        "y": pairs // 2 % 2,
        "z0": pairs // 4 % 2,
        "z1": pairs // 8,
        "x": lax.axis_index("mod"),
    }


def hop(bit, source, target, sems, index, there=None):
    return pltpu.make_async_remote_copy(
        src_ref=source,
        dst_ref=target,
        send_sem=sems[0].at[index],
        recv_sem=sems[1].at[index if there is None else there],
        device_id=partner(bit),
        device_id_type=pl.DeviceIdType.MESH,
    )


def lead_index(it, lead):
    index = []
    for size in reversed(lead):
        index.insert(0, it % size)
        it = it // size
    return tuple(index)


def accumulate(target, source):
    lead = target.shape[:-3]
    count = 1
    for size in lead:
        count *= size
    if count == 1:
        at = (0,) * len(lead)
        target[at] = target[at] + source[at]
        return

    def body(it, carry):
        at = lead_index(it, lead)
        target[at] = target[at] + source[at]
        return carry

    lax.fori_loop(0, count, body, 0)


class Unit:
    def __init__(self, own, arrivals, order, sems, base, finish):
        self.own, self.arrivals, self.order = own, arrivals, order
        self.sems, self.base, self.finish = sems, base, finish
        self.peers = {}

    def views(self, step):
        ref, names = self.own, list(BITS)
        for bit in self.order[:step]:
            ref, names = narrowed(ref, names, bit, 0)
        sent, _ = narrowed(ref, names, self.order[step], 1)
        kept, _ = narrowed(ref, names, self.order[step], 0)
        return sent, kept

    def copy(self, step):
        bit = self.order[step]
        sent, _ = self.views(step)
        peer = self.peers.get(bit, self)
        return hop(bit, sent, peer.arrivals[step], self.sems, self.base + step, peer.base + step)

    def arrival(self, step):
        sent, _ = self.views(step)
        return hop(self.order[step], sent, self.arrivals[step], self.sems, self.base + step)

    def start(self):
        self.copy(0).start()

    def advance(self, step):
        self.arrival(step).wait_recv()
        _, kept = self.views(step)
        if step == 4:
            self.finish(kept[...].astype(F32) + self.arrivals[4][...].astype(F32))
            return
        accumulate(kept, self.arrivals[step])
        self.copy(step + 1).start()

    def drain(self):
        for step in range(5):
            self.copy(step).wait_send()


def counts(here, pairs, text_len, patch_count):
    base = here["x"] * pairs
    return [text_len[base + pair] for pair in range(pairs)] + [patch_count[base + pair] for pair in range(pairs)]


def opening_kernel(pairs, slots, names, *refs):
    r = types.SimpleNamespace(**dict(zip(names, refs)))
    rows, width = r.seq.shape[1:]
    every, tail = pairs * rows, rows - slots
    here = place()
    lens = counts(here, pairs, r.text_len, r.patch_count)
    sems = (r.send_sem, r.recv_sem)
    barrier = pltpu.get_barrier_semaphore()
    pl.semaphore_signal(barrier, inc=1, device_id=partner("x"), device_id_type=pl.DeviceIdType.MESH)

    def moves(which, pair):
        source, target = ((r.inputs, r.seq), (r.cotangent, r.cot))[which]
        index = which * pairs + pair
        patches, texts = target.at[pair, pl.ds(0, slots)], target.at[pair, pl.ds(slots, tail)]
        near = lambda src, dst: pltpu.make_async_copy(src, dst, r.load_sem.at[index])
        return (
            hop("x", source.at[0, pair], patches, sems, index),
            hop("x", source.at[0, pairs + pair, pl.ds(0, tail)], texts, sems, index),
            near(source.at[0, pairs + pair], patches),
            near(source.at[0, pair, pl.ds(0, tail)], texts),
        )

    every_move = [(which, pair) for which in range(2) for pair in range(pairs)]
    weights = [
        pltpu.make_async_copy(source, target, r.load_sem.at[2 * pairs + index])
        for index, (source, target) in enumerate(((r.wqkv_in, r.wqkv), (r.wout_in, r.wout)))
    ]
    pl.semaphore_wait(barrier, 1)

    @pl.when(here["x"] == 1)
    def _():
        for move in every_move:
            moves(*move)[0].start()
        for move in every_move:
            moves(*move)[2].start()

    @pl.when(here["x"] == 0)
    def _():
        for move in every_move:
            moves(*move)[1].start()
        for move in every_move:
            moves(*move)[3].start()

    for copy in weights:
        copy.start()

    def arrived(which, pair):
        @pl.when(here["x"] == 1)
        def _():
            moves(which, pair)[1].wait_recv()
            moves(which, pair)[2].wait()

        @pl.when(here["x"] == 0)
        def _():
            moves(which, pair)[0].wait_recv()
            moves(which, pair)[3].wait()

    place_at = lax.broadcasted_iota(jnp.int32, (width, 1), 0)
    feature = lax.broadcasted_iota(jnp.int32, (width, width), 1)
    unit = width // 32
    block = place_at // unit
    bit = lambda shift: (block >> shift) & 1
    owner = (bit(0) << 4) + (bit(2) << 3) + (bit(3) << 2) + (bit(4) << 1) + bit(1)
    owner = owner ^ (lax.axis_index("pairs") * 2 + here["x"])
    source = owner * unit + (place_at - block * unit)
    r.order[...] = (source == feature).astype(F32).astype(BF16)
    vec = lambda index: r.vecs[index : index + 1, :]
    for copy in weights:
        copy.wait()
    for pair in range(pairs):
        arrived(0, pair)
        tokens = r.seq[pair].astype(F32)
        normed, _ = norm_parts(tokens)
        normal = (normed * vec(0) + vec(1)).astype(BF16)
        r.normal[pair] = normal
        for part, ref in enumerate((r.q_out, r.k_out, r.v_out)):
            made = dot(normal, r.wqkv[:, part * width : (part + 1) * width])
            if part == 0:
                made = (made + vec(2)) * 0.125
            if part == 2:
                made = made + vec(3)
            ref[pair] = made.astype(BF16)

        def step(group, carry):
            mix_heads(pair, group, lens[pair], lens[pairs + pair], slots, r.q_out, r.k_out, r.v_out, r.mixed)
            return carry

        lax.fori_loop(0, width // 128, step, 0)
        made = r.seq[pair].astype(F32) + dot(r.mixed[pair], r.wout[...]) + vec(4)
        r.hidden[pair * rows : (pair + 1) * rows, :] = made
    stores = [
        pltpu.make_async_copy(r.seq, r.seq_out, r.store_sem.at[0]),
        pltpu.make_async_copy(r.cot, r.cot_out, r.store_sem.at[1]),
    ]
    stores[0].start()
    r.mixed_out[...] = dot(r.order[...], r.mixed[...].reshape(every, width), 1, 1).astype(BF16)
    r.normal_out[...] = dot(r.order[...], r.normal[...].reshape(every, width), 1, 1).astype(BF16)
    for pair in range(pairs):
        arrived(1, pair)
    stores[1].start()

    @pl.when(here["x"] == 1)
    def _():
        for move in every_move:
            moves(*move)[0].wait_send()

    @pl.when(here["x"] == 0)
    def _():
        for move in every_move:
            moves(*move)[1].wait_send()

    for copy in stores:
        copy.wait()


def run_opening(text_len, patch_count, inputs, cotangent, vecs, wqkv, wout):
    _, group, slots, width = inputs.shape
    pairs = group // 2
    rows = padded(TEXT + slots)
    every = pairs * rows
    hbm = pl.BlockSpec(memory_space=pl.ANY)
    operands = dict(
        text_len=(text_len, smem_spec()),
        patch_count=(patch_count, smem_spec()),
        inputs=(inputs, hbm),
        cotangent=(cotangent, hbm),
        vecs=(vecs, whole_spec()),
        wqkv_in=(wqkv, hbm),
        wout_in=(wout, hbm),
    )
    cube = shape((pairs, rows, width), BF16)
    tall = shape((width, every), BF16)
    outs = dict(
        q_out=(cube, whole_spec()),
        k_out=(cube, whole_spec()),
        v_out=(cube, whole_spec()),
        hidden=(shape((every, width), F32), whole_spec()),
        mixed_out=(tall, whole_spec()),
        normal_out=(tall, whole_spec()),
        seq_out=(cube, hbm),
        cot_out=(cube, hbm),
        order=(shape((width, width), BF16), whole_spec()),
    )
    held = pltpu.VMEM((pairs, rows, width), BF16)
    scratch = dict(
        seq=held,
        cot=held,
        mixed=held,
        normal=held,
        wqkv=pltpu.VMEM(wqkv.shape, BF16),
        wout=pltpu.VMEM(wout.shape, BF16),
        send_sem=pltpu.SemaphoreType.DMA((2 * pairs,)),
        recv_sem=pltpu.SemaphoreType.DMA((2 * pairs,)),
        load_sem=pltpu.SemaphoreType.DMA((2 * pairs + 2,)),
        store_sem=pltpu.SemaphoreType.DMA((2,)),
    )
    names = list(operands) + list(outs) + list(scratch)
    return pl.pallas_call(
        functools.partial(opening_kernel, pairs, slots, names),
        out_shape=[kind for kind, _ in outs.values()],
        in_specs=[spec for _, spec in operands.values()],
        out_specs=[spec for _, spec in outs.values()],
        scratch_shapes=list(scratch.values()),
        compiler_params=pltpu.CompilerParams(collective_id=2, has_side_effects=True, vmem_limit_bytes=VMEM_LIMIT),
        name="opening",
    )(*[value for value, _ in operands.values()])


def fused_kernel(pairs, slots, names, *refs):
    r = types.SimpleNamespace(**dict(zip(names, refs)))
    rows, width = r.seq.shape[1:]
    every = pairs * rows
    tail = rows - slots
    here = place()
    lens = counts(here, pairs, r.text_len, r.patch_count)
    vec_in = lambda index: r.vecs[index : index + 1, :]
    sems = (r.send_sem, r.recv_sem)
    barrier = pltpu.get_barrier_semaphore()
    for bit in BITS:
        pl.semaphore_signal(barrier, inc=1, device_id=partner(bit), device_id_type=pl.DeviceIdType.MESH)

    def load(name, target, index):
        return pltpu.make_async_copy(getattr(r, name), getattr(r, target), r.load_sem.at[index])

    early = [load("hidden_in", "hidden", 0), load("order_in", "order", 1), load("cot_in", "cot", 2)]
    late = [
        load("mixed_in", "mixed_t", 3),
        load("normal_in", "normal_t", 4),
        load("seq_in", "seq", 5),
        load("q_in", "q", 6),
        load("k_in", "k", 7),
        load("v_in", "v", 8),
    ]

    def block_of(t):
        z1, z0 = 1 - t // 2, 1 - t % 2
        return flip(z0, here["z0"]) + 2 * flip(z1, here["z1"])

    def weight_loads(t, slot):
        start = pl.multiple_of(block_of(t) * width, width)
        return (
            pltpu.make_async_copy(r.wh.at[:, pl.ds(start, width)], r.wbuf.at[slot], r.w_sem.at[slot]),
            pltpu.make_async_copy(r.wd.at[pl.ds(start, width), :], r.wbuf.at[2 + slot], r.w_sem.at[2 + slot]),
        )

    early[0].start()
    early[1].start()
    for copy in weight_loads(0, 0):
        copy.start()
    early[2].start()
    early[0].wait()
    live = live_rows(lens, pairs, rows, slots)
    normed, _ = norm_parts(r.hidden[...])
    made = (normed * vec_in(5) + vec_in(6)).astype(BF16)
    r.normal2[...] = made
    early[1].wait()
    r.normal2_t[...] = dot(r.order[...], made, 1, 1).astype(BF16)
    r.total[...] = r.hidden[...] + vec_in(7)
    r.gnormal[...] = jnp.zeros_like(r.gnormal)
    early[2].wait()
    r.gdown[...] = (r.cot[...].reshape(every, width).astype(F32) * live).astype(BF16)
    r.unit_h[...] = jnp.zeros_like(r.unit_h)
    for copy in late:
        copy.start()
    r.zeros[...] = jnp.zeros_like(r.zeros)
    pl.semaphore_wait(barrier, len(BITS))

    def blanks():
        return [
            pltpu.make_async_copy(r.zeros, out.at[0, pair, pl.ds(tail, slots - tail)], r.zero_sem.at[2 * pair + index])
            for index, out in enumerate((r.block_out, r.input_grad))
            for pair in range(2 * pairs)
        ]

    @pl.when(here["x"] == 0)
    def _():
        for copy in blanks():
            copy.start()

    arrivals = lambda name, index: [getattr(r, name + str(step)).at[index] for step in range(5)]
    tasks = {}

    def at(tick, action):
        tasks.setdefault(tick, []).append(action)

    a_core = lambda t, y: hop("core", r.a_own.at[t, 1, y], r.a_core.at[t, y], sems, 2 * t + y)
    a_y = lambda t: hop("y", r.a_own.at[t, 0, 1], r.a_y.at[t], sems, 8 + t)
    a_z0 = lambda k: hop("z0", r.a_own.at[2 * k, 0, 0], r.a_z0.at[k], sems, 12 + k)
    a_x = lambda k: hop("x", r.a_own.at[2 * k + 1, 0, 0, 1], r.a_x.at[k], sems, 14 + k)
    a_z1 = lambda: hop("z1", r.a_own.at[1, 0, 0, 0], r.a_z1.at[0], sems, 16)

    def a_first(t):
        a_core(t, 1).wait_recv()
        accumulate(r.a_own.at[t, 0, 1], r.a_core.at[t, 1])
        a_y(t).start()
        a_core(t, 0).wait_recv()
        accumulate(r.a_own.at[t, 0, 0], r.a_core.at[t, 0])

    def a_second(t):
        k = t // 2
        a_y(t).wait_recv()
        accumulate(r.a_own.at[t, 0, 0], r.a_y.at[t])
        if t % 2 == 0:
            a_z0(k).start()
        else:
            a_z0(k).wait_recv()
            accumulate(r.a_own.at[t, 0, 0], r.a_z0.at[k])
            a_x(k).start()

    def a_third(k):
        a_x(k).wait_recv()
        accumulate(r.a_own.at[2 * k + 1, 0, 0, pl.ds(0, 1)], r.a_x.at[pl.ds(k, 1)])
        if k == 0:
            a_z1().start()

    def a_last():
        a_z1().wait_recv()
        r.out_a[...] = r.a_own[3, 0, 0, 0].astype(F32) + r.a_z1[0].astype(F32)

    for t in range(4):
        at(2 * t + 2, functools.partial(a_first, t))
        at(2 * t + 4, functools.partial(a_second, t))
    at(8, functools.partial(a_third, 0))
    at(12, functools.partial(a_third, 1))
    at(14, a_last)

    def b_finish(t):
        def finish(value):
            r.out_b[:, :, pl.ds(pl.multiple_of(block_of(t) * width, width), width)] = value

        return finish

    def c_finish(g):
        def finish(value):
            for part in range(3):
                cols = slice(part * width + 128 * g, part * width + 128 * g + 128)
                r.out_c[:, :, cols] = value[:, :, 128 * part : 128 * part + 128]

        return finish

    def o_finish(value):
        r.out_o[...] = value

    def plain(name):
        def finish(value):
            getattr(r, name)[...] = value

        return finish

    units = {}
    for t in range(4):
        units["b", t] = Unit(r.b_own.at[t], arrivals("b", t), ORDERS[1], sems, 20 + 5 * t, b_finish(t))
    for t in range(4):
        units["b", t].peers = {"z0": units["b", t ^ 1], "z1": units["b", t ^ 2]}
    groups = width // 128
    for g in range(groups):
        units["c", g] = Unit(r.c_own.at[g], arrivals("c", g), ORDERS[g % 2], sems, 40 + 5 * g, c_finish(g))
    units["o", 0] = Unit(r.o_own, arrivals("o", 0), ORDERS[0], sems, 70, o_finish)
    units["h", 0] = Unit(r.unit_h, arrivals("h", 0), ORDERS[1], sems, 75, plain("out_h"))
    units["v", 0] = Unit(r.unit_v, arrivals("v", 0), ORDERS[0], sems, 80, plain("out_v"))
    plans = {
        ("b", 0): [2, 6, 8, 10, 15],
        ("b", 1): [4, 6, 8, 10, 15],
        ("b", 2): [6, 11, 13, 14, 16],
        ("b", 3): [8, 11, 13, 14, 16],
    }
    plans["o", 0] = [9, 13, 15, 16, 17]
    plans["h", 0] = [9, 10, 11, 12, 13]
    for g in range(groups):
        plans["c", g] = [11 + 2 * g, 13 + 2 * g, 14 + 2 * g, 15 + 2 * g, 16 + 2 * g]
    for key, ticks in plans.items():
        for step, tick in enumerate(ticks):
            at(tick, functools.partial(units[key].advance, step))

    def run_tasks(ticks, now):
        for tick in ticks:
            if tick in tasks:

                @pl.when(now == tick)
                def _(tick=tick):
                    for action in tasks[tick]:
                        action()

    size = width // 2

    def feed_step(t, carry):
        slot = t % 2
        for copy in weight_loads(t, slot):
            copy.wait()

        @pl.when(t < 3)
        def _():
            for copy in weight_loads(t + 1, 1 - slot):
                copy.start()

        for sub in range(2):
            run_tasks([2 * k + sub for k in range(4)], 2 * t + sub)
            y = 1 - sub
            part = flip(y, here["y"])
            start = pl.multiple_of(part * size, size)
            wh = r.wbuf[slot, :, pl.ds(start, size)]
            wd = r.wbuf[2 + slot, pl.ds(start, size), :]
            before = dot(r.normal2[...], wh) + r.vecs[pl.ds(8 + block_of(t), 1), pl.ds(start, size)]
            active, slope = gelu_parts(before)
            active = active.astype(BF16)
            r.total[...] += dot(active, wd)
            fresh = dot(active, r.gdown[...], 0, 0)
            quarter = size // 4
            for core in range(2):
                for mod in range(2):
                    first = (2 * core + mod) * quarter
                    piece = fresh[first : first + quarter].reshape(quarter // 8, 8, width)
                    r.a_own[t, flip(core, here["core"]), y, flip(mod, here["x"])] = piece.astype(BF16)
            a_core(t, y).start()
            gbefore = (dot(r.gdown[...], wd, 1, 1) * slope).astype(BF16)
            r.gnormal[...] += dot(gbefore, wh, 1, 1)
            fresh = dot(r.normal2_t[...], gbefore)
            fresh = fresh.reshape((2,) * 5 + (width // 256, 8, size)).astype(BF16)
            r.b_own[t, :, :, :, :, :, :, :, pl.ds(start, size)] = fresh
            sums = jnp.sum(gbefore.astype(F32), axis=0, keepdims=True)
            z1, z0 = 1 - t // 2, 1 - t % 2
            for core in range(2):
                for mod in range(2):
                    first = (2 * core + mod) * quarter
                    r.unit_h[
                        flip(core, here["core"]), y, z0, flip(mod, here["x"]), z1, 0, 0:1, 0:quarter
                    ] = sums[:, first : first + quarter]
        hop("core", r.b_own.at[t, 1], r.b0.at[t], sems, 20 + 5 * t).start()
        return carry

    lax.fori_loop(0, 4, feed_step, 0)

    wout_load = pltpu.make_async_copy(r.wout, r.wbuf.at[3], r.w_sem.at[3])
    wout_load.start()
    wqkv_loads = [
        pltpu.make_async_copy(
            r.wqkv.at[:, pl.ds(part * width, width)], r.wbuf.at[part], r.w_sem.at[part]
        )
        for part in range(3)
    ]
    for copy in wqkv_loads:
        copy.start()
    units["h", 0].start()
    r.result[...] = (r.total[...] * live).astype(BF16).reshape(pairs, rows, width)

    def give(source, target, index):
        near = lambda src, dst: pltpu.make_async_copy(src, dst, r.give_sem.at[index])
        first_pairs, last_pairs = pl.ds(0, pairs), pl.ds(pairs, pairs)
        patches, texts = source.at[:, pl.ds(0, slots)], source.at[:, pl.ds(slots, tail)]
        return (
            hop("x", patches, target.at[0, first_pairs], sems, 85 + index),
            hop("x", texts, target.at[0, last_pairs, pl.ds(0, tail)], sems, 85 + index),
            near(patches, target.at[0, last_pairs]),
            near(texts, target.at[0, first_pairs, pl.ds(0, tail)]),
        )

    def give_start(copies):
        for which in range(2):

            @pl.when(here["x"] == which)
            def _():
                copies[which].start()
                copies[3 - which].start()

    def give_wait(copies):
        for which in range(2):

            @pl.when(here["x"] == which)
            def _():
                copies[1 - which].wait_recv()
                copies[which].wait_send()
                copies[3 - which].wait()

    result_copies = give(r.result, r.block_out, 0)
    give_start(result_copies)
    normed, factor = norm_parts(r.hidden[...])
    gnorm = r.gnormal[...]
    down = r.gdown[...].astype(F32)
    vec = [
        jnp.sum(gnorm * normed, axis=0, keepdims=True),
        jnp.sum(gnorm, axis=0, keepdims=True),
        jnp.sum(down, axis=0, keepdims=True),
    ]
    made = down + norm_back(gnorm, normed, factor, vec_in(5))
    gattended = made.astype(BF16)
    vec.append(jnp.sum(gattended.astype(F32), axis=0, keepdims=True))
    for index, value in enumerate(vec):
        r.vec[4 + index : 5 + index, :] = value
    r.gnormal[...] = made
    wout_load.wait()
    r.gmixed[...] = dot(gattended, r.wbuf[3], 1, 1).astype(BF16).reshape(pairs, rows, width)
    for copy in late:
        copy.wait()
    fresh = dot(r.mixed_t[...], gattended)
    r.o_own[...] = fresh.reshape((2,) * 5 + (width // 256, 8, width)).astype(BF16)
    units["o", 0].start()

    first = lax.broadcasted_iota(jnp.int32, (rows, 128), 1) < HEAD_DIM
    index = lax.broadcasted_iota(jnp.int32, (rows, 1), 0)

    def head_step(g, carry):
        base = g * 128
        off = pl.multiple_of(base, 128)
        for pair in range(pairs):
            run_tasks([8 + 2 * k + pair for k in range(groups)], 8 + 2 * g + pair)
            keys_live = live_slots(index, lens[pair], lens[pairs + pair], slots)
            q2 = r.q[pair, :, pl.ds(off, 128)]
            k2 = r.k[pair, :, pl.ds(off, 128)]
            v2 = r.v[pair, :, pl.ds(off, 128)]
            g2 = r.gmixed[pair, :, pl.ds(off, 128)]
            gq = gk = gv = None
            for half in range(2):
                keep = first if half == 0 else ~first
                zero = jnp.zeros_like(q2)
                qm = jnp.where(keep, q2, zero)
                km = jnp.where(keep, k2, zero)
                gm = jnp.where(keep, g2, zero)
                scores = jnp.where(keys_live, dot(k2, qm, 1, 1), MASKED)
                highest = jnp.max(scores, axis=0, keepdims=True)
                shifted = jnp.exp(scores - highest)
                probs = shifted * (1.0 / jnp.sum(shifted, axis=0, keepdims=True))
                gprobs = dot(v2, gm, 1, 1)
                row_dot = jnp.sum(probs * gprobs, axis=0, keepdims=True)
                gscores = (probs * (gprobs - row_dot)).astype(BF16)
                new_v = dot(probs.astype(BF16), gm)
                new_k = dot(gscores, qm)
                new_q = dot(gscores, km, 0, 0)
                gq = new_q if gq is None else gq + new_q
                gk = new_k if gk is None else gk + new_k
                gv = new_v if gv is None else gv + new_v
            r.gproj[pair, :, pl.ds(off, 128)] = (gq * 0.125).astype(BF16)
            r.gproj[pair, :, pl.ds(pl.multiple_of(base + width, 128), 128)] = gk.astype(BF16)
            r.gproj[pair, :, pl.ds(pl.multiple_of(base + 2 * width, 128), 128)] = gv.astype(BF16)
        pieces = [
            r.gproj[:, :, pl.ds(pl.multiple_of(base + part * width, 128), 128)].reshape(every, 128)
            for part in range(3)
        ]
        fresh = dot(r.normal_t[...], jnp.concatenate(pieces, axis=1))
        r.c_own[g] = fresh.reshape((2,) * 5 + (width // 256, 8, 384)).astype(BF16)
        hop("core", r.c_own.at[g, 1], r.c0.at[g], sems, 40 + 5 * g).start()
        return carry

    lax.fori_loop(0, groups, head_step, 0)

    def run_now(tick):
        for action in tasks.get(tick, []):
            action()

    tokens = r.seq[...].reshape(every, width).astype(F32)
    normed, factor = norm_parts(tokens)
    gnormal = jnp.zeros((every, width), F32)
    for part in range(3):
        run_now(20 + part)
        piece = r.gproj[:, :, part * width : (part + 1) * width].reshape(every, width)
        wqkv_loads[part].wait()
        gnormal += dot(piece, r.wbuf[part], 1, 1)
        if part == 0:
            r.vec[2:3, :] = jnp.sum(piece.astype(F32), axis=0, keepdims=True)
        if part == 2:
            r.vec[3:4, :] = jnp.sum(piece.astype(F32), axis=0, keepdims=True)
    run_now(23)
    r.vec[0:1, :] = jnp.sum(gnormal * normed, axis=0, keepdims=True)
    r.vec[1:2, :] = jnp.sum(gnormal, axis=0, keepdims=True)
    made = r.gnormal[...] + norm_back(gnormal, normed, factor, vec_in(0))
    r.grad_rows[...] = (made * live).astype(BF16).reshape(pairs, rows, width)
    grad_copies = give(r.grad_rows, r.input_grad, 1)
    give_start(grad_copies)
    run_now(24)
    rest = r.vec[...]
    ordered = jnp.zeros_like(rest)
    for _ in range(3):
        high = rest.astype(BF16)
        ordered += dot(high, r.order[...], 1, 1)
        rest = rest - high.astype(F32)
    r.unit_v[...] = jnp.zeros_like(r.unit_v)
    unit = width // 32
    for block in range(32):
        bits = tuple(block >> shift & 1 for shift in (4, 3, 2, 1, 0))
        r.unit_v[bits + (0, slice(None), slice(0, unit))] = ordered[:, block * unit : (block + 1) * unit]
    units["v", 0].start()
    run_now(25)
    run_now(26)
    for step in range(5):
        units["v", 0].advance(step)
    give_wait(result_copies)
    give_wait(grad_copies)

    @pl.when(here["x"] == 0)
    def _():
        for copy in blanks():
            copy.wait()

    for t in range(4):
        a_core(t, 0).wait_send()
        a_core(t, 1).wait_send()
        a_y(t).wait_send()
    for k in range(2):
        a_z0(k).wait_send()
        a_x(k).wait_send()
    a_z1().wait_send()
    for unit in units.values():
        unit.drain()


def run_fused(text_len, patch_count, vecs, hidden, cot, wh, wd, order, wqkv, wout, seq, q, k, v, mixed_t, normal_t, slots):
    pairs, rows, width = seq.shape
    every = pairs * rows
    wide = (2,) * 5
    eight = width // 256
    groups = width // 128

    def arrivals(name, count, tail, kind):
        return {name + str(step): pltpu.VMEM((count,) + (2,) * (4 - step) + tail, kind) for step in range(5)}

    flat = lambda kind: pltpu.VMEM((every, width), kind)
    cube = pltpu.VMEM((pairs, rows, width), BF16)
    tall = pltpu.VMEM((width, every), BF16)
    block = (width // 64, 8, width)
    scratch = dict(
        cot=cube,
        result=cube,
        grad_rows=cube,
        zeros=pltpu.VMEM((slots - (rows - slots), width), BF16),
        give_sem=pltpu.SemaphoreType.DMA((2,)),
        zero_sem=pltpu.SemaphoreType.DMA((4 * pairs,)),
        hidden=flat(F32),
        gdown=flat(BF16),
        seq=cube,
        q=cube,
        k=cube,
        v=cube,
        mixed_t=tall,
        normal_t=tall,
        wbuf=pltpu.VMEM((4, width, width), BF16),
        order=pltpu.VMEM((width, width), BF16),
        normal2=flat(BF16),
        normal2_t=tall,
        total=flat(F32),
        gnormal=flat(F32),
        gmixed=cube,
        gproj=pltpu.VMEM((pairs, rows, 3 * width), BF16),
        vec=pltpu.VMEM((8, width), F32),
        a_own=pltpu.VMEM((4, 2, 2, 2) + block, BF16),
        a_core=pltpu.VMEM((4, 2, 2) + block, BF16),
        a_y=pltpu.VMEM((4, 2) + block, BF16),
        a_z0=pltpu.VMEM((2, 2) + block, BF16),
        a_x=pltpu.VMEM((2,) + block, BF16),
        a_z1=pltpu.VMEM((1,) + block, BF16),
        b_own=pltpu.VMEM((4,) + wide + (eight, 8, width), BF16),
        **arrivals("b", 4, (eight, 8, width), BF16),
        c_own=pltpu.VMEM((groups,) + wide + (eight, 8, 384), BF16),
        **arrivals("c", groups, (eight, 8, 384), BF16),
        o_own=pltpu.VMEM(wide + (eight, 8, width), BF16),
        **arrivals("o", 1, (eight, 8, width), BF16),
        unit_h=pltpu.VMEM(wide + (1, 8, 128), F32),
        **arrivals("h", 1, (1, 8, 128), F32),
        unit_v=pltpu.VMEM(wide + (1, 8, 128), F32),
        **arrivals("v", 1, (1, 8, 128), F32),
        send_sem=pltpu.SemaphoreType.DMA((87,)),
        recv_sem=pltpu.SemaphoreType.DMA((87,)),
        load_sem=pltpu.SemaphoreType.DMA((9,)),
        w_sem=pltpu.SemaphoreType.DMA((4,)),
    )
    hbm = pl.BlockSpec(memory_space=pl.ANY)
    operands = dict(
        text_len=(text_len, smem_spec()),
        patch_count=(patch_count, smem_spec()),
        vecs=(vecs, whole_spec()),
        hidden_in=(hidden, hbm),
        cot_in=(cot, hbm),
        wh=(wh, hbm),
        wd=(wd, hbm),
        order_in=(order, hbm),
        wqkv=(wqkv, hbm),
        wout=(wout, hbm),
        seq_in=(seq, hbm),
        q_in=(q, hbm),
        k_in=(k, hbm),
        v_in=(v, hbm),
        mixed_in=(mixed_t, hbm),
        normal_in=(normal_t, hbm),
    )
    final = shape((1, 2 * pairs, slots, width), BF16)
    outs = dict(
        block_out=(final, hbm),
        input_grad=(final, hbm),
        out_a=(shape(block, F32), whole_spec()),
        out_b=(shape((eight, 8, 4 * width), F32), whole_spec()),
        out_c=(shape((eight, 8, 3 * width), F32), whole_spec()),
        out_o=(shape((eight, 8, width), F32), whole_spec()),
        out_h=(shape((1, 8, 128), F32), whole_spec()),
        out_v=(shape((1, 8, 128), F32), whole_spec()),
    )
    names = list(operands) + list(outs) + list(scratch)
    return pl.pallas_call(
        functools.partial(fused_kernel, pairs, slots, names),
        out_shape=[kind for kind, _ in outs.values()],
        in_specs=[spec for _, spec in operands.values()],
        out_specs=[spec for _, spec in outs.values()],
        scratch_shapes=list(scratch.values()),
        compiler_params=pltpu.CompilerParams(
            collective_id=1, has_side_effects=True, vmem_limit_bytes=67043328
        ),
        name="fused",
    )(*[value for value, _ in operands.values()])


def pair_bits():
    return lax.axis_size("pairs").bit_length() - 1


def swapped(array, axis, bit):
    size = lax.axis_size(axis)
    return lax.ppermute(array, axis, [(i, i ^ (1 << bit)) for i in range(size)])


def split_dims(array):
    bits = pair_bits() + 1
    return array.reshape((2,) * bits + (array.shape[0] >> bits,) + array.shape[1:])


def stage_orders():
    bits = pair_bits()
    ring = ["mod", 1, 2]
    orders = []
    for turn in range(3):
        orders.append([0] + ring[turn:] + ring[:turn] + list(range(3, bits)))
    return orders


def half_sum(array, names, name, last):
    axis, bit = ("mod", 0) if name == "mod" else ("pairs", name)
    mine = (lax.axis_index(axis) >> bit) & 1
    dim = names.index(name)
    sent = lax.dynamic_index_in_dim(array, 1 - mine, dim, keepdims=False)
    kept = lax.dynamic_index_in_dim(array, mine, dim, keepdims=False)
    came = swapped(sent, axis, bit)
    total = kept.astype(F32) + came.astype(F32)
    return (total if last else total.astype(BF16)), names[:dim] + names[dim + 1 :]


def scattered(array):
    width = array.shape[1]
    names0 = list(range(pair_bits() - 1, -1, -1)) + ["mod"]
    first, names1 = half_sum(split_dims(array), names0, 0, False)
    third = -(-width // 3 // 128) * 128
    pieces = []
    for turn, order in enumerate(stage_orders()):
        piece = first[..., turn * third : min(width, (turn + 1) * third)]
        names = list(names1)
        for place, name in enumerate(order[1:]):
            piece, names = half_sum(piece, names, name, place == len(order) - 2)
        pieces.append(piece)
    return jnp.concatenate(pieces, axis=1)


def on_device(
    inputs,
    cotangent,
    text_len,
    patch_count,
    norm1_gain,
    norm1_bias,
    qkv_weight,
    query_bias,
    value_bias,
    out_weight,
    out_bias,
    norm2_gain,
    norm2_bias,
    hidden_weight,
    hidden_bias,
    down_weight,
    down_bias,
):
    _, group, slots, width = inputs.shape
    half = group // 2
    rows = padded(TEXT + slots)
    mod = lax.axis_index("mod")
    is_text = mod == 0
    lens = lax.dynamic_slice_in_dim(jnp.stack([text_len, patch_count]), mod * half, half, 1)
    lens = lens.reshape(-1)

    def gathered(array):
        local = array[0]
        patches = lax.ppermute(local[:half], "mod", [(1, 0)])
        texts = lax.ppermute(local[half:, :TEXT], "mod", [(0, 1)])
        patches = jnp.where(is_text, patches, local[half:])
        texts = jnp.where(is_text, local[:half, :TEXT], texts)
        blank = jnp.zeros((half, rows - slots - TEXT, width), array.dtype)
        return jnp.concatenate([patches, texts, blank], axis=1)

    def returned(array):
        far_patches = lax.ppermute(array[:, :slots], "mod", [(0, 1)])
        far_texts = lax.ppermute(array[:, slots : slots + TEXT], "mod", [(1, 0)])
        return assembled(array, far_patches, far_texts)

    def assembled(array, far_patches, far_texts):
        patches, texts = array[:, :slots], array[:, slots : slots + TEXT]
        texts = jnp.concatenate([texts, far_texts], axis=0)
        texts = jnp.pad(texts, ((0, 0), (0, slots - TEXT), (0, 0)))
        patches = jnp.concatenate([far_patches, patches], axis=0)
        return jnp.where(is_text, texts, patches)[None]

    row = lambda vector: vector.reshape(1, -1)
    if lax.axis_size("pairs") == 16:
        parts = [norm1_gain, norm1_bias, query_bias, value_bias, out_bias, norm2_gain, norm2_bias, down_bias, hidden_bias]
        vecs = jnp.concatenate(parts).reshape(-1, width)
        made = run_opening(text_len, patch_count, inputs, cotangent, vecs, qkv_weight, out_weight)
        q, k, v, hidden, mixed, normal, seq, cot, order = made
        made = run_fused(
            text_len,
            patch_count,
            vecs,
            hidden,
            cot,
            hidden_weight,
            down_weight,
            order,
            qkv_weight,
            out_weight,
            seq,
            q,
            k,
            v,
            mixed,
            normal,
            slots,
        )
        block_out, input_grad, wd_out, wh_out, qkv_out, wo_out, hb_out, vec_out = made
        flat = lambda array: array.reshape(-1, array.shape[-1])
        wd_out, wh_out, qkv_out, wo_out = flat(wd_out), flat(wh_out), flat(qkv_out), flat(wo_out)
        vec_out = vec_out[0, :, : width // 32].T
        hb_out = hb_out[0, 0, : hidden_bias.shape[0] // 32]
    else:
        seq = gathered(inputs)
        cot = gathered(cotangent).reshape(half * rows, width)
        qkv_bias = row(jnp.concatenate([query_bias, jnp.zeros_like(query_bias), value_bias]))
        feature = jnp.arange(width, dtype=jnp.int32)
        order = (feature[:, None] == feature[None, :]).astype(BF16)
        q, k, v, hidden, mixed = run_forward(
            lens, seq, row(norm1_gain), row(norm1_bias), qkv_weight, qkv_bias, out_weight, row(out_bias), slots
        )
        chunks = 8
        steps = jnp.arange(chunks, dtype=jnp.int32)
        lens = jnp.concatenate([lens, jnp.zeros(4, jnp.int32), steps])
        result, ghidden, wh_grad, wd_grad, hb_grad, vec2 = run_feed(
            lens,
            hidden,
            cot,
            row(norm2_gain),
            row(norm2_bias),
            hidden_weight,
            row(hidden_bias),
            down_weight,
            row(down_bias),
            order,
            half,
            slots,
            chunks,
            False,
        )
        block_out = returned(result.reshape(half, rows, width))
        input_rows, qkvo_grad, vec1 = run_backward(
            lens,
            seq,
            row(norm1_gain),
            row(norm1_bias),
            q,
            k,
            v,
            mixed,
            ghidden,
            qkv_weight,
            out_weight,
            order,
            slots,
            False,
        )
        input_grad = returned(input_rows)
        strip = jnp.concatenate([vec1[:4], vec2[:4]], axis=0).T
        strip = jnp.concatenate([strip, hb_grad.reshape(width, -1)], axis=1).astype(BF16)
        strip = jnp.pad(strip, ((0, 0), (0, 128 - strip.shape[1])))
        wd_out, wh_out = scattered(wd_grad), scattered(wh_grad)
        qkvo_out = scattered(jnp.concatenate([qkvo_grad, strip], axis=1))
        vec_out = qkvo_out[:, 4 * width :]
        qkv_out, wo_out = qkvo_out[:, : 3 * width], qkvo_out[:, 3 * width : 4 * width]
        hb_out = vec_out[:, 8 : 8 + hidden_bias.shape[0] // width].reshape(-1)
    return (
        block_out,
        input_grad,
        vec_out[:, 0],
        vec_out[:, 1],
        qkv_out,
        vec_out[:, 2],
        vec_out[:, 3],
        wo_out,
        vec_out[:, 7],
        vec_out[:, 4],
        vec_out[:, 5],
        wh_out,
        hb_out,
        wd_out,
        vec_out[:, 6],
    )


def solution(mesh):
    whole = P()
    split = P("mod", "pairs", None, None)
    vector = P(("pairs", "mod"))
    matrix = P(("pairs", "mod"), None)
    return jax.shard_map(
        on_device,
        mesh=mesh,
        in_specs=(split, split, P("pairs"), P("pairs")) + (whole,) * 13,
        out_specs=(
            split,
            split,
            vector,
            vector,
            matrix,
            vector,
            vector,
            matrix,
            vector,
            vector,
            vector,
            matrix,
            vector,
            matrix,
            vector,
        ),
        check_vma=False,
    )
```

```python
import functools
import types

import jax
import jax.numpy as jnp
from jax import lax
from jax.experimental import pallas as pl
from jax.experimental.pallas import tpu as pltpu
from jax.sharding import PartitionSpec as P

HEADS = 12
HEAD_DIM = 64
TEXT = 40
EPSILON = 1e-06
MASKED = -1e30
F32 = jnp.float32
BF16 = jnp.bfloat16
VMEM_LIMIT = 60 * 1024 * 1024


def padded(count):
    return -(-count // 32) * 32


def dot(a, b, ca=1, cb=0):
    return lax.dot_general(a, b, (((ca,), (cb,)), ((), ())), preferred_element_type=F32)


def norm_parts(values):
    centre = jnp.mean(values, axis=-1, keepdims=True)
    centred = values - centre
    spread = jnp.mean(centred * centred, axis=-1, keepdims=True)
    factor = lax.rsqrt(spread + EPSILON)
    return centred * factor, factor


def norm_back(grad_out, normed, factor, norm_gain):
    grad_norm = grad_out * norm_gain
    mean_grad = jnp.mean(grad_norm, axis=-1, keepdims=True)
    second = jnp.mean(grad_norm * normed, axis=-1, keepdims=True)
    return (grad_norm - mean_grad - normed * second) * factor


def live_slots(index, text_count, patch_count, slots):
    return (index < patch_count) | ((index >= slots) & (index - slots < text_count))


def live_rows(lens, pairs, rows, slots):
    parts = []
    for pair in range(pairs):
        index = lax.broadcasted_iota(jnp.int32, (rows, 1), 0)
        parts.append(live_slots(index, lens[pair], lens[pairs + pair], slots).astype(F32))
    return jnp.concatenate(parts, axis=0)


def mix_heads(pair, group, text_count, patch_count, slots, q_in, k_in, v_in, mixed):
    rows = q_in.shape[1]
    first = lax.broadcasted_iota(jnp.int32, (rows, 128), 1) < HEAD_DIM
    column = lax.broadcasted_iota(jnp.int32, (1, rows), 1)
    off = pl.multiple_of(group * 128, 128)
    live = live_slots(column, text_count, patch_count, slots)
    q2 = q_in[pair, :, pl.ds(off, 128)]
    k2 = k_in[pair, :, pl.ds(off, 128)]
    v2 = v_in[pair, :, pl.ds(off, 128)]
    halves = []
    for half in range(2):
        keep = first if half == 0 else ~first
        qm = jnp.where(keep, q2, jnp.zeros_like(q2))
        scores = jnp.where(live, dot(qm, k2, 1, 1), MASKED)
        highest = jnp.max(scores, axis=-1, keepdims=True)
        shifted = jnp.exp(scores - highest)
        total = jnp.sum(shifted, axis=-1, keepdims=True)
        halves.append(dot(shifted.astype(BF16), v2) / total)
    mixed[pair, :, pl.ds(off, 128)] = jnp.where(first, halves[0], halves[1]).astype(BF16)


def forward_kernel(
    slots,
    lens,
    seq,
    gain,
    shift,
    wqkv,
    qkv_bias,
    wout,
    out_bias,
    q_out,
    k_out,
    v_out,
    hidden,
    mixed_out,
    mixed,
):
    pairs, rows, width = seq.shape
    tokens = seq[...].reshape(pairs * rows, width).astype(F32)
    normed, _ = norm_parts(tokens)
    normal = (normed * gain[...] + shift[...]).astype(BF16)
    for part, ref in enumerate((q_out, k_out, v_out)):
        cols = slice(part * width, (part + 1) * width)
        made = dot(normal, wqkv[:, cols]) + qkv_bias[:, cols]
        if part == 0:
            made = made * 0.125
        ref[...] = made.astype(BF16).reshape(pairs, rows, width)
    groups = width // 128

    def step(it, carry):
        pair = it // groups
        mix_heads(pair, it % groups, lens[pair], lens[pairs + pair], slots, q_out, k_out, v_out, mixed)
        return carry

    lax.fori_loop(0, pairs * groups, step, 0)
    rows_mixed = mixed[...].reshape(pairs * rows, width)
    mixed_out[...] = mixed[...]
    hidden[...] = tokens + dot(rows_mixed, wout[...]) + out_bias[...]


def gelu_parts(values):
    cumulative = 0.5 * (1.0 + lax.erf(values * 0.7071067811865476))
    density = jnp.exp(-0.5 * values * values) * 0.3989422804014327
    return values * cumulative, cumulative + values * density


def feed_kernel(
    pairs,
    slots,
    lens,
    hidden,
    cot,
    gain,
    shift,
    wh,
    hbias,
    wd,
    dbias,
    order,
    result,
    grad_hidden,
    wh_grad,
    wd_grad,
    hb_grad,
    vectors,
    normal,
    ordered,
    gdown,
    total,
    gnormal,
):
    chunk = pl.program_id(0)
    count = pl.num_programs(0)
    rows = hidden.shape[0] // pairs
    live = live_rows(lens, pairs, rows, slots)

    @pl.when(chunk == 0)
    def _():
        normed, _ = norm_parts(hidden[...])
        made = (normed * gain[...] + shift[...]).astype(BF16)
        normal[...] = made
        ordered[...] = dot(made, order[...]).astype(BF16)
        gdown[...] = (cot[...].astype(F32) * live).astype(BF16)
        total[...] = hidden[...] + dbias[...]
        gnormal[...] = jnp.zeros_like(gnormal)

    before = dot(normal[...], wh[...]) + hbias[...]
    active, slope = gelu_parts(before)
    active = active.astype(BF16)
    total[...] += dot(active, wd[...])
    fresh = dot(active, gdown[...], 0, 0)
    if wd_grad.ndim == 2:
        wd_grad[...] = fresh.astype(BF16)
    else:
        size = fresh.shape[0] // 4
        base = 2 * pairs
        for core in range(2):
            for mod in range(2):
                start = (2 * core + mod) * size
                piece = fresh[start : start + size].reshape(size // 8, 8, fresh.shape[1])
                wd_grad[lens[base + core], 0, 0, lens[base + 2 + mod], 0] = piece.astype(BF16)
    gbefore = (dot(gdown[...], wd[...], 1, 1) * slope).astype(BF16)
    gnormal[...] += dot(gbefore, wh[...], 1, 1)
    wh_grad[...] = dot(ordered[...], gbefore, 0, 0).reshape(wh_grad.shape).astype(BF16)
    hb_grad[...] = jnp.sum(gbefore.astype(F32), axis=0, keepdims=True)

    @pl.when(chunk == count - 1)
    def _():
        result[...] = (total[...] * live).astype(BF16)
        normed, factor = norm_parts(hidden[...])
        gnorm = gnormal[...]
        vectors[0:1, :] = jnp.sum(gnorm * normed, axis=0, keepdims=True)
        vectors[1:2, :] = jnp.sum(gnorm, axis=0, keepdims=True)
        down = gdown[...].astype(F32)
        vectors[2:3, :] = jnp.sum(down, axis=0, keepdims=True)
        made = down + norm_back(gnorm, normed, factor, gain[...])
        vectors[3:4, :] = jnp.sum(made.astype(BF16).astype(F32), axis=0, keepdims=True)
        grad_hidden[...] = made


def backward_kernel(
    slots,
    lens,
    seq,
    gain,
    shift,
    q_in,
    k_in,
    v_in,
    mixed,
    ghidden,
    wqkv,
    wout,
    order,
    input_grad,
    weight_grad,
    vectors,
    gmixed,
    gproj,
):
    pairs, rows, width = seq.shape
    every = pairs * rows
    gattended = ghidden[...].astype(BF16)
    gmixed[...] = dot(gattended, wout[...], 1, 1).astype(BF16).reshape(pairs, rows, width)
    ordered = dot(mixed[...].reshape(every, width), order[...]).astype(BF16)

    def put(first, last, value):
        target = (slice(None),) * (len(weight_grad.shape) - 1) + (slice(first, last),)
        value = value.reshape(weight_grad.shape[:-1] + (last - first,))
        weight_grad[target] = value.astype(BF16)

    put(3 * width, 4 * width, dot(ordered, gattended, 0, 0))
    first = lax.broadcasted_iota(jnp.int32, (rows, 128), 1) < HEAD_DIM
    index = lax.broadcasted_iota(jnp.int32, (rows, 1), 0)
    groups = width // 128

    def step(it, carry):
        pair = it // groups
        base = (it % groups) * 128
        off = pl.multiple_of(base, 128)
        live = live_slots(index, lens[pair], lens[pairs + pair], slots)
        q2 = q_in[pair, :, pl.ds(off, 128)]
        k2 = k_in[pair, :, pl.ds(off, 128)]
        v2 = v_in[pair, :, pl.ds(off, 128)]
        g2 = gmixed[pair, :, pl.ds(off, 128)]
        gq = gk = gv = None
        for half in range(2):
            keep = first if half == 0 else ~first
            zero = jnp.zeros_like(q2)
            qm = jnp.where(keep, q2, zero)
            km = jnp.where(keep, k2, zero)
            gm = jnp.where(keep, g2, zero)
            scores = jnp.where(live, dot(k2, qm, 1, 1), MASKED)
            highest = jnp.max(scores, axis=0, keepdims=True)
            shifted = jnp.exp(scores - highest)
            probs = shifted * (1.0 / jnp.sum(shifted, axis=0, keepdims=True))
            gprobs = dot(v2, gm, 1, 1)
            row_dot = jnp.sum(probs * gprobs, axis=0, keepdims=True)
            gscores = (probs * (gprobs - row_dot)).astype(BF16)
            new_v = dot(probs.astype(BF16), gm)
            new_k = dot(gscores, qm)
            new_q = dot(gscores, km, 0, 0)
            gq = new_q if gq is None else gq + new_q
            gk = new_k if gk is None else gk + new_k
            gv = new_v if gv is None else gv + new_v
        gproj[pair, :, pl.ds(off, 128)] = (gq * 0.125).astype(BF16)
        gproj[pair, :, pl.ds(pl.multiple_of(base + width, 128), 128)] = gk.astype(BF16)
        gproj[pair, :, pl.ds(pl.multiple_of(base + 2 * width, 128), 128)] = gv.astype(BF16)
        return carry

    lax.fori_loop(0, pairs * groups, step, 0)
    tokens = seq[...].reshape(every, width).astype(F32)
    normed, factor = norm_parts(tokens)
    normal = (normed * gain[...] + shift[...]).astype(BF16)
    ordered = dot(normal, order[...]).astype(BF16)
    gnormal = jnp.zeros((every, width), F32)
    for part in range(3):
        cols = slice(part * width, (part + 1) * width)
        piece = gproj[:, :, cols].reshape(every, width)
        gnormal += dot(piece, wqkv[:, cols], 1, 1)
        put(part * width, (part + 1) * width, dot(ordered, piece, 0, 0))
        if part == 0:
            vectors[2:3, :] = jnp.sum(piece.astype(F32), axis=0, keepdims=True)
        if part == 2:
            vectors[3:4, :] = jnp.sum(piece.astype(F32), axis=0, keepdims=True)
    vectors[0:1, :] = jnp.sum(gnormal * normed, axis=0, keepdims=True)
    vectors[1:2, :] = jnp.sum(gnormal, axis=0, keepdims=True)
    live = live_rows(lens, pairs, rows, slots)
    made = ghidden[...] + norm_back(gnormal, normed, factor, gain[...])
    input_grad[...] = (made * live).astype(BF16).reshape(pairs, rows, width)


def whole_spec():
    return pl.BlockSpec(memory_space=pltpu.VMEM)


def smem_spec():
    return pl.BlockSpec(memory_space=pltpu.SMEM)


def shape(dims, kind):
    return jax.ShapeDtypeStruct(dims, kind)


def run_forward(lens, seq, gain, shift, wqkv, qkv_bias, wout, out_bias, slots):
    pairs, rows, width = seq.shape
    every = pairs * rows
    cube = shape((pairs, rows, width), BF16)
    return pl.pallas_call(
        functools.partial(forward_kernel, slots),
        out_shape=[cube, cube, cube, shape((every, width), F32), cube],
        in_specs=[smem_spec()] + [whole_spec()] * 7,
        out_specs=[whole_spec()] * 5,
        scratch_shapes=[pltpu.VMEM((pairs, rows, width), BF16)],
        compiler_params=pltpu.CompilerParams(vmem_limit_bytes=VMEM_LIMIT),
        name="attention_forward",
    )(lens, seq, gain, shift, wqkv, qkv_bias, wout, out_bias)


def run_feed(lens, hidden, cot, gain, shift, wh, hbias, wd, dbias, order, pairs, slots, chunks, relative):
    every, width = hidden.shape
    ff = wh.shape[1]
    size = ff // chunks
    base = 2 * pairs + 4
    fixed = lambda dims: pl.BlockSpec(dims, lambda c, s: (0, 0))
    columns = lambda r: pl.BlockSpec((r, size), lambda c, s: (0, s[base + c]))
    rows = pl.BlockSpec((size, width), lambda c, s: (s[base + c], 0))
    if relative:
        part = size // 4 // 8
        wd_shape = shape((2, 2, 2, 2, 2, part, 8, width), BF16)
        wd_spec = pl.BlockSpec(
            (2, 1, 1, 2, 1, part, 8, width),
            lambda c, s: (0, c % 2, c // 2 % 2, 0, c // 4, 0, 0, 0),
        )
        wh_shape = shape((width // 8, 8, ff), BF16)
        wh_spec = pl.BlockSpec((width // 8, 8, size), lambda c, s: (0, 0, s[base + c]))
    else:
        wd_shape, wd_spec = shape((ff, width), BF16), rows
        wh_shape, wh_spec = shape((width, ff), BF16), columns(width)
    return pl.pallas_call(
        functools.partial(feed_kernel, pairs, slots),
        out_shape=[
            shape((every, width), BF16),
            shape((every, width), F32),
            wh_shape,
            wd_shape,
            shape((1, ff), F32),
            shape((8, width), F32),
        ],
        grid_spec=pltpu.PrefetchScalarGridSpec(
        num_scalar_prefetch=1,
        grid=(chunks,),
        in_specs=[
            fixed((every, width)),
            fixed((every, width)),
            fixed((1, width)),
            fixed((1, width)),
            columns(width),
            columns(1),
            rows,
            fixed((1, width)),
            fixed((width, width)),
        ],
        out_specs=[
            fixed((every, width)),
            fixed((every, width)),
            wh_spec,
            wd_spec,
            columns(1),
            fixed((8, width)),
        ],
        scratch_shapes=[
            pltpu.VMEM((every, width), BF16),
            pltpu.VMEM((every, width), BF16),
            pltpu.VMEM((every, width), BF16),
            pltpu.VMEM((every, width), F32),
            pltpu.VMEM((every, width), F32),
        ],
        ),
        compiler_params=pltpu.CompilerParams(vmem_limit_bytes=VMEM_LIMIT),
        cost_estimate=pl.CostEstimate(
            flops=12 * every * width * ff,
            bytes_accessed=24 * 2**20,
            transcendentals=2 * every * ff,
        ),
        name="feed_forward",
    )(lens, hidden, cot, gain, shift, wh, hbias, wd, dbias, order)


def run_backward(lens, seq, gain, shift, q, k, v, mixed, ghidden, wqkv, wout, order, slots, relative):
    pairs, rows, width = seq.shape
    every = pairs * rows
    return pl.pallas_call(
        functools.partial(backward_kernel, slots),
        out_shape=[
            shape((pairs, rows, width), BF16),
            shape((width // 8, 8, 4 * width) if relative else (width, 4 * width), BF16),
            shape((8, width), F32),
        ],
        in_specs=[smem_spec()] + [whole_spec()] * 11,
        out_specs=[whole_spec()] * 3,
        scratch_shapes=[
            pltpu.VMEM((pairs, rows, width), BF16),
            pltpu.VMEM((pairs, rows, 3 * width), BF16),
        ],
        compiler_params=pltpu.CompilerParams(vmem_limit_bytes=VMEM_LIMIT),
        cost_estimate=pl.CostEstimate(
            flops=4 * every * width * width * 4 + 20 * every * rows * width,
            bytes_accessed=20 * 2**20,
            transcendentals=every * rows * HEADS,
        ),
        name="attention_backward",
    )(lens, seq, gain, shift, q, k, v, mixed, ghidden, wqkv, wout, order)


BITS = ("core", "y", "z0", "x", "z1")
ORDERS = (("core", "y", "z0", "x", "z1"), ("core", "z0", "y", "x", "z1"))


def partner(bit):
    if bit == "x":
        return {"mod": 1 - lax.axis_index("mod")}
    size = {"core": 1, "y": 2, "z0": 4, "z1": 8}[bit]
    me = lax.axis_index("pairs")
    return {"pairs": me + size - 2 * size * (me // size % 2)}


def narrowed(ref, names, bit, value):
    dim = names.index(bit)
    index = (slice(None),) * dim + (value,)
    return ref.at[index], names[:dim] + names[dim + 1 :]


def flip(value, bit):
    return value + bit - 2 * value * bit


def place():
    pairs = lax.axis_index("pairs")
    return {
        "core": pairs % 2,
        "y": pairs // 2 % 2,
        "z0": pairs // 4 % 2,
        "z1": pairs // 8,
        "x": lax.axis_index("mod"),
    }


def hop(bit, source, target, sems, index, there=None):
    return pltpu.make_async_remote_copy(
        src_ref=source,
        dst_ref=target,
        send_sem=sems[0].at[index],
        recv_sem=sems[1].at[index if there is None else there],
        device_id=partner(bit),
        device_id_type=pl.DeviceIdType.MESH,
    )


def lead_index(it, lead):
    index = []
    for size in reversed(lead):
        index.insert(0, it % size)
        it = it // size
    return tuple(index)


def accumulate(target, source):
    lead = target.shape[:-3]
    count = 1
    for size in lead:
        count *= size
    if count == 1:
        at = (0,) * len(lead)
        target[at] = target[at] + source[at]
        return

    def body(it, carry):
        at = lead_index(it, lead)
        target[at] = target[at] + source[at]
        return carry

    lax.fori_loop(0, count, body, 0)


class Unit:
    def __init__(self, own, arrivals, order, sems, base, finish):
        self.own, self.arrivals, self.order = own, arrivals, order
        self.sems, self.base, self.finish = sems, base, finish
        self.peers = {}

    def views(self, step):
        ref, names = self.own, list(BITS)
        for bit in self.order[:step]:
            ref, names = narrowed(ref, names, bit, 0)
        sent, _ = narrowed(ref, names, self.order[step], 1)
        kept, _ = narrowed(ref, names, self.order[step], 0)
        return sent, kept

    def copy(self, step):
        bit = self.order[step]
        sent, _ = self.views(step)
        peer = self.peers.get(bit, self)
        return hop(bit, sent, peer.arrivals[step], self.sems, self.base + step, peer.base + step)

    def arrival(self, step):
        sent, _ = self.views(step)
        return hop(self.order[step], sent, self.arrivals[step], self.sems, self.base + step)

    def start(self):
        self.copy(0).start()

    def advance(self, step):
        self.arrival(step).wait_recv()
        _, kept = self.views(step)
        if step == 4:
            self.finish(kept[...].astype(F32) + self.arrivals[4][...].astype(F32))
            return
        accumulate(kept, self.arrivals[step])
        self.copy(step + 1).start()

    def drain(self):
        for step in range(5):
            self.copy(step).wait_send()


def counts(here, pairs, text_len, patch_count):
    base = here["x"] * pairs
    return [text_len[base + pair] for pair in range(pairs)] + [patch_count[base + pair] for pair in range(pairs)]


def opening_kernel(pairs, slots, names, *refs):
    r = types.SimpleNamespace(**dict(zip(names, refs)))
    rows, width = r.seq.shape[1:]
    every, tail = pairs * rows, rows - slots
    here = place()
    lens = counts(here, pairs, r.text_len, r.patch_count)
    sems = (r.send_sem, r.recv_sem)
    barrier = pltpu.get_barrier_semaphore()
    pl.semaphore_signal(barrier, inc=1, device_id=partner("x"), device_id_type=pl.DeviceIdType.MESH)

    def moves(which, pair):
        source, target = ((r.inputs, r.seq), (r.cotangent, r.cot))[which]
        index = which * pairs + pair
        patches, texts = target.at[pair, pl.ds(0, slots)], target.at[pair, pl.ds(slots, tail)]
        near = lambda src, dst: pltpu.make_async_copy(src, dst, r.load_sem.at[index])
        return (
            hop("x", source.at[0, pair], patches, sems, index),
            hop("x", source.at[0, pairs + pair, pl.ds(0, tail)], texts, sems, index),
            near(source.at[0, pairs + pair], patches),
            near(source.at[0, pair, pl.ds(0, tail)], texts),
        )

    every_move = [(which, pair) for which in range(2) for pair in range(pairs)]
    weights = [
        pltpu.make_async_copy(source, target, r.load_sem.at[2 * pairs + index])
        for index, (source, target) in enumerate(((r.wqkv_in, r.wqkv), (r.wout_in, r.wout)))
    ]
    pl.semaphore_wait(barrier, 1)

    @pl.when(here["x"] == 1)
    def _():
        for move in every_move:
            moves(*move)[0].start()
        for move in every_move:
            moves(*move)[2].start()

    @pl.when(here["x"] == 0)
    def _():
        for move in every_move:
            moves(*move)[1].start()
        for move in every_move:
            moves(*move)[3].start()

    for copy in weights:
        copy.start()

    def arrived(which, pair):
        @pl.when(here["x"] == 1)
        def _():
            moves(which, pair)[1].wait_recv()
            moves(which, pair)[2].wait()

        @pl.when(here["x"] == 0)
        def _():
            moves(which, pair)[0].wait_recv()
            moves(which, pair)[3].wait()

    place_at = lax.broadcasted_iota(jnp.int32, (width, 1), 0)
    feature = lax.broadcasted_iota(jnp.int32, (width, width), 1)
    unit = width // 32
    block = place_at // unit
    bit = lambda shift: (block >> shift) & 1
    owner = (bit(0) << 4) + (bit(2) << 3) + (bit(3) << 2) + (bit(4) << 1) + bit(1)
    owner = owner ^ (lax.axis_index("pairs") * 2 + here["x"])
    source = owner * unit + (place_at - block * unit)
    r.order[...] = (source == feature).astype(F32).astype(BF16)
    vec = lambda index: r.vecs[index : index + 1, :]
    for copy in weights:
        copy.wait()
    for pair in range(pairs):
        arrived(0, pair)
        tokens = r.seq[pair].astype(F32)
        normed, _ = norm_parts(tokens)
        normal = (normed * vec(0) + vec(1)).astype(BF16)
        r.normal[pair] = normal
        for part, ref in enumerate((r.q_out, r.k_out, r.v_out)):
            made = dot(normal, r.wqkv[:, part * width : (part + 1) * width])
            if part == 0:
                made = (made + vec(2)) * 0.125
            if part == 2:
                made = made + vec(3)
            ref[pair] = made.astype(BF16)

        def step(group, carry):
            mix_heads(pair, group, lens[pair], lens[pairs + pair], slots, r.q_out, r.k_out, r.v_out, r.mixed)
            return carry

        lax.fori_loop(0, width // 128, step, 0)
        made = r.seq[pair].astype(F32) + dot(r.mixed[pair], r.wout[...]) + vec(4)
        r.hidden[pair * rows : (pair + 1) * rows, :] = made
    stores = [
        pltpu.make_async_copy(r.seq, r.seq_out, r.store_sem.at[0]),
        pltpu.make_async_copy(r.cot, r.cot_out, r.store_sem.at[1]),
    ]
    stores[0].start()
    r.mixed_out[...] = dot(r.order[...], r.mixed[...].reshape(every, width), 1, 1).astype(BF16)
    r.normal_out[...] = dot(r.order[...], r.normal[...].reshape(every, width), 1, 1).astype(BF16)
    for pair in range(pairs):
        arrived(1, pair)
    stores[1].start()

    @pl.when(here["x"] == 1)
    def _():
        for move in every_move:
            moves(*move)[0].wait_send()

    @pl.when(here["x"] == 0)
    def _():
        for move in every_move:
            moves(*move)[1].wait_send()

    for copy in stores:
        copy.wait()


def run_opening(text_len, patch_count, inputs, cotangent, vecs, wqkv, wout):
    _, group, slots, width = inputs.shape
    pairs = group // 2
    rows = padded(TEXT + slots)
    every = pairs * rows
    hbm = pl.BlockSpec(memory_space=pl.ANY)
    operands = dict(
        text_len=(text_len, smem_spec()),
        patch_count=(patch_count, smem_spec()),
        inputs=(inputs, hbm),
        cotangent=(cotangent, hbm),
        vecs=(vecs, whole_spec()),
        wqkv_in=(wqkv, hbm),
        wout_in=(wout, hbm),
    )
    cube = shape((pairs, rows, width), BF16)
    tall = shape((width, every), BF16)
    outs = dict(
        q_out=(cube, whole_spec()),
        k_out=(cube, whole_spec()),
        v_out=(cube, whole_spec()),
        hidden=(shape((every, width), F32), whole_spec()),
        mixed_out=(tall, whole_spec()),
        normal_out=(tall, whole_spec()),
        seq_out=(cube, hbm),
        cot_out=(cube, hbm),
        order=(shape((width, width), BF16), whole_spec()),
    )
    held = pltpu.VMEM((pairs, rows, width), BF16)
    scratch = dict(
        seq=held,
        cot=held,
        mixed=held,
        normal=held,
        wqkv=pltpu.VMEM(wqkv.shape, BF16),
        wout=pltpu.VMEM(wout.shape, BF16),
        send_sem=pltpu.SemaphoreType.DMA((2 * pairs,)),
        recv_sem=pltpu.SemaphoreType.DMA((2 * pairs,)),
        load_sem=pltpu.SemaphoreType.DMA((2 * pairs + 2,)),
        store_sem=pltpu.SemaphoreType.DMA((2,)),
    )
    names = list(operands) + list(outs) + list(scratch)
    return pl.pallas_call(
        functools.partial(opening_kernel, pairs, slots, names),
        out_shape=[kind for kind, _ in outs.values()],
        in_specs=[spec for _, spec in operands.values()],
        out_specs=[spec for _, spec in outs.values()],
        scratch_shapes=list(scratch.values()),
        compiler_params=pltpu.CompilerParams(collective_id=2, has_side_effects=True, vmem_limit_bytes=VMEM_LIMIT),
        name="opening",
    )(*[value for value, _ in operands.values()])


A, B, C, O, H, V, R = range(7)
PLAN = {
    3: [(A, 0, 0)],
    4: [(B, 0, 0)],
    5: [(A, 0, 1)],
    6: [(B, 1, 0)],
    7: [(A, 0, 2), (A, 1, 0)],
    8: [(B, 2, 0), (B, 2, 1), (A, 1, 1)],
    10: [(B, 3, 0), (B, 3, 1)],
    11: [(A, 1, 2), (A, 2, 0), (B, 3, 2), (B, 4, 0)],
    12: [(A, 2, 1), (B, 0, 1), (B, 2, 2)],
    13: [(A, 0, 3), (B, 1, 1), (B, 3, 3), (B, 5, 0)],
    14: [(B, 2, 3), (A, 2, 2), (A, 3, 0)],
    15: [(B, 1, 2)],
    16: [(B, 0, 2), (B, 1, 3), (B, 6, 0), (B, 6, 1), (A, 3, 1), (R, 0, 0)],
    17: [(B, 7, 0), (B, 7, 1), (H, 0, 0), (B, 0, 3), (R, 0, 1)],
    18: [(A, 3, 2), (B, 7, 2)],
    19: [(B, 6, 2)],
    20: [(B, 4, 1)],
    21: [(O, 0, 0), (R, 0, 2)],
    22: [(A, 1, 3), (B, 5, 1), (B, 7, 3), (H, 0, 1), (A, 0, 4), (B, 7, 4), (B, 5, 2), (B, 6, 3), (B, 6, 4), (R, 0, 3)],
    23: [(R, 0, 4)],
    24: [(B, 5, 3), (B, 2, 4), (B, 3, 4), (B, 5, 4), (R, 0, 5)],
    25: [(O, 0, 1), (R, 0, 6)],
    26: [(B, 4, 2), (H, 0, 2), (B, 1, 4), (R, 0, 7)],
    27: [(C, 0, 0), (R, 0, 8)],
    28: [(O, 0, 2), (C, 1, 0), (B, 4, 3), (H, 0, 3), (B, 4, 4), (R, 0, 9)],
    29: [(C, 2, 0), (R, 1, 0)],
    30: [(C, 0, 1), (O, 0, 3), (C, 3, 0), (B, 0, 4), (H, 0, 4), (R, 1, 1)],
    31: [(C, 1, 1), (C, 4, 0), (R, 1, 2)],
    32: [(C, 0, 2), (C, 2, 1), (C, 5, 0), (O, 0, 4), (R, 1, 3)],
}
TAIL = [
    (C, 1, 2), (V, 0, 0), (C, 3, 1), (R, 1, 4), (C, 0, 3), (C, 2, 2),
    (C, 4, 1), (R, 2, 0), (C, 1, 3), (C, 3, 2), (C, 5, 1), (R, 2, 1),
    (C, 2, 3), (V, 0, 1), (C, 0, 4), (C, 4, 2), (R, 2, 2), (C, 3, 3),
    (C, 5, 2), (V, 0, 2), (C, 1, 4), (C, 4, 3), (R, 2, 3), (C, 2, 4),
    (C, 5, 3), (R, 2, 4), (V, 0, 3), (C, 3, 4), (C, 4, 4), (C, 5, 4),
    (V, 0, 4),
]


def fused_kernel(pairs, slots, names, *refs):
    r = types.SimpleNamespace(**dict(zip(names, refs)))
    rows, width = r.seq.shape[1:]
    every = pairs * rows
    tail = rows - slots
    here = place()
    lens = counts(here, pairs, r.text_len, r.patch_count)
    vec_in = lambda index: r.vecs[index : index + 1, :]
    sems = (r.send_sem, r.recv_sem)
    barrier = pltpu.get_barrier_semaphore()
    for bit in BITS:
        pl.semaphore_signal(barrier, inc=1, device_id=partner(bit), device_id_type=pl.DeviceIdType.MESH)

    def load(name, target, index):
        return pltpu.make_async_copy(getattr(r, name), getattr(r, target), r.load_sem.at[index])

    early = [load("hidden_in", "hidden", 0), load("order_in", "order", 1), load("cot_in", "cot", 2)]
    late = [
        load("mixed_in", "mixed_t", 3),
        load("normal_in", "normal_t", 4),
        load("seq_in", "seq", 5),
        load("q_in", "q", 6),
        load("k_in", "k", 7),
        load("v_in", "v", 8),
    ]

    def block_of(t):
        z1, z0 = 1 - t // 2, 1 - t % 2
        return flip(z0, here["z0"]) + 2 * flip(z1, here["z1"])

    def weight_loads(t, slot):
        start = pl.multiple_of(block_of(t) * width, width)
        return (
            pltpu.make_async_copy(r.wh.at[:, pl.ds(start, width)], r.wbuf.at[slot], r.w_sem.at[slot]),
            pltpu.make_async_copy(r.wd.at[pl.ds(start, width), :], r.wbuf.at[2 + slot], r.w_sem.at[2 + slot]),
        )

    early[0].start()
    early[1].start()
    for copy in weight_loads(0, 0):
        copy.start()
    early[2].start()
    early[0].wait()
    live = live_rows(lens, pairs, rows, slots)
    normed, _ = norm_parts(r.hidden[...])
    made = (normed * vec_in(5) + vec_in(6)).astype(BF16)
    r.normal2[...] = made
    early[1].wait()
    r.normal2_t[...] = dot(r.order[...], made, 1, 1).astype(BF16)
    r.total[...] = r.hidden[...] + vec_in(7)
    r.gnormal[...] = jnp.zeros_like(r.gnormal)
    early[2].wait()
    r.gdown[...] = (r.cot[...].reshape(every, width).astype(F32) * live).astype(BF16)
    r.unit_h[...] = jnp.zeros_like(r.unit_h)
    for copy in late:
        copy.start()
    r.zeros[...] = jnp.zeros_like(r.zeros)
    pl.semaphore_wait(barrier, len(BITS))

    def blanks():
        return [
            pltpu.make_async_copy(r.zeros, out.at[0, pair, pl.ds(tail, slots - tail)], r.zero_sem.at[2 * pair + index])
            for index, out in enumerate((r.block_out, r.input_grad))
            for pair in range(2 * pairs)
        ]

    @pl.when(here["x"] == 0)
    def _():
        for copy in blanks():
            copy.start()

    arrivals = lambda name, index: [getattr(r, name + str(step)).at[index] for step in range(5)]

    a_core = lambda t, y: hop("core", r.a_own.at[t, 1, y], r.a_core.at[t, y], sems, 2 * t + y)
    a_y = lambda t: hop("y", r.a_own.at[t, 0, 1], r.a_y.at[t], sems, 8 + t)
    a_z0 = lambda k: hop("z0", r.a_own.at[2 * k, 0, 0], r.a_z0.at[k], sems, 12 + k)
    a_x = lambda k: hop("x", r.a_own.at[2 * k + 1, 0, 0, 1], r.a_x.at[k], sems, 14 + k)
    a_z1 = lambda: hop("z1", r.a_own.at[1, 0, 0, 0], r.a_z1.at[0], sems, 16)

    def a_core_sum(t, y):
        a_core(t, y).wait_recv()
        accumulate(r.a_own.at[t, 0, y], r.a_core.at[t, y])
        if y == 1:
            a_y(t).start()

    def a_second(t):
        k = t // 2
        a_y(t).wait_recv()
        accumulate(r.a_own.at[t, 0, 0], r.a_y.at[t])
        if t % 2 == 0:
            a_z0(k).start()
        else:
            a_z0(k).wait_recv()
            accumulate(r.a_own.at[t, 0, 0], r.a_z0.at[k])
            a_x(k).start()

    def a_third(k):
        a_x(k).wait_recv()
        accumulate(r.a_own.at[2 * k + 1, 0, 0, pl.ds(0, 1)], r.a_x.at[pl.ds(k, 1)])
        if k == 0:
            a_z1().start()

    def a_last():
        a_z1().wait_recv()
        r.out_a[...] = r.a_own[3, 0, 0, 0].astype(F32) + r.a_z1[0].astype(F32)

    size = width // 2

    def b_columns(u):
        return block_of(u // 2) * width + flip(1 - u % 2, here["y"]) * size

    def b_finish(u):
        def finish(value):
            r.out_b[:, :, pl.ds(pl.multiple_of(b_columns(u), 128), size)] = value

        return finish

    def c_finish(g):
        def finish(value):
            for part in range(3):
                cols = slice(part * width + 128 * g, part * width + 128 * g + 128)
                r.out_c[:, :, cols] = value[:, :, 128 * part : 128 * part + 128]

        return finish

    def plain(target):
        def finish(value):
            target[...] = value

        return finish

    units = {}
    for u in range(8):
        units[B, u] = Unit(r.b_own.at[u], arrivals("b", u), ORDERS[1], sems, 20 + 5 * u, b_finish(u))
    for u in range(8):
        units[B, u].peers = {"y": units[B, u ^ 1], "z0": units[B, u ^ 2], "z1": units[B, u ^ 4]}
    groups = width // 128
    for g in range(groups):
        units[C, g] = Unit(r.c_own.at[g], arrivals("c", g), ORDERS[(g + 1) % 2], sems, 60 + 5 * g, c_finish(g))
    units[O, 0] = Unit(r.o_own, arrivals("o", 0), ORDERS[0], sems, 90, plain(r.out_o))
    units[H, 0] = Unit(r.unit_h, arrivals("h", 0), ORDERS[1], sems, 95, plain(r.out_h))
    units[V, 0] = Unit(r.unit_v, arrivals("v", 0), ORDERS[0], sems, 100, plain(r.out_v))

    def give(source, target, pair, index):
        near = lambda src, dst: pltpu.make_async_copy(src, dst, r.give_sem.at[index])
        part = lambda first, count: hop(
            "x", source.at[pair, pl.ds(first, count)], target.at[0, pair, pl.ds(first, count)], sems, 105 + index
        )
        patches, texts = source.at[pair, pl.ds(0, slots)], source.at[pair, pl.ds(slots, tail)]
        far_texts = hop("x", texts, target.at[0, pairs + pair, pl.ds(0, tail)], sems, 105 + index)
        near_texts = lambda: near(texts, target.at[0, pair, pl.ds(0, tail)])
        near_patches = lambda: near(patches, target.at[0, pairs + pair])
        return part, far_texts, near_texts, near_patches

    gives = [give(r.result, r.block_out, pair, pair) for pair in range(pairs)]
    gives += [give(r.grad_rows, r.input_grad, pair, pairs + pair) for pair in range(pairs)]

    def give_start(index):
        _, far_texts, near_texts, near_patches = gives[index]

        @pl.when(here["x"] == 0)
        def _():
            near_texts().start()

        @pl.when(here["x"] == 1)
        def _():
            far_texts.start()
            near_patches().start()

    def give_part(index, piece):
        @pl.when(here["x"] == 0)
        def _():
            gives[index][0](tail * piece, tail).start()

    def give_wait(index):
        part, far_texts, near_texts, near_patches = gives[index]

        @pl.when(here["x"] == 0)
        def _():
            far_texts.wait_recv()
            part(0, slots).wait_send()
            near_texts().wait()

        @pl.when(here["x"] == 1)
        def _():
            part(0, slots).wait_recv()
            far_texts.wait_send()
            near_patches().wait()

    def act(kind, piece, step):
        if kind == R:
            pieces = slots // tail
            give_part(step // pieces if piece == 0 else pairs + piece - 1, step % pieces)
        elif kind != A:
            units[kind, piece].advance(step)
        elif step < 2:
            a_core_sum(piece, 1 - step)
        else:
            (a_second, a_third, lambda _: a_last())[step - 2](piece)

    def run_now(tick):
        for item in PLAN.get(tick, []):
            act(*item)

    def run_tasks(ticks, now):
        for tick in ticks:
            if tick in PLAN:

                @pl.when(now == tick)
                def _(tick=tick):
                    run_now(tick)

    def feed_step(t, carry):
        slot = t % 2
        for copy in weight_loads(t, slot):
            copy.wait()

        @pl.when(t < 3)
        def _():
            for copy in weight_loads(t + 1, 1 - slot):
                copy.start()

        for sub in range(2):
            run_tasks([4 * k + 2 * sub for k in range(4)], 4 * t + 2 * sub)
            y = 1 - sub
            part = flip(y, here["y"])
            start = pl.multiple_of(part * size, size)
            wh = r.wbuf[slot, :, pl.ds(start, size)]
            wd = r.wbuf[2 + slot, pl.ds(start, size), :]
            before = dot(r.normal2[...], wh) + r.vecs[pl.ds(8 + block_of(t), 1), pl.ds(start, size)]
            active, slope = gelu_parts(before)
            active = active.astype(BF16)
            r.total[...] += dot(active, wd)
            fresh = dot(active, r.gdown[...], 0, 0)
            quarter = size // 4
            for core in range(2):
                for mod in range(2):
                    first = (2 * core + mod) * quarter
                    piece = fresh[first : first + quarter].reshape(quarter // 8, 8, width)
                    r.a_own[t, flip(core, here["core"]), y, flip(mod, here["x"])] = piece.astype(BF16)
            a_core(t, y).start()
            run_tasks([4 * k + 2 * sub + 1 for k in range(4)], 4 * t + 2 * sub + 1)
            gbefore = (dot(r.gdown[...], wd, 1, 1) * slope).astype(BF16)
            r.gnormal[...] += dot(gbefore, wh, 1, 1)
            fresh = dot(r.normal2_t[...], gbefore)
            fresh = fresh.reshape((2,) * 5 + (width // 256, 8, size)).astype(BF16)
            unit = 2 * t + sub
            r.b_own[unit] = fresh
            hop("core", r.b_own.at[unit, 1], r.b0.at[unit], sems, 20 + 5 * unit).start()
            sums = jnp.sum(gbefore.astype(F32), axis=0, keepdims=True)
            z1, z0 = 1 - t // 2, 1 - t % 2
            for core in range(2):
                for mod in range(2):
                    first = (2 * core + mod) * quarter
                    r.unit_h[
                        flip(core, here["core"]), y, z0, flip(mod, here["x"]), z1, 0, 0:1, 0:quarter
                    ] = sums[:, first : first + quarter]
        return carry

    lax.fori_loop(0, 4, feed_step, 0)

    wout_load = pltpu.make_async_copy(r.wout, r.wbuf.at[3], r.w_sem.at[3])
    wout_load.start()
    wqkv_loads = [
        pltpu.make_async_copy(
            r.wqkv.at[:, pl.ds(part * width, width)], r.wbuf.at[part], r.w_sem.at[part]
        )
        for part in range(3)
    ]
    for copy in wqkv_loads:
        copy.start()
    units[H, 0].start()
    r.result[...] = (r.total[...] * live).astype(BF16).reshape(pairs, rows, width)

    for pair in range(pairs):
        give_start(pair)
    run_now(16)
    normed, factor = norm_parts(r.hidden[...])
    gnorm = r.gnormal[...]
    down = r.gdown[...].astype(F32)
    vec = [
        jnp.sum(gnorm * normed, axis=0, keepdims=True),
        jnp.sum(gnorm, axis=0, keepdims=True),
        jnp.sum(down, axis=0, keepdims=True),
    ]
    made = down + norm_back(gnorm, normed, factor, vec_in(5))
    gattended = made.astype(BF16)
    vec.append(jnp.sum(gattended.astype(F32), axis=0, keepdims=True))
    for index, value in enumerate(vec):
        r.vec[4 + index : 5 + index, :] = value
    r.gnormal[...] = made
    run_now(17)
    wout_load.wait()
    r.gmixed[...] = dot(gattended, r.wbuf[3], 1, 1).astype(BF16).reshape(pairs, rows, width)
    for copy in late:
        copy.wait()
    fresh = dot(r.mixed_t[...], gattended)
    r.o_own[...] = fresh.reshape((2,) * 5 + (width // 256, 8, width)).astype(BF16)
    units[O, 0].start()
    for copy in wqkv_loads:
        copy.wait()

    first = lax.broadcasted_iota(jnp.int32, (rows, 128), 1) < HEAD_DIM
    index = lax.broadcasted_iota(jnp.int32, (rows, 1), 0)

    def project_back(pair):
        made = jnp.zeros((rows, width), F32)
        sums = []
        for part in range(3):
            piece = r.gproj[pair, :, part * width : (part + 1) * width]
            made += dot(piece, r.wbuf[part], 1, 1)
            sums.append(jnp.sum(piece.astype(F32), axis=0, keepdims=True))
        return made, sums

    def finish_pair(pair, grad, sums):
        normed, factor = norm_parts(r.seq[pair].astype(F32))
        sums = [
            jnp.sum(grad * normed, axis=0, keepdims=True),
            jnp.sum(grad, axis=0, keepdims=True),
            sums[0],
            sums[2],
        ]
        for index, value in enumerate(sums):
            r.vec[index : index + 1, :] = value if pair == 0 else r.vec[index : index + 1, :] + value
        span = slice(pair * rows, (pair + 1) * rows)
        made = r.gnormal[span, :] + norm_back(grad, normed, factor, vec_in(0))
        r.grad_rows[pair] = (made * live[span]).astype(BF16)
        give_start(pairs + pair)

    def head_step(it, carry):
        pair, g = it // groups, it % groups
        base = g * 128
        off = pl.multiple_of(base, 128)

        @pl.when(it == groups)
        def _():
            finish_pair(0, *project_back(0))

        run_tasks([18 + k for k in range(pairs * groups)], 18 + it)
        at_pair = here["x"] * pairs + pair
        keys_live = live_slots(index, r.text_len[at_pair], r.patch_count[at_pair], slots)
        q2 = r.q[pair, :, pl.ds(off, 128)]
        k2 = r.k[pair, :, pl.ds(off, 128)]
        v2 = r.v[pair, :, pl.ds(off, 128)]
        g2 = r.gmixed[pair, :, pl.ds(off, 128)]
        gq = gk = gv = None
        for half in range(2):
            keep = first if half == 0 else ~first
            zero = jnp.zeros_like(q2)
            qm = jnp.where(keep, q2, zero)
            km = jnp.where(keep, k2, zero)
            gm = jnp.where(keep, g2, zero)
            scores = jnp.where(keys_live, dot(k2, qm, 1, 1), MASKED)
            highest = jnp.max(scores, axis=0, keepdims=True)
            shifted = jnp.exp(scores - highest)
            probs = shifted * (1.0 / jnp.sum(shifted, axis=0, keepdims=True))
            gprobs = dot(v2, gm, 1, 1)
            row_dot = jnp.sum(probs * gprobs, axis=0, keepdims=True)
            gscores = (probs * (gprobs - row_dot)).astype(BF16)
            new_v = dot(probs.astype(BF16), gm)
            new_k = dot(gscores, qm)
            new_q = dot(gscores, km, 0, 0)
            gq = new_q if gq is None else gq + new_q
            gk = new_k if gk is None else gk + new_k
            gv = new_v if gv is None else gv + new_v
        r.gproj[pair, :, pl.ds(off, 128)] = (gq * 0.125).astype(BF16)
        r.gproj[pair, :, pl.ds(pl.multiple_of(base + width, 128), 128)] = gk.astype(BF16)
        r.gproj[pair, :, pl.ds(pl.multiple_of(base + 2 * width, 128), 128)] = gv.astype(BF16)

        @pl.when(it >= (pairs - 1) * groups)
        def _():
            pieces = [
                r.gproj[:, :, pl.ds(pl.multiple_of(base + part * width, 128), 128)].reshape(every, 128)
                for part in range(3)
            ]
            fresh = dot(r.normal_t[...], jnp.concatenate(pieces, axis=1))
            r.c_own[g] = fresh.reshape((2,) * 5 + (width // 256, 8, 384)).astype(BF16)
            hop("core", r.c_own.at[g, 1], r.c0.at[g], sems, 60 + 5 * g).start()

        return carry

    lax.fori_loop(0, pairs * groups, head_step, 0)

    run_now(30)
    made, sums = project_back(1)
    run_now(31)
    finish_pair(1, made, sums)
    rest = r.vec[...]
    ordered = jnp.zeros_like(rest)
    for _ in range(3):
        high = rest.astype(BF16)
        ordered += dot(high, r.order[...], 1, 1)
        rest = rest - high.astype(F32)
    r.unit_v[...] = jnp.zeros_like(r.unit_v)
    unit = width // 32
    for block in range(32):
        bits = tuple(block >> shift & 1 for shift in (4, 3, 2, 1, 0))
        r.unit_v[bits + (0, slice(None), slice(0, unit))] = ordered[:, block * unit : (block + 1) * unit]
    units[V, 0].start()
    run_now(32)
    for item in TAIL:
        act(*item)
    for number in range(2 * pairs):
        give_wait(number)

    @pl.when(here["x"] == 0)
    def _():
        for copy in blanks():
            copy.wait()

    for t in range(4):
        a_core(t, 0).wait_send()
        a_core(t, 1).wait_send()
        a_y(t).wait_send()
    for k in range(2):
        a_z0(k).wait_send()
        a_x(k).wait_send()
    a_z1().wait_send()
    for unit in units.values():
        unit.drain()


def run_fused(text_len, patch_count, vecs, hidden, cot, wh, wd, order, wqkv, wout, seq, q, k, v, mixed_t, normal_t, slots):
    pairs, rows, width = seq.shape
    every = pairs * rows
    wide = (2,) * 5
    eight = width // 256
    groups = width // 128

    def arrivals(name, count, tail, kind):
        return {name + str(step): pltpu.VMEM((count,) + (2,) * (4 - step) + tail, kind) for step in range(5)}

    flat = lambda kind: pltpu.VMEM((every, width), kind)
    cube = pltpu.VMEM((pairs, rows, width), BF16)
    tall = pltpu.VMEM((width, every), BF16)
    block = (width // 64, 8, width)
    scratch = dict(
        cot=cube,
        result=cube,
        grad_rows=cube,
        zeros=pltpu.VMEM((slots - (rows - slots), width), BF16),
        give_sem=pltpu.SemaphoreType.DMA((2 * pairs,)),
        zero_sem=pltpu.SemaphoreType.DMA((4 * pairs,)),
        hidden=flat(F32),
        gdown=flat(BF16),
        seq=cube,
        q=cube,
        k=cube,
        v=cube,
        mixed_t=tall,
        normal_t=tall,
        wbuf=pltpu.VMEM((4, width, width), BF16),
        order=pltpu.VMEM((width, width), BF16),
        normal2=flat(BF16),
        normal2_t=tall,
        total=flat(F32),
        gnormal=flat(F32),
        gmixed=cube,
        gproj=pltpu.VMEM((pairs, rows, 3 * width), BF16),
        vec=pltpu.VMEM((8, width), F32),
        a_own=pltpu.VMEM((4, 2, 2, 2) + block, BF16),
        a_core=pltpu.VMEM((4, 2, 2) + block, BF16),
        a_y=pltpu.VMEM((4, 2) + block, BF16),
        a_z0=pltpu.VMEM((2, 2) + block, BF16),
        a_x=pltpu.VMEM((2,) + block, BF16),
        a_z1=pltpu.VMEM((1,) + block, BF16),
        b_own=pltpu.VMEM((8,) + wide + (eight, 8, width // 2), BF16),
        **arrivals("b", 8, (eight, 8, width // 2), BF16),
        c_own=pltpu.VMEM((groups,) + wide + (eight, 8, 384), BF16),
        **arrivals("c", groups, (eight, 8, 384), BF16),
        o_own=pltpu.VMEM(wide + (eight, 8, width), BF16),
        **arrivals("o", 1, (eight, 8, width), BF16),
        unit_h=pltpu.VMEM(wide + (1, 8, 128), F32),
        **arrivals("h", 1, (1, 8, 128), F32),
        unit_v=pltpu.VMEM(wide + (1, 8, 128), F32),
        **arrivals("v", 1, (1, 8, 128), F32),
        send_sem=pltpu.SemaphoreType.DMA((105 + 2 * pairs,)),
        recv_sem=pltpu.SemaphoreType.DMA((105 + 2 * pairs,)),
        load_sem=pltpu.SemaphoreType.DMA((9,)),
        w_sem=pltpu.SemaphoreType.DMA((4,)),
    )
    hbm = pl.BlockSpec(memory_space=pl.ANY)
    operands = dict(
        text_len=(text_len, smem_spec()),
        patch_count=(patch_count, smem_spec()),
        vecs=(vecs, whole_spec()),
        hidden_in=(hidden, hbm),
        cot_in=(cot, hbm),
        wh=(wh, hbm),
        wd=(wd, hbm),
        order_in=(order, hbm),
        wqkv=(wqkv, hbm),
        wout=(wout, hbm),
        seq_in=(seq, hbm),
        q_in=(q, hbm),
        k_in=(k, hbm),
        v_in=(v, hbm),
        mixed_in=(mixed_t, hbm),
        normal_in=(normal_t, hbm),
    )
    final = shape((1, 2 * pairs, slots, width), BF16)
    outs = dict(
        block_out=(final, hbm),
        input_grad=(final, hbm),
        out_a=(shape(block, F32), whole_spec()),
        out_b=(shape((eight, 8, 4 * width), F32), whole_spec()),
        out_c=(shape((eight, 8, 3 * width), F32), whole_spec()),
        out_o=(shape((eight, 8, width), F32), whole_spec()),
        out_h=(shape((1, 8, 128), F32), whole_spec()),
        out_v=(shape((1, 8, 128), F32), whole_spec()),
    )
    names = list(operands) + list(outs) + list(scratch)
    return pl.pallas_call(
        functools.partial(fused_kernel, pairs, slots, names),
        out_shape=[kind for kind, _ in outs.values()],
        in_specs=[spec for _, spec in operands.values()],
        out_specs=[spec for _, spec in outs.values()],
        scratch_shapes=list(scratch.values()),
        compiler_params=pltpu.CompilerParams(
            collective_id=1, has_side_effects=True, vmem_limit_bytes=67043328
        ),
        name="fused",
    )(*[value for value, _ in operands.values()])


def pair_bits():
    return lax.axis_size("pairs").bit_length() - 1


def swapped(array, axis, bit):
    size = lax.axis_size(axis)
    return lax.ppermute(array, axis, [(i, i ^ (1 << bit)) for i in range(size)])


def split_dims(array):
    bits = pair_bits() + 1
    return array.reshape((2,) * bits + (array.shape[0] >> bits,) + array.shape[1:])


def stage_orders():
    bits = pair_bits()
    ring = ["mod", 1, 2]
    orders = []
    for turn in range(3):
        orders.append([0] + ring[turn:] + ring[:turn] + list(range(3, bits)))
    return orders


def half_sum(array, names, name, last):
    axis, bit = ("mod", 0) if name == "mod" else ("pairs", name)
    mine = (lax.axis_index(axis) >> bit) & 1
    dim = names.index(name)
    sent = lax.dynamic_index_in_dim(array, 1 - mine, dim, keepdims=False)
    kept = lax.dynamic_index_in_dim(array, mine, dim, keepdims=False)
    came = swapped(sent, axis, bit)
    total = kept.astype(F32) + came.astype(F32)
    return (total if last else total.astype(BF16)), names[:dim] + names[dim + 1 :]


def scattered(array):
    width = array.shape[1]
    names0 = list(range(pair_bits() - 1, -1, -1)) + ["mod"]
    first, names1 = half_sum(split_dims(array), names0, 0, False)
    third = -(-width // 3 // 128) * 128
    pieces = []
    for turn, order in enumerate(stage_orders()):
        piece = first[..., turn * third : min(width, (turn + 1) * third)]
        names = list(names1)
        for place, name in enumerate(order[1:]):
            piece, names = half_sum(piece, names, name, place == len(order) - 2)
        pieces.append(piece)
    return jnp.concatenate(pieces, axis=1)


def on_device(
    inputs,
    cotangent,
    text_len,
    patch_count,
    norm1_gain,
    norm1_bias,
    qkv_weight,
    query_bias,
    value_bias,
    out_weight,
    out_bias,
    norm2_gain,
    norm2_bias,
    hidden_weight,
    hidden_bias,
    down_weight,
    down_bias,
):
    _, group, slots, width = inputs.shape
    half = group // 2
    rows = padded(TEXT + slots)
    mod = lax.axis_index("mod")
    is_text = mod == 0
    lens = lax.dynamic_slice_in_dim(jnp.stack([text_len, patch_count]), mod * half, half, 1)
    lens = lens.reshape(-1)

    def gathered(array):
        local = array[0]
        patches = lax.ppermute(local[:half], "mod", [(1, 0)])
        texts = lax.ppermute(local[half:, :TEXT], "mod", [(0, 1)])
        patches = jnp.where(is_text, patches, local[half:])
        texts = jnp.where(is_text, local[:half, :TEXT], texts)
        blank = jnp.zeros((half, rows - slots - TEXT, width), array.dtype)
        return jnp.concatenate([patches, texts, blank], axis=1)

    def returned(array):
        far_patches = lax.ppermute(array[:, :slots], "mod", [(0, 1)])
        far_texts = lax.ppermute(array[:, slots : slots + TEXT], "mod", [(1, 0)])
        return assembled(array, far_patches, far_texts)

    def assembled(array, far_patches, far_texts):
        patches, texts = array[:, :slots], array[:, slots : slots + TEXT]
        texts = jnp.concatenate([texts, far_texts], axis=0)
        texts = jnp.pad(texts, ((0, 0), (0, slots - TEXT), (0, 0)))
        patches = jnp.concatenate([far_patches, patches], axis=0)
        return jnp.where(is_text, texts, patches)[None]

    row = lambda vector: vector.reshape(1, -1)
    if lax.axis_size("pairs") == 16:
        parts = [norm1_gain, norm1_bias, query_bias, value_bias, out_bias, norm2_gain, norm2_bias, down_bias, hidden_bias]
        vecs = jnp.concatenate(parts).reshape(-1, width)
        made = run_opening(text_len, patch_count, inputs, cotangent, vecs, qkv_weight, out_weight)
        q, k, v, hidden, mixed, normal, seq, cot, order = made
        made = run_fused(
            text_len,
            patch_count,
            vecs,
            hidden,
            cot,
            hidden_weight,
            down_weight,
            order,
            qkv_weight,
            out_weight,
            seq,
            q,
            k,
            v,
            mixed,
            normal,
            slots,
        )
        block_out, input_grad, wd_out, wh_out, qkv_out, wo_out, hb_out, vec_out = made
        flat = lambda array: array.reshape(-1, array.shape[-1])
        wd_out, wh_out, qkv_out, wo_out = flat(wd_out), flat(wh_out), flat(qkv_out), flat(wo_out)
        vec_out = vec_out[0, :, : width // 32].T
        hb_out = hb_out[0, 0, : hidden_bias.shape[0] // 32]
    else:
        seq = gathered(inputs)
        cot = gathered(cotangent).reshape(half * rows, width)
        qkv_bias = row(jnp.concatenate([query_bias, jnp.zeros_like(query_bias), value_bias]))
        feature = jnp.arange(width, dtype=jnp.int32)
        order = (feature[:, None] == feature[None, :]).astype(BF16)
        q, k, v, hidden, mixed = run_forward(
            lens, seq, row(norm1_gain), row(norm1_bias), qkv_weight, qkv_bias, out_weight, row(out_bias), slots
        )
        chunks = 8
        steps = jnp.arange(chunks, dtype=jnp.int32)
        lens = jnp.concatenate([lens, jnp.zeros(4, jnp.int32), steps])
        result, ghidden, wh_grad, wd_grad, hb_grad, vec2 = run_feed(
            lens,
            hidden,
            cot,
            row(norm2_gain),
            row(norm2_bias),
            hidden_weight,
            row(hidden_bias),
            down_weight,
            row(down_bias),
            order,
            half,
            slots,
            chunks,
            False,
        )
        block_out = returned(result.reshape(half, rows, width))
        input_rows, qkvo_grad, vec1 = run_backward(
            lens,
            seq,
            row(norm1_gain),
            row(norm1_bias),
            q,
            k,
            v,
            mixed,
            ghidden,
            qkv_weight,
            out_weight,
            order,
            slots,
            False,
        )
        input_grad = returned(input_rows)
        strip = jnp.concatenate([vec1[:4], vec2[:4]], axis=0).T
        strip = jnp.concatenate([strip, hb_grad.reshape(width, -1)], axis=1).astype(BF16)
        strip = jnp.pad(strip, ((0, 0), (0, 128 - strip.shape[1])))
        wd_out, wh_out = scattered(wd_grad), scattered(wh_grad)
        qkvo_out = scattered(jnp.concatenate([qkvo_grad, strip], axis=1))
        vec_out = qkvo_out[:, 4 * width :]
        qkv_out, wo_out = qkvo_out[:, : 3 * width], qkvo_out[:, 3 * width : 4 * width]
        hb_out = vec_out[:, 8 : 8 + hidden_bias.shape[0] // width].reshape(-1)
    return (
        block_out,
        input_grad,
        vec_out[:, 0],
        vec_out[:, 1],
        qkv_out,
        vec_out[:, 2],
        vec_out[:, 3],
        wo_out,
        vec_out[:, 7],
        vec_out[:, 4],
        vec_out[:, 5],
        wh_out,
        hb_out,
        wd_out,
        vec_out[:, 6],
    )


def solution(mesh):
    whole = P()
    split = P("mod", "pairs", None, None)
    vector = P(("pairs", "mod"))
    matrix = P(("pairs", "mod"), None)
    return jax.shard_map(
        on_device,
        mesh=mesh,
        in_specs=(split, split, P("pairs"), P("pairs")) + (whole,) * 13,
        out_specs=(
            split,
            split,
            vector,
            vector,
            matrix,
            vector,
            vector,
            matrix,
            vector,
            vector,
            vector,
            matrix,
            vector,
            matrix,
            vector,
        ),
        check_vma=False,
    )
```

```python
import functools
import types

import jax
import jax.numpy as jnp
from jax import lax
from jax.experimental import pallas as pl
from jax.experimental.pallas import tpu as pltpu
from jax.sharding import PartitionSpec as P

HEADS = 12
HEAD_DIM = 64
TEXT = 40
EPSILON = 1e-06
MASKED = -1e30
F32 = jnp.float32
BF16 = jnp.bfloat16
VMEM_LIMIT = 60 * 1024 * 1024


def padded(count):
    return -(-count // 32) * 32


def dot(a, b, ca=1, cb=0):
    return lax.dot_general(a, b, (((ca,), (cb,)), ((), ())), preferred_element_type=F32)


def norm_parts(values):
    centre = jnp.mean(values, axis=-1, keepdims=True)
    centred = values - centre
    spread = jnp.mean(centred * centred, axis=-1, keepdims=True)
    factor = lax.rsqrt(spread + EPSILON)
    return centred * factor, factor


def norm_back(grad_out, normed, factor, norm_gain):
    grad_norm = grad_out * norm_gain
    mean_grad = jnp.mean(grad_norm, axis=-1, keepdims=True)
    second = jnp.mean(grad_norm * normed, axis=-1, keepdims=True)
    return (grad_norm - mean_grad - normed * second) * factor


def live_slots(index, text_count, patch_count, slots):
    return (index < patch_count) | ((index >= slots) & (index - slots < text_count))


def live_rows(lens, pairs, rows, slots):
    parts = []
    for pair in range(pairs):
        index = lax.broadcasted_iota(jnp.int32, (rows, 1), 0)
        parts.append(live_slots(index, lens[pair], lens[pairs + pair], slots).astype(F32))
    return jnp.concatenate(parts, axis=0)


def mix_heads(pair, group, text_count, patch_count, slots, q_in, k_in, v_in, mixed):
    rows = q_in.shape[1]
    first = lax.broadcasted_iota(jnp.int32, (rows, 128), 1) < HEAD_DIM
    column = lax.broadcasted_iota(jnp.int32, (1, rows), 1)
    off = pl.multiple_of(group * 128, 128)
    live = live_slots(column, text_count, patch_count, slots)
    q2 = q_in[pair, :, pl.ds(off, 128)]
    k2 = k_in[pair, :, pl.ds(off, 128)]
    v2 = v_in[pair, :, pl.ds(off, 128)]
    halves = []
    for half in range(2):
        keep = first if half == 0 else ~first
        qm = jnp.where(keep, q2, jnp.zeros_like(q2))
        scores = jnp.where(live, dot(qm, k2, 1, 1), MASKED)
        highest = jnp.max(scores, axis=-1, keepdims=True)
        shifted = jnp.exp(scores - highest)
        total = jnp.sum(shifted, axis=-1, keepdims=True)
        halves.append(dot(shifted.astype(BF16), v2) / total)
    mixed[pair, :, pl.ds(off, 128)] = jnp.where(first, halves[0], halves[1]).astype(BF16)


def forward_kernel(
    slots,
    lens,
    seq,
    gain,
    shift,
    wqkv,
    qkv_bias,
    wout,
    out_bias,
    q_out,
    k_out,
    v_out,
    hidden,
    mixed_out,
    mixed,
):
    pairs, rows, width = seq.shape
    tokens = seq[...].reshape(pairs * rows, width).astype(F32)
    normed, _ = norm_parts(tokens)
    normal = (normed * gain[...] + shift[...]).astype(BF16)
    for part, ref in enumerate((q_out, k_out, v_out)):
        cols = slice(part * width, (part + 1) * width)
        made = dot(normal, wqkv[:, cols]) + qkv_bias[:, cols]
        if part == 0:
            made = made * 0.125
        ref[...] = made.astype(BF16).reshape(pairs, rows, width)
    groups = width // 128

    def step(it, carry):
        pair = it // groups
        mix_heads(pair, it % groups, lens[pair], lens[pairs + pair], slots, q_out, k_out, v_out, mixed)
        return carry

    lax.fori_loop(0, pairs * groups, step, 0)
    rows_mixed = mixed[...].reshape(pairs * rows, width)
    mixed_out[...] = mixed[...]
    hidden[...] = tokens + dot(rows_mixed, wout[...]) + out_bias[...]


def gelu_parts(values):
    cumulative = 0.5 * (1.0 + lax.erf(values * 0.7071067811865476))
    density = jnp.exp(-0.5 * values * values) * 0.3989422804014327
    return values * cumulative, cumulative + values * density


def feed_kernel(
    pairs,
    slots,
    lens,
    hidden,
    cot,
    gain,
    shift,
    wh,
    hbias,
    wd,
    dbias,
    order,
    result,
    grad_hidden,
    wh_grad,
    wd_grad,
    hb_grad,
    vectors,
    normal,
    ordered,
    gdown,
    total,
    gnormal,
):
    chunk = pl.program_id(0)
    count = pl.num_programs(0)
    rows = hidden.shape[0] // pairs
    live = live_rows(lens, pairs, rows, slots)

    @pl.when(chunk == 0)
    def _():
        normed, _ = norm_parts(hidden[...])
        made = (normed * gain[...] + shift[...]).astype(BF16)
        normal[...] = made
        ordered[...] = dot(made, order[...]).astype(BF16)
        gdown[...] = (cot[...].astype(F32) * live).astype(BF16)
        total[...] = hidden[...] + dbias[...]
        gnormal[...] = jnp.zeros_like(gnormal)

    before = dot(normal[...], wh[...]) + hbias[...]
    active, slope = gelu_parts(before)
    active = active.astype(BF16)
    total[...] += dot(active, wd[...])
    fresh = dot(active, gdown[...], 0, 0)
    if wd_grad.ndim == 2:
        wd_grad[...] = fresh.astype(BF16)
    else:
        size = fresh.shape[0] // 4
        base = 2 * pairs
        for core in range(2):
            for mod in range(2):
                start = (2 * core + mod) * size
                piece = fresh[start : start + size].reshape(size // 8, 8, fresh.shape[1])
                wd_grad[lens[base + core], 0, 0, lens[base + 2 + mod], 0] = piece.astype(BF16)
    gbefore = (dot(gdown[...], wd[...], 1, 1) * slope).astype(BF16)
    gnormal[...] += dot(gbefore, wh[...], 1, 1)
    wh_grad[...] = dot(ordered[...], gbefore, 0, 0).reshape(wh_grad.shape).astype(BF16)
    hb_grad[...] = jnp.sum(gbefore.astype(F32), axis=0, keepdims=True)

    @pl.when(chunk == count - 1)
    def _():
        result[...] = (total[...] * live).astype(BF16)
        normed, factor = norm_parts(hidden[...])
        gnorm = gnormal[...]
        vectors[0:1, :] = jnp.sum(gnorm * normed, axis=0, keepdims=True)
        vectors[1:2, :] = jnp.sum(gnorm, axis=0, keepdims=True)
        down = gdown[...].astype(F32)
        vectors[2:3, :] = jnp.sum(down, axis=0, keepdims=True)
        made = down + norm_back(gnorm, normed, factor, gain[...])
        vectors[3:4, :] = jnp.sum(made.astype(BF16).astype(F32), axis=0, keepdims=True)
        grad_hidden[...] = made


def backward_kernel(
    slots,
    lens,
    seq,
    gain,
    shift,
    q_in,
    k_in,
    v_in,
    mixed,
    ghidden,
    wqkv,
    wout,
    order,
    input_grad,
    weight_grad,
    vectors,
    gmixed,
    gproj,
):
    pairs, rows, width = seq.shape
    every = pairs * rows
    gattended = ghidden[...].astype(BF16)
    gmixed[...] = dot(gattended, wout[...], 1, 1).astype(BF16).reshape(pairs, rows, width)
    ordered = dot(mixed[...].reshape(every, width), order[...]).astype(BF16)

    def put(first, last, value):
        target = (slice(None),) * (len(weight_grad.shape) - 1) + (slice(first, last),)
        value = value.reshape(weight_grad.shape[:-1] + (last - first,))
        weight_grad[target] = value.astype(BF16)

    put(3 * width, 4 * width, dot(ordered, gattended, 0, 0))
    first = lax.broadcasted_iota(jnp.int32, (rows, 128), 1) < HEAD_DIM
    index = lax.broadcasted_iota(jnp.int32, (rows, 1), 0)
    groups = width // 128

    def step(it, carry):
        pair = it // groups
        base = (it % groups) * 128
        off = pl.multiple_of(base, 128)
        live = live_slots(index, lens[pair], lens[pairs + pair], slots)
        q2 = q_in[pair, :, pl.ds(off, 128)]
        k2 = k_in[pair, :, pl.ds(off, 128)]
        v2 = v_in[pair, :, pl.ds(off, 128)]
        g2 = gmixed[pair, :, pl.ds(off, 128)]
        gq = gk = gv = None
        for half in range(2):
            keep = first if half == 0 else ~first
            zero = jnp.zeros_like(q2)
            qm = jnp.where(keep, q2, zero)
            km = jnp.where(keep, k2, zero)
            gm = jnp.where(keep, g2, zero)
            scores = jnp.where(live, dot(k2, qm, 1, 1), MASKED)
            highest = jnp.max(scores, axis=0, keepdims=True)
            shifted = jnp.exp(scores - highest)
            probs = shifted * (1.0 / jnp.sum(shifted, axis=0, keepdims=True))
            gprobs = dot(v2, gm, 1, 1)
            row_dot = jnp.sum(probs * gprobs, axis=0, keepdims=True)
            gscores = (probs * (gprobs - row_dot)).astype(BF16)
            new_v = dot(probs.astype(BF16), gm)
            new_k = dot(gscores, qm)
            new_q = dot(gscores, km, 0, 0)
            gq = new_q if gq is None else gq + new_q
            gk = new_k if gk is None else gk + new_k
            gv = new_v if gv is None else gv + new_v
        gproj[pair, :, pl.ds(off, 128)] = (gq * 0.125).astype(BF16)
        gproj[pair, :, pl.ds(pl.multiple_of(base + width, 128), 128)] = gk.astype(BF16)
        gproj[pair, :, pl.ds(pl.multiple_of(base + 2 * width, 128), 128)] = gv.astype(BF16)
        return carry

    lax.fori_loop(0, pairs * groups, step, 0)
    tokens = seq[...].reshape(every, width).astype(F32)
    normed, factor = norm_parts(tokens)
    normal = (normed * gain[...] + shift[...]).astype(BF16)
    ordered = dot(normal, order[...]).astype(BF16)
    gnormal = jnp.zeros((every, width), F32)
    for part in range(3):
        cols = slice(part * width, (part + 1) * width)
        piece = gproj[:, :, cols].reshape(every, width)
        gnormal += dot(piece, wqkv[:, cols], 1, 1)
        put(part * width, (part + 1) * width, dot(ordered, piece, 0, 0))
        if part == 0:
            vectors[2:3, :] = jnp.sum(piece.astype(F32), axis=0, keepdims=True)
        if part == 2:
            vectors[3:4, :] = jnp.sum(piece.astype(F32), axis=0, keepdims=True)
    vectors[0:1, :] = jnp.sum(gnormal * normed, axis=0, keepdims=True)
    vectors[1:2, :] = jnp.sum(gnormal, axis=0, keepdims=True)
    live = live_rows(lens, pairs, rows, slots)
    made = ghidden[...] + norm_back(gnormal, normed, factor, gain[...])
    input_grad[...] = (made * live).astype(BF16).reshape(pairs, rows, width)


def whole_spec():
    return pl.BlockSpec(memory_space=pltpu.VMEM)


def smem_spec():
    return pl.BlockSpec(memory_space=pltpu.SMEM)


def shape(dims, kind):
    return jax.ShapeDtypeStruct(dims, kind)


def run_forward(lens, seq, gain, shift, wqkv, qkv_bias, wout, out_bias, slots):
    pairs, rows, width = seq.shape
    every = pairs * rows
    cube = shape((pairs, rows, width), BF16)
    return pl.pallas_call(
        functools.partial(forward_kernel, slots),
        out_shape=[cube, cube, cube, shape((every, width), F32), cube],
        in_specs=[smem_spec()] + [whole_spec()] * 7,
        out_specs=[whole_spec()] * 5,
        scratch_shapes=[pltpu.VMEM((pairs, rows, width), BF16)],
        compiler_params=pltpu.CompilerParams(vmem_limit_bytes=VMEM_LIMIT),
        name="attention_forward",
    )(lens, seq, gain, shift, wqkv, qkv_bias, wout, out_bias)


def run_feed(lens, hidden, cot, gain, shift, wh, hbias, wd, dbias, order, pairs, slots, chunks, relative):
    every, width = hidden.shape
    ff = wh.shape[1]
    size = ff // chunks
    base = 2 * pairs + 4
    fixed = lambda dims: pl.BlockSpec(dims, lambda c, s: (0, 0))
    columns = lambda r: pl.BlockSpec((r, size), lambda c, s: (0, s[base + c]))
    rows = pl.BlockSpec((size, width), lambda c, s: (s[base + c], 0))
    if relative:
        part = size // 4 // 8
        wd_shape = shape((2, 2, 2, 2, 2, part, 8, width), BF16)
        wd_spec = pl.BlockSpec(
            (2, 1, 1, 2, 1, part, 8, width),
            lambda c, s: (0, c % 2, c // 2 % 2, 0, c // 4, 0, 0, 0),
        )
        wh_shape = shape((width // 8, 8, ff), BF16)
        wh_spec = pl.BlockSpec((width // 8, 8, size), lambda c, s: (0, 0, s[base + c]))
    else:
        wd_shape, wd_spec = shape((ff, width), BF16), rows
        wh_shape, wh_spec = shape((width, ff), BF16), columns(width)
    return pl.pallas_call(
        functools.partial(feed_kernel, pairs, slots),
        out_shape=[
            shape((every, width), BF16),
            shape((every, width), F32),
            wh_shape,
            wd_shape,
            shape((1, ff), F32),
            shape((8, width), F32),
        ],
        grid_spec=pltpu.PrefetchScalarGridSpec(
        num_scalar_prefetch=1,
        grid=(chunks,),
        in_specs=[
            fixed((every, width)),
            fixed((every, width)),
            fixed((1, width)),
            fixed((1, width)),
            columns(width),
            columns(1),
            rows,
            fixed((1, width)),
            fixed((width, width)),
        ],
        out_specs=[
            fixed((every, width)),
            fixed((every, width)),
            wh_spec,
            wd_spec,
            columns(1),
            fixed((8, width)),
        ],
        scratch_shapes=[
            pltpu.VMEM((every, width), BF16),
            pltpu.VMEM((every, width), BF16),
            pltpu.VMEM((every, width), BF16),
            pltpu.VMEM((every, width), F32),
            pltpu.VMEM((every, width), F32),
        ],
        ),
        compiler_params=pltpu.CompilerParams(vmem_limit_bytes=VMEM_LIMIT),
        cost_estimate=pl.CostEstimate(
            flops=12 * every * width * ff,
            bytes_accessed=24 * 2**20,
            transcendentals=2 * every * ff,
        ),
        name="feed_forward",
    )(lens, hidden, cot, gain, shift, wh, hbias, wd, dbias, order)


def run_backward(lens, seq, gain, shift, q, k, v, mixed, ghidden, wqkv, wout, order, slots, relative):
    pairs, rows, width = seq.shape
    every = pairs * rows
    return pl.pallas_call(
        functools.partial(backward_kernel, slots),
        out_shape=[
            shape((pairs, rows, width), BF16),
            shape((width // 8, 8, 4 * width) if relative else (width, 4 * width), BF16),
            shape((8, width), F32),
        ],
        in_specs=[smem_spec()] + [whole_spec()] * 11,
        out_specs=[whole_spec()] * 3,
        scratch_shapes=[
            pltpu.VMEM((pairs, rows, width), BF16),
            pltpu.VMEM((pairs, rows, 3 * width), BF16),
        ],
        compiler_params=pltpu.CompilerParams(vmem_limit_bytes=VMEM_LIMIT),
        cost_estimate=pl.CostEstimate(
            flops=4 * every * width * width * 4 + 20 * every * rows * width,
            bytes_accessed=20 * 2**20,
            transcendentals=every * rows * HEADS,
        ),
        name="attention_backward",
    )(lens, seq, gain, shift, q, k, v, mixed, ghidden, wqkv, wout, order)


BITS = ("core", "y", "z0", "x", "z1")
ORDERS = (("core", "y", "z0", "x", "z1"), ("core", "z0", "y", "x", "z1"))


def partner(bit):
    if bit == "x":
        return {"mod": 1 - lax.axis_index("mod")}
    size = {"core": 1, "y": 2, "z0": 4, "z1": 8}[bit]
    me = lax.axis_index("pairs")
    return {"pairs": me + size - 2 * size * (me // size % 2)}


def narrowed(ref, names, bit, value):
    dim = names.index(bit)
    index = (slice(None),) * dim + (value,)
    return ref.at[index], names[:dim] + names[dim + 1 :]


def flip(value, bit):
    return value + bit - 2 * value * bit


def place():
    pairs = lax.axis_index("pairs")
    return {
        "core": pairs % 2,
        "y": pairs // 2 % 2,
        "z0": pairs // 4 % 2,
        "z1": pairs // 8,
        "x": lax.axis_index("mod"),
    }


def hop(bit, source, target, sems, index, there=None):
    return pltpu.make_async_remote_copy(
        src_ref=source,
        dst_ref=target,
        send_sem=sems[0].at[index],
        recv_sem=sems[1].at[index if there is None else there],
        device_id=partner(bit),
        device_id_type=pl.DeviceIdType.MESH,
    )


def lead_index(it, lead):
    index = []
    for size in reversed(lead):
        index.insert(0, it % size)
        it = it // size
    return tuple(index)


def accumulate(target, source):
    lead = target.shape[:-3]
    tiles = target.shape[-3] * target.shape[-2] * target.shape[-1] // 1024
    while lead and tiles * lead[-1] <= 72:
        tiles *= lead[-1]
        lead = lead[:-1]
    count = 1
    for size in lead:
        count *= size

    def add(at):
        target[at] = target[at] + source[at]

    if count == 1:
        add((0,) * len(lead) if lead else (Ellipsis,))
        return

    def body(it, carry):
        add(lead_index(it, lead))
        return carry

    lax.fori_loop(0, count, body, 0)


class Unit:
    def __init__(self, own, arrivals, order, sems, base, finish):
        self.own, self.arrivals, self.order = own, arrivals, order
        self.sems, self.base, self.finish = sems, base, finish
        self.peers = {}

    def views(self, step):
        ref, names = self.own, list(BITS)
        for bit in self.order[:step]:
            ref, names = narrowed(ref, names, bit, 0)
        sent, _ = narrowed(ref, names, self.order[step], 1)
        kept, _ = narrowed(ref, names, self.order[step], 0)
        return sent, kept

    def copy(self, step):
        bit = self.order[step]
        sent, _ = self.views(step)
        peer = self.peers.get(bit, self)
        return hop(bit, sent, peer.arrivals[step], self.sems, self.base + step, peer.base + step)

    def arrival(self, step):
        sent, _ = self.views(step)
        return hop(self.order[step], sent, self.arrivals[step], self.sems, self.base + step)

    def start(self):
        self.copy(0).start()

    def advance(self, step):
        self.arrival(step).wait_recv()
        _, kept = self.views(step)
        if step == 4:
            self.finish(kept[...].astype(F32) + self.arrivals[4][...].astype(F32))
            return
        accumulate(kept, self.arrivals[step])
        self.copy(step + 1).start()

    def drain(self):
        for step in range(5):
            self.copy(step).wait_send()


def counts(here, pairs, text_len, patch_count):
    base = here["x"] * pairs
    return [text_len[base + pair] for pair in range(pairs)] + [patch_count[base + pair] for pair in range(pairs)]


def opening_kernel(pairs, slots, names, *refs):
    r = types.SimpleNamespace(**dict(zip(names, refs)))
    rows, width = r.seq.shape[1:]
    every, tail = pairs * rows, rows - slots
    here = place()
    lens = counts(here, pairs, r.text_len, r.patch_count)
    sems = (r.send_sem, r.recv_sem)
    barrier = pltpu.get_barrier_semaphore()
    pl.semaphore_signal(barrier, inc=1, device_id=partner("x"), device_id_type=pl.DeviceIdType.MESH)

    def moves(which, pair):
        source, target = ((r.inputs, r.seq), (r.cotangent, r.cot))[which]
        index = which * pairs + pair
        patches, texts = target.at[pair, pl.ds(0, slots)], target.at[pair, pl.ds(slots, tail)]
        near = lambda src, dst: pltpu.make_async_copy(src, dst, r.load_sem.at[index])
        return (
            hop("x", source.at[0, pair], patches, sems, index),
            hop("x", source.at[0, pairs + pair, pl.ds(0, tail)], texts, sems, index),
            near(source.at[0, pairs + pair], patches),
            near(source.at[0, pair, pl.ds(0, tail)], texts),
        )

    every_move = [(which, pair) for which in range(2) for pair in range(pairs)]
    weights = [
        pltpu.make_async_copy(source, target, r.load_sem.at[2 * pairs + index])
        for index, (source, target) in enumerate(((r.wqkv_in, r.wqkv), (r.wout_in, r.wout)))
    ]
    pl.semaphore_wait(barrier, 1)

    @pl.when(here["x"] == 1)
    def _():
        for move in every_move:
            moves(*move)[0].start()
        for move in every_move:
            moves(*move)[2].start()

    @pl.when(here["x"] == 0)
    def _():
        for move in every_move:
            moves(*move)[1].start()
        for move in every_move:
            moves(*move)[3].start()

    for copy in weights:
        copy.start()

    def arrived(which, pair):
        @pl.when(here["x"] == 1)
        def _():
            moves(which, pair)[1].wait_recv()
            moves(which, pair)[2].wait()

        @pl.when(here["x"] == 0)
        def _():
            moves(which, pair)[0].wait_recv()
            moves(which, pair)[3].wait()

    place_at = lax.broadcasted_iota(jnp.int32, (width, 1), 0)
    feature = lax.broadcasted_iota(jnp.int32, (width, width), 1)
    unit = width // 32
    block = place_at // unit
    bit = lambda shift: (block >> shift) & 1
    owner = (bit(0) << 4) + (bit(2) << 3) + (bit(3) << 2) + (bit(4) << 1) + bit(1)
    owner = owner ^ (lax.axis_index("pairs") * 2 + here["x"])
    source = owner * unit + (place_at - block * unit)
    r.order[...] = (source == feature).astype(F32).astype(BF16)
    row = 0
    for index in range(9):
        part = getattr(r, str(index))
        for first in range(0, part.shape[0], width):
            r.vecs[row : row + 1, :] = part[first : first + width].reshape(1, width)
            row += 1
    vec = lambda index: r.vecs[index : index + 1, :]
    for copy in weights:
        copy.wait()
    for pair in range(pairs):
        arrived(0, pair)
        tokens = r.seq[pair].astype(F32)
        normed, _ = norm_parts(tokens)
        normal = (normed * vec(0) + vec(1)).astype(BF16)
        r.normal[pair] = normal
        for part, ref in enumerate((r.q_out, r.k_out, r.v_out)):
            made = dot(normal, r.wqkv[:, part * width : (part + 1) * width])
            if part == 0:
                made = (made + vec(2)) * 0.125
            if part == 2:
                made = made + vec(3)
            ref[pair] = made.astype(BF16)

        def step(group, carry):
            mix_heads(pair, group, lens[pair], lens[pairs + pair], slots, r.q_out, r.k_out, r.v_out, r.mixed)
            return carry

        lax.fori_loop(0, width // 128, step, 0)
        made = r.seq[pair].astype(F32) + dot(r.mixed[pair], r.wout[...]) + vec(4)
        r.hidden[pair * rows : (pair + 1) * rows, :] = made
    stores = [
        pltpu.make_async_copy(r.seq, r.seq_out, r.store_sem.at[0]),
        pltpu.make_async_copy(r.cot, r.cot_out, r.store_sem.at[1]),
    ]
    stores[0].start()
    r.mixed_out[...] = dot(r.order[...], r.mixed[...].reshape(every, width), 1, 1).astype(BF16)
    r.normal_out[...] = dot(r.order[...], r.normal[...].reshape(every, width), 1, 1).astype(BF16)
    normed, _ = norm_parts(r.hidden[...])
    made = (normed * vec(5) + vec(6)).astype(BF16)
    r.normal2[...] = made
    r.normal2_t[...] = dot(r.order[...], made, 1, 1).astype(BF16)
    for pair in range(pairs):
        arrived(1, pair)
    stores[1].start()

    @pl.when(here["x"] == 1)
    def _():
        for move in every_move:
            moves(*move)[0].wait_send()

    @pl.when(here["x"] == 0)
    def _():
        for move in every_move:
            moves(*move)[1].wait_send()

    for copy in stores:
        copy.wait()


def run_opening(text_len, patch_count, inputs, cotangent, parts, wqkv, wout):
    _, group, slots, width = inputs.shape
    pairs = group // 2
    rows = padded(TEXT + slots)
    every = pairs * rows
    hbm = pl.BlockSpec(memory_space=pl.ANY)
    operands = dict(
        text_len=(text_len, smem_spec()),
        patch_count=(patch_count, smem_spec()),
        inputs=(inputs, hbm),
        cotangent=(cotangent, hbm),
        wqkv_in=(wqkv, hbm),
        wout_in=(wout, hbm),
    )
    operands.update((index, (part, whole_spec())) for index, part in enumerate(parts))
    count = sum(part.shape[0] for part in parts) // width
    cube = shape((pairs, rows, width), BF16)
    tall = shape((width, every), BF16)
    outs = dict(
        vecs=(shape((count, width), F32), whole_spec()),
        q_out=(cube, whole_spec()),
        k_out=(cube, whole_spec()),
        v_out=(cube, whole_spec()),
        hidden=(shape((every, width), F32), whole_spec()),
        mixed_out=(tall, whole_spec()),
        normal_out=(tall, whole_spec()),
        normal2=(shape((every, width), BF16), whole_spec()),
        normal2_t=(tall, whole_spec()),
        seq_out=(cube, hbm),
        cot_out=(cube, hbm),
        order=(shape((width, width), BF16), whole_spec()),
    )
    held = pltpu.VMEM((pairs, rows, width), BF16)
    scratch = dict(
        seq=held,
        cot=held,
        mixed=held,
        normal=held,
        wqkv=pltpu.VMEM(wqkv.shape, BF16),
        wout=pltpu.VMEM(wout.shape, BF16),
        send_sem=pltpu.SemaphoreType.DMA((2 * pairs,)),
        recv_sem=pltpu.SemaphoreType.DMA((2 * pairs,)),
        load_sem=pltpu.SemaphoreType.DMA((2 * pairs + 2,)),
        store_sem=pltpu.SemaphoreType.DMA((2,)),
    )
    names = [str(name) for name in (*operands, *outs, *scratch)]
    return pl.pallas_call(
        functools.partial(opening_kernel, pairs, slots, names),
        out_shape=[kind for kind, _ in outs.values()],
        in_specs=[spec for _, spec in operands.values()],
        out_specs=[spec for _, spec in outs.values()],
        scratch_shapes=list(scratch.values()),
        compiler_params=pltpu.CompilerParams(collective_id=2, has_side_effects=True, vmem_limit_bytes=VMEM_LIMIT),
        name="opening",
    )(*[value for value, _ in operands.values()])


A, B, C, O, H, V, R = range(7)
PLAN = {
    3: [(A, 0, 0)],
    4: [(B, 0, 0)],
    5: [(A, 0, 1)],
    6: [(B, 1, 0)],
    7: [(A, 0, 2), (A, 1, 0)],
    8: [(B, 2, 0), (B, 2, 1)],
    9: [(A, 1, 1)],
    10: [(B, 3, 0), (B, 3, 1)],
    11: [(A, 2, 0), (A, 1, 2)],
    12: [(B, 2, 2), (B, 3, 2), (B, 4, 0)],
    13: [(A, 2, 1), (B, 0, 1)],
    14: [(A, 0, 3), (B, 1, 1), (B, 2, 3), (B, 3, 3), (B, 5, 0), (A, 3, 0)],
    15: [(A, 2, 2), (B, 1, 2), (B, 6, 0), (B, 6, 1)],
    16: [(A, 3, 1), (B, 0, 2), (B, 1, 3), (R, 0, 0)],
    17: [(R, 0, 1)],
    18: [(B, 0, 3), (B, 7, 0), (B, 7, 1), (H, 0, 0), (R, 0, 2)],
    19: [(R, 0, 3)],
    20: [(B, 7, 2)],
    21: [(A, 3, 2), (O, 0, 0), (B, 6, 2)],
    23: [(B, 4, 1), (B, 7, 3), (B, 7, 4), (R, 0, 4)],
    24: [(A, 1, 3), (B, 5, 1), (B, 6, 3), (H, 0, 1), (A, 0, 4), (B, 3, 4), (B, 6, 4), (R, 0, 5)],
    25: [(O, 0, 1), (R, 0, 6)],
    26: [(B, 5, 2), (B, 2, 4), (R, 0, 7)],
    27: [(C, 0, 0), (B, 4, 2), (H, 0, 2), (R, 0, 8)],
    28: [(O, 0, 2), (C, 1, 0), (B, 5, 3), (B, 5, 4)],
    29: [(C, 2, 0), (B, 4, 3), (H, 0, 3), (B, 4, 4), (R, 0, 9)],
    30: [(C, 0, 1), (C, 3, 0), (B, 1, 4), (O, 0, 3), (R, 1, 0)],
    31: [(C, 1, 1), (C, 4, 0), (B, 0, 4), (H, 0, 4), (R, 1, 1)],
    32: [(C, 2, 1), (C, 5, 0), (C, 0, 2), (R, 1, 2)],
}
TAIL = [
    (C, 1, 2), (V, 0, 0), (C, 3, 1), (R, 1, 3), (C, 0, 3), (O, 0, 4),
    (C, 2, 2), (C, 4, 1), (C, 1, 3), (R, 1, 4), (C, 3, 2), (C, 5, 1),
    (R, 2, 0), (C, 2, 3), (V, 0, 1), (C, 0, 4), (C, 4, 2), (R, 2, 1),
    (C, 3, 3), (C, 5, 2), (V, 0, 2), (C, 1, 4), (C, 4, 3), (R, 2, 2),
    (C, 2, 4), (C, 5, 3), (R, 2, 3), (V, 0, 3), (C, 3, 4), (C, 4, 4),
    (C, 5, 4), (R, 2, 4), (V, 0, 4),
]


def fused_kernel(pairs, slots, names, *refs):
    r = types.SimpleNamespace(**dict(zip(names, refs)))
    rows, width = r.seq.shape[1:]
    every = pairs * rows
    tail = rows - slots
    here = place()
    lens = counts(here, pairs, r.text_len, r.patch_count)
    vec_in = lambda index: r.vecs[index : index + 1, :]
    sems = (r.send_sem, r.recv_sem)
    barrier = pltpu.get_barrier_semaphore()
    for bit in BITS:
        pl.semaphore_signal(barrier, inc=1, device_id=partner(bit), device_id_type=pl.DeviceIdType.MESH)

    def load(name, target, index):
        return pltpu.make_async_copy(getattr(r, name), getattr(r, target), r.load_sem.at[index])

    early = [
        load("normal2_in", "normal2", 0),
        load("cot_in", "cot", 1),
        load("normal2_t_in", "normal2_t", 2),
        load("hidden_in", "hidden", 9),
    ]
    late = [
        load("mixed_in", "mixed_t", 3),
        load("normal_in", "normal_t", 4),
        load("seq_in", "seq", 5),
        load("q_in", "q", 6),
        load("k_in", "k", 7),
        load("v_in", "v", 8),
        load("order_in", "order", 10),
    ]

    def block_of(t):
        z1, z0 = 1 - t // 2, 1 - t % 2
        return flip(z0, here["z0"]) + 2 * flip(z1, here["z1"])

    def weight_loads(t, slot):
        start = pl.multiple_of(block_of(t) * width, width)
        return (
            pltpu.make_async_copy(r.wh.at[:, pl.ds(start, width)], r.wbuf.at[slot], r.w_sem.at[slot]),
            pltpu.make_async_copy(r.wd.at[pl.ds(start, width), :], r.wbuf.at[2 + slot], r.w_sem.at[2 + slot]),
        )

    early[0].start()
    for copy in weight_loads(0, 0):
        copy.start()
    for copy in early[1:]:
        copy.start()
    r.gnormal[...] = jnp.zeros_like(r.gnormal)
    live = live_rows(lens, pairs, rows, slots)
    for copy in early:
        copy.wait()
    r.total[...] = r.hidden[...] + vec_in(7)
    r.gdown[...] = (r.cot[...].reshape(every, width).astype(F32) * live).astype(BF16)
    r.unit_h[...] = jnp.zeros_like(r.unit_h)
    for copy in late:
        copy.start()
    pl.semaphore_wait(barrier, len(BITS))

    arrivals = lambda name, index: [getattr(r, name + str(step)).at[index] for step in range(5)]

    a_core = lambda t, y: hop("core", r.a_own.at[t, 1, y], r.a_core.at[t, y], sems, 2 * t + y)
    a_y = lambda t: hop("y", r.a_own.at[t, 0, 1], r.a_y.at[t], sems, 8 + t)
    a_z0 = lambda k: hop("z0", r.a_own.at[2 * k, 0, 0], r.a_z0.at[k], sems, 12 + k)
    a_x = lambda k: hop("x", r.a_own.at[2 * k + 1, 0, 0, 1], r.a_x.at[k], sems, 14 + k)
    a_z1 = lambda: hop("z1", r.a_own.at[1, 0, 0, 0], r.a_z1.at[0], sems, 16)

    def a_core_sum(t, y):
        a_core(t, y).wait_recv()
        accumulate(r.a_own.at[t, 0, y], r.a_core.at[t, y])
        if y == 1:
            a_y(t).start()

    def a_second(t):
        k = t // 2
        a_y(t).wait_recv()
        accumulate(r.a_own.at[t, 0, 0], r.a_y.at[t])
        if t % 2 == 0:
            a_z0(k).start()
        else:
            a_z0(k).wait_recv()
            accumulate(r.a_own.at[t, 0, 0], r.a_z0.at[k])
            a_x(k).start()

    def a_third(k):
        a_x(k).wait_recv()
        accumulate(r.a_own.at[2 * k + 1, 0, 0, pl.ds(0, 1)], r.a_x.at[pl.ds(k, 1)])
        if k == 0:
            a_z1().start()

    def a_last():
        a_z1().wait_recv()
        r.out_a[...] = r.a_own[3, 0, 0, 0].astype(F32) + r.a_z1[0].astype(F32)

    size = width // 2

    def b_columns(u):
        return block_of(u // 2) * width + flip(1 - u % 2, here["y"]) * size

    def b_finish(u):
        def finish(value):
            r.out_b[:, :, pl.ds(pl.multiple_of(b_columns(u), 128), size)] = value

        return finish

    def c_finish(g):
        def finish(value):
            for part in range(3):
                cols = slice(part * width + 128 * g, part * width + 128 * g + 128)
                r.out_c[:, :, cols] = value[:, :, 128 * part : 128 * part + 128]

        return finish

    def plain(target):
        def finish(value):
            target[...] = value

        return finish

    units = {}
    for u in range(8):
        units[B, u] = Unit(r.b_own.at[u], arrivals("b", u), ORDERS[1], sems, 20 + 5 * u, b_finish(u))
    for u in range(8):
        units[B, u].peers = {"y": units[B, u ^ 1], "z0": units[B, u ^ 2], "z1": units[B, u ^ 4]}
    groups = width // 128
    for g in range(groups):
        units[C, g] = Unit(r.c_own.at[g], arrivals("c", g), ORDERS[(g + 1) % 2], sems, 60 + 5 * g, c_finish(g))
    units[O, 0] = Unit(r.o_own, arrivals("o", 0), ORDERS[0], sems, 90, plain(r.out_o))
    units[H, 0] = Unit(r.unit_h, arrivals("h", 0), ORDERS[1], sems, 95, plain(r.out_v.at[pl.ds(1, 1)]))
    units[V, 0] = Unit(r.unit_v, arrivals("v", 0), ORDERS[0], sems, 100, plain(r.out_v.at[pl.ds(0, 1)]))

    def give(source, target, pair, index):
        near = lambda src, dst: pltpu.make_async_copy(src, dst, r.give_sem.at[index])
        part = lambda first, count: hop(
            "x", source.at[pair, pl.ds(first, count)], target.at[0, pair, pl.ds(first, count)], sems, 105 + index
        )
        patches, texts = source.at[pair, pl.ds(0, slots)], source.at[pair, pl.ds(slots, tail)]
        far_texts = hop("x", texts, target.at[0, pairs + pair, pl.ds(0, tail)], sems, 105 + index)
        near_texts = lambda: near(texts, target.at[0, pair, pl.ds(0, tail)])
        near_patches = lambda: near(patches, target.at[0, pairs + pair])
        return part, far_texts, near_texts, near_patches

    gives = [give(r.result, r.block_out, pair, pair) for pair in range(pairs)]
    gives += [give(r.grad_rows, r.input_grad, pair, pairs + pair) for pair in range(pairs)]

    def give_start(index):
        _, far_texts, near_texts, near_patches = gives[index]

        @pl.when(here["x"] == 0)
        def _():
            near_texts().start()

        @pl.when(here["x"] == 1)
        def _():
            far_texts.start()
            near_patches().start()

    def give_part(index, piece):
        @pl.when(here["x"] == 0)
        def _():
            gives[index][0](tail * piece, tail).start()

    def give_wait(index):
        part, far_texts, near_texts, near_patches = gives[index]

        @pl.when(here["x"] == 0)
        def _():
            far_texts.wait_recv()
            part(0, slots).wait_send()
            near_texts().wait()

        @pl.when(here["x"] == 1)
        def _():
            part(0, slots).wait_recv()
            far_texts.wait_send()
            near_patches().wait()

    def act(kind, piece, step):
        if kind == R:
            pieces = slots // tail
            give_part(step // pieces if piece == 0 else pairs + piece - 1, step % pieces)
        elif kind != A:
            units[kind, piece].advance(step)
        elif step < 2:
            a_core_sum(piece, 1 - step)
        else:
            (a_second, a_third, lambda _: a_last())[step - 2](piece)

    def run_now(tick):
        for item in PLAN.get(tick, []):
            act(*item)

    def run_tasks(ticks, now):
        for tick in ticks:
            if tick in PLAN:

                @pl.when(now == tick)
                def _(tick=tick):
                    run_now(tick)

    def feed_step(t, carry):
        slot = t % 2
        for copy in weight_loads(t, slot):
            copy.wait()

        @pl.when(t < 3)
        def _():
            for copy in weight_loads(t + 1, 1 - slot):
                copy.start()

        for sub in range(2):
            run_tasks([4 * k + 2 * sub for k in range(4)], 4 * t + 2 * sub)
            y = 1 - sub
            part = flip(y, here["y"])
            start = pl.multiple_of(part * size, size)
            wh = r.wbuf[slot, :, pl.ds(start, size)]
            wd = r.wbuf[2 + slot, pl.ds(start, size), :]
            before = dot(r.normal2[...], wh) + r.vecs[pl.ds(8 + block_of(t), 1), pl.ds(start, size)]
            active, slope = gelu_parts(before)
            active = active.astype(BF16)
            r.total[...] += dot(active, wd)
            fresh = dot(active, r.gdown[...], 0, 0)
            quarter = size // 4
            for core in range(2):
                for mod in range(2):
                    first = (2 * core + mod) * quarter
                    piece = fresh[first : first + quarter].reshape(quarter // 8, 8, width)
                    r.a_own[t, flip(core, here["core"]), y, flip(mod, here["x"])] = piece.astype(BF16)
            a_core(t, y).start()
            run_tasks([4 * k + 2 * sub + 1 for k in range(4)], 4 * t + 2 * sub + 1)
            gbefore = (dot(r.gdown[...], wd, 1, 1) * slope).astype(BF16)
            r.gnormal[...] += dot(gbefore, wh, 1, 1)
            fresh = dot(r.normal2_t[...], gbefore)
            fresh = fresh.reshape((2,) * 5 + (width // 256, 8, size)).astype(BF16)
            unit = 2 * t + sub
            r.b_own[unit] = fresh
            hop("core", r.b_own.at[unit, 1], r.b0.at[unit], sems, 20 + 5 * unit).start()
            sums = jnp.sum(gbefore.astype(F32), axis=0, keepdims=True)
            z1, z0 = 1 - t // 2, 1 - t % 2
            for core in range(2):
                for mod in range(2):
                    first = (2 * core + mod) * quarter
                    r.unit_h[
                        flip(core, here["core"]), y, z0, flip(mod, here["x"]), z1, 0, 0:1, 0:quarter
                    ] = sums[:, first : first + quarter]
        return carry

    lax.fori_loop(0, 4, feed_step, 0)

    wout_load = pltpu.make_async_copy(r.wout, r.wbuf.at[3], r.w_sem.at[3])
    wout_load.start()
    wqkv_loads = [
        pltpu.make_async_copy(
            r.wqkv.at[:, pl.ds(part * width, width)], r.wbuf.at[part], r.w_sem.at[part]
        )
        for part in range(3)
    ]
    for copy in wqkv_loads:
        copy.start()
    units[H, 0].start()
    r.result[...] = (r.total[...] * live).astype(BF16).reshape(pairs, rows, width)

    for pair in range(pairs):
        give_start(pair)
    run_now(16)
    normed, factor = norm_parts(r.hidden[...])
    gnorm = r.gnormal[...]
    down = r.gdown[...].astype(F32)
    vec = [
        jnp.sum(gnorm * normed, axis=0, keepdims=True),
        jnp.sum(gnorm, axis=0, keepdims=True),
        jnp.sum(down, axis=0, keepdims=True),
    ]
    made = down + norm_back(gnorm, normed, factor, vec_in(5))
    gattended = made.astype(BF16)
    vec.append(jnp.sum(gattended.astype(F32), axis=0, keepdims=True))
    for index, value in enumerate(vec):
        r.vec[4 + index : 5 + index, :] = value
    r.gnormal[...] = made
    run_now(17)
    wout_load.wait()
    r.gmixed[...] = dot(gattended, r.wbuf[3], 1, 1).astype(BF16).reshape(pairs, rows, width)
    for copy in late:
        copy.wait()
    fresh = dot(r.mixed_t[...], gattended)
    r.o_own[...] = fresh.reshape((2,) * 5 + (width // 256, 8, width)).astype(BF16)
    units[O, 0].start()
    for copy in wqkv_loads:
        copy.wait()

    first = lax.broadcasted_iota(jnp.int32, (rows, 128), 1) < HEAD_DIM
    index = lax.broadcasted_iota(jnp.int32, (rows, 1), 0)

    def project_back(pair):
        made = jnp.zeros((rows, width), F32)
        sums = []
        for part in range(3):
            piece = r.gproj[pair, :, part * width : (part + 1) * width]
            made += dot(piece, r.wbuf[part], 1, 1)
            sums.append(jnp.sum(piece.astype(F32), axis=0, keepdims=True))
        return made, sums

    def finish_pair(pair, grad, sums):
        normed, factor = norm_parts(r.seq[pair].astype(F32))
        sums = [
            jnp.sum(grad * normed, axis=0, keepdims=True),
            jnp.sum(grad, axis=0, keepdims=True),
            sums[0],
            sums[2],
        ]
        for index, value in enumerate(sums):
            r.vec[index : index + 1, :] = value if pair == 0 else r.vec[index : index + 1, :] + value
        span = slice(pair * rows, (pair + 1) * rows)
        made = r.gnormal[span, :] + norm_back(grad, normed, factor, vec_in(0))
        r.grad_rows[pair] = (made * live[span]).astype(BF16)
        give_start(pairs + pair)

    def head_step(it, carry):
        pair, g = it // groups, it % groups
        base = g * 128
        off = pl.multiple_of(base, 128)

        @pl.when(it == groups)
        def _():
            finish_pair(0, *project_back(0))

        run_tasks([18 + k for k in range(pairs * groups)], 18 + it)
        at_pair = here["x"] * pairs + pair
        keys_live = live_slots(index, r.text_len[at_pair], r.patch_count[at_pair], slots)
        q2 = r.q[pair, :, pl.ds(off, 128)]
        k2 = r.k[pair, :, pl.ds(off, 128)]
        v2 = r.v[pair, :, pl.ds(off, 128)]
        g2 = r.gmixed[pair, :, pl.ds(off, 128)]
        gq = gk = gv = None
        for half in range(2):
            keep = first if half == 0 else ~first
            zero = jnp.zeros_like(q2)
            qm = jnp.where(keep, q2, zero)
            km = jnp.where(keep, k2, zero)
            gm = jnp.where(keep, g2, zero)
            scores = jnp.where(keys_live, dot(k2, qm, 1, 1), MASKED)
            highest = jnp.max(scores, axis=0, keepdims=True)
            shifted = jnp.exp(scores - highest)
            probs = shifted * (1.0 / jnp.sum(shifted, axis=0, keepdims=True))
            gprobs = dot(v2, gm, 1, 1)
            row_dot = jnp.sum(probs * gprobs, axis=0, keepdims=True)
            gscores = (probs * (gprobs - row_dot)).astype(BF16)
            new_v = dot(probs.astype(BF16), gm)
            new_k = dot(gscores, qm)
            new_q = dot(gscores, km, 0, 0)
            gq = new_q if gq is None else gq + new_q
            gk = new_k if gk is None else gk + new_k
            gv = new_v if gv is None else gv + new_v
        r.gproj[pair, :, pl.ds(off, 128)] = (gq * 0.125).astype(BF16)
        r.gproj[pair, :, pl.ds(pl.multiple_of(base + width, 128), 128)] = gk.astype(BF16)
        r.gproj[pair, :, pl.ds(pl.multiple_of(base + 2 * width, 128), 128)] = gv.astype(BF16)

        @pl.when(it >= (pairs - 1) * groups)
        def _():
            pieces = [
                r.gproj[:, :, pl.ds(pl.multiple_of(base + part * width, 128), 128)].reshape(every, 128)
                for part in range(3)
            ]
            fresh = dot(r.normal_t[...], jnp.concatenate(pieces, axis=1))
            r.c_own[g] = fresh.reshape((2,) * 5 + (width // 256, 8, 384)).astype(BF16)
            hop("core", r.c_own.at[g, 1], r.c0.at[g], sems, 60 + 5 * g).start()

        return carry

    lax.fori_loop(0, pairs * groups, head_step, 0)

    run_now(30)
    made, sums = project_back(1)
    run_now(31)
    finish_pair(1, made, sums)
    rest = r.vec[...]
    ordered = jnp.zeros_like(rest)
    for _ in range(3):
        high = rest.astype(BF16)
        ordered += dot(high, r.order[...], 1, 1)
        rest = rest - high.astype(F32)
    r.unit_v[...] = jnp.zeros_like(r.unit_v)
    unit = width // 32
    for block in range(32):
        bits = tuple(block >> shift & 1 for shift in (4, 3, 2, 1, 0))
        r.unit_v[bits + (0, slice(None), slice(0, unit))] = ordered[:, block * unit : (block + 1) * unit]
    units[V, 0].start()
    run_now(32)
    for item in TAIL:
        act(*item)
    for number in range(2 * pairs):
        give_wait(number)
    for t in range(4):
        a_core(t, 0).wait_send()
        a_core(t, 1).wait_send()
        a_y(t).wait_send()
    for k in range(2):
        a_z0(k).wait_send()
        a_x(k).wait_send()
    a_z1().wait_send()
    for unit in units.values():
        unit.drain()


def run_fused(text_len, patch_count, vecs, hidden, cot, wh, wd, order, wqkv, wout, seq, q, k, v, mixed_t, normal_t, normal2, normal2_t, slots):
    pairs, rows, width = seq.shape
    every = pairs * rows
    wide = (2,) * 5
    eight = width // 256
    groups = width // 128

    def arrivals(name, count, tail, kind):
        return {name + str(step): pltpu.VMEM((count,) + (2,) * (4 - step) + tail, kind) for step in range(5)}

    flat = lambda kind: pltpu.VMEM((every, width), kind)
    cube = pltpu.VMEM((pairs, rows, width), BF16)
    tall = pltpu.VMEM((width, every), BF16)
    block = (width // 64, 8, width)
    scratch = dict(
        cot=cube,
        result=cube,
        grad_rows=cube,
        give_sem=pltpu.SemaphoreType.DMA((2 * pairs,)),
        hidden=flat(F32),
        gdown=flat(BF16),
        seq=cube,
        q=cube,
        k=cube,
        v=cube,
        mixed_t=tall,
        normal_t=tall,
        wbuf=pltpu.VMEM((4, width, width), BF16),
        order=pltpu.VMEM((width, width), BF16),
        normal2=flat(BF16),
        normal2_t=tall,
        total=flat(F32),
        gnormal=flat(F32),
        gmixed=cube,
        gproj=pltpu.VMEM((pairs, rows, 3 * width), BF16),
        vec=pltpu.VMEM((8, width), F32),
        a_own=pltpu.VMEM((4, 2, 2, 2) + block, BF16),
        a_core=pltpu.VMEM((4, 2, 2) + block, BF16),
        a_y=pltpu.VMEM((4, 2) + block, BF16),
        a_z0=pltpu.VMEM((2, 2) + block, BF16),
        a_x=pltpu.VMEM((2,) + block, BF16),
        a_z1=pltpu.VMEM((1,) + block, BF16),
        b_own=pltpu.VMEM((8,) + wide + (eight, 8, width // 2), BF16),
        **arrivals("b", 8, (eight, 8, width // 2), BF16),
        c_own=pltpu.VMEM((groups,) + wide + (eight, 8, 384), BF16),
        **arrivals("c", groups, (eight, 8, 384), BF16),
        o_own=pltpu.VMEM(wide + (eight, 8, width), BF16),
        **arrivals("o", 1, (eight, 8, width), BF16),
        unit_h=pltpu.VMEM(wide + (1, 8, 128), F32),
        **arrivals("h", 1, (1, 8, 128), F32),
        unit_v=pltpu.VMEM(wide + (1, 8, 128), F32),
        **arrivals("v", 1, (1, 8, 128), F32),
        send_sem=pltpu.SemaphoreType.DMA((105 + 2 * pairs,)),
        recv_sem=pltpu.SemaphoreType.DMA((105 + 2 * pairs,)),
        load_sem=pltpu.SemaphoreType.DMA((11,)),
        w_sem=pltpu.SemaphoreType.DMA((4,)),
    )
    hbm = pl.BlockSpec(memory_space=pl.ANY)
    operands = dict(
        text_len=(text_len, smem_spec()),
        patch_count=(patch_count, smem_spec()),
        vecs=(vecs, whole_spec()),
        hidden_in=(hidden, hbm),
        cot_in=(cot, hbm),
        wh=(wh, hbm),
        wd=(wd, hbm),
        order_in=(order, hbm),
        wqkv=(wqkv, hbm),
        wout=(wout, hbm),
        seq_in=(seq, hbm),
        q_in=(q, hbm),
        k_in=(k, hbm),
        v_in=(v, hbm),
        mixed_in=(mixed_t, hbm),
        normal_in=(normal_t, hbm),
        normal2_in=(normal2, hbm),
        normal2_t_in=(normal2_t, hbm),
    )
    final = shape((1, 2 * pairs, slots, width), BF16)
    outs = dict(
        block_out=(final, hbm),
        input_grad=(final, hbm),
        out_a=(shape(block, F32), whole_spec()),
        out_b=(shape((eight, 8, 4 * width), F32), whole_spec()),
        out_c=(shape((eight, 8, 3 * width), F32), whole_spec()),
        out_o=(shape((eight, 8, width), F32), whole_spec()),
        out_v=(shape((2, 8, 128), F32), whole_spec()),
    )
    names = list(operands) + list(outs) + list(scratch)
    return pl.pallas_call(
        functools.partial(fused_kernel, pairs, slots, names),
        out_shape=[kind for kind, _ in outs.values()],
        in_specs=[spec for _, spec in operands.values()],
        out_specs=[spec for _, spec in outs.values()],
        scratch_shapes=list(scratch.values()),
        compiler_params=pltpu.CompilerParams(
            collective_id=1, has_side_effects=True, vmem_limit_bytes=67043328
        ),
        name="fused",
    )(*[value for value, _ in operands.values()])


def pair_bits():
    return lax.axis_size("pairs").bit_length() - 1


def swapped(array, axis, bit):
    size = lax.axis_size(axis)
    return lax.ppermute(array, axis, [(i, i ^ (1 << bit)) for i in range(size)])


def split_dims(array):
    bits = pair_bits() + 1
    return array.reshape((2,) * bits + (array.shape[0] >> bits,) + array.shape[1:])


def stage_orders():
    bits = pair_bits()
    ring = ["mod", 1, 2]
    orders = []
    for turn in range(3):
        orders.append([0] + ring[turn:] + ring[:turn] + list(range(3, bits)))
    return orders


def half_sum(array, names, name, last):
    axis, bit = ("mod", 0) if name == "mod" else ("pairs", name)
    mine = (lax.axis_index(axis) >> bit) & 1
    dim = names.index(name)
    sent = lax.dynamic_index_in_dim(array, 1 - mine, dim, keepdims=False)
    kept = lax.dynamic_index_in_dim(array, mine, dim, keepdims=False)
    came = swapped(sent, axis, bit)
    total = kept.astype(F32) + came.astype(F32)
    return (total if last else total.astype(BF16)), names[:dim] + names[dim + 1 :]


def scattered(array):
    width = array.shape[1]
    names0 = list(range(pair_bits() - 1, -1, -1)) + ["mod"]
    first, names1 = half_sum(split_dims(array), names0, 0, False)
    third = -(-width // 3 // 128) * 128
    pieces = []
    for turn, order in enumerate(stage_orders()):
        piece = first[..., turn * third : min(width, (turn + 1) * third)]
        names = list(names1)
        for place, name in enumerate(order[1:]):
            piece, names = half_sum(piece, names, name, place == len(order) - 2)
        pieces.append(piece)
    return jnp.concatenate(pieces, axis=1)


def on_device(
    inputs,
    cotangent,
    text_len,
    patch_count,
    norm1_gain,
    norm1_bias,
    qkv_weight,
    query_bias,
    value_bias,
    out_weight,
    out_bias,
    norm2_gain,
    norm2_bias,
    hidden_weight,
    hidden_bias,
    down_weight,
    down_bias,
):
    _, group, slots, width = inputs.shape
    half = group // 2
    rows = padded(TEXT + slots)
    mod = lax.axis_index("mod")
    is_text = mod == 0
    lens = lax.dynamic_slice_in_dim(jnp.stack([text_len, patch_count]), mod * half, half, 1)
    lens = lens.reshape(-1)

    def gathered(array):
        local = array[0]
        patches = lax.ppermute(local[:half], "mod", [(1, 0)])
        texts = lax.ppermute(local[half:, :TEXT], "mod", [(0, 1)])
        patches = jnp.where(is_text, patches, local[half:])
        texts = jnp.where(is_text, local[:half, :TEXT], texts)
        blank = jnp.zeros((half, rows - slots - TEXT, width), array.dtype)
        return jnp.concatenate([patches, texts, blank], axis=1)

    def returned(array):
        far_patches = lax.ppermute(array[:, :slots], "mod", [(0, 1)])
        far_texts = lax.ppermute(array[:, slots : slots + TEXT], "mod", [(1, 0)])
        return assembled(array, far_patches, far_texts)

    def assembled(array, far_patches, far_texts):
        patches, texts = array[:, :slots], array[:, slots : slots + TEXT]
        texts = jnp.concatenate([texts, far_texts], axis=0)
        texts = jnp.pad(texts, ((0, 0), (0, slots - TEXT), (0, 0)))
        patches = jnp.concatenate([far_patches, patches], axis=0)
        return jnp.where(is_text, texts, patches)[None]

    row = lambda vector: vector.reshape(1, -1)
    if lax.axis_size("pairs") == 16:
        parts = [norm1_gain, norm1_bias, query_bias, value_bias, out_bias, norm2_gain, norm2_bias, down_bias, hidden_bias]
        made = run_opening(text_len, patch_count, inputs, cotangent, parts, qkv_weight, out_weight)
        vecs, q, k, v, hidden, mixed, normal, normal2, normal2_t, seq, cot, order = made
        made = run_fused(
            text_len,
            patch_count,
            vecs,
            hidden,
            cot,
            hidden_weight,
            down_weight,
            order,
            qkv_weight,
            out_weight,
            seq,
            q,
            k,
            v,
            mixed,
            normal,
            normal2,
            normal2_t,
            slots,
        )
        block_out, input_grad, wd_out, wh_out, qkv_out, wo_out, vectors = made
        slot = lax.broadcasted_iota(jnp.int32, (1, 1, slots, 1), 2)
        blank = is_text & (slot >= TEXT)
        block_out = jnp.where(blank, jnp.zeros((), BF16), block_out)
        input_grad = jnp.where(blank, jnp.zeros((), BF16), input_grad)
        flat = lambda array: array.reshape(-1, array.shape[-1])
        wd_out, wh_out, qkv_out, wo_out = flat(wd_out), flat(wh_out), flat(qkv_out), flat(wo_out)
        vec_out = [vectors[0, index, : width // 32] for index in range(8)]
        hb_out = vectors[1, 0, : hidden_bias.shape[0] // 32]
    else:
        seq = gathered(inputs)
        cot = gathered(cotangent).reshape(half * rows, width)
        qkv_bias = row(jnp.concatenate([query_bias, jnp.zeros_like(query_bias), value_bias]))
        feature = jnp.arange(width, dtype=jnp.int32)
        order = (feature[:, None] == feature[None, :]).astype(BF16)
        q, k, v, hidden, mixed = run_forward(
            lens, seq, row(norm1_gain), row(norm1_bias), qkv_weight, qkv_bias, out_weight, row(out_bias), slots
        )
        chunks = 8
        steps = jnp.arange(chunks, dtype=jnp.int32)
        lens = jnp.concatenate([lens, jnp.zeros(4, jnp.int32), steps])
        result, ghidden, wh_grad, wd_grad, hb_grad, vec2 = run_feed(
            lens,
            hidden,
            cot,
            row(norm2_gain),
            row(norm2_bias),
            hidden_weight,
            row(hidden_bias),
            down_weight,
            row(down_bias),
            order,
            half,
            slots,
            chunks,
            False,
        )
        block_out = returned(result.reshape(half, rows, width))
        input_rows, qkvo_grad, vec1 = run_backward(
            lens,
            seq,
            row(norm1_gain),
            row(norm1_bias),
            q,
            k,
            v,
            mixed,
            ghidden,
            qkv_weight,
            out_weight,
            order,
            slots,
            False,
        )
        input_grad = returned(input_rows)
        strip = jnp.concatenate([vec1[:4], vec2[:4]], axis=0).T
        strip = jnp.concatenate([strip, hb_grad.reshape(width, -1)], axis=1).astype(BF16)
        strip = jnp.pad(strip, ((0, 0), (0, 128 - strip.shape[1])))
        wd_out, wh_out = scattered(wd_grad), scattered(wh_grad)
        qkvo_out = scattered(jnp.concatenate([qkvo_grad, strip], axis=1))
        vec_out = qkvo_out[:, 4 * width :]
        qkv_out, wo_out = qkvo_out[:, : 3 * width], qkvo_out[:, 3 * width : 4 * width]
        hb_out = vec_out[:, 8 : 8 + hidden_bias.shape[0] // width].reshape(-1)
        vec_out = [vec_out[:, index] for index in range(8)]
    return (
        block_out,
        input_grad,
        vec_out[0],
        vec_out[1],
        qkv_out,
        vec_out[2],
        vec_out[3],
        wo_out,
        vec_out[7],
        vec_out[4],
        vec_out[5],
        wh_out,
        hb_out,
        wd_out,
        vec_out[6],
    )


def solution(mesh):
    whole = P()
    split = P("mod", "pairs", None, None)
    vector = P(("pairs", "mod"))
    matrix = P(("pairs", "mod"), None)
    return jax.shard_map(
        on_device,
        mesh=mesh,
        in_specs=(split, split, P("pairs"), P("pairs")) + (whole,) * 13,
        out_specs=(
            split,
            split,
            vector,
            vector,
            matrix,
            vector,
            vector,
            matrix,
            vector,
            vector,
            vector,
            matrix,
            vector,
            matrix,
            vector,
        ),
        check_vma=False,
    )
```

```python
import functools
import types

import jax
import jax.numpy as jnp
from jax import lax
from jax.experimental import pallas as pl
from jax.experimental.pallas import tpu as pltpu
from jax.sharding import PartitionSpec as P

HEADS = 12
HEAD_DIM = 64
TEXT = 40
EPSILON = 1e-06
MASKED = -1e30
F32 = jnp.float32
BF16 = jnp.bfloat16
VMEM_LIMIT = 60 * 1024 * 1024


def padded(count):
    return -(-count // 32) * 32


def dot(a, b, ca=1, cb=0):
    return lax.dot_general(a, b, (((ca,), (cb,)), ((), ())), preferred_element_type=F32)


def norm_parts(values):
    centre = jnp.mean(values, axis=-1, keepdims=True)
    centred = values - centre
    spread = jnp.mean(centred * centred, axis=-1, keepdims=True)
    factor = lax.rsqrt(spread + EPSILON)
    return centred * factor, factor


def norm_back(grad_out, normed, factor, norm_gain):
    grad_norm = grad_out * norm_gain
    mean_grad = jnp.mean(grad_norm, axis=-1, keepdims=True)
    second = jnp.mean(grad_norm * normed, axis=-1, keepdims=True)
    return (grad_norm - mean_grad - normed * second) * factor


def live_slots(index, text_count, patch_count, slots):
    return (index < patch_count) | ((index >= slots) & (index - slots < text_count))


def live_rows(lens, pairs, rows, slots):
    parts = []
    for pair in range(pairs):
        index = lax.broadcasted_iota(jnp.int32, (rows, 1), 0)
        parts.append(live_slots(index, lens[pair], lens[pairs + pair], slots).astype(F32))
    return jnp.concatenate(parts, axis=0)


def mix_heads(pair, group, text_count, patch_count, slots, q_in, k_in, v_in, mixed):
    rows = q_in.shape[1]
    first = lax.broadcasted_iota(jnp.int32, (rows, 128), 1) < HEAD_DIM
    column = lax.broadcasted_iota(jnp.int32, (1, rows), 1)
    off = pl.multiple_of(group * 128, 128)
    live = live_slots(column, text_count, patch_count, slots)
    q2 = q_in[pair, :, pl.ds(off, 128)]
    k2 = k_in[pair, :, pl.ds(off, 128)]
    v2 = v_in[pair, :, pl.ds(off, 128)]
    halves = []
    for half in range(2):
        keep = first if half == 0 else ~first
        qm = jnp.where(keep, q2, jnp.zeros_like(q2))
        scores = jnp.where(live, dot(qm, k2, 1, 1), MASKED)
        highest = jnp.max(scores, axis=-1, keepdims=True)
        shifted = jnp.exp(scores - highest)
        total = jnp.sum(shifted, axis=-1, keepdims=True)
        halves.append(dot(shifted.astype(BF16), v2) / total)
    mixed[pair, :, pl.ds(off, 128)] = jnp.where(first, halves[0], halves[1]).astype(BF16)


def forward_kernel(
    slots,
    lens,
    seq,
    gain,
    shift,
    wqkv,
    qkv_bias,
    wout,
    out_bias,
    q_out,
    k_out,
    v_out,
    hidden,
    mixed_out,
    mixed,
):
    pairs, rows, width = seq.shape
    tokens = seq[...].reshape(pairs * rows, width).astype(F32)
    normed, _ = norm_parts(tokens)
    normal = (normed * gain[...] + shift[...]).astype(BF16)
    for part, ref in enumerate((q_out, k_out, v_out)):
        cols = slice(part * width, (part + 1) * width)
        made = dot(normal, wqkv[:, cols]) + qkv_bias[:, cols]
        if part == 0:
            made = made * 0.125
        ref[...] = made.astype(BF16).reshape(pairs, rows, width)
    groups = width // 128

    def step(it, carry):
        pair = it // groups
        mix_heads(pair, it % groups, lens[pair], lens[pairs + pair], slots, q_out, k_out, v_out, mixed)
        return carry

    lax.fori_loop(0, pairs * groups, step, 0)
    rows_mixed = mixed[...].reshape(pairs * rows, width)
    mixed_out[...] = mixed[...]
    hidden[...] = tokens + dot(rows_mixed, wout[...]) + out_bias[...]


def gelu_parts(values):
    cumulative = 0.5 * (1.0 + lax.erf(values * 0.7071067811865476))
    density = jnp.exp(-0.5 * values * values) * 0.3989422804014327
    return values * cumulative, cumulative + values * density


def feed_kernel(
    pairs,
    slots,
    lens,
    hidden,
    cot,
    gain,
    shift,
    wh,
    hbias,
    wd,
    dbias,
    order,
    result,
    grad_hidden,
    wh_grad,
    wd_grad,
    hb_grad,
    vectors,
    normal,
    ordered,
    gdown,
    total,
    gnormal,
):
    chunk = pl.program_id(0)
    count = pl.num_programs(0)
    rows = hidden.shape[0] // pairs
    live = live_rows(lens, pairs, rows, slots)

    @pl.when(chunk == 0)
    def _():
        normed, _ = norm_parts(hidden[...])
        made = (normed * gain[...] + shift[...]).astype(BF16)
        normal[...] = made
        ordered[...] = dot(made, order[...]).astype(BF16)
        gdown[...] = (cot[...].astype(F32) * live).astype(BF16)
        total[...] = hidden[...] + dbias[...]
        gnormal[...] = jnp.zeros_like(gnormal)

    before = dot(normal[...], wh[...]) + hbias[...]
    active, slope = gelu_parts(before)
    active = active.astype(BF16)
    total[...] += dot(active, wd[...])
    fresh = dot(active, gdown[...], 0, 0)
    if wd_grad.ndim == 2:
        wd_grad[...] = fresh.astype(BF16)
    else:
        size = fresh.shape[0] // 4
        base = 2 * pairs
        for core in range(2):
            for mod in range(2):
                start = (2 * core + mod) * size
                piece = fresh[start : start + size].reshape(size // 8, 8, fresh.shape[1])
                wd_grad[lens[base + core], 0, 0, lens[base + 2 + mod], 0] = piece.astype(BF16)
    gbefore = (dot(gdown[...], wd[...], 1, 1) * slope).astype(BF16)
    gnormal[...] += dot(gbefore, wh[...], 1, 1)
    wh_grad[...] = dot(ordered[...], gbefore, 0, 0).reshape(wh_grad.shape).astype(BF16)
    hb_grad[...] = jnp.sum(gbefore.astype(F32), axis=0, keepdims=True)

    @pl.when(chunk == count - 1)
    def _():
        result[...] = (total[...] * live).astype(BF16)
        normed, factor = norm_parts(hidden[...])
        gnorm = gnormal[...]
        vectors[0:1, :] = jnp.sum(gnorm * normed, axis=0, keepdims=True)
        vectors[1:2, :] = jnp.sum(gnorm, axis=0, keepdims=True)
        down = gdown[...].astype(F32)
        vectors[2:3, :] = jnp.sum(down, axis=0, keepdims=True)
        made = down + norm_back(gnorm, normed, factor, gain[...])
        vectors[3:4, :] = jnp.sum(made.astype(BF16).astype(F32), axis=0, keepdims=True)
        grad_hidden[...] = made


def backward_kernel(
    slots,
    lens,
    seq,
    gain,
    shift,
    q_in,
    k_in,
    v_in,
    mixed,
    ghidden,
    wqkv,
    wout,
    order,
    input_grad,
    weight_grad,
    vectors,
    gmixed,
    gproj,
):
    pairs, rows, width = seq.shape
    every = pairs * rows
    gattended = ghidden[...].astype(BF16)
    gmixed[...] = dot(gattended, wout[...], 1, 1).astype(BF16).reshape(pairs, rows, width)
    ordered = dot(mixed[...].reshape(every, width), order[...]).astype(BF16)

    def put(first, last, value):
        target = (slice(None),) * (len(weight_grad.shape) - 1) + (slice(first, last),)
        value = value.reshape(weight_grad.shape[:-1] + (last - first,))
        weight_grad[target] = value.astype(BF16)

    put(3 * width, 4 * width, dot(ordered, gattended, 0, 0))
    first = lax.broadcasted_iota(jnp.int32, (rows, 128), 1) < HEAD_DIM
    index = lax.broadcasted_iota(jnp.int32, (rows, 1), 0)
    groups = width // 128

    def step(it, carry):
        pair = it // groups
        base = (it % groups) * 128
        off = pl.multiple_of(base, 128)
        live = live_slots(index, lens[pair], lens[pairs + pair], slots)
        q2 = q_in[pair, :, pl.ds(off, 128)]
        k2 = k_in[pair, :, pl.ds(off, 128)]
        v2 = v_in[pair, :, pl.ds(off, 128)]
        g2 = gmixed[pair, :, pl.ds(off, 128)]
        gq = gk = gv = None
        for half in range(2):
            keep = first if half == 0 else ~first
            zero = jnp.zeros_like(q2)
            qm = jnp.where(keep, q2, zero)
            km = jnp.where(keep, k2, zero)
            gm = jnp.where(keep, g2, zero)
            scores = jnp.where(live, dot(k2, qm, 1, 1), MASKED)
            highest = jnp.max(scores, axis=0, keepdims=True)
            shifted = jnp.exp(scores - highest)
            probs = shifted * (1.0 / jnp.sum(shifted, axis=0, keepdims=True))
            gprobs = dot(v2, gm, 1, 1)
            row_dot = jnp.sum(probs * gprobs, axis=0, keepdims=True)
            gscores = (probs * (gprobs - row_dot)).astype(BF16)
            new_v = dot(probs.astype(BF16), gm)
            new_k = dot(gscores, qm)
            new_q = dot(gscores, km, 0, 0)
            gq = new_q if gq is None else gq + new_q
            gk = new_k if gk is None else gk + new_k
            gv = new_v if gv is None else gv + new_v
        gproj[pair, :, pl.ds(off, 128)] = (gq * 0.125).astype(BF16)
        gproj[pair, :, pl.ds(pl.multiple_of(base + width, 128), 128)] = gk.astype(BF16)
        gproj[pair, :, pl.ds(pl.multiple_of(base + 2 * width, 128), 128)] = gv.astype(BF16)
        return carry

    lax.fori_loop(0, pairs * groups, step, 0)
    tokens = seq[...].reshape(every, width).astype(F32)
    normed, factor = norm_parts(tokens)
    normal = (normed * gain[...] + shift[...]).astype(BF16)
    ordered = dot(normal, order[...]).astype(BF16)
    gnormal = jnp.zeros((every, width), F32)
    for part in range(3):
        cols = slice(part * width, (part + 1) * width)
        piece = gproj[:, :, cols].reshape(every, width)
        gnormal += dot(piece, wqkv[:, cols], 1, 1)
        put(part * width, (part + 1) * width, dot(ordered, piece, 0, 0))
        if part == 0:
            vectors[2:3, :] = jnp.sum(piece.astype(F32), axis=0, keepdims=True)
        if part == 2:
            vectors[3:4, :] = jnp.sum(piece.astype(F32), axis=0, keepdims=True)
    vectors[0:1, :] = jnp.sum(gnormal * normed, axis=0, keepdims=True)
    vectors[1:2, :] = jnp.sum(gnormal, axis=0, keepdims=True)
    live = live_rows(lens, pairs, rows, slots)
    made = ghidden[...] + norm_back(gnormal, normed, factor, gain[...])
    input_grad[...] = (made * live).astype(BF16).reshape(pairs, rows, width)


def whole_spec():
    return pl.BlockSpec(memory_space=pltpu.VMEM)


def smem_spec():
    return pl.BlockSpec(memory_space=pltpu.SMEM)


def shape(dims, kind):
    return jax.ShapeDtypeStruct(dims, kind)


def run_forward(lens, seq, gain, shift, wqkv, qkv_bias, wout, out_bias, slots):
    pairs, rows, width = seq.shape
    every = pairs * rows
    cube = shape((pairs, rows, width), BF16)
    return pl.pallas_call(
        functools.partial(forward_kernel, slots),
        out_shape=[cube, cube, cube, shape((every, width), F32), cube],
        in_specs=[smem_spec()] + [whole_spec()] * 7,
        out_specs=[whole_spec()] * 5,
        scratch_shapes=[pltpu.VMEM((pairs, rows, width), BF16)],
        compiler_params=pltpu.CompilerParams(vmem_limit_bytes=VMEM_LIMIT),
        name="attention_forward",
    )(lens, seq, gain, shift, wqkv, qkv_bias, wout, out_bias)


def run_feed(lens, hidden, cot, gain, shift, wh, hbias, wd, dbias, order, pairs, slots, chunks, relative):
    every, width = hidden.shape
    ff = wh.shape[1]
    size = ff // chunks
    base = 2 * pairs + 4
    fixed = lambda dims: pl.BlockSpec(dims, lambda c, s: (0, 0))
    columns = lambda r: pl.BlockSpec((r, size), lambda c, s: (0, s[base + c]))
    rows = pl.BlockSpec((size, width), lambda c, s: (s[base + c], 0))
    if relative:
        part = size // 4 // 8
        wd_shape = shape((2, 2, 2, 2, 2, part, 8, width), BF16)
        wd_spec = pl.BlockSpec(
            (2, 1, 1, 2, 1, part, 8, width),
            lambda c, s: (0, c % 2, c // 2 % 2, 0, c // 4, 0, 0, 0),
        )
        wh_shape = shape((width // 8, 8, ff), BF16)
        wh_spec = pl.BlockSpec((width // 8, 8, size), lambda c, s: (0, 0, s[base + c]))
    else:
        wd_shape, wd_spec = shape((ff, width), BF16), rows
        wh_shape, wh_spec = shape((width, ff), BF16), columns(width)
    return pl.pallas_call(
        functools.partial(feed_kernel, pairs, slots),
        out_shape=[
            shape((every, width), BF16),
            shape((every, width), F32),
            wh_shape,
            wd_shape,
            shape((1, ff), F32),
            shape((8, width), F32),
        ],
        grid_spec=pltpu.PrefetchScalarGridSpec(
        num_scalar_prefetch=1,
        grid=(chunks,),
        in_specs=[
            fixed((every, width)),
            fixed((every, width)),
            fixed((1, width)),
            fixed((1, width)),
            columns(width),
            columns(1),
            rows,
            fixed((1, width)),
            fixed((width, width)),
        ],
        out_specs=[
            fixed((every, width)),
            fixed((every, width)),
            wh_spec,
            wd_spec,
            columns(1),
            fixed((8, width)),
        ],
        scratch_shapes=[
            pltpu.VMEM((every, width), BF16),
            pltpu.VMEM((every, width), BF16),
            pltpu.VMEM((every, width), BF16),
            pltpu.VMEM((every, width), F32),
            pltpu.VMEM((every, width), F32),
        ],
        ),
        compiler_params=pltpu.CompilerParams(vmem_limit_bytes=VMEM_LIMIT),
        cost_estimate=pl.CostEstimate(
            flops=12 * every * width * ff,
            bytes_accessed=24 * 2**20,
            transcendentals=2 * every * ff,
        ),
        name="feed_forward",
    )(lens, hidden, cot, gain, shift, wh, hbias, wd, dbias, order)


def run_backward(lens, seq, gain, shift, q, k, v, mixed, ghidden, wqkv, wout, order, slots, relative):
    pairs, rows, width = seq.shape
    every = pairs * rows
    return pl.pallas_call(
        functools.partial(backward_kernel, slots),
        out_shape=[
            shape((pairs, rows, width), BF16),
            shape((width // 8, 8, 4 * width) if relative else (width, 4 * width), BF16),
            shape((8, width), F32),
        ],
        in_specs=[smem_spec()] + [whole_spec()] * 11,
        out_specs=[whole_spec()] * 3,
        scratch_shapes=[
            pltpu.VMEM((pairs, rows, width), BF16),
            pltpu.VMEM((pairs, rows, 3 * width), BF16),
        ],
        compiler_params=pltpu.CompilerParams(vmem_limit_bytes=VMEM_LIMIT),
        cost_estimate=pl.CostEstimate(
            flops=4 * every * width * width * 4 + 20 * every * rows * width,
            bytes_accessed=20 * 2**20,
            transcendentals=every * rows * HEADS,
        ),
        name="attention_backward",
    )(lens, seq, gain, shift, q, k, v, mixed, ghidden, wqkv, wout, order)


BITS = ("core", "y", "z0", "x", "z1")
ORDERS = (("core", "y", "z0", "x", "z1"), ("core", "z0", "y", "x", "z1"))


def partner(bit):
    if bit == "x":
        return {"mod": 1 - lax.axis_index("mod")}
    size = {"core": 1, "y": 2, "z0": 4, "z1": 8}[bit]
    me = lax.axis_index("pairs")
    return {"pairs": me + size - 2 * size * (me // size % 2)}


def narrowed(ref, names, bit, value):
    dim = names.index(bit)
    index = (slice(None),) * dim + (value,)
    return ref.at[index], names[:dim] + names[dim + 1 :]


def flip(value, bit):
    return value + bit - 2 * value * bit


def place():
    pairs = lax.axis_index("pairs")
    return {
        "core": pairs % 2,
        "y": pairs // 2 % 2,
        "z0": pairs // 4 % 2,
        "z1": pairs // 8,
        "x": lax.axis_index("mod"),
    }


def hop(bit, source, target, sems, index, there=None):
    return pltpu.make_async_remote_copy(
        src_ref=source,
        dst_ref=target,
        send_sem=sems[0].at[index],
        recv_sem=sems[1].at[index if there is None else there],
        device_id=partner(bit),
        device_id_type=pl.DeviceIdType.MESH,
    )


def lead_index(it, lead):
    index = []
    for size in reversed(lead):
        index.insert(0, it % size)
        it = it // size
    return tuple(index)


def accumulate(target, source):
    lead = target.shape[:-3]
    tiles = target.shape[-3] * target.shape[-2] * target.shape[-1] // 1024
    while lead and tiles * lead[-1] <= 72:
        tiles *= lead[-1]
        lead = lead[:-1]
    count = 1
    for size in lead:
        count *= size

    def add(at):
        target[at] = target[at] + source[at]

    if count == 1:
        add((0,) * len(lead) if lead else (Ellipsis,))
        return

    def body(it, carry):
        add(lead_index(it, lead))
        return carry

    lax.fori_loop(0, count, body, 0)


class Unit:
    def __init__(self, own, arrivals, order, sems, base, finish):
        self.own, self.arrivals, self.order = own, arrivals, order
        self.sems, self.base, self.finish = sems, base, finish
        self.peers = {}

    def views(self, step):
        ref, names = self.own, list(BITS)
        for bit in self.order[:step]:
            ref, names = narrowed(ref, names, bit, 0)
        sent, _ = narrowed(ref, names, self.order[step], 1)
        kept, _ = narrowed(ref, names, self.order[step], 0)
        return sent, kept

    def copy(self, step):
        bit = self.order[step]
        sent, _ = self.views(step)
        peer = self.peers.get(bit, self)
        return hop(bit, sent, peer.arrivals[step], self.sems, self.base + step, peer.base + step)

    def arrival(self, step):
        sent, _ = self.views(step)
        return hop(self.order[step], sent, self.arrivals[step], self.sems, self.base + step)

    def start(self):
        self.copy(0).start()

    def advance(self, step):
        self.arrival(step).wait_recv()
        _, kept = self.views(step)
        if step == 4:
            self.finish(kept[...].astype(F32) + self.arrivals[4][...].astype(F32))
            return
        accumulate(kept, self.arrivals[step])
        self.copy(step + 1).start()

    def drain(self):
        for step in range(5):
            self.copy(step).wait_send()


STORED = [
    "q_out",
    "k_out",
    "v_out",
    "hidden",
    "seq",
    "order",
    "mixed_out",
    "normal_out",
    "normal2",
    "normal2_t",
    "cot",
]


def counts(here, pairs, text_len, patch_count):
    base = here["x"] * pairs
    return [text_len[base + pair] for pair in range(pairs)] + [patch_count[base + pair] for pair in range(pairs)]


def opening_kernel(pairs, slots, names, *refs):
    r = types.SimpleNamespace(**dict(zip(names, refs)))
    rows, width = r.seq.shape[1:]
    every, tail = pairs * rows, rows - slots
    here = place()
    lens = counts(here, pairs, r.text_len, r.patch_count)
    sems = (r.send_sem, r.recv_sem)
    barrier = pltpu.get_barrier_semaphore()
    pl.semaphore_signal(barrier, inc=1, device_id=partner("x"), device_id_type=pl.DeviceIdType.MESH)

    def moves(which, pair):
        source, target = ((r.inputs, r.seq), (r.cotangent, r.cot))[which]
        index = which * pairs + pair
        patches, texts = target.at[pair, pl.ds(0, slots)], target.at[pair, pl.ds(slots, tail)]
        near = lambda src, dst: pltpu.make_async_copy(src, dst, r.load_sem.at[index])
        return (
            hop("x", source.at[0, pair], patches, sems, index),
            hop("x", source.at[0, pairs + pair, pl.ds(0, tail)], texts, sems, index),
            near(source.at[0, pairs + pair], patches),
            near(source.at[0, pair, pl.ds(0, tail)], texts),
        )

    every_move = [(which, pair) for which in range(2) for pair in range(pairs)]
    weights = [
        pltpu.make_async_copy(source, target, r.load_sem.at[2 * pairs + index])
        for index, (source, target) in enumerate(((r.wqkv_in, r.wqkv), (r.wout_in, r.wout)))
    ]
    pl.semaphore_wait(barrier, 1)

    @pl.when(here["x"] == 1)
    def _():
        for move in every_move:
            moves(*move)[0].start()
        for move in every_move:
            moves(*move)[2].start()

    @pl.when(here["x"] == 0)
    def _():
        for move in every_move:
            moves(*move)[1].start()
        for move in every_move:
            moves(*move)[3].start()

    for copy in weights:
        copy.start()

    def arrived(which, pair):
        @pl.when(here["x"] == 1)
        def _():
            moves(which, pair)[1].wait_recv()
            moves(which, pair)[2].wait()

        @pl.when(here["x"] == 0)
        def _():
            moves(which, pair)[0].wait_recv()
            moves(which, pair)[3].wait()

    place_at = lax.broadcasted_iota(jnp.int32, (width, 1), 0)
    feature = lax.broadcasted_iota(jnp.int32, (width, width), 1)
    unit = width // 32
    block = place_at // unit
    bit = lambda shift: (block >> shift) & 1
    owner = (bit(0) << 4) + (bit(2) << 3) + (bit(3) << 2) + (bit(4) << 1) + bit(1)
    owner = owner ^ (lax.axis_index("pairs") * 2 + here["x"])
    source = owner * unit + (place_at - block * unit)
    r.order[...] = (source == feature).astype(F32).astype(BF16)
    row = 0
    for index in range(9):
        part = getattr(r, str(index))
        for first in range(0, part.shape[0], width):
            r.vecs[row : row + 1, :] = part[first : first + width].reshape(1, width)
            row += 1
    vec = lambda index: r.vecs[index : index + 1, :]
    for copy in weights:
        copy.wait()
    for pair in range(pairs):
        arrived(0, pair)
        tokens = r.seq[pair].astype(F32)
        normed, _ = norm_parts(tokens)
        normal = (normed * vec(0) + vec(1)).astype(BF16)
        r.normal[pair] = normal
        for part, ref in enumerate((r.q_out, r.k_out, r.v_out)):
            made = dot(normal, r.wqkv[:, part * width : (part + 1) * width])
            if part == 0:
                made = (made + vec(2)) * 0.125
            if part == 2:
                made = made + vec(3)
            ref[pair] = made.astype(BF16)

        def step(group, carry):
            mix_heads(pair, group, lens[pair], lens[pairs + pair], slots, r.q_out, r.k_out, r.v_out, r.mixed)
            return carry

        lax.fori_loop(0, width // 128, step, 0)
        made = r.seq[pair].astype(F32) + dot(r.mixed[pair], r.wout[...]) + vec(4)
        r.hidden[pair * rows : (pair + 1) * rows, :] = made
    stores = [
        pltpu.make_async_copy(getattr(r, name), getattr(r, str(20 + index)), r.store_sem.at[index])
        for index, name in enumerate(STORED)
    ]
    for copy in stores[:6]:
        copy.start()
    r.mixed_out[...] = dot(r.order[...], r.mixed[...].reshape(every, width), 1, 1).astype(BF16)
    r.normal_out[...] = dot(r.order[...], r.normal[...].reshape(every, width), 1, 1).astype(BF16)
    normed, _ = norm_parts(r.hidden[...])
    made = (normed * vec(5) + vec(6)).astype(BF16)
    r.normal2[...] = made
    r.normal2_t[...] = dot(r.order[...], made, 1, 1).astype(BF16)
    for copy in stores[6:10]:
        copy.start()
    for pair in range(pairs):
        arrived(1, pair)
    stores[10].start()

    @pl.when(here["x"] == 1)
    def _():
        for move in every_move:
            moves(*move)[0].wait_send()

    @pl.when(here["x"] == 0)
    def _():
        for move in every_move:
            moves(*move)[1].wait_send()

    for copy in stores:
        copy.wait()


def run_opening(text_len, patch_count, inputs, cotangent, parts, wqkv, wout):
    _, group, slots, width = inputs.shape
    pairs = group // 2
    rows = padded(TEXT + slots)
    every = pairs * rows
    hbm = pl.BlockSpec(memory_space=pl.ANY)
    operands = dict(
        text_len=(text_len, smem_spec()),
        patch_count=(patch_count, smem_spec()),
        inputs=(inputs, hbm),
        cotangent=(cotangent, hbm),
        wqkv_in=(wqkv, hbm),
        wout_in=(wout, hbm),
    )
    operands.update((index, (part, whole_spec())) for index, part in enumerate(parts))
    count = sum(part.shape[0] for part in parts) // width
    cube = shape((pairs, rows, width), BF16)
    tall = shape((width, every), BF16)
    outs = dict(
        vecs=(shape((count, width), F32), whole_spec()),
    )
    long = shape((every, width), F32)
    flat = shape((every, width), BF16)
    square = shape((width, width), BF16)
    kinds = [cube, cube, cube, long, cube, square, tall, tall, flat, tall, cube]
    outs.update((20 + index, (kind, hbm)) for index, kind in enumerate(kinds))
    held = pltpu.VMEM((pairs, rows, width), BF16)
    scratch = dict(
        seq=held,
        cot=held,
        mixed=held,
        normal=held,
        q_out=held,
        k_out=held,
        v_out=held,
        hidden=pltpu.VMEM(long.shape, F32),
        order=pltpu.VMEM(square.shape, BF16),
        mixed_out=pltpu.VMEM(tall.shape, BF16),
        normal_out=pltpu.VMEM(tall.shape, BF16),
        normal2=pltpu.VMEM(flat.shape, BF16),
        normal2_t=pltpu.VMEM(tall.shape, BF16),
        wqkv=pltpu.VMEM(wqkv.shape, BF16),
        wout=pltpu.VMEM(wout.shape, BF16),
        send_sem=pltpu.SemaphoreType.DMA((2 * pairs,)),
        recv_sem=pltpu.SemaphoreType.DMA((2 * pairs,)),
        load_sem=pltpu.SemaphoreType.DMA((2 * pairs + 2,)),
        store_sem=pltpu.SemaphoreType.DMA((len(kinds),)),
    )
    names = [str(name) for name in (*operands, *outs, *scratch)]
    return pl.pallas_call(
        functools.partial(opening_kernel, pairs, slots, names),
        out_shape=[kind for kind, _ in outs.values()],
        in_specs=[spec for _, spec in operands.values()],
        out_specs=[spec for _, spec in outs.values()],
        scratch_shapes=list(scratch.values()),
        compiler_params=pltpu.CompilerParams(collective_id=2, has_side_effects=True, vmem_limit_bytes=VMEM_LIMIT),
        name="opening",
    )(*[value for value, _ in operands.values()])


A, B, C, O, H, V, R = range(7)
PLAN = {
    3: [(A, 0, 0)],
    4: [(B, 0, 0)],
    5: [(A, 0, 1)],
    6: [(B, 1, 0)],
    7: [(A, 0, 2), (A, 1, 0)],
    8: [(B, 2, 0), (B, 2, 1)],
    9: [(A, 1, 1)],
    10: [(B, 3, 0), (B, 3, 1)],
    11: [(A, 1, 2), (A, 2, 0), (B, 4, 0), (B, 3, 2)],
    12: [(A, 2, 1), (B, 0, 1), (B, 2, 2)],
    13: [(A, 0, 3)],
    14: [(B, 1, 1), (B, 2, 3), (B, 3, 3), (B, 5, 0)],
    15: [(A, 2, 2), (A, 3, 0), (B, 1, 2), (B, 6, 0), (B, 6, 1)],
    16: [(A, 3, 1), (B, 0, 2), (B, 1, 3), (R, 0, 0)],
    17: [(R, 0, 1)],
    18: [(B, 0, 3), (B, 7, 0), (B, 7, 1), (H, 0, 0), (R, 0, 2)],
    19: [(R, 0, 3)],
    20: [(A, 3, 2), (O, 0, 0), (B, 7, 2)],
    21: [(B, 6, 2)],
    22: [(C, 0, 0), (B, 4, 1), (R, 0, 4)],
    23: [(A, 1, 3), (A, 0, 4), (R, 0, 5)],
    24: [(C, 1, 0), (B, 5, 1), (B, 6, 3), (B, 7, 3), (H, 0, 1), (B, 6, 4), (B, 7, 4), (R, 0, 6)],
    25: [(O, 0, 1), (R, 0, 7)],
    26: [(C, 0, 1), (C, 2, 0), (B, 5, 2), (B, 2, 4), (B, 3, 4), (R, 0, 8)],
    27: [(O, 0, 2), (C, 1, 1), (B, 4, 2), (B, 5, 3), (H, 0, 2), (B, 5, 4)],
    28: [(C, 0, 2), (R, 0, 9)],
    29: [(O, 0, 3), (C, 2, 1), (B, 4, 3), (H, 0, 3), (B, 1, 4), (B, 4, 4), (C, 1, 2), (R, 1, 0)],
    30: [(C, 0, 3), (C, 3, 0), (R, 1, 1)],
    31: [(C, 1, 3), (C, 2, 2), (C, 4, 0), (B, 0, 4), (O, 0, 4), (H, 0, 4), (R, 1, 2)],
    32: [(C, 5, 0), (C, 0, 4), (R, 1, 3)],
}
TAIL = [
    (C, 2, 3), (C, 3, 1), (R, 1, 4), (V, 0, 0), (C, 4, 1), (R, 2, 0),
    (C, 1, 4), (C, 3, 2), (C, 5, 1), (V, 0, 1), (R, 2, 1), (C, 4, 2),
    (V, 0, 2), (C, 2, 4), (C, 3, 3), (R, 2, 2), (C, 5, 2), (C, 4, 3),
    (R, 2, 3), (V, 0, 3), (C, 5, 3), (R, 2, 4), (C, 3, 4), (C, 4, 4),
    (V, 0, 4), (C, 5, 4),
]


def fused_kernel(pairs, slots, names, *refs):
    r = types.SimpleNamespace(**dict(zip(names, refs)))
    rows, width = r.seq.shape[1:]
    every = pairs * rows
    tail = rows - slots
    here = place()
    lens = counts(here, pairs, r.text_len, r.patch_count)
    vec_in = lambda index: r.vecs[index : index + 1, :]
    sems = (r.send_sem, r.recv_sem)
    barrier = pltpu.get_barrier_semaphore()
    for bit in BITS:
        pl.semaphore_signal(barrier, inc=1, device_id=partner(bit), device_id_type=pl.DeviceIdType.MESH)

    def load(name, target, index):
        return pltpu.make_async_copy(getattr(r, name), getattr(r, target), r.load_sem.at[index])

    early = [
        load("normal2_in", "normal2", 0),
        load("cot_in", "cot", 1),
        load("normal2_t_in", "normal2_t", 2),
        load("hidden_in", "hidden", 9),
    ]
    late = [
        load("mixed_in", "mixed_t", 3),
        load("normal_in", "normal_t", 4),
        load("seq_in", "seq", 5),
        load("q_in", "q", 6),
        load("k_in", "k", 7),
        load("v_in", "v", 8),
        load("order_in", "order", 10),
    ]

    def block_of(t):
        z1, z0 = 1 - t // 2, 1 - t % 2
        return flip(z0, here["z0"]) + 2 * flip(z1, here["z1"])

    def weight_loads(t, slot):
        start = pl.multiple_of(block_of(t) * width, width)
        return (
            pltpu.make_async_copy(r.wh.at[:, pl.ds(start, width)], r.wbuf.at[slot], r.w_sem.at[slot]),
            pltpu.make_async_copy(r.wd.at[pl.ds(start, width), :], r.wbuf.at[2 + slot], r.w_sem.at[2 + slot]),
        )

    early[0].start()
    for copy in weight_loads(0, 0):
        copy.start()
    for copy in early[1:]:
        copy.start()
    r.gnormal[...] = jnp.zeros_like(r.gnormal)
    live = live_rows(lens, pairs, rows, slots)
    for copy in early:
        copy.wait()
    r.total[...] = r.hidden[...] + vec_in(7)
    r.gdown[...] = (r.cot[...].reshape(every, width).astype(F32) * live).astype(BF16)
    r.unit_h[...] = jnp.zeros_like(r.unit_h)
    for copy in late:
        copy.start()
    pl.semaphore_wait(barrier, len(BITS))

    arrivals = lambda name, index: [getattr(r, name + str(step)).at[index] for step in range(5)]

    a_core = lambda t, y: hop("core", r.a_own.at[t, 1, y], r.a_core.at[t, y], sems, 2 * t + y)
    a_y = lambda t: hop("y", r.a_own.at[t, 0, 1], r.a_y.at[t], sems, 8 + t)
    a_z0 = lambda k: hop("z0", r.a_own.at[2 * k, 0, 0], r.a_z0.at[k], sems, 12 + k)
    a_x = lambda k: hop("x", r.a_own.at[2 * k + 1, 0, 0, 1], r.a_x.at[k], sems, 14 + k)
    a_z1 = lambda: hop("z1", r.a_own.at[1, 0, 0, 0], r.a_z1.at[0], sems, 16)

    def a_core_sum(t, y):
        a_core(t, y).wait_recv()
        accumulate(r.a_own.at[t, 0, y], r.a_core.at[t, y])
        if y == 1:
            a_y(t).start()

    def a_second(t):
        k = t // 2
        a_y(t).wait_recv()
        accumulate(r.a_own.at[t, 0, 0], r.a_y.at[t])
        if t % 2 == 0:
            a_z0(k).start()
        else:
            a_z0(k).wait_recv()
            accumulate(r.a_own.at[t, 0, 0], r.a_z0.at[k])
            a_x(k).start()

    def a_third(k):
        a_x(k).wait_recv()
        accumulate(r.a_own.at[2 * k + 1, 0, 0, pl.ds(0, 1)], r.a_x.at[pl.ds(k, 1)])
        if k == 0:
            a_z1().start()

    def a_last():
        a_z1().wait_recv()
        r.out_a[...] = r.a_own[3, 0, 0, 0].astype(F32) + r.a_z1[0].astype(F32)

    size = width // 2

    def b_columns(u):
        return block_of(u // 2) * width + flip(1 - u % 2, here["y"]) * size

    def b_finish(u):
        def finish(value):
            r.out_b[:, :, pl.ds(pl.multiple_of(b_columns(u), 128), size)] = value

        return finish

    def c_finish(g):
        def finish(value):
            for part in range(3):
                cols = slice(part * width + 128 * g, part * width + 128 * g + 128)
                r.out_c[:, :, cols] = value[:, :, 128 * part : 128 * part + 128]

        return finish

    def plain(target):
        def finish(value):
            target[...] = value

        return finish

    units = {}
    for u in range(8):
        units[B, u] = Unit(r.b_own.at[u], arrivals("b", u), ORDERS[1], sems, 20 + 5 * u, b_finish(u))
    for u in range(8):
        units[B, u].peers = {"y": units[B, u ^ 1], "z0": units[B, u ^ 2], "z1": units[B, u ^ 4]}
    groups = width // 128
    for g in range(groups):
        units[C, g] = Unit(r.c_own.at[g], arrivals("c", g), ORDERS[(1, 0, 1, 1, 0, 1)[g]], sems, 60 + 5 * g, c_finish(g))
    units[O, 0] = Unit(r.o_own, arrivals("o", 0), ORDERS[0], sems, 90, plain(r.out_o))
    units[H, 0] = Unit(r.unit_h, arrivals("h", 0), ORDERS[1], sems, 95, plain(r.out_v.at[pl.ds(1, 1)]))
    units[V, 0] = Unit(r.unit_v, arrivals("v", 0), ORDERS[0], sems, 100, plain(r.out_v.at[pl.ds(0, 1)]))

    def give(source, target, pair, index):
        near = lambda src, dst: pltpu.make_async_copy(src, dst, r.give_sem.at[index])
        part = lambda first, count: hop(
            "x", source.at[pair, pl.ds(first, count)], target.at[0, pair, pl.ds(first, count)], sems, 105 + index
        )
        patches, texts = source.at[pair, pl.ds(0, slots)], source.at[pair, pl.ds(slots, tail)]
        far_texts = hop("x", texts, target.at[0, pairs + pair, pl.ds(0, tail)], sems, 105 + index)
        near_texts = lambda: near(texts, target.at[0, pair, pl.ds(0, tail)])
        near_patches = lambda: near(patches, target.at[0, pairs + pair])
        return part, far_texts, near_texts, near_patches

    gives = [give(r.result, r.block_out, pair, pair) for pair in range(pairs)]
    gives += [give(r.grad_rows, r.input_grad, pair, pairs + pair) for pair in range(pairs)]

    def give_start(index):
        _, far_texts, near_texts, near_patches = gives[index]

        @pl.when(here["x"] == 0)
        def _():
            near_texts().start()

        @pl.when(here["x"] == 1)
        def _():
            far_texts.start()
            near_patches().start()

    def give_part(index, piece):
        @pl.when(here["x"] == 0)
        def _():
            gives[index][0](tail * piece, tail).start()

    def give_wait(index):
        part, far_texts, near_texts, near_patches = gives[index]

        @pl.when(here["x"] == 0)
        def _():
            far_texts.wait_recv()
            part(0, slots).wait_send()
            near_texts().wait()

        @pl.when(here["x"] == 1)
        def _():
            part(0, slots).wait_recv()
            far_texts.wait_send()
            near_patches().wait()

    def act(kind, piece, step):
        if kind == R:
            pieces = slots // tail
            give_part(step // pieces if piece == 0 else pairs + piece - 1, step % pieces)
        elif kind != A:
            units[kind, piece].advance(step)
        elif step < 2:
            a_core_sum(piece, 1 - step)
        else:
            (a_second, a_third, lambda _: a_last())[step - 2](piece)

    def run_now(tick):
        for item in PLAN.get(tick, []):
            act(*item)

    def run_tasks(ticks, now):
        for tick in ticks:
            if tick in PLAN:

                @pl.when(now == tick)
                def _(tick=tick):
                    run_now(tick)

    def feed_step(t, carry):
        slot = t % 2
        for copy in weight_loads(t, slot):
            copy.wait()

        @pl.when(t < 3)
        def _():
            for copy in weight_loads(t + 1, 1 - slot):
                copy.start()

        for sub in range(2):
            run_tasks([4 * k + 2 * sub for k in range(4)], 4 * t + 2 * sub)
            y = 1 - sub
            part = flip(y, here["y"])
            start = pl.multiple_of(part * size, size)
            wh = r.wbuf[slot, :, pl.ds(start, size)]
            wd = r.wbuf[2 + slot, pl.ds(start, size), :]
            before = dot(r.normal2[...], wh) + r.vecs[pl.ds(8 + block_of(t), 1), pl.ds(start, size)]
            active, slope = gelu_parts(before)
            active = active.astype(BF16)
            r.total[...] += dot(active, wd)
            fresh = dot(active, r.gdown[...], 0, 0)
            quarter = size // 4
            for core in range(2):
                for mod in range(2):
                    first = (2 * core + mod) * quarter
                    piece = fresh[first : first + quarter].reshape(quarter // 8, 8, width)
                    r.a_own[t, flip(core, here["core"]), y, flip(mod, here["x"])] = piece.astype(BF16)
            a_core(t, y).start()
            run_tasks([4 * k + 2 * sub + 1 for k in range(4)], 4 * t + 2 * sub + 1)
            gbefore = (dot(r.gdown[...], wd, 1, 1) * slope).astype(BF16)
            r.gnormal[...] += dot(gbefore, wh, 1, 1)
            fresh = dot(r.normal2_t[...], gbefore)
            fresh = fresh.reshape((2,) * 5 + (width // 256, 8, size)).astype(BF16)
            unit = 2 * t + sub
            r.b_own[unit] = fresh
            hop("core", r.b_own.at[unit, 1], r.b0.at[unit], sems, 20 + 5 * unit).start()
            sums = jnp.sum(gbefore.astype(F32), axis=0, keepdims=True)
            z1, z0 = 1 - t // 2, 1 - t % 2
            for core in range(2):
                for mod in range(2):
                    first = (2 * core + mod) * quarter
                    r.unit_h[
                        flip(core, here["core"]), y, z0, flip(mod, here["x"]), z1, 0, 0:1, 0:quarter
                    ] = sums[:, first : first + quarter]
        return carry

    lax.fori_loop(0, 4, feed_step, 0)

    wout_load = pltpu.make_async_copy(r.wout, r.wbuf.at[3], r.w_sem.at[3])
    wout_load.start()
    wqkv_loads = [
        pltpu.make_async_copy(
            r.wqkv.at[:, pl.ds(part * width, width)], r.wbuf.at[part], r.w_sem.at[part]
        )
        for part in range(3)
    ]
    for copy in wqkv_loads:
        copy.start()
    units[H, 0].start()
    r.result[...] = (r.total[...] * live).astype(BF16).reshape(pairs, rows, width)

    for pair in range(pairs):
        give_start(pair)
    run_now(16)
    normed, factor = norm_parts(r.hidden[...])
    gnorm = r.gnormal[...]
    down = r.gdown[...].astype(F32)
    vec = [
        jnp.sum(gnorm * normed, axis=0, keepdims=True),
        jnp.sum(gnorm, axis=0, keepdims=True),
        jnp.sum(down, axis=0, keepdims=True),
    ]
    made = down + norm_back(gnorm, normed, factor, vec_in(5))
    gattended = made.astype(BF16)
    vec.append(jnp.sum(gattended.astype(F32), axis=0, keepdims=True))
    for index, value in enumerate(vec):
        r.vec[4 + index : 5 + index, :] = value
    r.gnormal[...] = made
    run_now(17)
    wout_load.wait()
    r.gmixed[...] = dot(gattended, r.wbuf[3], 1, 1).astype(BF16).reshape(pairs, rows, width)
    for copy in late:
        copy.wait()
    fresh = dot(r.mixed_t[...], gattended)
    r.o_own[...] = fresh.reshape((2,) * 5 + (width // 256, 8, width)).astype(BF16)
    units[O, 0].start()
    for copy in wqkv_loads:
        copy.wait()

    first = lax.broadcasted_iota(jnp.int32, (rows, 128), 1) < HEAD_DIM
    index = lax.broadcasted_iota(jnp.int32, (rows, 1), 0)

    def project_back(pair):
        made = jnp.zeros((rows, width), F32)
        sums = []
        for part in range(3):
            piece = r.gproj[pair, :, part * width : (part + 1) * width]
            made += dot(piece, r.wbuf[part], 1, 1)
            sums.append(jnp.sum(piece.astype(F32), axis=0, keepdims=True))
        return made, sums

    def finish_pair(pair, grad, sums):
        normed, factor = norm_parts(r.seq[pair].astype(F32))
        sums = [
            jnp.sum(grad * normed, axis=0, keepdims=True),
            jnp.sum(grad, axis=0, keepdims=True),
            sums[0],
            sums[2],
        ]
        for index, value in enumerate(sums):
            r.vec[index : index + 1, :] = value if pair == 0 else r.vec[index : index + 1, :] + value
        span = slice(pair * rows, (pair + 1) * rows)
        made = r.gnormal[span, :] + norm_back(grad, normed, factor, vec_in(0))
        r.grad_rows[pair] = (made * live[span]).astype(BF16)
        give_start(pairs + pair)

    def head_step(it, carry):
        late = it // groups
        pair = (1 - late) * (it % 2) + it // 9
        g = (1 - late) * (it // 2) + late * (3 + it % 3)
        base = g * 128
        off = pl.multiple_of(base, 128)

        @pl.when(it == 9)
        def _():
            finish_pair(0, *project_back(0))

        run_tasks([18 + k for k in range(pairs * groups)], 18 + it)
        at_pair = here["x"] * pairs + pair
        keys_live = live_slots(index, r.text_len[at_pair], r.patch_count[at_pair], slots)
        q2 = r.q[pair, :, pl.ds(off, 128)]
        k2 = r.k[pair, :, pl.ds(off, 128)]
        v2 = r.v[pair, :, pl.ds(off, 128)]
        g2 = r.gmixed[pair, :, pl.ds(off, 128)]
        gq = gk = gv = None
        for half in range(2):
            keep = first if half == 0 else ~first
            zero = jnp.zeros_like(q2)
            qm = jnp.where(keep, q2, zero)
            km = jnp.where(keep, k2, zero)
            gm = jnp.where(keep, g2, zero)
            scores = jnp.where(keys_live, dot(k2, qm, 1, 1), MASKED)
            highest = jnp.max(scores, axis=0, keepdims=True)
            shifted = jnp.exp(scores - highest)
            probs = shifted * (1.0 / jnp.sum(shifted, axis=0, keepdims=True))
            gprobs = dot(v2, gm, 1, 1)
            row_dot = jnp.sum(probs * gprobs, axis=0, keepdims=True)
            gscores = (probs * (gprobs - row_dot)).astype(BF16)
            new_v = dot(probs.astype(BF16), gm)
            new_k = dot(gscores, qm)
            new_q = dot(gscores, km, 0, 0)
            gq = new_q if gq is None else gq + new_q
            gk = new_k if gk is None else gk + new_k
            gv = new_v if gv is None else gv + new_v
        r.gproj[pair, :, pl.ds(off, 128)] = (gq * 0.125).astype(BF16)
        r.gproj[pair, :, pl.ds(pl.multiple_of(base + width, 128), 128)] = gk.astype(BF16)
        r.gproj[pair, :, pl.ds(pl.multiple_of(base + 2 * width, 128), 128)] = gv.astype(BF16)

        @pl.when(pair == pairs - 1)
        def _():
            pieces = [
                r.gproj[:, :, pl.ds(pl.multiple_of(base + part * width, 128), 128)].reshape(every, 128)
                for part in range(3)
            ]
            fresh = dot(r.normal_t[...], jnp.concatenate(pieces, axis=1))
            r.c_own[g] = fresh.reshape((2,) * 5 + (width // 256, 8, 384)).astype(BF16)
            hop("core", r.c_own.at[g, 1], r.c0.at[g], sems, 60 + 5 * g).start()

        return carry

    lax.fori_loop(0, pairs * groups, head_step, 0)

    run_now(30)
    made, sums = project_back(1)
    run_now(31)
    finish_pair(1, made, sums)
    rest = r.vec[...]
    ordered = jnp.zeros_like(rest)
    for _ in range(3):
        high = rest.astype(BF16)
        ordered += dot(high, r.order[...], 1, 1)
        rest = rest - high.astype(F32)
    r.unit_v[...] = jnp.zeros_like(r.unit_v)
    unit = width // 32
    for block in range(32):
        bits = tuple(block >> shift & 1 for shift in (4, 3, 2, 1, 0))
        r.unit_v[bits + (0, slice(None), slice(0, unit))] = ordered[:, block * unit : (block + 1) * unit]
    units[V, 0].start()
    run_now(32)
    for item in TAIL:
        act(*item)
    for number in range(2 * pairs):
        give_wait(number)
    for t in range(4):
        a_core(t, 0).wait_send()
        a_core(t, 1).wait_send()
        a_y(t).wait_send()
    for k in range(2):
        a_z0(k).wait_send()
        a_x(k).wait_send()
    a_z1().wait_send()
    for unit in units.values():
        unit.drain()


def run_fused(text_len, patch_count, vecs, hidden, cot, wh, wd, order, wqkv, wout, seq, q, k, v, mixed_t, normal_t, normal2, normal2_t, slots):
    pairs, rows, width = seq.shape
    every = pairs * rows
    wide = (2,) * 5
    eight = width // 256
    groups = width // 128

    def arrivals(name, count, tail, kind):
        return {name + str(step): pltpu.VMEM((count,) + (2,) * (4 - step) + tail, kind) for step in range(5)}

    flat = lambda kind: pltpu.VMEM((every, width), kind)
    cube = pltpu.VMEM((pairs, rows, width), BF16)
    tall = pltpu.VMEM((width, every), BF16)
    block = (width // 64, 8, width)
    scratch = dict(
        cot=cube,
        result=cube,
        grad_rows=cube,
        give_sem=pltpu.SemaphoreType.DMA((2 * pairs,)),
        hidden=flat(F32),
        gdown=flat(BF16),
        seq=cube,
        q=cube,
        k=cube,
        v=cube,
        mixed_t=tall,
        normal_t=tall,
        wbuf=pltpu.VMEM((4, width, width), BF16),
        order=pltpu.VMEM((width, width), BF16),
        normal2=flat(BF16),
        normal2_t=tall,
        total=flat(F32),
        gnormal=flat(F32),
        gmixed=cube,
        gproj=pltpu.VMEM((pairs, rows, 3 * width), BF16),
        vec=pltpu.VMEM((8, width), F32),
        a_own=pltpu.VMEM((4, 2, 2, 2) + block, BF16),
        a_core=pltpu.VMEM((4, 2, 2) + block, BF16),
        a_y=pltpu.VMEM((4, 2) + block, BF16),
        a_z0=pltpu.VMEM((2, 2) + block, BF16),
        a_x=pltpu.VMEM((2,) + block, BF16),
        a_z1=pltpu.VMEM((1,) + block, BF16),
        b_own=pltpu.VMEM((8,) + wide + (eight, 8, width // 2), BF16),
        **arrivals("b", 8, (eight, 8, width // 2), BF16),
        c_own=pltpu.VMEM((groups,) + wide + (eight, 8, 384), BF16),
        **arrivals("c", groups, (eight, 8, 384), BF16),
        o_own=pltpu.VMEM(wide + (eight, 8, width), BF16),
        **arrivals("o", 1, (eight, 8, width), BF16),
        unit_h=pltpu.VMEM(wide + (1, 8, 128), F32),
        **arrivals("h", 1, (1, 8, 128), F32),
        unit_v=pltpu.VMEM(wide + (1, 8, 128), F32),
        **arrivals("v", 1, (1, 8, 128), F32),
        send_sem=pltpu.SemaphoreType.DMA((105 + 2 * pairs,)),
        recv_sem=pltpu.SemaphoreType.DMA((105 + 2 * pairs,)),
        load_sem=pltpu.SemaphoreType.DMA((11,)),
        w_sem=pltpu.SemaphoreType.DMA((4,)),
    )
    hbm = pl.BlockSpec(memory_space=pl.ANY)
    operands = dict(
        text_len=(text_len, smem_spec()),
        patch_count=(patch_count, smem_spec()),
        vecs=(vecs, whole_spec()),
        hidden_in=(hidden, hbm),
        cot_in=(cot, hbm),
        wh=(wh, hbm),
        wd=(wd, hbm),
        order_in=(order, hbm),
        wqkv=(wqkv, hbm),
        wout=(wout, hbm),
        seq_in=(seq, hbm),
        q_in=(q, hbm),
        k_in=(k, hbm),
        v_in=(v, hbm),
        mixed_in=(mixed_t, hbm),
        normal_in=(normal_t, hbm),
        normal2_in=(normal2, hbm),
        normal2_t_in=(normal2_t, hbm),
    )
    final = shape((1, 2 * pairs, slots, width), BF16)
    outs = dict(
        block_out=(final, hbm),
        input_grad=(final, hbm),
        out_a=(shape(block, F32), whole_spec()),
        out_b=(shape((eight, 8, 4 * width), F32), whole_spec()),
        out_c=(shape((eight, 8, 3 * width), F32), whole_spec()),
        out_o=(shape((eight, 8, width), F32), whole_spec()),
        out_v=(shape((2, 8, 128), F32), whole_spec()),
    )
    names = list(operands) + list(outs) + list(scratch)
    return pl.pallas_call(
        functools.partial(fused_kernel, pairs, slots, names),
        out_shape=[kind for kind, _ in outs.values()],
        in_specs=[spec for _, spec in operands.values()],
        out_specs=[spec for _, spec in outs.values()],
        scratch_shapes=list(scratch.values()),
        compiler_params=pltpu.CompilerParams(
            collective_id=1, has_side_effects=True, vmem_limit_bytes=67043328
        ),
        name="fused",
    )(*[value for value, _ in operands.values()])


def closing_kernel(*refs):
    count = len(refs) // 2
    for index in range(count):
        value = refs[index][...]
        if index < 2:
            slot = lax.broadcasted_iota(jnp.int32, value.shape, 2)
            last = TEXT + lax.axis_index("mod") * value.shape[2]
            value = jnp.where(slot < last, value, jnp.zeros_like(value))
        refs[count + index][...] = value


def run_closing(*arrays):
    return pl.pallas_call(
        closing_kernel,
        out_shape=[shape(array.shape, array.dtype) for array in arrays],
        in_specs=[whole_spec()] * len(arrays),
        out_specs=[whole_spec()] * len(arrays),
        name="closing",
    )(*arrays)


def pair_bits():
    return lax.axis_size("pairs").bit_length() - 1


def swapped(array, axis, bit):
    size = lax.axis_size(axis)
    return lax.ppermute(array, axis, [(i, i ^ (1 << bit)) for i in range(size)])


def split_dims(array):
    bits = pair_bits() + 1
    return array.reshape((2,) * bits + (array.shape[0] >> bits,) + array.shape[1:])


def stage_orders():
    bits = pair_bits()
    ring = ["mod", 1, 2]
    orders = []
    for turn in range(3):
        orders.append([0] + ring[turn:] + ring[:turn] + list(range(3, bits)))
    return orders


def half_sum(array, names, name, last):
    axis, bit = ("mod", 0) if name == "mod" else ("pairs", name)
    mine = (lax.axis_index(axis) >> bit) & 1
    dim = names.index(name)
    sent = lax.dynamic_index_in_dim(array, 1 - mine, dim, keepdims=False)
    kept = lax.dynamic_index_in_dim(array, mine, dim, keepdims=False)
    came = swapped(sent, axis, bit)
    total = kept.astype(F32) + came.astype(F32)
    return (total if last else total.astype(BF16)), names[:dim] + names[dim + 1 :]


def scattered(array):
    width = array.shape[1]
    names0 = list(range(pair_bits() - 1, -1, -1)) + ["mod"]
    first, names1 = half_sum(split_dims(array), names0, 0, False)
    third = -(-width // 3 // 128) * 128
    pieces = []
    for turn, order in enumerate(stage_orders()):
        piece = first[..., turn * third : min(width, (turn + 1) * third)]
        names = list(names1)
        for place, name in enumerate(order[1:]):
            piece, names = half_sum(piece, names, name, place == len(order) - 2)
        pieces.append(piece)
    return jnp.concatenate(pieces, axis=1)


def on_device(
    inputs,
    cotangent,
    text_len,
    patch_count,
    norm1_gain,
    norm1_bias,
    qkv_weight,
    query_bias,
    value_bias,
    out_weight,
    out_bias,
    norm2_gain,
    norm2_bias,
    hidden_weight,
    hidden_bias,
    down_weight,
    down_bias,
):
    _, group, slots, width = inputs.shape
    half = group // 2
    rows = padded(TEXT + slots)
    mod = lax.axis_index("mod")
    is_text = mod == 0
    lens = lax.dynamic_slice_in_dim(jnp.stack([text_len, patch_count]), mod * half, half, 1)
    lens = lens.reshape(-1)

    def gathered(array):
        local = array[0]
        patches = lax.ppermute(local[:half], "mod", [(1, 0)])
        texts = lax.ppermute(local[half:, :TEXT], "mod", [(0, 1)])
        patches = jnp.where(is_text, patches, local[half:])
        texts = jnp.where(is_text, local[:half, :TEXT], texts)
        blank = jnp.zeros((half, rows - slots - TEXT, width), array.dtype)
        return jnp.concatenate([patches, texts, blank], axis=1)

    def returned(array):
        far_patches = lax.ppermute(array[:, :slots], "mod", [(0, 1)])
        far_texts = lax.ppermute(array[:, slots : slots + TEXT], "mod", [(1, 0)])
        return assembled(array, far_patches, far_texts)

    def assembled(array, far_patches, far_texts):
        patches, texts = array[:, :slots], array[:, slots : slots + TEXT]
        texts = jnp.concatenate([texts, far_texts], axis=0)
        texts = jnp.pad(texts, ((0, 0), (0, slots - TEXT), (0, 0)))
        patches = jnp.concatenate([far_patches, patches], axis=0)
        return jnp.where(is_text, texts, patches)[None]

    row = lambda vector: vector.reshape(1, -1)
    if lax.axis_size("pairs") == 16:
        parts = [norm1_gain, norm1_bias, query_bias, value_bias, out_bias, norm2_gain, norm2_bias, down_bias, hidden_bias]
        made = run_opening(text_len, patch_count, inputs, cotangent, parts, qkv_weight, out_weight)
        vecs, q, k, v, hidden, seq, order, mixed, normal, normal2, normal2_t, cot = made
        made = run_fused(
            text_len,
            patch_count,
            vecs,
            hidden,
            cot,
            hidden_weight,
            down_weight,
            order,
            qkv_weight,
            out_weight,
            seq,
            q,
            k,
            v,
            mixed,
            normal,
            normal2,
            normal2_t,
            slots,
        )
        block_out, input_grad, wd_out, wh_out, qkv_out, wo_out, vectors = made
        flat = lambda array: array.reshape(-1, array.shape[-1])
        wd_out, wh_out, qkv_out, wo_out = flat(wd_out), flat(wh_out), flat(qkv_out), flat(wo_out)
        made = run_closing(block_out, input_grad, wd_out, wh_out, qkv_out, wo_out)
        block_out, input_grad, wd_out, wh_out, qkv_out, wo_out = made
        vec_out = [vectors[0, index, : width // 32] for index in range(8)]
        hb_out = vectors[1, 0, : hidden_bias.shape[0] // 32]
    else:
        seq = gathered(inputs)
        cot = gathered(cotangent).reshape(half * rows, width)
        qkv_bias = row(jnp.concatenate([query_bias, jnp.zeros_like(query_bias), value_bias]))
        feature = jnp.arange(width, dtype=jnp.int32)
        order = (feature[:, None] == feature[None, :]).astype(BF16)
        q, k, v, hidden, mixed = run_forward(
            lens, seq, row(norm1_gain), row(norm1_bias), qkv_weight, qkv_bias, out_weight, row(out_bias), slots
        )
        chunks = 8
        steps = jnp.arange(chunks, dtype=jnp.int32)
        lens = jnp.concatenate([lens, jnp.zeros(4, jnp.int32), steps])
        result, ghidden, wh_grad, wd_grad, hb_grad, vec2 = run_feed(
            lens,
            hidden,
            cot,
            row(norm2_gain),
            row(norm2_bias),
            hidden_weight,
            row(hidden_bias),
            down_weight,
            row(down_bias),
            order,
            half,
            slots,
            chunks,
            False,
        )
        block_out = returned(result.reshape(half, rows, width))
        input_rows, qkvo_grad, vec1 = run_backward(
            lens,
            seq,
            row(norm1_gain),
            row(norm1_bias),
            q,
            k,
            v,
            mixed,
            ghidden,
            qkv_weight,
            out_weight,
            order,
            slots,
            False,
        )
        input_grad = returned(input_rows)
        strip = jnp.concatenate([vec1[:4], vec2[:4]], axis=0).T
        strip = jnp.concatenate([strip, hb_grad.reshape(width, -1)], axis=1).astype(BF16)
        strip = jnp.pad(strip, ((0, 0), (0, 128 - strip.shape[1])))
        wd_out, wh_out = scattered(wd_grad), scattered(wh_grad)
        qkvo_out = scattered(jnp.concatenate([qkvo_grad, strip], axis=1))
        vec_out = qkvo_out[:, 4 * width :]
        qkv_out, wo_out = qkvo_out[:, : 3 * width], qkvo_out[:, 3 * width : 4 * width]
        hb_out = vec_out[:, 8 : 8 + hidden_bias.shape[0] // width].reshape(-1)
        vec_out = [vec_out[:, index] for index in range(8)]
    return (
        block_out,
        input_grad,
        vec_out[0],
        vec_out[1],
        qkv_out,
        vec_out[2],
        vec_out[3],
        wo_out,
        vec_out[7],
        vec_out[4],
        vec_out[5],
        wh_out,
        hb_out,
        wd_out,
        vec_out[6],
    )


def solution(mesh):
    whole = P()
    split = P("mod", "pairs", None, None)
    vector = P(("pairs", "mod"))
    matrix = P(("pairs", "mod"), None)
    return jax.shard_map(
        on_device,
        mesh=mesh,
        in_specs=(split, split, P("pairs"), P("pairs")) + (whole,) * 13,
        out_specs=(
            split,
            split,
            vector,
            vector,
            matrix,
            vector,
            vector,
            matrix,
            vector,
            vector,
            vector,
            matrix,
            vector,
            matrix,
            vector,
        ),
        check_vma=False,
    )
```

```python
import functools
import types

import jax
import jax.numpy as jnp
from jax import lax
from jax.experimental import pallas as pl
from jax.experimental.pallas import tpu as pltpu
from jax.sharding import PartitionSpec as P

HEADS = 12
HEAD_DIM = 64
TEXT = 40
EPSILON = 1e-06
MASKED = -1e30
F32 = jnp.float32
BF16 = jnp.bfloat16
VMEM_LIMIT = 60 * 1024 * 1024


def padded(count):
    return -(-count // 32) * 32


def dot(a, b, ca=1, cb=0):
    return lax.dot_general(a, b, (((ca,), (cb,)), ((), ())), preferred_element_type=F32)


def norm_parts(values):
    centre = jnp.mean(values, axis=-1, keepdims=True)
    centred = values - centre
    spread = jnp.mean(centred * centred, axis=-1, keepdims=True)
    factor = lax.rsqrt(spread + EPSILON)
    return centred * factor, factor


def norm_back(grad_out, normed, factor, norm_gain):
    grad_norm = grad_out * norm_gain
    mean_grad = jnp.mean(grad_norm, axis=-1, keepdims=True)
    second = jnp.mean(grad_norm * normed, axis=-1, keepdims=True)
    return (grad_norm - mean_grad - normed * second) * factor


def live_slots(index, text_count, patch_count, slots):
    return (index < patch_count) | ((index >= slots) & (index - slots < text_count))


def live_rows(lens, pairs, rows, slots):
    parts = []
    for pair in range(pairs):
        index = lax.broadcasted_iota(jnp.int32, (rows, 1), 0)
        parts.append(live_slots(index, lens[pair], lens[pairs + pair], slots).astype(F32))
    return jnp.concatenate(parts, axis=0)


def mix_heads(pair, group, text_count, patch_count, slots, q_in, k_in, v_in, mixed):
    rows = q_in.shape[1]
    first = lax.broadcasted_iota(jnp.int32, (rows, 128), 1) < HEAD_DIM
    column = lax.broadcasted_iota(jnp.int32, (1, rows), 1)
    off = pl.multiple_of(group * 128, 128)
    live = live_slots(column, text_count, patch_count, slots)
    q2 = q_in[pair, :, pl.ds(off, 128)]
    k2 = k_in[pair, :, pl.ds(off, 128)]
    v2 = v_in[pair, :, pl.ds(off, 128)]
    halves = []
    for half in range(2):
        keep = first if half == 0 else ~first
        qm = jnp.where(keep, q2, jnp.zeros_like(q2))
        scores = jnp.where(live, dot(qm, k2, 1, 1), MASKED)
        highest = jnp.max(scores, axis=-1, keepdims=True)
        shifted = jnp.exp(scores - highest)
        total = jnp.sum(shifted, axis=-1, keepdims=True)
        halves.append(dot(shifted.astype(BF16), v2) / total)
    mixed[pair, :, pl.ds(off, 128)] = jnp.where(first, halves[0], halves[1]).astype(BF16)


def forward_kernel(
    slots,
    lens,
    seq,
    gain,
    shift,
    wqkv,
    qkv_bias,
    wout,
    out_bias,
    q_out,
    k_out,
    v_out,
    hidden,
    mixed_out,
    mixed,
):
    pairs, rows, width = seq.shape
    tokens = seq[...].reshape(pairs * rows, width).astype(F32)
    normed, _ = norm_parts(tokens)
    normal = (normed * gain[...] + shift[...]).astype(BF16)
    for part, ref in enumerate((q_out, k_out, v_out)):
        cols = slice(part * width, (part + 1) * width)
        made = dot(normal, wqkv[:, cols]) + qkv_bias[:, cols]
        if part == 0:
            made = made * 0.125
        ref[...] = made.astype(BF16).reshape(pairs, rows, width)
    groups = width // 128

    def step(it, carry):
        pair = it // groups
        mix_heads(pair, it % groups, lens[pair], lens[pairs + pair], slots, q_out, k_out, v_out, mixed)
        return carry

    lax.fori_loop(0, pairs * groups, step, 0)
    rows_mixed = mixed[...].reshape(pairs * rows, width)
    mixed_out[...] = mixed[...]
    hidden[...] = tokens + dot(rows_mixed, wout[...]) + out_bias[...]


def gelu_parts(values):
    cumulative = 0.5 * (1.0 + lax.erf(values * 0.7071067811865476))
    density = jnp.exp(-0.5 * values * values) * 0.3989422804014327
    return values * cumulative, cumulative + values * density


def feed_kernel(
    pairs,
    slots,
    lens,
    hidden,
    cot,
    gain,
    shift,
    wh,
    hbias,
    wd,
    dbias,
    order,
    result,
    grad_hidden,
    wh_grad,
    wd_grad,
    hb_grad,
    vectors,
    normal,
    ordered,
    gdown,
    total,
    gnormal,
):
    chunk = pl.program_id(0)
    count = pl.num_programs(0)
    rows = hidden.shape[0] // pairs
    live = live_rows(lens, pairs, rows, slots)

    @pl.when(chunk == 0)
    def _():
        normed, _ = norm_parts(hidden[...])
        made = (normed * gain[...] + shift[...]).astype(BF16)
        normal[...] = made
        ordered[...] = dot(made, order[...]).astype(BF16)
        gdown[...] = (cot[...].astype(F32) * live).astype(BF16)
        total[...] = hidden[...] + dbias[...]
        gnormal[...] = jnp.zeros_like(gnormal)

    before = dot(normal[...], wh[...]) + hbias[...]
    active, slope = gelu_parts(before)
    active = active.astype(BF16)
    total[...] += dot(active, wd[...])
    fresh = dot(active, gdown[...], 0, 0)
    if wd_grad.ndim == 2:
        wd_grad[...] = fresh.astype(BF16)
    else:
        size = fresh.shape[0] // 4
        base = 2 * pairs
        for core in range(2):
            for mod in range(2):
                start = (2 * core + mod) * size
                piece = fresh[start : start + size].reshape(size // 8, 8, fresh.shape[1])
                wd_grad[lens[base + core], 0, 0, lens[base + 2 + mod], 0] = piece.astype(BF16)
    gbefore = (dot(gdown[...], wd[...], 1, 1) * slope).astype(BF16)
    gnormal[...] += dot(gbefore, wh[...], 1, 1)
    wh_grad[...] = dot(ordered[...], gbefore, 0, 0).reshape(wh_grad.shape).astype(BF16)
    hb_grad[...] = jnp.sum(gbefore.astype(F32), axis=0, keepdims=True)

    @pl.when(chunk == count - 1)
    def _():
        result[...] = (total[...] * live).astype(BF16)
        normed, factor = norm_parts(hidden[...])
        gnorm = gnormal[...]
        vectors[0:1, :] = jnp.sum(gnorm * normed, axis=0, keepdims=True)
        vectors[1:2, :] = jnp.sum(gnorm, axis=0, keepdims=True)
        down = gdown[...].astype(F32)
        vectors[2:3, :] = jnp.sum(down, axis=0, keepdims=True)
        made = down + norm_back(gnorm, normed, factor, gain[...])
        vectors[3:4, :] = jnp.sum(made.astype(BF16).astype(F32), axis=0, keepdims=True)
        grad_hidden[...] = made


def backward_kernel(
    slots,
    lens,
    seq,
    gain,
    shift,
    q_in,
    k_in,
    v_in,
    mixed,
    ghidden,
    wqkv,
    wout,
    order,
    input_grad,
    weight_grad,
    vectors,
    gmixed,
    gproj,
):
    pairs, rows, width = seq.shape
    every = pairs * rows
    gattended = ghidden[...].astype(BF16)
    gmixed[...] = dot(gattended, wout[...], 1, 1).astype(BF16).reshape(pairs, rows, width)
    ordered = dot(mixed[...].reshape(every, width), order[...]).astype(BF16)

    def put(first, last, value):
        target = (slice(None),) * (len(weight_grad.shape) - 1) + (slice(first, last),)
        value = value.reshape(weight_grad.shape[:-1] + (last - first,))
        weight_grad[target] = value.astype(BF16)

    put(3 * width, 4 * width, dot(ordered, gattended, 0, 0))
    first = lax.broadcasted_iota(jnp.int32, (rows, 128), 1) < HEAD_DIM
    index = lax.broadcasted_iota(jnp.int32, (rows, 1), 0)
    groups = width // 128

    def step(it, carry):
        pair = it // groups
        base = (it % groups) * 128
        off = pl.multiple_of(base, 128)
        live = live_slots(index, lens[pair], lens[pairs + pair], slots)
        q2 = q_in[pair, :, pl.ds(off, 128)]
        k2 = k_in[pair, :, pl.ds(off, 128)]
        v2 = v_in[pair, :, pl.ds(off, 128)]
        g2 = gmixed[pair, :, pl.ds(off, 128)]
        gq = gk = gv = None
        for half in range(2):
            keep = first if half == 0 else ~first
            zero = jnp.zeros_like(q2)
            qm = jnp.where(keep, q2, zero)
            km = jnp.where(keep, k2, zero)
            gm = jnp.where(keep, g2, zero)
            scores = jnp.where(live, dot(k2, qm, 1, 1), MASKED)
            highest = jnp.max(scores, axis=0, keepdims=True)
            shifted = jnp.exp(scores - highest)
            probs = shifted * (1.0 / jnp.sum(shifted, axis=0, keepdims=True))
            gprobs = dot(v2, gm, 1, 1)
            row_dot = jnp.sum(probs * gprobs, axis=0, keepdims=True)
            gscores = (probs * (gprobs - row_dot)).astype(BF16)
            new_v = dot(probs.astype(BF16), gm)
            new_k = dot(gscores, qm)
            new_q = dot(gscores, km, 0, 0)
            gq = new_q if gq is None else gq + new_q
            gk = new_k if gk is None else gk + new_k
            gv = new_v if gv is None else gv + new_v
        gproj[pair, :, pl.ds(off, 128)] = (gq * 0.125).astype(BF16)
        gproj[pair, :, pl.ds(pl.multiple_of(base + width, 128), 128)] = gk.astype(BF16)
        gproj[pair, :, pl.ds(pl.multiple_of(base + 2 * width, 128), 128)] = gv.astype(BF16)
        return carry

    lax.fori_loop(0, pairs * groups, step, 0)
    tokens = seq[...].reshape(every, width).astype(F32)
    normed, factor = norm_parts(tokens)
    normal = (normed * gain[...] + shift[...]).astype(BF16)
    ordered = dot(normal, order[...]).astype(BF16)
    gnormal = jnp.zeros((every, width), F32)
    for part in range(3):
        cols = slice(part * width, (part + 1) * width)
        piece = gproj[:, :, cols].reshape(every, width)
        gnormal += dot(piece, wqkv[:, cols], 1, 1)
        put(part * width, (part + 1) * width, dot(ordered, piece, 0, 0))
        if part == 0:
            vectors[2:3, :] = jnp.sum(piece.astype(F32), axis=0, keepdims=True)
        if part == 2:
            vectors[3:4, :] = jnp.sum(piece.astype(F32), axis=0, keepdims=True)
    vectors[0:1, :] = jnp.sum(gnormal * normed, axis=0, keepdims=True)
    vectors[1:2, :] = jnp.sum(gnormal, axis=0, keepdims=True)
    live = live_rows(lens, pairs, rows, slots)
    made = ghidden[...] + norm_back(gnormal, normed, factor, gain[...])
    input_grad[...] = (made * live).astype(BF16).reshape(pairs, rows, width)


def whole_spec():
    return pl.BlockSpec(memory_space=pltpu.VMEM)


def smem_spec():
    return pl.BlockSpec(memory_space=pltpu.SMEM)


def shape(dims, kind):
    return jax.ShapeDtypeStruct(dims, kind)


def run_forward(lens, seq, gain, shift, wqkv, qkv_bias, wout, out_bias, slots):
    pairs, rows, width = seq.shape
    every = pairs * rows
    cube = shape((pairs, rows, width), BF16)
    return pl.pallas_call(
        functools.partial(forward_kernel, slots),
        out_shape=[cube, cube, cube, shape((every, width), F32), cube],
        in_specs=[smem_spec()] + [whole_spec()] * 7,
        out_specs=[whole_spec()] * 5,
        scratch_shapes=[pltpu.VMEM((pairs, rows, width), BF16)],
        compiler_params=pltpu.CompilerParams(vmem_limit_bytes=VMEM_LIMIT),
        name="attention_forward",
    )(lens, seq, gain, shift, wqkv, qkv_bias, wout, out_bias)


def run_feed(lens, hidden, cot, gain, shift, wh, hbias, wd, dbias, order, pairs, slots, chunks, relative):
    every, width = hidden.shape
    ff = wh.shape[1]
    size = ff // chunks
    base = 2 * pairs + 4
    fixed = lambda dims: pl.BlockSpec(dims, lambda c, s: (0, 0))
    columns = lambda r: pl.BlockSpec((r, size), lambda c, s: (0, s[base + c]))
    rows = pl.BlockSpec((size, width), lambda c, s: (s[base + c], 0))
    if relative:
        part = size // 4 // 8
        wd_shape = shape((2, 2, 2, 2, 2, part, 8, width), BF16)
        wd_spec = pl.BlockSpec(
            (2, 1, 1, 2, 1, part, 8, width),
            lambda c, s: (0, c % 2, c // 2 % 2, 0, c // 4, 0, 0, 0),
        )
        wh_shape = shape((width // 8, 8, ff), BF16)
        wh_spec = pl.BlockSpec((width // 8, 8, size), lambda c, s: (0, 0, s[base + c]))
    else:
        wd_shape, wd_spec = shape((ff, width), BF16), rows
        wh_shape, wh_spec = shape((width, ff), BF16), columns(width)
    return pl.pallas_call(
        functools.partial(feed_kernel, pairs, slots),
        out_shape=[
            shape((every, width), BF16),
            shape((every, width), F32),
            wh_shape,
            wd_shape,
            shape((1, ff), F32),
            shape((8, width), F32),
        ],
        grid_spec=pltpu.PrefetchScalarGridSpec(
        num_scalar_prefetch=1,
        grid=(chunks,),
        in_specs=[
            fixed((every, width)),
            fixed((every, width)),
            fixed((1, width)),
            fixed((1, width)),
            columns(width),
            columns(1),
            rows,
            fixed((1, width)),
            fixed((width, width)),
        ],
        out_specs=[
            fixed((every, width)),
            fixed((every, width)),
            wh_spec,
            wd_spec,
            columns(1),
            fixed((8, width)),
        ],
        scratch_shapes=[
            pltpu.VMEM((every, width), BF16),
            pltpu.VMEM((every, width), BF16),
            pltpu.VMEM((every, width), BF16),
            pltpu.VMEM((every, width), F32),
            pltpu.VMEM((every, width), F32),
        ],
        ),
        compiler_params=pltpu.CompilerParams(vmem_limit_bytes=VMEM_LIMIT),
        cost_estimate=pl.CostEstimate(
            flops=12 * every * width * ff,
            bytes_accessed=24 * 2**20,
            transcendentals=2 * every * ff,
        ),
        name="feed_forward",
    )(lens, hidden, cot, gain, shift, wh, hbias, wd, dbias, order)


def run_backward(lens, seq, gain, shift, q, k, v, mixed, ghidden, wqkv, wout, order, slots, relative):
    pairs, rows, width = seq.shape
    every = pairs * rows
    return pl.pallas_call(
        functools.partial(backward_kernel, slots),
        out_shape=[
            shape((pairs, rows, width), BF16),
            shape((width // 8, 8, 4 * width) if relative else (width, 4 * width), BF16),
            shape((8, width), F32),
        ],
        in_specs=[smem_spec()] + [whole_spec()] * 11,
        out_specs=[whole_spec()] * 3,
        scratch_shapes=[
            pltpu.VMEM((pairs, rows, width), BF16),
            pltpu.VMEM((pairs, rows, 3 * width), BF16),
        ],
        compiler_params=pltpu.CompilerParams(vmem_limit_bytes=VMEM_LIMIT),
        cost_estimate=pl.CostEstimate(
            flops=4 * every * width * width * 4 + 20 * every * rows * width,
            bytes_accessed=20 * 2**20,
            transcendentals=every * rows * HEADS,
        ),
        name="attention_backward",
    )(lens, seq, gain, shift, q, k, v, mixed, ghidden, wqkv, wout, order)


BITS = ("core", "y", "z0", "x", "z1")
ORDERS = (("core", "y", "z0", "x", "z1"), ("core", "z0", "y", "x", "z1"))


def partner(bit):
    if bit == "x":
        return {"mod": 1 - lax.axis_index("mod")}
    size = {"core": 1, "y": 2, "z0": 4, "z1": 8}[bit]
    me = lax.axis_index("pairs")
    return {"pairs": me + size - 2 * size * (me // size % 2)}


def narrowed(ref, names, bit, value):
    dim = names.index(bit)
    index = (slice(None),) * dim + (value,)
    return ref.at[index], names[:dim] + names[dim + 1 :]


def flip(value, bit):
    return value + bit - 2 * value * bit


def place():
    pairs = lax.axis_index("pairs")
    return {
        "core": pairs % 2,
        "y": pairs // 2 % 2,
        "z0": pairs // 4 % 2,
        "z1": pairs // 8,
        "x": lax.axis_index("mod"),
    }


def hop(bit, source, target, sems, index, there=None):
    return pltpu.make_async_remote_copy(
        src_ref=source,
        dst_ref=target,
        send_sem=sems[0].at[index],
        recv_sem=sems[1].at[index if there is None else there],
        device_id=partner(bit),
        device_id_type=pl.DeviceIdType.MESH,
    )


def lead_index(it, lead):
    index = []
    for size in reversed(lead):
        index.insert(0, it % size)
        it = it // size
    return tuple(index)


def accumulate(target, source):
    lead = target.shape[:-3]
    tiles = target.shape[-3] * target.shape[-2] * target.shape[-1] // 1024
    while lead and tiles * lead[-1] <= 72:
        tiles *= lead[-1]
        lead = lead[:-1]
    count = 1
    for size in lead:
        count *= size

    def add(at):
        target[at] = target[at] + source[at]

    if count == 1:
        add((0,) * len(lead) if lead else (Ellipsis,))
        return

    def body(it, carry):
        add(lead_index(it, lead))
        return carry

    lax.fori_loop(0, count, body, 0)


class Unit:
    def __init__(self, own, arrivals, order, sems, base, finish):
        self.own, self.arrivals, self.order = own, arrivals, order
        self.sems, self.base, self.finish = sems, base, finish
        self.peers = {}

    def views(self, step):
        ref, names = self.own, list(BITS)
        for bit in self.order[:step]:
            ref, names = narrowed(ref, names, bit, 0)
        sent, _ = narrowed(ref, names, self.order[step], 1)
        kept, _ = narrowed(ref, names, self.order[step], 0)
        return sent, kept

    def copy(self, step):
        bit = self.order[step]
        sent, _ = self.views(step)
        peer = self.peers.get(bit, self)
        return hop(bit, sent, peer.arrivals[step], self.sems, self.base + step, peer.base + step)

    def arrival(self, step):
        sent, _ = self.views(step)
        return hop(self.order[step], sent, self.arrivals[step], self.sems, self.base + step)

    def start(self):
        self.copy(0).start()

    def advance(self, step):
        self.arrival(step).wait_recv()
        _, kept = self.views(step)
        if step == 4:
            self.finish(kept[...].astype(F32) + self.arrivals[4][...].astype(F32))
            return
        accumulate(kept, self.arrivals[step])
        self.copy(step + 1).start()

    def drain(self):
        for step in range(5):
            self.copy(step).wait_send()


STORED = [
    "q_out",
    "k_out",
    "v_out",
    "hidden",
    "seq",
    "order",
    "mixed_out",
    "normal_out",
    "normal2",
    "normal2_t",
    "cot",
]


def counts(here, pairs, text_len, patch_count):
    base = here["x"] * pairs
    return [text_len[base + pair] for pair in range(pairs)] + [patch_count[base + pair] for pair in range(pairs)]


def opening_kernel(pairs, slots, names, *refs):
    r = types.SimpleNamespace(**dict(zip(names, refs)))
    rows, width = r.seq.shape[1:]
    every, tail = pairs * rows, rows - slots
    here = place()
    lens = counts(here, pairs, r.text_len, r.patch_count)
    sems = (r.send_sem, r.recv_sem)
    barrier = pltpu.get_barrier_semaphore()
    pl.semaphore_signal(barrier, inc=1, device_id=partner("x"), device_id_type=pl.DeviceIdType.MESH)

    def moves(which, pair):
        source, target = ((r.inputs, r.seq), (r.cotangent, r.cot))[which]
        index = which * pairs + pair
        patches, texts = target.at[pair, pl.ds(0, slots)], target.at[pair, pl.ds(slots, tail)]
        near = lambda src, dst: pltpu.make_async_copy(src, dst, r.load_sem.at[index])
        return (
            hop("x", source.at[0, pair], patches, sems, index),
            hop("x", source.at[0, pairs + pair, pl.ds(0, tail)], texts, sems, index),
            near(source.at[0, pairs + pair], patches),
            near(source.at[0, pair, pl.ds(0, tail)], texts),
        )

    every_move = [(which, pair) for which in range(2) for pair in range(pairs)]
    weights = [
        pltpu.make_async_copy(source, target, r.load_sem.at[2 * pairs + index])
        for index, (source, target) in enumerate(((r.wqkv_in, r.wqkv), (r.wout_in, r.wout)))
    ]
    pl.semaphore_wait(barrier, 1)

    @pl.when(here["x"] == 1)
    def _():
        for move in every_move:
            moves(*move)[0].start()
        for move in every_move:
            moves(*move)[2].start()

    @pl.when(here["x"] == 0)
    def _():
        for move in every_move:
            moves(*move)[1].start()
        for move in every_move:
            moves(*move)[3].start()

    for copy in weights:
        copy.start()

    def arrived(which, pair):
        @pl.when(here["x"] == 1)
        def _():
            moves(which, pair)[1].wait_recv()
            moves(which, pair)[2].wait()

        @pl.when(here["x"] == 0)
        def _():
            moves(which, pair)[0].wait_recv()
            moves(which, pair)[3].wait()

    place_at = lax.broadcasted_iota(jnp.int32, (width, 1), 0)
    feature = lax.broadcasted_iota(jnp.int32, (width, width), 1)
    unit = width // 32
    block = place_at // unit
    bit = lambda shift: (block >> shift) & 1
    owner = (bit(0) << 4) + (bit(2) << 3) + (bit(3) << 2) + (bit(4) << 1) + bit(1)
    owner = owner ^ (lax.axis_index("pairs") * 2 + here["x"])
    source = owner * unit + (place_at - block * unit)
    r.order[...] = (source == feature).astype(F32).astype(BF16)
    row = 0
    for index in range(9):
        part = getattr(r, str(index))
        for first in range(0, part.shape[0], width):
            r.vecs[row : row + 1, :] = part[first : first + width].reshape(1, width)
            row += 1
    vec = lambda index: r.vecs[index : index + 1, :]
    for copy in weights:
        copy.wait()
    for pair in range(pairs):
        arrived(0, pair)
        tokens = r.seq[pair].astype(F32)
        normed, _ = norm_parts(tokens)
        normal = (normed * vec(0) + vec(1)).astype(BF16)
        r.normal[pair] = normal
        for part, ref in enumerate((r.q_out, r.k_out, r.v_out)):
            made = dot(normal, r.wqkv[:, part * width : (part + 1) * width])
            if part == 0:
                made = (made + vec(2)) * 0.125
            if part == 2:
                made = made + vec(3)
            ref[pair] = made.astype(BF16)

        def step(group, carry):
            mix_heads(pair, group, lens[pair], lens[pairs + pair], slots, r.q_out, r.k_out, r.v_out, r.mixed)
            return carry

        lax.fori_loop(0, width // 128, step, 0)
        made = r.seq[pair].astype(F32) + dot(r.mixed[pair], r.wout[...]) + vec(4)
        r.hidden[pair * rows : (pair + 1) * rows, :] = made
    stores = [
        pltpu.make_async_copy(getattr(r, name), getattr(r, str(20 + index)), r.store_sem.at[index])
        for index, name in enumerate(STORED)
    ]
    for copy in stores[:6]:
        copy.start()
    r.mixed_out[...] = dot(r.order[...], r.mixed[...].reshape(every, width), 1, 1).astype(BF16)
    r.normal_out[...] = dot(r.order[...], r.normal[...].reshape(every, width), 1, 1).astype(BF16)
    normed, _ = norm_parts(r.hidden[...])
    made = (normed * vec(5) + vec(6)).astype(BF16)
    r.normal2[...] = made
    r.normal2_t[...] = dot(r.order[...], made, 1, 1).astype(BF16)
    for copy in stores[6:10]:
        copy.start()
    for pair in range(pairs):
        arrived(1, pair)
    stores[10].start()

    @pl.when(here["x"] == 1)
    def _():
        for move in every_move:
            moves(*move)[0].wait_send()

    @pl.when(here["x"] == 0)
    def _():
        for move in every_move:
            moves(*move)[1].wait_send()

    for copy in stores:
        copy.wait()


def run_opening(text_len, patch_count, inputs, cotangent, parts, wqkv, wout):
    _, group, slots, width = inputs.shape
    pairs = group // 2
    rows = padded(TEXT + slots)
    every = pairs * rows
    hbm = pl.BlockSpec(memory_space=pl.ANY)
    operands = dict(
        text_len=(text_len, smem_spec()),
        patch_count=(patch_count, smem_spec()),
        inputs=(inputs, hbm),
        cotangent=(cotangent, hbm),
        wqkv_in=(wqkv, hbm),
        wout_in=(wout, hbm),
    )
    operands.update((index, (part, whole_spec())) for index, part in enumerate(parts))
    count = sum(part.shape[0] for part in parts) // width
    cube = shape((pairs, rows, width), BF16)
    tall = shape((width, every), BF16)
    outs = dict(
        vecs=(shape((count, width), F32), whole_spec()),
    )
    long = shape((every, width), F32)
    flat = shape((every, width), BF16)
    square = shape((width, width), BF16)
    kinds = [cube, cube, cube, long, cube, square, tall, tall, flat, tall, cube]
    outs.update((20 + index, (kind, hbm)) for index, kind in enumerate(kinds))
    held = pltpu.VMEM((pairs, rows, width), BF16)
    scratch = dict(
        seq=held,
        cot=held,
        mixed=held,
        normal=held,
        q_out=held,
        k_out=held,
        v_out=held,
        hidden=pltpu.VMEM(long.shape, F32),
        order=pltpu.VMEM(square.shape, BF16),
        mixed_out=pltpu.VMEM(tall.shape, BF16),
        normal_out=pltpu.VMEM(tall.shape, BF16),
        normal2=pltpu.VMEM(flat.shape, BF16),
        normal2_t=pltpu.VMEM(tall.shape, BF16),
        wqkv=pltpu.VMEM(wqkv.shape, BF16),
        wout=pltpu.VMEM(wout.shape, BF16),
        send_sem=pltpu.SemaphoreType.DMA((2 * pairs,)),
        recv_sem=pltpu.SemaphoreType.DMA((2 * pairs,)),
        load_sem=pltpu.SemaphoreType.DMA((2 * pairs + 2,)),
        store_sem=pltpu.SemaphoreType.DMA((len(kinds),)),
    )
    names = [str(name) for name in (*operands, *outs, *scratch)]
    return pl.pallas_call(
        functools.partial(opening_kernel, pairs, slots, names),
        out_shape=[kind for kind, _ in outs.values()],
        in_specs=[spec for _, spec in operands.values()],
        out_specs=[spec for _, spec in outs.values()],
        scratch_shapes=list(scratch.values()),
        compiler_params=pltpu.CompilerParams(collective_id=2, has_side_effects=True, vmem_limit_bytes=VMEM_LIMIT),
        name="opening",
    )(*[value for value, _ in operands.values()])


A, B, C, O, H, V, R = range(7)
PLAN = {
    3: [(A, 0, 0)],
    4: [(A, 0, 1), (B, 0, 0)],
    5: [(B, 1, 0)],
    7: [(A, 0, 2), (A, 1, 0)],
    8: [(A, 1, 1), (B, 2, 0), (B, 2, 1)],
    9: [(B, 3, 0), (B, 3, 1)],
    11: [(A, 2, 0)],
    12: [(A, 1, 2), (A, 2, 1), (B, 0, 1), (B, 2, 2), (B, 3, 2), (B, 4, 0), (B, 5, 0)],
    14: [(B, 1, 1)],
    15: [(A, 0, 3), (A, 2, 2), (A, 3, 0), (B, 2, 3)],
    16: [(A, 3, 1), (B, 0, 2), (B, 1, 2), (B, 3, 3), (B, 6, 0), (B, 6, 1), (B, 7, 0), (B, 7, 1), (H, 0, 0), (R, 0, 0)],
    17: [(B, 0, 3), (R, 0, 1)],
    18: [(B, 1, 3), (R, 0, 2)],
    19: [(B, 7, 2), (R, 0, 3)],
    20: [(A, 3, 2), (B, 6, 2)],
    21: [(O, 0, 0), (B, 7, 3), (B, 7, 4)],
    22: [(C, 0, 0), (B, 4, 1), (R, 0, 4)],
    23: [(B, 3, 4), (B, 5, 1), (R, 0, 5)],
    24: [(A, 1, 3), (C, 1, 0), (B, 6, 3), (H, 0, 1), (A, 0, 4), (B, 6, 4), (R, 0, 6)],
    25: [(R, 0, 7)],
    26: [(C, 0, 1), (O, 0, 1), (C, 2, 0), (B, 2, 4), (R, 0, 8)],
    27: [(B, 4, 2), (B, 5, 2), (R, 0, 9)],
    28: [(O, 0, 2), (C, 1, 1), (H, 0, 2)],
    29: [(C, 0, 2), (B, 4, 3), (B, 5, 3), (B, 4, 4), (B, 5, 4), (R, 1, 0)],
    30: [(C, 1, 2), (C, 3, 0), (C, 2, 1), (O, 0, 3), (C, 4, 0), (H, 0, 3), (B, 0, 4), (R, 1, 1)],
    31: [(C, 0, 3), (B, 1, 4), (R, 1, 2)],
    32: [(C, 1, 3), (C, 5, 0), (O, 0, 4), (H, 0, 4), (R, 1, 3)],
}
TAIL = [
    (C, 3, 1), (V, 0, 0), (R, 1, 4), (C, 2, 2), (C, 0, 4), (C, 5, 1),
    (R, 2, 0), (C, 4, 1), (R, 2, 1), (C, 1, 4), (C, 3, 2), (C, 2, 3),
    (V, 0, 1), (C, 5, 2), (V, 0, 2), (R, 2, 2), (C, 4, 2), (C, 3, 3),
    (C, 5, 3), (R, 2, 3), (V, 0, 3), (C, 2, 4), (C, 4, 3), (R, 2, 4),
    (C, 3, 4), (C, 5, 4), (V, 0, 4), (C, 4, 4),
]


def fused_kernel(pairs, slots, names, *refs):
    r = types.SimpleNamespace(**dict(zip(names, refs)))
    rows, width = r.seq.shape[1:]
    every = pairs * rows
    tail = rows - slots
    here = place()
    lens = counts(here, pairs, r.text_len, r.patch_count)
    vec_in = lambda index: r.vecs[index : index + 1, :]
    sems = (r.send_sem, r.recv_sem)
    barrier = pltpu.get_barrier_semaphore()
    for bit in BITS:
        pl.semaphore_signal(barrier, inc=1, device_id=partner(bit), device_id_type=pl.DeviceIdType.MESH)

    def load(name, target, index):
        return pltpu.make_async_copy(getattr(r, name), getattr(r, target), r.load_sem.at[index])

    early = [
        load("normal2_in", "normal2", 0),
        load("cot_in", "cot", 1),
        load("normal2_t_in", "normal2_t", 2),
        load("hidden_in", "hidden", 9),
    ]
    late = [
        load("mixed_in", "mixed_t", 3),
        load("normal_in", "normal_t", 4),
        load("seq_in", "seq", 5),
        load("q_in", "q", 6),
        load("k_in", "k", 7),
        load("v_in", "v", 8),
        load("order_in", "order", 10),
    ]

    def block_of(t):
        z1, z0 = 1 - t // 2, 1 - t % 2
        return flip(z0, here["z0"]) + 2 * flip(z1, here["z1"])

    def weight_loads(t, slot):
        start = pl.multiple_of(block_of(t) * width, width)
        return (
            pltpu.make_async_copy(r.wh.at[:, pl.ds(start, width)], r.wbuf.at[slot], r.w_sem.at[slot]),
            pltpu.make_async_copy(r.wd.at[pl.ds(start, width), :], r.wbuf.at[2 + slot], r.w_sem.at[2 + slot]),
        )

    early[0].start()
    for copy in weight_loads(0, 0):
        copy.start()
    for copy in early[1:]:
        copy.start()
    r.gnormal[...] = jnp.zeros_like(r.gnormal)
    live = live_rows(lens, pairs, rows, slots)
    r.total[...] = jnp.zeros_like(r.total)
    for copy in early[:3]:
        copy.wait()
    r.gdown[...] = (r.cot[...].reshape(every, width).astype(F32) * live).astype(BF16)
    r.unit_h[...] = jnp.zeros_like(r.unit_h)
    for copy in late:
        copy.start()
    pl.semaphore_wait(barrier, len(BITS))

    arrivals = lambda name, index: [getattr(r, name + str(step)).at[index] for step in range(5)]

    a_core = lambda t, y: hop("core", r.a_own.at[t, 1, y], r.a_core.at[t, y], sems, 2 * t + y)
    a_y = lambda t: hop("y", r.a_own.at[t, 0, 1], r.a_y.at[t], sems, 8 + t)
    a_z0 = lambda k: hop("z0", r.a_own.at[2 * k, 0, 0], r.a_z0.at[k], sems, 12 + k)
    a_x = lambda k: hop("x", r.a_own.at[2 * k + 1, 0, 0, 1], r.a_x.at[k], sems, 14 + k)
    a_z1 = lambda: hop("z1", r.a_own.at[1, 0, 0, 0], r.a_z1.at[0], sems, 16)

    def a_core_sum(t, y):
        a_core(t, y).wait_recv()
        accumulate(r.a_own.at[t, 0, y], r.a_core.at[t, y])
        if y == 1:
            a_y(t).start()

    def a_second(t):
        k = t // 2
        a_y(t).wait_recv()
        accumulate(r.a_own.at[t, 0, 0], r.a_y.at[t])
        if t % 2 == 0:
            a_z0(k).start()
        else:
            a_z0(k).wait_recv()
            accumulate(r.a_own.at[t, 0, 0], r.a_z0.at[k])
            a_x(k).start()

    def a_third(k):
        a_x(k).wait_recv()
        accumulate(r.a_own.at[2 * k + 1, 0, 0, pl.ds(0, 1)], r.a_x.at[pl.ds(k, 1)])
        if k == 0:
            a_z1().start()

    def a_last():
        a_z1().wait_recv()
        r.out_a[...] = r.a_own[3, 0, 0, 0].astype(F32) + r.a_z1[0].astype(F32)

    size = width // 2

    def b_columns(u):
        return block_of(u // 2) * width + flip(1 - u % 2, here["y"]) * size

    def b_finish(u):
        def finish(value):
            r.out_b[:, :, pl.ds(pl.multiple_of(b_columns(u), 128), size)] = value

        return finish

    def c_finish(g):
        def finish(value):
            for part in range(3):
                cols = slice(part * width + 128 * g, part * width + 128 * g + 128)
                r.out_c[:, :, cols] = value[:, :, 128 * part : 128 * part + 128]

        return finish

    def plain(target):
        def finish(value):
            target[...] = value

        return finish

    units = {}
    for u in range(8):
        units[B, u] = Unit(r.b_own.at[u], arrivals("b", u), ORDERS[1], sems, 20 + 5 * u, b_finish(u))
    for u in range(8):
        units[B, u].peers = {"y": units[B, u ^ 1], "z0": units[B, u ^ 2], "z1": units[B, u ^ 4]}
    groups = width // 128
    for g in range(groups):
        units[C, g] = Unit(r.c_own.at[g], arrivals("c", g), ORDERS[(1, 0, 0, 1, 1, 0)[g]], sems, 60 + 5 * g, c_finish(g))
    units[O, 0] = Unit(r.o_own, arrivals("o", 0), ORDERS[0], sems, 90, plain(r.out_o))
    units[H, 0] = Unit(r.unit_h, arrivals("h", 0), ORDERS[1], sems, 95, plain(r.out_v.at[pl.ds(1, 1)]))
    units[V, 0] = Unit(r.unit_v, arrivals("v", 0), ORDERS[0], sems, 100, plain(r.out_v.at[pl.ds(0, 1)]))

    def give(source, target, pair, index):
        near = lambda src, dst: pltpu.make_async_copy(src, dst, r.give_sem.at[index])
        part = lambda first, count: hop(
            "x", source.at[pair, pl.ds(first, count)], target.at[0, pair, pl.ds(first, count)], sems, 105 + index
        )
        patches, texts = source.at[pair, pl.ds(0, slots)], source.at[pair, pl.ds(slots, tail)]
        far_texts = hop("x", texts, target.at[0, pairs + pair, pl.ds(0, tail)], sems, 105 + index)
        near_texts = lambda: near(texts, target.at[0, pair, pl.ds(0, tail)])
        near_patches = lambda: near(patches, target.at[0, pairs + pair])
        return part, far_texts, near_texts, near_patches

    gives = [give(r.result, r.block_out, pair, pair) for pair in range(pairs)]
    gives += [give(r.grad_rows, r.input_grad, pair, pairs + pair) for pair in range(pairs)]

    def give_start(index):
        _, far_texts, near_texts, near_patches = gives[index]

        @pl.when(here["x"] == 0)
        def _():
            near_texts().start()

        @pl.when(here["x"] == 1)
        def _():
            far_texts.start()
            near_patches().start()

    def give_part(index, piece):
        @pl.when(here["x"] == 0)
        def _():
            gives[index][0](tail * piece, tail).start()

    def give_wait(index):
        part, far_texts, near_texts, near_patches = gives[index]

        @pl.when(here["x"] == 0)
        def _():
            far_texts.wait_recv()
            part(0, slots).wait_send()
            near_texts().wait()

        @pl.when(here["x"] == 1)
        def _():
            part(0, slots).wait_recv()
            far_texts.wait_send()
            near_patches().wait()

    def act(kind, piece, step):
        if kind == R:
            pieces = slots // tail
            give_part(step // pieces if piece == 0 else pairs + piece - 1, step % pieces)
        elif kind != A:
            units[kind, piece].advance(step)
        elif step < 2:
            a_core_sum(piece, 1 - step)
        else:
            (a_second, a_third, lambda _: a_last())[step - 2](piece)

    def run_now(tick):
        for item in PLAN.get(tick, []):
            act(*item)

    def run_tasks(ticks, now):
        for tick in ticks:
            if tick in PLAN:

                @pl.when(now == tick)
                def _(tick=tick):
                    run_now(tick)

    def feed_step(t, carry):
        slot = t % 2
        for copy in weight_loads(t, slot):
            copy.wait()

        @pl.when(t < 3)
        def _():
            for copy in weight_loads(t + 1, 1 - slot):
                copy.start()

        for sub in range(2):
            run_tasks([4 * k + 2 * sub for k in range(4)], 4 * t + 2 * sub)
            y = 1 - sub
            part = flip(y, here["y"])
            start = pl.multiple_of(part * size, size)
            wh = r.wbuf[slot, :, pl.ds(start, size)]
            wd = r.wbuf[2 + slot, pl.ds(start, size), :]
            before = dot(r.normal2[...], wh) + r.vecs[pl.ds(8 + block_of(t), 1), pl.ds(start, size)]
            active, slope = gelu_parts(before)
            active = active.astype(BF16)
            r.gproj[:, :, pl.ds(start, size)] = active.reshape(pairs, rows, size)
            fresh = dot(active, r.gdown[...], 0, 0)
            quarter = size // 4
            for core in range(2):
                for mod in range(2):
                    first = (2 * core + mod) * quarter
                    piece = fresh[first : first + quarter].reshape(quarter // 8, 8, width)
                    r.a_own[t, flip(core, here["core"]), y, flip(mod, here["x"])] = piece.astype(BF16)
            a_core(t, y).start()
            run_tasks([4 * k + 2 * sub + 1 for k in range(4)], 4 * t + 2 * sub + 1)
            gbefore = (dot(r.gdown[...], wd, 1, 1) * slope).astype(BF16)
            right = pl.multiple_of(width + start, 128)
            r.gproj[:, :, pl.ds(right, size)] = gbefore.reshape(pairs, rows, size)
            fresh = dot(r.normal2_t[...], gbefore)
            fresh = fresh.reshape((2,) * 5 + (width // 256, 8, size)).astype(BF16)
            unit = 2 * t + sub
            r.b_own[unit] = fresh
            hop("core", r.b_own.at[unit, 1], r.b0.at[unit], sems, 20 + 5 * unit).start()
            sums = jnp.sum(gbefore.astype(F32), axis=0, keepdims=True)
            z1, z0 = 1 - t // 2, 1 - t % 2
            for core in range(2):
                for mod in range(2):
                    first = (2 * core + mod) * quarter
                    r.unit_h[
                        flip(core, here["core"]), y, z0, flip(mod, here["x"]), z1, 0, 0:1, 0:quarter
                    ] = sums[:, first : first + quarter]
        r.total[...] += dot(r.gproj[:, :, 0:width].reshape(every, width), r.wbuf[2 + slot])
        r.gnormal[...] += dot(r.gproj[:, :, width : 2 * width].reshape(every, width), r.wbuf[slot], 1, 1)
        return carry

    lax.fori_loop(0, 4, feed_step, 0)

    wout_load = pltpu.make_async_copy(r.wout, r.wbuf.at[3], r.w_sem.at[3])
    wout_load.start()
    wqkv_loads = [
        pltpu.make_async_copy(
            r.wqkv.at[:, pl.ds(part * width, width)], r.wbuf.at[part], r.w_sem.at[part]
        )
        for part in range(3)
    ]
    for copy in wqkv_loads:
        copy.start()
    units[H, 0].start()
    early[3].wait()
    r.result[...] = ((r.hidden[...] + r.total[...] + vec_in(7)) * live).astype(BF16).reshape(pairs, rows, width)

    for pair in range(pairs):
        give_start(pair)
    run_now(16)
    normed, factor = norm_parts(r.hidden[...])
    gnorm = r.gnormal[...]
    down = r.gdown[...].astype(F32)
    vec = [
        jnp.sum(gnorm * normed, axis=0, keepdims=True),
        jnp.sum(gnorm, axis=0, keepdims=True),
        jnp.sum(down, axis=0, keepdims=True),
    ]
    made = down + norm_back(gnorm, normed, factor, vec_in(5))
    gattended = made.astype(BF16)
    vec.append(jnp.sum(gattended.astype(F32), axis=0, keepdims=True))
    for index, value in enumerate(vec):
        r.vec[4 + index : 5 + index, :] = value
    r.gnormal[...] = made
    run_now(17)
    wout_load.wait()
    r.gmixed[...] = dot(gattended, r.wbuf[3], 1, 1).astype(BF16).reshape(pairs, rows, width)
    for copy in late:
        copy.wait()
    fresh = dot(r.mixed_t[...], gattended)
    r.o_own[...] = fresh.reshape((2,) * 5 + (width // 256, 8, width)).astype(BF16)
    units[O, 0].start()
    for copy in wqkv_loads:
        copy.wait()

    first = lax.broadcasted_iota(jnp.int32, (rows, 128), 1) < HEAD_DIM
    index = lax.broadcasted_iota(jnp.int32, (rows, 1), 0)

    def project_back(pair):
        made = jnp.zeros((rows, width), F32)
        sums = []
        for part in range(3):
            piece = r.gproj[pair, :, part * width : (part + 1) * width]
            made += dot(piece, r.wbuf[part], 1, 1)
            sums.append(jnp.sum(piece.astype(F32), axis=0, keepdims=True))
        return made, sums

    def finish_pair(pair, grad, sums):
        normed, factor = norm_parts(r.seq[pair].astype(F32))
        sums = [
            jnp.sum(grad * normed, axis=0, keepdims=True),
            jnp.sum(grad, axis=0, keepdims=True),
            sums[0],
            sums[2],
        ]
        for index, value in enumerate(sums):
            r.vec[index : index + 1, :] = value if pair == 0 else r.vec[index : index + 1, :] + value
        span = slice(pair * rows, (pair + 1) * rows)
        made = r.gnormal[span, :] + norm_back(grad, normed, factor, vec_in(0))
        r.grad_rows[pair] = (made * live[span]).astype(BF16)
        give_start(pairs + pair)

    def head_step(it, carry):
        late = it // groups
        pair = (1 - late) * (it % 2) + it // 9
        g = (1 - late) * (it // 2) + late * (3 + it % 3)
        base = g * 128
        off = pl.multiple_of(base, 128)

        @pl.when(it == 9)
        def _():
            finish_pair(0, *project_back(0))

        run_tasks([18 + k for k in range(pairs * groups)], 18 + it)
        at_pair = here["x"] * pairs + pair
        keys_live = live_slots(index, r.text_len[at_pair], r.patch_count[at_pair], slots)
        q2 = r.q[pair, :, pl.ds(off, 128)]
        k2 = r.k[pair, :, pl.ds(off, 128)]
        v2 = r.v[pair, :, pl.ds(off, 128)]
        g2 = r.gmixed[pair, :, pl.ds(off, 128)]
        gq = gk = gv = None
        for half in range(2):
            keep = first if half == 0 else ~first
            zero = jnp.zeros_like(q2)
            qm = jnp.where(keep, q2, zero)
            km = jnp.where(keep, k2, zero)
            gm = jnp.where(keep, g2, zero)
            scores = jnp.where(keys_live, dot(k2, qm, 1, 1), MASKED)
            highest = jnp.max(scores, axis=0, keepdims=True)
            shifted = jnp.exp(scores - highest)
            probs = shifted * (1.0 / jnp.sum(shifted, axis=0, keepdims=True))
            gprobs = dot(v2, gm, 1, 1)
            row_dot = jnp.sum(probs * gprobs, axis=0, keepdims=True)
            gscores = (probs * (gprobs - row_dot)).astype(BF16)
            new_v = dot(probs.astype(BF16), gm)
            new_k = dot(gscores, qm)
            new_q = dot(gscores, km, 0, 0)
            gq = new_q if gq is None else gq + new_q
            gk = new_k if gk is None else gk + new_k
            gv = new_v if gv is None else gv + new_v
        r.gproj[pair, :, pl.ds(off, 128)] = (gq * 0.125).astype(BF16)
        r.gproj[pair, :, pl.ds(pl.multiple_of(base + width, 128), 128)] = gk.astype(BF16)
        r.gproj[pair, :, pl.ds(pl.multiple_of(base + 2 * width, 128), 128)] = gv.astype(BF16)

        @pl.when(pair == pairs - 1)
        def _():
            pieces = [
                r.gproj[:, :, pl.ds(pl.multiple_of(base + part * width, 128), 128)].reshape(every, 128)
                for part in range(3)
            ]
            fresh = dot(r.normal_t[...], jnp.concatenate(pieces, axis=1))
            r.c_own[g] = fresh.reshape((2,) * 5 + (width // 256, 8, 384)).astype(BF16)
            hop("core", r.c_own.at[g, 1], r.c0.at[g], sems, 60 + 5 * g).start()

        return carry

    lax.fori_loop(0, pairs * groups, head_step, 0)

    run_now(30)
    made, sums = project_back(1)
    run_now(31)
    finish_pair(1, made, sums)
    rest = r.vec[...]
    ordered = jnp.zeros_like(rest)
    for _ in range(3):
        high = rest.astype(BF16)
        ordered += dot(high, r.order[...], 1, 1)
        rest = rest - high.astype(F32)
    r.unit_v[...] = jnp.zeros_like(r.unit_v)
    unit = width // 32
    for block in range(32):
        bits = tuple(block >> shift & 1 for shift in (4, 3, 2, 1, 0))
        r.unit_v[bits + (0, slice(None), slice(0, unit))] = ordered[:, block * unit : (block + 1) * unit]
    units[V, 0].start()
    run_now(32)
    for item in TAIL:
        act(*item)
    for number in range(2 * pairs):
        give_wait(number)
    for t in range(4):
        a_core(t, 0).wait_send()
        a_core(t, 1).wait_send()
        a_y(t).wait_send()
    for k in range(2):
        a_z0(k).wait_send()
        a_x(k).wait_send()
    a_z1().wait_send()
    for unit in units.values():
        unit.drain()


def run_fused(text_len, patch_count, vecs, hidden, cot, wh, wd, order, wqkv, wout, seq, q, k, v, mixed_t, normal_t, normal2, normal2_t, slots):
    pairs, rows, width = seq.shape
    every = pairs * rows
    wide = (2,) * 5
    eight = width // 256
    groups = width // 128

    def arrivals(name, count, tail, kind):
        return {name + str(step): pltpu.VMEM((count,) + (2,) * (4 - step) + tail, kind) for step in range(5)}

    flat = lambda kind: pltpu.VMEM((every, width), kind)
    cube = pltpu.VMEM((pairs, rows, width), BF16)
    tall = pltpu.VMEM((width, every), BF16)
    block = (width // 64, 8, width)
    scratch = dict(
        cot=cube,
        result=cube,
        grad_rows=cube,
        give_sem=pltpu.SemaphoreType.DMA((2 * pairs,)),
        hidden=flat(F32),
        gdown=flat(BF16),
        seq=cube,
        q=cube,
        k=cube,
        v=cube,
        mixed_t=tall,
        normal_t=tall,
        wbuf=pltpu.VMEM((4, width, width), BF16),
        order=pltpu.VMEM((width, width), BF16),
        normal2=flat(BF16),
        normal2_t=tall,
        total=flat(F32),
        gnormal=flat(F32),
        gmixed=cube,
        gproj=pltpu.VMEM((pairs, rows, 3 * width), BF16),
        vec=pltpu.VMEM((8, width), F32),
        a_own=pltpu.VMEM((4, 2, 2, 2) + block, BF16),
        a_core=pltpu.VMEM((4, 2, 2) + block, BF16),
        a_y=pltpu.VMEM((4, 2) + block, BF16),
        a_z0=pltpu.VMEM((2, 2) + block, BF16),
        a_x=pltpu.VMEM((2,) + block, BF16),
        a_z1=pltpu.VMEM((1,) + block, BF16),
        b_own=pltpu.VMEM((8,) + wide + (eight, 8, width // 2), BF16),
        **arrivals("b", 8, (eight, 8, width // 2), BF16),
        c_own=pltpu.VMEM((groups,) + wide + (eight, 8, 384), BF16),
        **arrivals("c", groups, (eight, 8, 384), BF16),
        o_own=pltpu.VMEM(wide + (eight, 8, width), BF16),
        **arrivals("o", 1, (eight, 8, width), BF16),
        unit_h=pltpu.VMEM(wide + (1, 8, 128), F32),
        **arrivals("h", 1, (1, 8, 128), F32),
        unit_v=pltpu.VMEM(wide + (1, 8, 128), F32),
        **arrivals("v", 1, (1, 8, 128), F32),
        send_sem=pltpu.SemaphoreType.DMA((105 + 2 * pairs,)),
        recv_sem=pltpu.SemaphoreType.DMA((105 + 2 * pairs,)),
        load_sem=pltpu.SemaphoreType.DMA((11,)),
        w_sem=pltpu.SemaphoreType.DMA((4,)),
    )
    hbm = pl.BlockSpec(memory_space=pl.ANY)
    operands = dict(
        text_len=(text_len, smem_spec()),
        patch_count=(patch_count, smem_spec()),
        vecs=(vecs, whole_spec()),
        hidden_in=(hidden, hbm),
        cot_in=(cot, hbm),
        wh=(wh, hbm),
        wd=(wd, hbm),
        order_in=(order, hbm),
        wqkv=(wqkv, hbm),
        wout=(wout, hbm),
        seq_in=(seq, hbm),
        q_in=(q, hbm),
        k_in=(k, hbm),
        v_in=(v, hbm),
        mixed_in=(mixed_t, hbm),
        normal_in=(normal_t, hbm),
        normal2_in=(normal2, hbm),
        normal2_t_in=(normal2_t, hbm),
    )
    final = shape((1, 2 * pairs, slots, width), BF16)
    outs = dict(
        block_out=(final, hbm),
        input_grad=(final, hbm),
        out_a=(shape(block, F32), whole_spec()),
        out_b=(shape((eight, 8, 4 * width), F32), whole_spec()),
        out_c=(shape((eight, 8, 3 * width), F32), whole_spec()),
        out_o=(shape((eight, 8, width), F32), whole_spec()),
        out_v=(shape((2, 8, 128), F32), whole_spec()),
    )
    names = list(operands) + list(outs) + list(scratch)
    return pl.pallas_call(
        functools.partial(fused_kernel, pairs, slots, names),
        out_shape=[kind for kind, _ in outs.values()],
        in_specs=[spec for _, spec in operands.values()],
        out_specs=[spec for _, spec in outs.values()],
        scratch_shapes=list(scratch.values()),
        compiler_params=pltpu.CompilerParams(
            collective_id=1, has_side_effects=True, vmem_limit_bytes=67043328
        ),
        name="fused",
    )(*[value for value, _ in operands.values()])


def closing_kernel(*refs):
    count = len(refs) // 2
    for index in range(count):
        value = refs[index][...]
        if index < 2:
            slot = lax.broadcasted_iota(jnp.int32, value.shape, 2)
            last = TEXT + lax.axis_index("mod") * value.shape[2]
            value = jnp.where(slot < last, value, jnp.zeros_like(value))
        refs[count + index][...] = value


def run_closing(*arrays):
    return pl.pallas_call(
        closing_kernel,
        out_shape=[shape(array.shape, array.dtype) for array in arrays],
        in_specs=[whole_spec()] * len(arrays),
        out_specs=[whole_spec()] * len(arrays),
        name="closing",
    )(*arrays)


def pair_bits():
    return lax.axis_size("pairs").bit_length() - 1


def swapped(array, axis, bit):
    size = lax.axis_size(axis)
    return lax.ppermute(array, axis, [(i, i ^ (1 << bit)) for i in range(size)])


def split_dims(array):
    bits = pair_bits() + 1
    return array.reshape((2,) * bits + (array.shape[0] >> bits,) + array.shape[1:])


def stage_orders():
    bits = pair_bits()
    ring = ["mod", 1, 2]
    orders = []
    for turn in range(3):
        orders.append([0] + ring[turn:] + ring[:turn] + list(range(3, bits)))
    return orders


def half_sum(array, names, name, last):
    axis, bit = ("mod", 0) if name == "mod" else ("pairs", name)
    mine = (lax.axis_index(axis) >> bit) & 1
    dim = names.index(name)
    sent = lax.dynamic_index_in_dim(array, 1 - mine, dim, keepdims=False)
    kept = lax.dynamic_index_in_dim(array, mine, dim, keepdims=False)
    came = swapped(sent, axis, bit)
    total = kept.astype(F32) + came.astype(F32)
    return (total if last else total.astype(BF16)), names[:dim] + names[dim + 1 :]


def scattered(array):
    width = array.shape[1]
    names0 = list(range(pair_bits() - 1, -1, -1)) + ["mod"]
    first, names1 = half_sum(split_dims(array), names0, 0, False)
    third = -(-width // 3 // 128) * 128
    pieces = []
    for turn, order in enumerate(stage_orders()):
        piece = first[..., turn * third : min(width, (turn + 1) * third)]
        names = list(names1)
        for place, name in enumerate(order[1:]):
            piece, names = half_sum(piece, names, name, place == len(order) - 2)
        pieces.append(piece)
    return jnp.concatenate(pieces, axis=1)


def on_device(
    inputs,
    cotangent,
    text_len,
    patch_count,
    norm1_gain,
    norm1_bias,
    qkv_weight,
    query_bias,
    value_bias,
    out_weight,
    out_bias,
    norm2_gain,
    norm2_bias,
    hidden_weight,
    hidden_bias,
    down_weight,
    down_bias,
):
    _, group, slots, width = inputs.shape
    half = group // 2
    rows = padded(TEXT + slots)
    mod = lax.axis_index("mod")
    is_text = mod == 0
    lens = lax.dynamic_slice_in_dim(jnp.stack([text_len, patch_count]), mod * half, half, 1)
    lens = lens.reshape(-1)

    def gathered(array):
        local = array[0]
        patches = lax.ppermute(local[:half], "mod", [(1, 0)])
        texts = lax.ppermute(local[half:, :TEXT], "mod", [(0, 1)])
        patches = jnp.where(is_text, patches, local[half:])
        texts = jnp.where(is_text, local[:half, :TEXT], texts)
        blank = jnp.zeros((half, rows - slots - TEXT, width), array.dtype)
        return jnp.concatenate([patches, texts, blank], axis=1)

    def returned(array):
        far_patches = lax.ppermute(array[:, :slots], "mod", [(0, 1)])
        far_texts = lax.ppermute(array[:, slots : slots + TEXT], "mod", [(1, 0)])
        return assembled(array, far_patches, far_texts)

    def assembled(array, far_patches, far_texts):
        patches, texts = array[:, :slots], array[:, slots : slots + TEXT]
        texts = jnp.concatenate([texts, far_texts], axis=0)
        texts = jnp.pad(texts, ((0, 0), (0, slots - TEXT), (0, 0)))
        patches = jnp.concatenate([far_patches, patches], axis=0)
        return jnp.where(is_text, texts, patches)[None]

    row = lambda vector: vector.reshape(1, -1)
    if lax.axis_size("pairs") == 16:
        parts = [norm1_gain, norm1_bias, query_bias, value_bias, out_bias, norm2_gain, norm2_bias, down_bias, hidden_bias]
        made = run_opening(text_len, patch_count, inputs, cotangent, parts, qkv_weight, out_weight)
        vecs, q, k, v, hidden, seq, order, mixed, normal, normal2, normal2_t, cot = made
        made = run_fused(
            text_len,
            patch_count,
            vecs,
            hidden,
            cot,
            hidden_weight,
            down_weight,
            order,
            qkv_weight,
            out_weight,
            seq,
            q,
            k,
            v,
            mixed,
            normal,
            normal2,
            normal2_t,
            slots,
        )
        block_out, input_grad, wd_out, wh_out, qkv_out, wo_out, vectors = made
        flat = lambda array: array.reshape(-1, array.shape[-1])
        wd_out, wh_out, qkv_out, wo_out = flat(wd_out), flat(wh_out), flat(qkv_out), flat(wo_out)
        made = run_closing(block_out, input_grad, wd_out, wh_out, qkv_out, wo_out)
        block_out, input_grad, wd_out, wh_out, qkv_out, wo_out = made
        vec_out = [vectors[0, index, : width // 32] for index in range(8)]
        hb_out = vectors[1, 0, : hidden_bias.shape[0] // 32]
    else:
        seq = gathered(inputs)
        cot = gathered(cotangent).reshape(half * rows, width)
        qkv_bias = row(jnp.concatenate([query_bias, jnp.zeros_like(query_bias), value_bias]))
        feature = jnp.arange(width, dtype=jnp.int32)
        order = (feature[:, None] == feature[None, :]).astype(BF16)
        q, k, v, hidden, mixed = run_forward(
            lens, seq, row(norm1_gain), row(norm1_bias), qkv_weight, qkv_bias, out_weight, row(out_bias), slots
        )
        chunks = 8
        steps = jnp.arange(chunks, dtype=jnp.int32)
        lens = jnp.concatenate([lens, jnp.zeros(4, jnp.int32), steps])
        result, ghidden, wh_grad, wd_grad, hb_grad, vec2 = run_feed(
            lens,
            hidden,
            cot,
            row(norm2_gain),
            row(norm2_bias),
            hidden_weight,
            row(hidden_bias),
            down_weight,
            row(down_bias),
            order,
            half,
            slots,
            chunks,
            False,
        )
        block_out = returned(result.reshape(half, rows, width))
        input_rows, qkvo_grad, vec1 = run_backward(
            lens,
            seq,
            row(norm1_gain),
            row(norm1_bias),
            q,
            k,
            v,
            mixed,
            ghidden,
            qkv_weight,
            out_weight,
            order,
            slots,
            False,
        )
        input_grad = returned(input_rows)
        strip = jnp.concatenate([vec1[:4], vec2[:4]], axis=0).T
        strip = jnp.concatenate([strip, hb_grad.reshape(width, -1)], axis=1).astype(BF16)
        strip = jnp.pad(strip, ((0, 0), (0, 128 - strip.shape[1])))
        wd_out, wh_out = scattered(wd_grad), scattered(wh_grad)
        qkvo_out = scattered(jnp.concatenate([qkvo_grad, strip], axis=1))
        vec_out = qkvo_out[:, 4 * width :]
        qkv_out, wo_out = qkvo_out[:, : 3 * width], qkvo_out[:, 3 * width : 4 * width]
        hb_out = vec_out[:, 8 : 8 + hidden_bias.shape[0] // width].reshape(-1)
        vec_out = [vec_out[:, index] for index in range(8)]
    return (
        block_out,
        input_grad,
        vec_out[0],
        vec_out[1],
        qkv_out,
        vec_out[2],
        vec_out[3],
        wo_out,
        vec_out[7],
        vec_out[4],
        vec_out[5],
        wh_out,
        hb_out,
        wd_out,
        vec_out[6],
    )


def solution(mesh):
    whole = P()
    split = P("mod", "pairs", None, None)
    vector = P(("pairs", "mod"))
    matrix = P(("pairs", "mod"), None)
    return jax.shard_map(
        on_device,
        mesh=mesh,
        in_specs=(split, split, P("pairs"), P("pairs")) + (whole,) * 13,
        out_specs=(
            split,
            split,
            vector,
            vector,
            matrix,
            vector,
            vector,
            matrix,
            vector,
            vector,
            vector,
            matrix,
            vector,
            matrix,
            vector,
        ),
        check_vma=False,
    )
```

```python
import functools
import types

import jax
import jax.numpy as jnp
from jax import lax
from jax.experimental import pallas as pl
from jax.experimental.pallas import tpu as pltpu
from jax.sharding import PartitionSpec as P

HEADS = 12
HEAD_DIM = 64
TEXT = 40
EPSILON = 1e-06
MASKED = -1e30
F32 = jnp.float32
BF16 = jnp.bfloat16
VMEM_LIMIT = 60 * 1024 * 1024


def padded(count):
    return -(-count // 32) * 32


def dot(a, b, ca=1, cb=0):
    return lax.dot_general(a, b, (((ca,), (cb,)), ((), ())), preferred_element_type=F32)


def norm_parts(values):
    centre = jnp.mean(values, axis=-1, keepdims=True)
    centred = values - centre
    spread = jnp.mean(centred * centred, axis=-1, keepdims=True)
    factor = lax.rsqrt(spread + EPSILON)
    return centred * factor, factor


def norm_back(grad_out, normed, factor, norm_gain):
    grad_norm = grad_out * norm_gain
    mean_grad = jnp.mean(grad_norm, axis=-1, keepdims=True)
    second = jnp.mean(grad_norm * normed, axis=-1, keepdims=True)
    return (grad_norm - mean_grad - normed * second) * factor


def live_slots(index, text_count, patch_count, slots):
    return (index < patch_count) | ((index >= slots) & (index - slots < text_count))


def live_rows(lens, pairs, rows, slots):
    parts = []
    for pair in range(pairs):
        index = lax.broadcasted_iota(jnp.int32, (rows, 1), 0)
        parts.append(live_slots(index, lens[pair], lens[pairs + pair], slots).astype(F32))
    return jnp.concatenate(parts, axis=0)


def mix_heads(pair, group, text_count, patch_count, slots, q_in, k_in, v_in, mixed):
    rows = q_in.shape[1]
    first = lax.broadcasted_iota(jnp.int32, (rows, 128), 1) < HEAD_DIM
    column = lax.broadcasted_iota(jnp.int32, (1, rows), 1)
    off = pl.multiple_of(group * 128, 128)
    live = live_slots(column, text_count, patch_count, slots)
    q2 = q_in[pair, :, pl.ds(off, 128)]
    k2 = k_in[pair, :, pl.ds(off, 128)]
    v2 = v_in[pair, :, pl.ds(off, 128)]
    halves = []
    for half in range(2):
        keep = first if half == 0 else ~first
        qm = jnp.where(keep, q2, jnp.zeros_like(q2))
        scores = jnp.where(live, dot(qm, k2, 1, 1), MASKED)
        highest = jnp.max(scores, axis=-1, keepdims=True)
        shifted = jnp.exp(scores - highest)
        total = jnp.sum(shifted, axis=-1, keepdims=True)
        halves.append(dot(shifted.astype(BF16), v2) / total)
    mixed[pair, :, pl.ds(off, 128)] = jnp.where(first, halves[0], halves[1]).astype(BF16)


def forward_kernel(
    slots,
    lens,
    seq,
    gain,
    shift,
    wqkv,
    qkv_bias,
    wout,
    out_bias,
    q_out,
    k_out,
    v_out,
    hidden,
    mixed_out,
    mixed,
):
    pairs, rows, width = seq.shape
    tokens = seq[...].reshape(pairs * rows, width).astype(F32)
    normed, _ = norm_parts(tokens)
    normal = (normed * gain[...] + shift[...]).astype(BF16)
    for part, ref in enumerate((q_out, k_out, v_out)):
        cols = slice(part * width, (part + 1) * width)
        made = dot(normal, wqkv[:, cols]) + qkv_bias[:, cols]
        if part == 0:
            made = made * 0.125
        ref[...] = made.astype(BF16).reshape(pairs, rows, width)
    groups = width // 128

    def step(it, carry):
        pair = it // groups
        mix_heads(pair, it % groups, lens[pair], lens[pairs + pair], slots, q_out, k_out, v_out, mixed)
        return carry

    lax.fori_loop(0, pairs * groups, step, 0)
    rows_mixed = mixed[...].reshape(pairs * rows, width)
    mixed_out[...] = mixed[...]
    hidden[...] = tokens + dot(rows_mixed, wout[...]) + out_bias[...]


def gelu_parts(values):
    cumulative = 0.5 * (1.0 + lax.erf(values * 0.7071067811865476))
    density = jnp.exp(-0.5 * values * values) * 0.3989422804014327
    return values * cumulative, cumulative + values * density


def feed_kernel(
    pairs,
    slots,
    lens,
    hidden,
    cot,
    gain,
    shift,
    wh,
    hbias,
    wd,
    dbias,
    order,
    result,
    grad_hidden,
    wh_grad,
    wd_grad,
    hb_grad,
    vectors,
    normal,
    ordered,
    gdown,
    total,
    gnormal,
):
    chunk = pl.program_id(0)
    count = pl.num_programs(0)
    rows = hidden.shape[0] // pairs
    live = live_rows(lens, pairs, rows, slots)

    @pl.when(chunk == 0)
    def _():
        normed, _ = norm_parts(hidden[...])
        made = (normed * gain[...] + shift[...]).astype(BF16)
        normal[...] = made
        ordered[...] = dot(made, order[...]).astype(BF16)
        gdown[...] = (cot[...].astype(F32) * live).astype(BF16)
        total[...] = hidden[...] + dbias[...]
        gnormal[...] = jnp.zeros_like(gnormal)

    before = dot(normal[...], wh[...]) + hbias[...]
    active, slope = gelu_parts(before)
    active = active.astype(BF16)
    total[...] += dot(active, wd[...])
    fresh = dot(active, gdown[...], 0, 0)
    if wd_grad.ndim == 2:
        wd_grad[...] = fresh.astype(BF16)
    else:
        size = fresh.shape[0] // 4
        base = 2 * pairs
        for core in range(2):
            for mod in range(2):
                start = (2 * core + mod) * size
                piece = fresh[start : start + size].reshape(size // 8, 8, fresh.shape[1])
                wd_grad[lens[base + core], 0, 0, lens[base + 2 + mod], 0] = piece.astype(BF16)
    gbefore = (dot(gdown[...], wd[...], 1, 1) * slope).astype(BF16)
    gnormal[...] += dot(gbefore, wh[...], 1, 1)
    wh_grad[...] = dot(ordered[...], gbefore, 0, 0).reshape(wh_grad.shape).astype(BF16)
    hb_grad[...] = jnp.sum(gbefore.astype(F32), axis=0, keepdims=True)

    @pl.when(chunk == count - 1)
    def _():
        result[...] = (total[...] * live).astype(BF16)
        normed, factor = norm_parts(hidden[...])
        gnorm = gnormal[...]
        vectors[0:1, :] = jnp.sum(gnorm * normed, axis=0, keepdims=True)
        vectors[1:2, :] = jnp.sum(gnorm, axis=0, keepdims=True)
        down = gdown[...].astype(F32)
        vectors[2:3, :] = jnp.sum(down, axis=0, keepdims=True)
        made = down + norm_back(gnorm, normed, factor, gain[...])
        vectors[3:4, :] = jnp.sum(made.astype(BF16).astype(F32), axis=0, keepdims=True)
        grad_hidden[...] = made


def backward_kernel(
    slots,
    lens,
    seq,
    gain,
    shift,
    q_in,
    k_in,
    v_in,
    mixed,
    ghidden,
    wqkv,
    wout,
    order,
    input_grad,
    weight_grad,
    vectors,
    gmixed,
    gproj,
):
    pairs, rows, width = seq.shape
    every = pairs * rows
    gattended = ghidden[...].astype(BF16)
    gmixed[...] = dot(gattended, wout[...], 1, 1).astype(BF16).reshape(pairs, rows, width)
    ordered = dot(mixed[...].reshape(every, width), order[...]).astype(BF16)

    def put(first, last, value):
        target = (slice(None),) * (len(weight_grad.shape) - 1) + (slice(first, last),)
        value = value.reshape(weight_grad.shape[:-1] + (last - first,))
        weight_grad[target] = value.astype(BF16)

    put(3 * width, 4 * width, dot(ordered, gattended, 0, 0))
    first = lax.broadcasted_iota(jnp.int32, (rows, 128), 1) < HEAD_DIM
    index = lax.broadcasted_iota(jnp.int32, (rows, 1), 0)
    groups = width // 128

    def step(it, carry):
        pair = it // groups
        base = (it % groups) * 128
        off = pl.multiple_of(base, 128)
        live = live_slots(index, lens[pair], lens[pairs + pair], slots)
        q2 = q_in[pair, :, pl.ds(off, 128)]
        k2 = k_in[pair, :, pl.ds(off, 128)]
        v2 = v_in[pair, :, pl.ds(off, 128)]
        g2 = gmixed[pair, :, pl.ds(off, 128)]
        gq = gk = gv = None
        for half in range(2):
            keep = first if half == 0 else ~first
            zero = jnp.zeros_like(q2)
            qm = jnp.where(keep, q2, zero)
            km = jnp.where(keep, k2, zero)
            gm = jnp.where(keep, g2, zero)
            scores = jnp.where(live, dot(k2, qm, 1, 1), MASKED)
            highest = jnp.max(scores, axis=0, keepdims=True)
            shifted = jnp.exp(scores - highest)
            probs = shifted * (1.0 / jnp.sum(shifted, axis=0, keepdims=True))
            gprobs = dot(v2, gm, 1, 1)
            row_dot = jnp.sum(probs * gprobs, axis=0, keepdims=True)
            gscores = (probs * (gprobs - row_dot)).astype(BF16)
            new_v = dot(probs.astype(BF16), gm)
            new_k = dot(gscores, qm)
            new_q = dot(gscores, km, 0, 0)
            gq = new_q if gq is None else gq + new_q
            gk = new_k if gk is None else gk + new_k
            gv = new_v if gv is None else gv + new_v
        gproj[pair, :, pl.ds(off, 128)] = (gq * 0.125).astype(BF16)
        gproj[pair, :, pl.ds(pl.multiple_of(base + width, 128), 128)] = gk.astype(BF16)
        gproj[pair, :, pl.ds(pl.multiple_of(base + 2 * width, 128), 128)] = gv.astype(BF16)
        return carry

    lax.fori_loop(0, pairs * groups, step, 0)
    tokens = seq[...].reshape(every, width).astype(F32)
    normed, factor = norm_parts(tokens)
    normal = (normed * gain[...] + shift[...]).astype(BF16)
    ordered = dot(normal, order[...]).astype(BF16)
    gnormal = jnp.zeros((every, width), F32)
    for part in range(3):
        cols = slice(part * width, (part + 1) * width)
        piece = gproj[:, :, cols].reshape(every, width)
        gnormal += dot(piece, wqkv[:, cols], 1, 1)
        put(part * width, (part + 1) * width, dot(ordered, piece, 0, 0))
        if part == 0:
            vectors[2:3, :] = jnp.sum(piece.astype(F32), axis=0, keepdims=True)
        if part == 2:
            vectors[3:4, :] = jnp.sum(piece.astype(F32), axis=0, keepdims=True)
    vectors[0:1, :] = jnp.sum(gnormal * normed, axis=0, keepdims=True)
    vectors[1:2, :] = jnp.sum(gnormal, axis=0, keepdims=True)
    live = live_rows(lens, pairs, rows, slots)
    made = ghidden[...] + norm_back(gnormal, normed, factor, gain[...])
    input_grad[...] = (made * live).astype(BF16).reshape(pairs, rows, width)


def whole_spec():
    return pl.BlockSpec(memory_space=pltpu.VMEM)


def smem_spec():
    return pl.BlockSpec(memory_space=pltpu.SMEM)


def shape(dims, kind):
    return jax.ShapeDtypeStruct(dims, kind)


def run_forward(lens, seq, gain, shift, wqkv, qkv_bias, wout, out_bias, slots):
    pairs, rows, width = seq.shape
    every = pairs * rows
    cube = shape((pairs, rows, width), BF16)
    return pl.pallas_call(
        functools.partial(forward_kernel, slots),
        out_shape=[cube, cube, cube, shape((every, width), F32), cube],
        in_specs=[smem_spec()] + [whole_spec()] * 7,
        out_specs=[whole_spec()] * 5,
        scratch_shapes=[pltpu.VMEM((pairs, rows, width), BF16)],
        compiler_params=pltpu.CompilerParams(vmem_limit_bytes=VMEM_LIMIT),
        name="attention_forward",
    )(lens, seq, gain, shift, wqkv, qkv_bias, wout, out_bias)


def run_feed(lens, hidden, cot, gain, shift, wh, hbias, wd, dbias, order, pairs, slots, chunks, relative):
    every, width = hidden.shape
    ff = wh.shape[1]
    size = ff // chunks
    base = 2 * pairs + 4
    fixed = lambda dims: pl.BlockSpec(dims, lambda c, s: (0, 0))
    columns = lambda r: pl.BlockSpec((r, size), lambda c, s: (0, s[base + c]))
    rows = pl.BlockSpec((size, width), lambda c, s: (s[base + c], 0))
    if relative:
        part = size // 4 // 8
        wd_shape = shape((2, 2, 2, 2, 2, part, 8, width), BF16)
        wd_spec = pl.BlockSpec(
            (2, 1, 1, 2, 1, part, 8, width),
            lambda c, s: (0, c % 2, c // 2 % 2, 0, c // 4, 0, 0, 0),
        )
        wh_shape = shape((width // 8, 8, ff), BF16)
        wh_spec = pl.BlockSpec((width // 8, 8, size), lambda c, s: (0, 0, s[base + c]))
    else:
        wd_shape, wd_spec = shape((ff, width), BF16), rows
        wh_shape, wh_spec = shape((width, ff), BF16), columns(width)
    return pl.pallas_call(
        functools.partial(feed_kernel, pairs, slots),
        out_shape=[
            shape((every, width), BF16),
            shape((every, width), F32),
            wh_shape,
            wd_shape,
            shape((1, ff), F32),
            shape((8, width), F32),
        ],
        grid_spec=pltpu.PrefetchScalarGridSpec(
        num_scalar_prefetch=1,
        grid=(chunks,),
        in_specs=[
            fixed((every, width)),
            fixed((every, width)),
            fixed((1, width)),
            fixed((1, width)),
            columns(width),
            columns(1),
            rows,
            fixed((1, width)),
            fixed((width, width)),
        ],
        out_specs=[
            fixed((every, width)),
            fixed((every, width)),
            wh_spec,
            wd_spec,
            columns(1),
            fixed((8, width)),
        ],
        scratch_shapes=[
            pltpu.VMEM((every, width), BF16),
            pltpu.VMEM((every, width), BF16),
            pltpu.VMEM((every, width), BF16),
            pltpu.VMEM((every, width), F32),
            pltpu.VMEM((every, width), F32),
        ],
        ),
        compiler_params=pltpu.CompilerParams(vmem_limit_bytes=VMEM_LIMIT),
        cost_estimate=pl.CostEstimate(
            flops=12 * every * width * ff,
            bytes_accessed=24 * 2**20,
            transcendentals=2 * every * ff,
        ),
        name="feed_forward",
    )(lens, hidden, cot, gain, shift, wh, hbias, wd, dbias, order)


def run_backward(lens, seq, gain, shift, q, k, v, mixed, ghidden, wqkv, wout, order, slots, relative):
    pairs, rows, width = seq.shape
    every = pairs * rows
    return pl.pallas_call(
        functools.partial(backward_kernel, slots),
        out_shape=[
            shape((pairs, rows, width), BF16),
            shape((width // 8, 8, 4 * width) if relative else (width, 4 * width), BF16),
            shape((8, width), F32),
        ],
        in_specs=[smem_spec()] + [whole_spec()] * 11,
        out_specs=[whole_spec()] * 3,
        scratch_shapes=[
            pltpu.VMEM((pairs, rows, width), BF16),
            pltpu.VMEM((pairs, rows, 3 * width), BF16),
        ],
        compiler_params=pltpu.CompilerParams(vmem_limit_bytes=VMEM_LIMIT),
        cost_estimate=pl.CostEstimate(
            flops=4 * every * width * width * 4 + 20 * every * rows * width,
            bytes_accessed=20 * 2**20,
            transcendentals=every * rows * HEADS,
        ),
        name="attention_backward",
    )(lens, seq, gain, shift, q, k, v, mixed, ghidden, wqkv, wout, order)


BITS = ("core", "y", "z0", "x", "z1")
ORDERS = (("core", "y", "z0", "x", "z1"), ("core", "z0", "y", "x", "z1"))


def partner(bit):
    if bit == "x":
        return {"mod": 1 - lax.axis_index("mod")}
    size = {"core": 1, "y": 2, "z0": 4, "z1": 8}[bit]
    me = lax.axis_index("pairs")
    return {"pairs": me + size - 2 * size * (me // size % 2)}


def narrowed(ref, names, bit, value):
    dim = names.index(bit)
    index = (slice(None),) * dim + (value,)
    return ref.at[index], names[:dim] + names[dim + 1 :]


def flip(value, bit):
    return value + bit - 2 * value * bit


def place():
    pairs = lax.axis_index("pairs")
    return {
        "core": pairs % 2,
        "y": pairs // 2 % 2,
        "z0": pairs // 4 % 2,
        "z1": pairs // 8,
        "x": lax.axis_index("mod"),
    }


def hop(bit, source, target, sems, index, there=None):
    return pltpu.make_async_remote_copy(
        src_ref=source,
        dst_ref=target,
        send_sem=sems[0].at[index],
        recv_sem=sems[1].at[index if there is None else there],
        device_id=partner(bit),
        device_id_type=pl.DeviceIdType.MESH,
    )


def lead_index(it, lead):
    index = []
    for size in reversed(lead):
        index.insert(0, it % size)
        it = it // size
    return tuple(index)


def accumulate(target, source):
    lead = target.shape[:-3]
    tiles = target.shape[-3] * target.shape[-2] * target.shape[-1] // 1024
    while lead and tiles * lead[-1] <= 72:
        tiles *= lead[-1]
        lead = lead[:-1]
    count = 1
    for size in lead:
        count *= size

    def add(at):
        target[at] = target[at] + source[at]

    if count == 1:
        add((0,) * len(lead) if lead else (Ellipsis,))
        return

    def body(it, carry):
        add(lead_index(it, lead))
        return carry

    lax.fori_loop(0, count, body, 0)


class Unit:
    def __init__(self, own, arrivals, order, sems, base, finish):
        self.own, self.arrivals, self.order = own, arrivals, order
        self.sems, self.base, self.finish = sems, base, finish
        self.peers = {}

    def views(self, step):
        ref, names = self.own, list(BITS)
        for bit in self.order[:step]:
            ref, names = narrowed(ref, names, bit, 0)
        sent, _ = narrowed(ref, names, self.order[step], 1)
        kept, _ = narrowed(ref, names, self.order[step], 0)
        return sent, kept

    def copy(self, step):
        bit = self.order[step]
        sent, _ = self.views(step)
        peer = self.peers.get(bit, self)
        return hop(bit, sent, peer.arrivals[step], self.sems, self.base + step, peer.base + step)

    def arrival(self, step):
        sent, _ = self.views(step)
        return hop(self.order[step], sent, self.arrivals[step], self.sems, self.base + step)

    def start(self):
        self.copy(0).start()

    def advance(self, step):
        self.arrival(step).wait_recv()
        _, kept = self.views(step)
        if step == 4:
            self.finish(kept[...].astype(F32) + self.arrivals[4][...].astype(F32))
            return
        accumulate(kept, self.arrivals[step])
        self.copy(step + 1).start()

    def drain(self):
        for step in range(5):
            self.copy(step).wait_send()


STORED = [
    "q_out",
    "k_out",
    "v_out",
    "hidden",
    "seq",
    "order",
    "mixed_out",
    "normal_out",
    "normal2",
    "normal2_t",
    "cot",
]


def counts(here, pairs, text_len, patch_count):
    base = here["x"] * pairs
    return [text_len[base + pair] for pair in range(pairs)] + [patch_count[base + pair] for pair in range(pairs)]


def opening_kernel(pairs, slots, names, *refs):
    r = types.SimpleNamespace(**dict(zip(names, refs)))
    rows, width = r.seq.shape[1:]
    every, tail = pairs * rows, rows - slots
    here = place()
    lens = counts(here, pairs, r.text_len, r.patch_count)
    sems = (r.send_sem, r.recv_sem)
    barrier = pltpu.get_barrier_semaphore()
    pl.semaphore_signal(barrier, inc=1, device_id=partner("x"), device_id_type=pl.DeviceIdType.MESH)

    def moves(which, pair):
        source, target = ((r.inputs, r.seq), (r.cotangent, r.cot))[which]
        index = which * pairs + pair
        patches, texts = target.at[pair, pl.ds(0, slots)], target.at[pair, pl.ds(slots, tail)]
        near = lambda src, dst: pltpu.make_async_copy(src, dst, r.load_sem.at[index])
        return (
            hop("x", source.at[0, pair], patches, sems, index),
            hop("x", source.at[0, pairs + pair, pl.ds(0, tail)], texts, sems, index),
            near(source.at[0, pairs + pair], patches),
            near(source.at[0, pair, pl.ds(0, tail)], texts),
        )

    every_move = [(which, pair) for which in range(2) for pair in range(pairs)]
    weights = [
        pltpu.make_async_copy(source, target, r.load_sem.at[2 * pairs + index])
        for index, (source, target) in enumerate(((r.wqkv_in, r.wqkv), (r.wout_in, r.wout)))
    ]
    pl.semaphore_wait(barrier, 1)

    @pl.when(here["x"] == 1)
    def _():
        for move in every_move:
            moves(*move)[0].start()
        for move in every_move:
            moves(*move)[2].start()

    @pl.when(here["x"] == 0)
    def _():
        for move in every_move:
            moves(*move)[1].start()
        for move in every_move:
            moves(*move)[3].start()

    for copy in weights:
        copy.start()

    def arrived(which, pair):
        @pl.when(here["x"] == 1)
        def _():
            moves(which, pair)[1].wait_recv()
            moves(which, pair)[2].wait()

        @pl.when(here["x"] == 0)
        def _():
            moves(which, pair)[0].wait_recv()
            moves(which, pair)[3].wait()

    place_at = lax.broadcasted_iota(jnp.int32, (width, 1), 0)
    feature = lax.broadcasted_iota(jnp.int32, (width, width), 1)
    unit = width // 32
    block = place_at // unit
    bit = lambda shift: (block >> shift) & 1
    owner = (bit(0) << 4) + (bit(2) << 3) + (bit(3) << 2) + (bit(4) << 1) + bit(1)
    owner = owner ^ (lax.axis_index("pairs") * 2 + here["x"])
    source = owner * unit + (place_at - block * unit)
    r.order[...] = (source == feature).astype(F32).astype(BF16)
    row = 0
    for index in range(9):
        part = getattr(r, str(index))
        for first in range(0, part.shape[0], width):
            r.vecs[row : row + 1, :] = part[first : first + width].reshape(1, width)
            row += 1
    vec = lambda index: r.vecs[index : index + 1, :]
    for copy in weights:
        copy.wait()
    for pair in range(pairs):
        arrived(0, pair)
        tokens = r.seq[pair].astype(F32)
        normed, _ = norm_parts(tokens)
        normal = (normed * vec(0) + vec(1)).astype(BF16)
        r.normal[pair] = normal
        for part, ref in enumerate((r.q_out, r.k_out, r.v_out)):
            made = dot(normal, r.wqkv[:, part * width : (part + 1) * width])
            if part == 0:
                made = (made + vec(2)) * 0.125
            if part == 2:
                made = made + vec(3)
            ref[pair] = made.astype(BF16)

        def step(group, carry):
            mix_heads(pair, group, lens[pair], lens[pairs + pair], slots, r.q_out, r.k_out, r.v_out, r.mixed)
            return carry

        lax.fori_loop(0, width // 128, step, 0)
        made = r.seq[pair].astype(F32) + dot(r.mixed[pair], r.wout[...]) + vec(4)
        r.hidden[pair * rows : (pair + 1) * rows, :] = made
    stores = [
        pltpu.make_async_copy(getattr(r, name), getattr(r, str(20 + index)), r.store_sem.at[index])
        for index, name in enumerate(STORED)
    ]
    for copy in stores[:6]:
        copy.start()
    r.mixed_out[...] = dot(r.order[...], r.mixed[...].reshape(every, width), 1, 1).astype(BF16)
    r.normal_out[...] = dot(r.order[...], r.normal[...].reshape(every, width), 1, 1).astype(BF16)
    normed, _ = norm_parts(r.hidden[...])
    made = (normed * vec(5) + vec(6)).astype(BF16)
    r.normal2[...] = made
    r.normal2_t[...] = dot(r.order[...], made, 1, 1).astype(BF16)
    for copy in stores[6:10]:
        copy.start()
    for pair in range(pairs):
        arrived(1, pair)
    stores[10].start()

    @pl.when(here["x"] == 1)
    def _():
        for move in every_move:
            moves(*move)[0].wait_send()

    @pl.when(here["x"] == 0)
    def _():
        for move in every_move:
            moves(*move)[1].wait_send()

    for copy in stores:
        copy.wait()


def run_opening(text_len, patch_count, inputs, cotangent, parts, wqkv, wout):
    _, group, slots, width = inputs.shape
    pairs = group // 2
    rows = padded(TEXT + slots)
    every = pairs * rows
    hbm = pl.BlockSpec(memory_space=pl.ANY)
    operands = dict(
        text_len=(text_len, smem_spec()),
        patch_count=(patch_count, smem_spec()),
        inputs=(inputs, hbm),
        cotangent=(cotangent, hbm),
        wqkv_in=(wqkv, hbm),
        wout_in=(wout, hbm),
    )
    operands.update((index, (part, whole_spec())) for index, part in enumerate(parts))
    count = sum(part.shape[0] for part in parts) // width
    cube = shape((pairs, rows, width), BF16)
    tall = shape((width, every), BF16)
    outs = dict(
        vecs=(shape((count, width), F32), whole_spec()),
    )
    long = shape((every, width), F32)
    flat = shape((every, width), BF16)
    square = shape((width, width), BF16)
    kinds = [cube, cube, cube, long, cube, square, tall, tall, flat, tall, cube]
    outs.update((20 + index, (kind, hbm)) for index, kind in enumerate(kinds))
    held = pltpu.VMEM((pairs, rows, width), BF16)
    scratch = dict(
        seq=held,
        cot=held,
        mixed=held,
        normal=held,
        q_out=held,
        k_out=held,
        v_out=held,
        hidden=pltpu.VMEM(long.shape, F32),
        order=pltpu.VMEM(square.shape, BF16),
        mixed_out=pltpu.VMEM(tall.shape, BF16),
        normal_out=pltpu.VMEM(tall.shape, BF16),
        normal2=pltpu.VMEM(flat.shape, BF16),
        normal2_t=pltpu.VMEM(tall.shape, BF16),
        wqkv=pltpu.VMEM(wqkv.shape, BF16),
        wout=pltpu.VMEM(wout.shape, BF16),
        send_sem=pltpu.SemaphoreType.DMA((2 * pairs,)),
        recv_sem=pltpu.SemaphoreType.DMA((2 * pairs,)),
        load_sem=pltpu.SemaphoreType.DMA((2 * pairs + 2,)),
        store_sem=pltpu.SemaphoreType.DMA((len(kinds),)),
    )
    names = [str(name) for name in (*operands, *outs, *scratch)]
    return pl.pallas_call(
        functools.partial(opening_kernel, pairs, slots, names),
        out_shape=[kind for kind, _ in outs.values()],
        in_specs=[spec for _, spec in operands.values()],
        out_specs=[spec for _, spec in outs.values()],
        scratch_shapes=list(scratch.values()),
        compiler_params=pltpu.CompilerParams(collective_id=2, has_side_effects=True, vmem_limit_bytes=VMEM_LIMIT),
        name="opening",
    )(*[value for value, _ in operands.values()])


A, B, C, O, H, V, R = range(7)
PLAN = {
    3: [(A, 0, 0)],
    4: [(B, 0, 0)],
    5: [(A, 0, 1)],
    6: [(B, 1, 0)],
    7: [(A, 1, 0)],
    8: [(A, 0, 2), (B, 2, 0), (B, 2, 1)],
    9: [(A, 1, 1)],
    10: [(B, 3, 0), (B, 3, 1)],
    11: [(A, 2, 0)],
    12: [(B, 3, 2), (B, 4, 0)],
    13: [(A, 1, 2), (A, 2, 1), (B, 2, 2)],
    14: [(B, 0, 1), (B, 3, 3), (B, 5, 0)],
    15: [(A, 3, 0), (B, 1, 1)],
    16: [(A, 0, 3), (A, 2, 2), (B, 1, 2), (B, 2, 3), (B, 6, 0), (B, 6, 1), (A, 3, 1), (R, 0, 0)],
    17: [(R, 0, 1)],
    18: [(B, 1, 3), (B, 7, 0), (B, 7, 1), (H, 0, 0), (R, 0, 2)],
    19: [(R, 0, 3)],
    20: [(R, 0, 4)],
    21: [(B, 0, 2), (O, 0, 0), (R, 0, 5)],
    22: [(B, 7, 2), (B, 6, 2), (A, 3, 2), (C, 0, 0)],
    23: [(B, 0, 3)],
    24: [(C, 1, 0), (B, 4, 1), (R, 0, 6)],
    25: [(B, 6, 3), (B, 7, 3), (B, 6, 4), (B, 7, 4), (R, 0, 7)],
    26: [(B, 5, 1)],
    27: [(A, 1, 3), (O, 0, 1), (C, 1, 1), (C, 2, 0), (H, 0, 1), (A, 0, 4), (B, 2, 4), (B, 3, 4), (C, 0, 1), (R, 0, 8)],
    28: [(B, 5, 2), (R, 0, 9)],
    29: [(B, 4, 2), (H, 0, 2), (R, 1, 0)],
    30: [(C, 0, 2), (O, 0, 2), (C, 3, 0), (B, 5, 3), (B, 5, 4)],
    31: [(C, 1, 2), (C, 4, 0)],
    32: [(B, 4, 3), (H, 0, 3), (B, 4, 4), (R, 1, 1)],
}
TAIL = [
    (C, 5, 0), (C, 2, 1), (C, 0, 3), (O, 0, 3), (R, 1, 2), (V, 0, 0),
    (C, 1, 3), (C, 3, 1), (R, 1, 3), (C, 4, 1), (B, 1, 4), (C, 2, 2),
    (V, 0, 1), (R, 1, 4), (B, 0, 4), (C, 5, 1), (H, 0, 4), (C, 3, 2),
    (C, 0, 4), (C, 2, 3), (R, 2, 0), (C, 4, 2), (V, 0, 2), (O, 0, 4),
    (C, 5, 2), (C, 1, 4), (C, 3, 3), (C, 4, 3), (R, 2, 1), (V, 0, 3),
    (C, 5, 3), (R, 2, 2), (C, 2, 4), (C, 3, 4), (C, 4, 4), (R, 2, 3),
    (V, 0, 4), (C, 5, 4), (R, 2, 4),
]


def fused_kernel(pairs, slots, names, *refs):
    r = types.SimpleNamespace(**dict(zip(names, refs)))
    rows, width = r.seq.shape[1:]
    every = pairs * rows
    tail = rows - slots
    here = place()
    lens = counts(here, pairs, r.text_len, r.patch_count)
    vec_in = lambda index: r.vecs[index : index + 1, :]
    sems = (r.send_sem, r.recv_sem)
    barrier = pltpu.get_barrier_semaphore()
    for bit in BITS:
        pl.semaphore_signal(barrier, inc=1, device_id=partner(bit), device_id_type=pl.DeviceIdType.MESH)

    def load(name, target, index):
        return pltpu.make_async_copy(getattr(r, name), getattr(r, target), r.load_sem.at[index])

    early = [
        load("normal2_in", "normal2", 0),
        load("cot_in", "cot", 1),
        load("normal2_t_in", "normal2_t", 2),
        load("hidden_in", "hidden", 9),
    ]
    late = [
        load("mixed_in", "mixed_t", 3),
        load("normal_in", "normal_t", 4),
        load("seq_in", "seq", 5),
        load("q_in", "q", 6),
        load("k_in", "k", 7),
        load("v_in", "v", 8),
        load("order_in", "order", 10),
    ]

    def block_of(t):
        z1, z0 = 1 - t // 2, 1 - t % 2
        return flip(z0, here["z0"]) + 2 * flip(z1, here["z1"])

    def weight_loads(t, slot):
        start = pl.multiple_of(block_of(t) * width, width)
        return (
            pltpu.make_async_copy(r.wh.at[:, pl.ds(start, width)], r.wbuf.at[slot], r.w_sem.at[slot]),
            pltpu.make_async_copy(r.wd.at[pl.ds(start, width), :], r.wbuf.at[2 + slot], r.w_sem.at[2 + slot]),
        )

    early[0].start()
    for copy in weight_loads(0, 0):
        copy.start()
    for copy in early[1:]:
        copy.start()
    r.gnormal[...] = jnp.zeros_like(r.gnormal)
    live = live_rows(lens, pairs, rows, slots)
    r.total[...] = jnp.zeros_like(r.total)
    for copy in early[:3]:
        copy.wait()
    r.gdown[...] = (r.cot[...].reshape(every, width).astype(F32) * live).astype(BF16)
    r.unit_h[...] = jnp.zeros_like(r.unit_h)
    for copy in late:
        copy.start()
    pl.semaphore_wait(barrier, len(BITS))

    arrivals = lambda name, index: [getattr(r, name + str(step)).at[index] for step in range(5)]

    a_core = lambda t, y: hop("core", r.a_own.at[t, 1, y], r.a_core.at[t, y], sems, 2 * t + y)
    a_y = lambda t: hop("y", r.a_own.at[t, 0, 1], r.a_y.at[t], sems, 8 + t)
    a_z0 = lambda k: hop("z0", r.a_own.at[2 * k, 0, 0], r.a_z0.at[k], sems, 12 + k)
    a_x = lambda k: hop("x", r.a_own.at[2 * k + 1, 0, 0, 1], r.a_x.at[k], sems, 14 + k)
    a_z1 = lambda: hop("z1", r.a_own.at[1, 0, 0, 0], r.a_z1.at[0], sems, 16)

    def a_core_sum(t, y):
        a_core(t, y).wait_recv()
        accumulate(r.a_own.at[t, 0, y], r.a_core.at[t, y])
        if y == 1:
            a_y(t).start()

    def a_second(t):
        k = t // 2
        a_y(t).wait_recv()
        accumulate(r.a_own.at[t, 0, 0], r.a_y.at[t])
        if t % 2 == 0:
            a_z0(k).start()
        else:
            a_z0(k).wait_recv()
            accumulate(r.a_own.at[t, 0, 0], r.a_z0.at[k])
            a_x(k).start()

    def a_third(k):
        a_x(k).wait_recv()
        accumulate(r.a_own.at[2 * k + 1, 0, 0, pl.ds(0, 1)], r.a_x.at[pl.ds(k, 1)])
        if k == 0:
            a_z1().start()

    def a_last():
        a_z1().wait_recv()
        r.out_a[...] = r.a_own[3, 0, 0, 0].astype(F32) + r.a_z1[0].astype(F32)

    size = width // 2

    def b_columns(u):
        return block_of(u // 2) * width + flip(1 - u % 2, here["y"]) * size

    def b_finish(u):
        def finish(value):
            r.out_b[:, :, pl.ds(pl.multiple_of(b_columns(u), 128), size)] = value

        return finish

    def c_finish(g):
        def finish(value):
            for part in range(3):
                cols = slice(part * width + 128 * g, part * width + 128 * g + 128)
                r.out_c[:, :, cols] = value[:, :, 128 * part : 128 * part + 128]

        return finish

    def plain(target):
        def finish(value):
            target[...] = value

        return finish

    units = {}
    for u in range(8):
        units[B, u] = Unit(r.b_own.at[u], arrivals("b", u), ORDERS[1], sems, 20 + 5 * u, b_finish(u))
    for u in range(8):
        units[B, u].peers = {"y": units[B, u ^ 1], "z0": units[B, u ^ 2], "z1": units[B, u ^ 4]}
    groups = width // 128
    for g in range(groups):
        units[C, g] = Unit(r.c_own.at[g], arrivals("c", g), ORDERS[(1, 0, 1, 1, 0, 1)[g]], sems, 60 + 5 * g, c_finish(g))
    units[O, 0] = Unit(r.o_own, arrivals("o", 0), ORDERS[0], sems, 90, plain(r.out_o))
    units[H, 0] = Unit(r.unit_h, arrivals("h", 0), ORDERS[1], sems, 95, plain(r.out_v.at[pl.ds(1, 1)]))
    units[V, 0] = Unit(r.unit_v, arrivals("v", 0), ORDERS[0], sems, 100, plain(r.out_v.at[pl.ds(0, 1)]))

    def give(source, target, pair, index):
        near = lambda src, dst: pltpu.make_async_copy(src, dst, r.give_sem.at[index])
        part = lambda first, count: hop(
            "x", source.at[pair, pl.ds(first, count)], target.at[0, pair, pl.ds(first, count)], sems, 105 + index
        )
        patches, texts = source.at[pair, pl.ds(0, slots)], source.at[pair, pl.ds(slots, tail)]
        far_texts = hop("x", texts, target.at[0, pairs + pair, pl.ds(0, tail)], sems, 105 + index)
        near_texts = lambda: near(texts, target.at[0, pair, pl.ds(0, tail)])
        near_patches = lambda: near(patches, target.at[0, pairs + pair])
        return part, far_texts, near_texts, near_patches

    gives = [give(r.result, r.block_out, pair, pair) for pair in range(pairs)]
    gives += [give(r.grad_rows, r.input_grad, pair, pairs + pair) for pair in range(pairs)]

    def give_start(index):
        _, far_texts, near_texts, near_patches = gives[index]

        @pl.when(here["x"] == 0)
        def _():
            near_texts().start()

        @pl.when(here["x"] == 1)
        def _():
            far_texts.start()
            near_patches().start()

    def give_part(index, piece):
        @pl.when(here["x"] == 0)
        def _():
            gives[index][0](tail * piece, tail).start()

    def give_wait(index):
        part, far_texts, near_texts, near_patches = gives[index]

        @pl.when(here["x"] == 0)
        def _():
            far_texts.wait_recv()
            part(0, slots).wait_send()
            near_texts().wait()

        @pl.when(here["x"] == 1)
        def _():
            part(0, slots).wait_recv()
            far_texts.wait_send()
            near_patches().wait()

    def act(kind, piece, step):
        if kind == R:
            pieces = slots // tail
            give_part(step // pieces if piece == 0 else pairs + piece - 1, step % pieces)
        elif kind != A:
            units[kind, piece].advance(step)
        elif step < 2:
            a_core_sum(piece, 1 - step)
        else:
            (a_second, a_third, lambda _: a_last())[step - 2](piece)

    def run_now(tick):
        for item in PLAN.get(tick, []):
            act(*item)

    def run_tasks(ticks, now):
        for tick in ticks:
            if tick in PLAN:

                @pl.when(now == tick)
                def _(tick=tick):
                    run_now(tick)

    def feed_step(t, carry):
        slot = t % 2
        for copy in weight_loads(t, slot):
            copy.wait()

        @pl.when(t < 3)
        def _():
            for copy in weight_loads(t + 1, 1 - slot):
                copy.start()

        for sub in range(2):
            run_tasks([4 * k + 2 * sub for k in range(4)], 4 * t + 2 * sub)
            y = 1 - sub
            part = flip(y, here["y"])
            start = pl.multiple_of(part * size, size)
            wh = r.wbuf[slot, :, pl.ds(start, size)]
            wd = r.wbuf[2 + slot, pl.ds(start, size), :]
            before = dot(r.normal2[...], wh) + r.vecs[pl.ds(8 + block_of(t), 1), pl.ds(start, size)]
            active, slope = gelu_parts(before)
            active = active.astype(BF16)
            r.total[...] += dot(active, wd)
            fresh = dot(active, r.gdown[...], 0, 0)
            quarter = size // 4
            for core in range(2):
                for mod in range(2):
                    first = (2 * core + mod) * quarter
                    piece = fresh[first : first + quarter].reshape(quarter // 8, 8, width)
                    r.a_own[t, flip(core, here["core"]), y, flip(mod, here["x"])] = piece.astype(BF16)
            a_core(t, y).start()
            run_tasks([4 * k + 2 * sub + 1 for k in range(4)], 4 * t + 2 * sub + 1)
            gbefore = (dot(r.gdown[...], wd, 1, 1) * slope).astype(BF16)
            r.gnormal[...] += dot(gbefore, wh, 1, 1)
            fresh = dot(r.normal2_t[...], gbefore)
            fresh = fresh.reshape((2,) * 5 + (width // 256, 8, size)).astype(BF16)
            unit = 2 * t + sub
            r.b_own[unit] = fresh
            hop("core", r.b_own.at[unit, 1], r.b0.at[unit], sems, 20 + 5 * unit).start()
            sums = jnp.sum(gbefore.astype(F32), axis=0, keepdims=True)
            z1, z0 = 1 - t // 2, 1 - t % 2
            for core in range(2):
                for mod in range(2):
                    first = (2 * core + mod) * quarter
                    r.unit_h[
                        flip(core, here["core"]), y, z0, flip(mod, here["x"]), z1, 0, 0:1, 0:quarter
                    ] = sums[:, first : first + quarter]
        return carry

    lax.fori_loop(0, 4, feed_step, 0)

    wout_load = pltpu.make_async_copy(r.wout, r.wbuf.at[3], r.w_sem.at[3])
    wout_load.start()
    wqkv_loads = [
        pltpu.make_async_copy(
            r.wqkv.at[:, pl.ds(part * width, width)], r.wbuf.at[part], r.w_sem.at[part]
        )
        for part in range(3)
    ]
    for copy in wqkv_loads:
        copy.start()
    units[H, 0].start()
    early[3].wait()
    r.result[...] = ((r.hidden[...] + r.total[...] + vec_in(7)) * live).astype(BF16).reshape(pairs, rows, width)

    for pair in range(pairs):
        give_start(pair)
    run_now(16)
    normed, factor = norm_parts(r.hidden[...])
    gnorm = r.gnormal[...]
    down = r.gdown[...].astype(F32)
    vec = [
        jnp.sum(gnorm * normed, axis=0, keepdims=True),
        jnp.sum(gnorm, axis=0, keepdims=True),
        jnp.sum(down, axis=0, keepdims=True),
    ]
    made = down + norm_back(gnorm, normed, factor, vec_in(5))
    gattended = made.astype(BF16)
    vec.append(jnp.sum(gattended.astype(F32), axis=0, keepdims=True))
    for index, value in enumerate(vec):
        r.vec[4 + index : 5 + index, :] = value
    r.gnormal[...] = made
    run_now(17)
    wout_load.wait()
    r.gmixed[...] = dot(gattended, r.wbuf[3], 1, 1).astype(BF16).reshape(pairs, rows, width)
    for copy in late:
        copy.wait()
    fresh = dot(r.mixed_t[...], gattended)
    r.o_own[...] = fresh.reshape((2,) * 5 + (width // 256, 8, width)).astype(BF16)
    units[O, 0].start()
    for copy in wqkv_loads:
        copy.wait()

    first = lax.broadcasted_iota(jnp.int32, (rows, 128), 1) < HEAD_DIM
    index = lax.broadcasted_iota(jnp.int32, (rows, 1), 0)

    def project_back(pair):
        made = jnp.zeros((rows, width), F32)
        sums = []
        for part in range(3):
            piece = r.gproj[pair, :, part * width : (part + 1) * width]
            made += dot(piece, r.wbuf[part], 1, 1)
            sums.append(jnp.sum(piece.astype(F32), axis=0, keepdims=True))
        return made, sums

    def finish_pair(pair, grad, sums):
        normed, factor = norm_parts(r.seq[pair].astype(F32))
        sums = [
            jnp.sum(grad * normed, axis=0, keepdims=True),
            jnp.sum(grad, axis=0, keepdims=True),
            sums[0],
            sums[2],
        ]
        for index, value in enumerate(sums):
            r.vec[index : index + 1, :] = value if pair == 0 else r.vec[index : index + 1, :] + value
        span = slice(pair * rows, (pair + 1) * rows)
        made = r.gnormal[span, :] + norm_back(grad, normed, factor, vec_in(0))
        r.grad_rows[pair] = (made * live[span]).astype(BF16)
        give_start(pairs + pair)

    def head_step(it, carry):
        late = it // groups
        pair = (1 - late) * (it % 2) + it // 9
        g = (1 - late) * (it // 2) + late * (3 + it % 3)
        base = g * 128
        off = pl.multiple_of(base, 128)

        @pl.when(it == 9)
        def _():
            finish_pair(0, *project_back(0))

        run_tasks([18 + k for k in range(pairs * groups)], 18 + it)
        at_pair = here["x"] * pairs + pair
        keys_live = live_slots(index, r.text_len[at_pair], r.patch_count[at_pair], slots)
        q2 = r.q[pair, :, pl.ds(off, 128)]
        k2 = r.k[pair, :, pl.ds(off, 128)]
        v2 = r.v[pair, :, pl.ds(off, 128)]
        g2 = r.gmixed[pair, :, pl.ds(off, 128)]
        gq = gk = gv = None
        for half in range(2):
            keep = first if half == 0 else ~first
            zero = jnp.zeros_like(q2)
            qm = jnp.where(keep, q2, zero)
            km = jnp.where(keep, k2, zero)
            gm = jnp.where(keep, g2, zero)
            scores = jnp.where(keys_live, dot(k2, qm, 1, 1), MASKED)
            highest = jnp.max(scores, axis=0, keepdims=True)
            shifted = jnp.exp(scores - highest)
            probs = shifted * (1.0 / jnp.sum(shifted, axis=0, keepdims=True))
            gprobs = dot(v2, gm, 1, 1)
            row_dot = jnp.sum(probs * gprobs, axis=0, keepdims=True)
            gscores = (probs * (gprobs - row_dot)).astype(BF16)
            new_v = dot(probs.astype(BF16), gm)
            new_k = dot(gscores, qm)
            new_q = dot(gscores, km, 0, 0)
            gq = new_q if gq is None else gq + new_q
            gk = new_k if gk is None else gk + new_k
            gv = new_v if gv is None else gv + new_v
        r.gproj[pair, :, pl.ds(off, 128)] = (gq * 0.125).astype(BF16)
        r.gproj[pair, :, pl.ds(pl.multiple_of(base + width, 128), 128)] = gk.astype(BF16)
        r.gproj[pair, :, pl.ds(pl.multiple_of(base + 2 * width, 128), 128)] = gv.astype(BF16)

        @pl.when(pair == pairs - 1)
        def _():
            pieces = [
                r.gproj[:, :, pl.ds(pl.multiple_of(base + part * width, 128), 128)].reshape(every, 128)
                for part in range(3)
            ]
            fresh = dot(r.normal_t[...], jnp.concatenate(pieces, axis=1))
            r.c_own[g] = fresh.reshape((2,) * 5 + (width // 256, 8, 384)).astype(BF16)
            hop("core", r.c_own.at[g, 1], r.c0.at[g], sems, 60 + 5 * g).start()

        return carry

    lax.fori_loop(0, pairs * groups, head_step, 0)

    run_now(30)
    made, sums = project_back(1)
    run_now(31)
    finish_pair(1, made, sums)
    rest = r.vec[...]
    ordered = jnp.zeros_like(rest)
    for _ in range(3):
        high = rest.astype(BF16)
        ordered += dot(high, r.order[...], 1, 1)
        rest = rest - high.astype(F32)
    r.unit_v[...] = jnp.zeros_like(r.unit_v)
    unit = width // 32
    for block in range(32):
        bits = tuple(block >> shift & 1 for shift in (4, 3, 2, 1, 0))
        r.unit_v[bits + (0, slice(None), slice(0, unit))] = ordered[:, block * unit : (block + 1) * unit]
    units[V, 0].start()
    run_now(32)
    for item in TAIL:
        act(*item)
    for number in range(2 * pairs):
        give_wait(number)
    for t in range(4):
        a_core(t, 0).wait_send()
        a_core(t, 1).wait_send()
        a_y(t).wait_send()
    for k in range(2):
        a_z0(k).wait_send()
        a_x(k).wait_send()
    a_z1().wait_send()
    for unit in units.values():
        unit.drain()


def run_fused(text_len, patch_count, vecs, hidden, cot, wh, wd, order, wqkv, wout, seq, q, k, v, mixed_t, normal_t, normal2, normal2_t, slots):
    pairs, rows, width = seq.shape
    every = pairs * rows
    wide = (2,) * 5
    eight = width // 256
    groups = width // 128

    def arrivals(name, count, tail, kind):
        return {name + str(step): pltpu.VMEM((count,) + (2,) * (4 - step) + tail, kind) for step in range(5)}

    flat = lambda kind: pltpu.VMEM((every, width), kind)
    cube = pltpu.VMEM((pairs, rows, width), BF16)
    tall = pltpu.VMEM((width, every), BF16)
    block = (width // 64, 8, width)
    scratch = dict(
        cot=cube,
        result=cube,
        grad_rows=cube,
        give_sem=pltpu.SemaphoreType.DMA((2 * pairs,)),
        hidden=flat(F32),
        gdown=flat(BF16),
        seq=cube,
        q=cube,
        k=cube,
        v=cube,
        mixed_t=tall,
        normal_t=tall,
        wbuf=pltpu.VMEM((4, width, width), BF16),
        order=pltpu.VMEM((width, width), BF16),
        normal2=flat(BF16),
        normal2_t=tall,
        total=flat(F32),
        gnormal=flat(F32),
        gmixed=cube,
        gproj=pltpu.VMEM((pairs, rows, 3 * width), BF16),
        vec=pltpu.VMEM((8, width), F32),
        a_own=pltpu.VMEM((4, 2, 2, 2) + block, BF16),
        a_core=pltpu.VMEM((4, 2, 2) + block, BF16),
        a_y=pltpu.VMEM((4, 2) + block, BF16),
        a_z0=pltpu.VMEM((2, 2) + block, BF16),
        a_x=pltpu.VMEM((2,) + block, BF16),
        a_z1=pltpu.VMEM((1,) + block, BF16),
        b_own=pltpu.VMEM((8,) + wide + (eight, 8, width // 2), BF16),
        **arrivals("b", 8, (eight, 8, width // 2), BF16),
        c_own=pltpu.VMEM((groups,) + wide + (eight, 8, 384), BF16),
        **arrivals("c", groups, (eight, 8, 384), BF16),
        o_own=pltpu.VMEM(wide + (eight, 8, width), BF16),
        **arrivals("o", 1, (eight, 8, width), BF16),
        unit_h=pltpu.VMEM(wide + (1, 8, 128), F32),
        **arrivals("h", 1, (1, 8, 128), F32),
        unit_v=pltpu.VMEM(wide + (1, 8, 128), F32),
        **arrivals("v", 1, (1, 8, 128), F32),
        send_sem=pltpu.SemaphoreType.DMA((105 + 2 * pairs,)),
        recv_sem=pltpu.SemaphoreType.DMA((105 + 2 * pairs,)),
        load_sem=pltpu.SemaphoreType.DMA((11,)),
        w_sem=pltpu.SemaphoreType.DMA((4,)),
    )
    hbm = pl.BlockSpec(memory_space=pl.ANY)
    operands = dict(
        text_len=(text_len, smem_spec()),
        patch_count=(patch_count, smem_spec()),
        vecs=(vecs, whole_spec()),
        hidden_in=(hidden, hbm),
        cot_in=(cot, hbm),
        wh=(wh, hbm),
        wd=(wd, hbm),
        order_in=(order, hbm),
        wqkv=(wqkv, hbm),
        wout=(wout, hbm),
        seq_in=(seq, hbm),
        q_in=(q, hbm),
        k_in=(k, hbm),
        v_in=(v, hbm),
        mixed_in=(mixed_t, hbm),
        normal_in=(normal_t, hbm),
        normal2_in=(normal2, hbm),
        normal2_t_in=(normal2_t, hbm),
    )
    final = shape((1, 2 * pairs, slots, width), BF16)
    outs = dict(
        block_out=(final, hbm),
        input_grad=(final, hbm),
        out_a=(shape(block, F32), whole_spec()),
        out_b=(shape((eight, 8, 4 * width), F32), whole_spec()),
        out_c=(shape((eight, 8, 3 * width), F32), whole_spec()),
        out_o=(shape((eight, 8, width), F32), whole_spec()),
        out_v=(shape((2, 8, 128), F32), whole_spec()),
    )
    names = list(operands) + list(outs) + list(scratch)
    return pl.pallas_call(
        functools.partial(fused_kernel, pairs, slots, names),
        out_shape=[kind for kind, _ in outs.values()],
        in_specs=[spec for _, spec in operands.values()],
        out_specs=[spec for _, spec in outs.values()],
        scratch_shapes=list(scratch.values()),
        compiler_params=pltpu.CompilerParams(
            collective_id=1, has_side_effects=True, vmem_limit_bytes=67043328
        ),
        name="fused",
    )(*[value for value, _ in operands.values()])


def closing_kernel(*refs):
    count = len(refs) // 2
    for index in range(count):
        value = refs[index][...]
        if index < 2:
            slot = lax.broadcasted_iota(jnp.int32, value.shape, 2)
            last = TEXT + lax.axis_index("mod") * value.shape[2]
            value = jnp.where(slot < last, value, jnp.zeros_like(value))
        refs[count + index][...] = value


def run_closing(*arrays):
    return pl.pallas_call(
        closing_kernel,
        out_shape=[shape(array.shape, array.dtype) for array in arrays],
        in_specs=[whole_spec()] * len(arrays),
        out_specs=[whole_spec()] * len(arrays),
        name="closing",
    )(*arrays)


def pair_bits():
    return lax.axis_size("pairs").bit_length() - 1


def swapped(array, axis, bit):
    size = lax.axis_size(axis)
    return lax.ppermute(array, axis, [(i, i ^ (1 << bit)) for i in range(size)])


def split_dims(array):
    bits = pair_bits() + 1
    return array.reshape((2,) * bits + (array.shape[0] >> bits,) + array.shape[1:])


def stage_orders():
    bits = pair_bits()
    ring = ["mod", 1, 2]
    orders = []
    for turn in range(3):
        orders.append([0] + ring[turn:] + ring[:turn] + list(range(3, bits)))
    return orders


def half_sum(array, names, name, last):
    axis, bit = ("mod", 0) if name == "mod" else ("pairs", name)
    mine = (lax.axis_index(axis) >> bit) & 1
    dim = names.index(name)
    sent = lax.dynamic_index_in_dim(array, 1 - mine, dim, keepdims=False)
    kept = lax.dynamic_index_in_dim(array, mine, dim, keepdims=False)
    came = swapped(sent, axis, bit)
    total = kept.astype(F32) + came.astype(F32)
    return (total if last else total.astype(BF16)), names[:dim] + names[dim + 1 :]


def scattered(array):
    width = array.shape[1]
    names0 = list(range(pair_bits() - 1, -1, -1)) + ["mod"]
    first, names1 = half_sum(split_dims(array), names0, 0, False)
    third = -(-width // 3 // 128) * 128
    pieces = []
    for turn, order in enumerate(stage_orders()):
        piece = first[..., turn * third : min(width, (turn + 1) * third)]
        names = list(names1)
        for place, name in enumerate(order[1:]):
            piece, names = half_sum(piece, names, name, place == len(order) - 2)
        pieces.append(piece)
    return jnp.concatenate(pieces, axis=1)


def on_device(
    inputs,
    cotangent,
    text_len,
    patch_count,
    norm1_gain,
    norm1_bias,
    qkv_weight,
    query_bias,
    value_bias,
    out_weight,
    out_bias,
    norm2_gain,
    norm2_bias,
    hidden_weight,
    hidden_bias,
    down_weight,
    down_bias,
):
    _, group, slots, width = inputs.shape
    half = group // 2
    rows = padded(TEXT + slots)
    mod = lax.axis_index("mod")
    is_text = mod == 0
    lens = lax.dynamic_slice_in_dim(jnp.stack([text_len, patch_count]), mod * half, half, 1)
    lens = lens.reshape(-1)

    def gathered(array):
        local = array[0]
        patches = lax.ppermute(local[:half], "mod", [(1, 0)])
        texts = lax.ppermute(local[half:, :TEXT], "mod", [(0, 1)])
        patches = jnp.where(is_text, patches, local[half:])
        texts = jnp.where(is_text, local[:half, :TEXT], texts)
        blank = jnp.zeros((half, rows - slots - TEXT, width), array.dtype)
        return jnp.concatenate([patches, texts, blank], axis=1)

    def returned(array):
        far_patches = lax.ppermute(array[:, :slots], "mod", [(0, 1)])
        far_texts = lax.ppermute(array[:, slots : slots + TEXT], "mod", [(1, 0)])
        return assembled(array, far_patches, far_texts)

    def assembled(array, far_patches, far_texts):
        patches, texts = array[:, :slots], array[:, slots : slots + TEXT]
        texts = jnp.concatenate([texts, far_texts], axis=0)
        texts = jnp.pad(texts, ((0, 0), (0, slots - TEXT), (0, 0)))
        patches = jnp.concatenate([far_patches, patches], axis=0)
        return jnp.where(is_text, texts, patches)[None]

    row = lambda vector: vector.reshape(1, -1)
    if lax.axis_size("pairs") == 16:
        parts = [norm1_gain, norm1_bias, query_bias, value_bias, out_bias, norm2_gain, norm2_bias, down_bias, hidden_bias]
        made = run_opening(text_len, patch_count, inputs, cotangent, parts, qkv_weight, out_weight)
        vecs, q, k, v, hidden, seq, order, mixed, normal, normal2, normal2_t, cot = made
        made = run_fused(
            text_len,
            patch_count,
            vecs,
            hidden,
            cot,
            hidden_weight,
            down_weight,
            order,
            qkv_weight,
            out_weight,
            seq,
            q,
            k,
            v,
            mixed,
            normal,
            normal2,
            normal2_t,
            slots,
        )
        block_out, input_grad, wd_out, wh_out, qkv_out, wo_out, vectors = made
        flat = lambda array: array.reshape(-1, array.shape[-1])
        wd_out, wh_out, qkv_out, wo_out = flat(wd_out), flat(wh_out), flat(qkv_out), flat(wo_out)
        made = run_closing(block_out, input_grad, wd_out, wh_out, qkv_out, wo_out)
        block_out, input_grad, wd_out, wh_out, qkv_out, wo_out = made
        vec_out = [vectors[0, index, : width // 32] for index in range(8)]
        hb_out = vectors[1, 0, : hidden_bias.shape[0] // 32]
    else:
        seq = gathered(inputs)
        cot = gathered(cotangent).reshape(half * rows, width)
        qkv_bias = row(jnp.concatenate([query_bias, jnp.zeros_like(query_bias), value_bias]))
        feature = jnp.arange(width, dtype=jnp.int32)
        order = (feature[:, None] == feature[None, :]).astype(BF16)
        q, k, v, hidden, mixed = run_forward(
            lens, seq, row(norm1_gain), row(norm1_bias), qkv_weight, qkv_bias, out_weight, row(out_bias), slots
        )
        chunks = 8
        steps = jnp.arange(chunks, dtype=jnp.int32)
        lens = jnp.concatenate([lens, jnp.zeros(4, jnp.int32), steps])
        result, ghidden, wh_grad, wd_grad, hb_grad, vec2 = run_feed(
            lens,
            hidden,
            cot,
            row(norm2_gain),
            row(norm2_bias),
            hidden_weight,
            row(hidden_bias),
            down_weight,
            row(down_bias),
            order,
            half,
            slots,
            chunks,
            False,
        )
        block_out = returned(result.reshape(half, rows, width))
        input_rows, qkvo_grad, vec1 = run_backward(
            lens,
            seq,
            row(norm1_gain),
            row(norm1_bias),
            q,
            k,
            v,
            mixed,
            ghidden,
            qkv_weight,
            out_weight,
            order,
            slots,
            False,
        )
        input_grad = returned(input_rows)
        strip = jnp.concatenate([vec1[:4], vec2[:4]], axis=0).T
        strip = jnp.concatenate([strip, hb_grad.reshape(width, -1)], axis=1).astype(BF16)
        strip = jnp.pad(strip, ((0, 0), (0, 128 - strip.shape[1])))
        wd_out, wh_out = scattered(wd_grad), scattered(wh_grad)
        qkvo_out = scattered(jnp.concatenate([qkvo_grad, strip], axis=1))
        vec_out = qkvo_out[:, 4 * width :]
        qkv_out, wo_out = qkvo_out[:, : 3 * width], qkvo_out[:, 3 * width : 4 * width]
        hb_out = vec_out[:, 8 : 8 + hidden_bias.shape[0] // width].reshape(-1)
        vec_out = [vec_out[:, index] for index in range(8)]
    return (
        block_out,
        input_grad,
        vec_out[0],
        vec_out[1],
        qkv_out,
        vec_out[2],
        vec_out[3],
        wo_out,
        vec_out[7],
        vec_out[4],
        vec_out[5],
        wh_out,
        hb_out,
        wd_out,
        vec_out[6],
    )


def solution(mesh):
    whole = P()
    split = P("mod", "pairs", None, None)
    vector = P(("pairs", "mod"))
    matrix = P(("pairs", "mod"), None)
    return jax.shard_map(
        on_device,
        mesh=mesh,
        in_specs=(split, split, P("pairs"), P("pairs")) + (whole,) * 13,
        out_specs=(
            split,
            split,
            vector,
            vector,
            matrix,
            vector,
            vector,
            matrix,
            vector,
            vector,
            vector,
            matrix,
            vector,
            matrix,
            vector,
        ),
        check_vma=False,
    )
```
